32 devices in a mesh: dp: 8 (over z, y), head: 4 (over x, core).
Axes of the slice: x: 2, y: 2, z: 4, core: 2. Of those that a mesh axis runs over, the one named last changes fastest.
Arguments:
- layer_input: bfloat16 [12288, 1024], P('dp'), may hold values from -6 to 6
- proj_weight: bfloat16 [4, 1024, 1024], P(None, None, 'head'), may hold values from -0.1875 to 0.1875
- conv_weight: float32 [3, 4, 1024], P(None, None, 'head'), may hold values from -3 to 3
- persist_kv: float32 [2, 16, 16, 64], P(None, 'head'), may hold values from -4 to 4
- memory_in: float32 [16, 64, 256], P('head'), may hold values from -4 to 4
- memory_out: float32 [16, 256, 64], P('head'), may hold values from -0.375 to 0.375
- memory_gate: float32 [1024, 3, 16], P(None, None, 'head'), may hold values from -3 to 3
- out_weight: bfloat16 [1024, 1024], P(None, 'head'), may hold values from -0.375 to 0.375
- ffn_in: bfloat16 [2, 1024, 4096], P(None, None, 'head'), may hold values from -0.1875 to 0.1875
- ffn_out: bfloat16 [4096, 1024], P('head'), may hold values from -0.09375 to 0.09375
- norm_gains: float32 [2, 1024], replicated, may hold values from 0.5 to 1.5
- seq_len: int32 [8], P('dp'), may hold values from 192 to 1536, as said below
- out_grad: bfloat16 [12288, 1024], P('dp', 'head'), may hold values from -6 to 6
Outputs:
- layer_output: bfloat16 [12288, 1024], P('dp', 'head')
- input_grad: float32 [12288, 1024], P('dp', 'head')
- proj_grad: float32 [4, 1024, 1024], P(None, None, 'head')
- conv_grad: float32 [3, 4, 1024], P(None, None, 'head')
- persist_grad: float32 [2, 16, 16, 64], P(None, 'head')
- memory_in_grad: float32 [16, 64, 256], P('head')
- memory_out_grad: float32 [16, 256, 64], P('head')
- memory_gate_grad: float32 [1024, 3, 16], P(None, None, 'head')
- out_weight_grad: float32 [1024, 1024], P(None, 'head')
- ffn_in_grad: float32 [2, 1024, 4096], P(None, None, 'head')
- ffn_out_grad: float32 [4096, 1024], P('head')
- gains_grad: float32 [2, 1024], replicated
The draws below stay inside these ranges and needn't reach their ends.
Inputs may be any that keep to these rules, and one draw needn't show every extreme that they name: Tokens of sequence g are its first seq_len[g] positions; some sequence fills all 1536 positions.
All inputs are finite; a program needn't handle non-finite values.
Results may differ from the reference program's by a relative error of at most 0.02.
Values may be sent and summed in bfloat16 or wider, within the bound.
No kernel may reach another device: no remote copies, remote signals or barrier semaphores. Data moves between devices by JAX's collectives and lax.ppermute only.
A program may use at most 384 MiB of HBM per device.

```python
import jax
import jax.numpy as jnp
from jax import lax

D = 1024
NH = 16
HS = 64
FF = 4096
MEM_HID = 256
PERSIST = 16
CONV = 4
SPAN = 512
SLOT = 1536
TOKENS = 12288
N_DP = 8


def draw_seq_len(key, part):
    first_key, second_key = jax.random.split(key)
    lengths = jax.random.randint(first_key, (N_DP,), SLOT // 8, SLOT + 1)
    longest = jax.random.randint(second_key, (), 0, N_DP)
    return jnp.where(jnp.arange(N_DP) == longest, SLOT, lengths).astype(jnp.int32)


def steps_of(key, shape, cuts, smallest, high):
    gain, own = 1.0, jax.random.fold_in(key, 6)
    for axis_at, shards_of in cuts:
        heights = jnp.exp(jax.random.uniform(jax.random.fold_in(own, axis_at), (shards_of,), jnp.float32, smallest / len(cuts), high / len(cuts)))
        gain = gain * jnp.repeat(heights, shape[axis_at] // shards_of).reshape([-1 if axis == axis_at else 1 for axis in range(len(shape))])
    return gain


def noise(rng, shape, deviation, bound, cuts=(), kind=jnp.bfloat16):
    gain = steps_of(rng, shape, cuts, -0.22, 0.18) if cuts else 1.0
    values = jax.random.normal(rng, shape, jnp.float32) * deviation * gain
    return jnp.minimum(jnp.maximum(values, -bound), bound).astype(kind)


def setup_inputs(seed: int = 0) -> dict:
    key_list = jax.random.split(jax.random.key(seed), 14)
    layer_input = noise(key_list[0], (TOKENS, D), 1.0, 6.0, ((0, 8),))
    proj_weight = noise(key_list[1], (4, D, D), D ** -0.5, 0.1875, ((2, 4),))
    conv_weight = noise(key_list[2], (3, CONV, D), 0.5, 3.0, ((2, 4),), jnp.float32)
    persist_kv = noise(key_list[3], (2, NH, PERSIST, HS), 1.0, 4.0, ((1, 4),), jnp.float32)
    memory_in = noise(key_list[4], (NH, HS, MEM_HID), 1.0, 4.0, ((0, 4),), jnp.float32)
    memory_out = noise(key_list[5], (NH, MEM_HID, HS), MEM_HID ** -0.5, 0.375, ((0, 4),), jnp.float32)
    memory_gate = noise(key_list[6], (D, 3, NH), 0.5, 3.0, ((2, 4),), jnp.float32)
    out_weight = noise(key_list[7], (D, D), (D // 4) ** -0.5, 0.375, ((1, 4),))
    ffn_in = noise(key_list[8], (2, D, FF), D ** -0.5, 0.1875, ((2, 4),))
    ffn_out = noise(key_list[9], (FF, D), FF ** -0.5, 0.09375, ((0, 4),))
    norm_gains = jnp.clip(1.0 + 0.1 * jax.random.normal(key_list[10], (2, D), jnp.float32), 0.5, 1.5)
    seq_len = draw_seq_len(jax.random.fold_in(key_list[13], 71), 0)
    out_grad = noise(key_list[12], (TOKENS, D), 1.0, 6.0, ((0, 8), (1, 4)))
    return dict(layer_input=layer_input, proj_weight=proj_weight, conv_weight=conv_weight, persist_kv=persist_kv, memory_in=memory_in, memory_out=memory_out, memory_gate=memory_gate, out_weight=out_weight, ffn_in=ffn_in, ffn_out=ffn_out, norm_gains=norm_gains, seq_len=seq_len, out_grad=out_grad)


HIGH = lax.Precision.HIGHEST
NORM_EPS = 1e-05
UNIT_EPS = 1e-06
SCORE_SCALE = 8.0
MASKED = -1e+30

@jax.custom_vjp
def low(v):
    return lax.optimization_barrier(v.astype(jnp.bfloat16)).astype(jnp.float32)

@jax.custom_vjp
def low_back(v):
    return v

def low_keep(v):
    return (low(v), None)

def low_pass(kept, grad):
    return (grad,)

def back_keep(v):
    return (v, None)

def back_low(kept, grad):
    return (low(grad),)
low.defvjp(low_keep, low_pass)
low_back.defvjp(back_keep, back_low)

def memory_net(rows_in, first_layer, second_layer):
    return jnp.dot(jax.nn.silu(jnp.dot(rows_in, first_layer, precision=HIGH)), second_layer, precision=HIGH)

def memory_head(queries, keys_in, values_in, logits, first_layer, second_layer, valid_rows):
    span_count = logits.shape[0]
    span_rows = queries.shape[0] // span_count

    def advance(state_now, span_item):
        first_now, second_now, moment_one, moment_two = state_now
        query_span, key_span, value_span, logit_span, valid_span = span_item
        recalled = memory_net(query_span, first_now, second_now)
        counted = jnp.maximum(jnp.sum(valid_span), 1.0)

        def inner_loss(first_try, second_try):
            residue = memory_net(key_span, first_try, second_try) - value_span
            return jnp.sum(valid_span[:, None] * residue * residue) / (2.0 * counted)
        grad_one, grad_two = jax.grad(inner_loss, argnums=(0, 1))(first_now, second_now)
        step_size = 0.2 * jax.nn.sigmoid(logit_span[0])
        momentum_keep = jax.nn.sigmoid(logit_span[1])
        forget = 0.5 * jax.nn.sigmoid(logit_span[2])
        moment_one = momentum_keep * moment_one - step_size * grad_one
        moment_two = momentum_keep * moment_two - step_size * grad_two
        first_next = (1.0 - forget) * first_now + moment_one
        second_next = (1.0 - forget) * second_now + moment_two
        return ((first_next, second_next, moment_one, moment_two), recalled)
    initial = (first_layer, second_layer, jnp.zeros_like(first_layer), jnp.zeros_like(second_layer))
    span_items = (queries.reshape(span_count, span_rows, -1), keys_in.reshape(span_count, span_rows, -1), values_in.reshape(span_count, span_rows, -1), logits, valid_rows.reshape(span_count, span_rows))
    final_state, recalled = lax.scan(advance, initial, span_items)
    return recalled.reshape(queries.shape[0], -1)

def memory_all(queries, keys_in, values_in, normed, gate_weight, first_layer, second_layer, valid_rows):
    span_count = queries.shape[0] // SPAN
    width = normed.shape[1]
    grouped = normed.reshape(span_count, SPAN, width)
    valid_grouped = valid_rows.reshape(span_count, SPAN)
    counted = jnp.maximum(lax.optimization_barrier(jnp.sum(valid_grouped, 1)), 1.0)
    means = jnp.einsum('ctd,ct->cd', grouped, valid_grouped, precision=HIGH) / counted[:, None]
    logits = jnp.einsum('cd,dgh->hcg', means, gate_weight, precision=HIGH)
    return jax.vmap(memory_head, in_axes=(1, 1, 1, 0, 0, 0, None), out_axes=1)(queries, keys_in, values_in, logits, first_layer, second_layer, valid_rows)

def conv_rows(values_in, kernel):
    summed = jnp.zeros_like(values_in)
    for offset in range(kernel.shape[0]):
        shifted = jnp.pad(values_in, ((offset, 0), (0, 0)))[:values_in.shape[0]]
        summed = summed + kernel[offset] * shifted
    return summed

def unit_rows(values_in):
    return values_in * lax.rsqrt(lax.optimization_barrier(jnp.sum(values_in * values_in, -1, keepdims=True)) + UNIT_EPS)

def prepare(query_pre, key_pre, value_pre, kernels):
    length = query_pre.shape[0]
    queries = unit_rows(jax.nn.silu(conv_rows(query_pre, kernels[0])).reshape(length, -1, HS))
    keys_out = unit_rows(jax.nn.silu(conv_rows(key_pre, kernels[1])).reshape(length, -1, HS))
    values_out = jax.nn.silu(conv_rows(value_pre, kernels[2])).reshape(length, -1, HS)
    return (queries, keys_out, values_out)

def persist(persist_pair):
    return (unit_rows(persist_pair[0]), persist_pair[1])

def attend(queries, keys_all, values_all):
    length, head_count, head_size = queries.shape
    block_rows = min(512, length)
    blocks = length // block_rows
    persist_rows = keys_all.shape[1] - length
    key_place = jnp.concatenate([jnp.full((persist_rows,), -1, jnp.int32), jnp.arange(length, dtype=jnp.int32)])

    def one_block(block_item):
        query_block, block_start = block_item
        scores = SCORE_SCALE * jnp.einsum('qhd,hkd->hqk', query_block, keys_all, precision=HIGH)
        scores = low_back(scores)
        query_place = block_start + jnp.arange(block_rows, dtype=jnp.int32)
        allowed = key_place[None, None, :] <= query_place[None, :, None]
        scores = jnp.where(allowed, scores, MASKED)
        weights = low(jax.nn.softmax(scores, axis=-1))
        return jnp.einsum('hqk,hkd->qhd', weights, values_all, precision=HIGH)
    starts = jnp.arange(blocks, dtype=jnp.int32) * block_rows
    result = lax.map(jax.checkpoint(one_block), (queries.reshape(blocks, block_rows, head_count, head_size), starts))
    return result.reshape(length, head_count, head_size)

def sequence_layer(rows_in, valid_len, weights_all):
    proj, kernels, persist_pair, first_layer, second_layer, gate_weight, out_weight, ffn_in, ffn_out, gains = weights_all
    positions = jnp.arange(SLOT, dtype=jnp.int32)
    valid_rows = (positions < valid_len).astype(jnp.float32)
    scale_one = lax.rsqrt(lax.optimization_barrier(jnp.mean(rows_in * rows_in, -1, keepdims=True)) + NORM_EPS)
    normed = rows_in * scale_one * gains[0]
    normed_low = low(normed)
    projected = low_back(jnp.einsum('td,idf->itf', normed_low, proj, precision=HIGH))
    queries, keys_out, values_out = prepare(projected[0], projected[1], projected[2], kernels)
    queries, keys_out, values_out = (low(queries), low(keys_out), low(values_out))
    persist_keys, persist_values = persist(persist_pair)
    keys_all = jnp.concatenate([low(persist_keys), jnp.transpose(keys_out, (1, 0, 2))], 1)
    values_all = jnp.concatenate([low(persist_values), jnp.transpose(values_out, (1, 0, 2))], 1)
    attended = low_back(attend(queries, keys_all, values_all))
    recalled = memory_all(queries, keys_out, values_out, normed, gate_weight, first_layer, second_layer, valid_rows)
    gate_act = jax.nn.sigmoid(projected[3]).reshape(SLOT, -1, HS)
    mixed_rows = low(((attended + recalled) * gate_act).reshape(SLOT, D))
    branch = low_back(jnp.dot(mixed_rows, out_weight, precision=HIGH))
    residual = rows_in + branch
    scale_two = lax.rsqrt(lax.optimization_barrier(jnp.mean(residual * residual, -1, keepdims=True)) + NORM_EPS)
    normed_two = low(residual * scale_two * gains[1])
    ffn_pre = jnp.einsum('td,idf->itf', normed_two, ffn_in, precision=HIGH)
    gate_pre = low_back(ffn_pre[0])
    up_pre = low_back(ffn_pre[1])
    hidden = low(jax.nn.silu(gate_pre) * up_pre)
    ffn_rows = low_back(jnp.dot(hidden, ffn_out, precision=HIGH))
    return residual + ffn_rows

def reference(layer_input, proj_weight, conv_weight, persist_kv, memory_in, memory_out, memory_gate, out_weight, ffn_in, ffn_out, norm_gains, seq_len, out_grad):
    floats = tuple((argument.astype(jnp.float32) for argument in (layer_input, proj_weight, conv_weight, persist_kv, memory_in, memory_out, memory_gate, out_weight, ffn_in, ffn_out, norm_gains)))

    def forward(rows_all, *weights_all):
        grouped = rows_all.reshape(N_DP, SLOT, D)

        def one_sequence(seq_item):
            return sequence_layer(seq_item[0], seq_item[1], weights_all)
        return lax.map(jax.checkpoint(one_sequence), (grouped, seq_len)).reshape(TOKENS, D)
    output, pullback = jax.vjp(forward, *floats)
    gradients = pullback(out_grad.astype(jnp.float32))
    return (output.astype(jnp.bfloat16), gradients[0], gradients[1], gradients[2], gradients[3], gradients[4], gradients[5], gradients[6], gradients[7], gradients[8], gradients[9], gradients[10])
```

```python
import functools

import jax
import jax.numpy as jnp
from jax import lax
from jax.experimental import pallas as pl
from jax.experimental.pallas import tpu as pltpu
from jax.sharding import PartitionSpec as P

F32 = jnp.float32
BF16 = jnp.bfloat16
HIGH = lax.Precision.HIGHEST
NORM_EPS = 1e-05
UNIT_EPS = 1e-06
SCORE_SCALE = 8.0
SPAN = 512
HALO = 8
GATE_ROWS = 128


def dot_nn(left, right):
    return jnp.dot(left, right, preferred_element_type=F32)


def dot_nt(left, right, precision=None):
    return lax.dot_general(
        left, right, (((1,), (1,)), ((), ())), preferred_element_type=F32, precision=precision
    )


def two_parts(value):
    high = value.astype(BF16)
    return high, (value - high.astype(F32)).astype(BF16)


def iota(shape, axis):
    return lax.broadcasted_iota(jnp.int32, shape, axis)


def head_blocks(cols, shift):
    same = (iota((cols, cols), 0) >> shift) == (iota((cols, cols), 1) >> shift)
    return jnp.where(same, 1.0, 0.0).astype(BF16)


def head_sum(value, blocks):
    high, rest = two_parts(value)
    return dot_nn(high, blocks) + dot_nn(rest, blocks)


def valid_column(seq_ref, start, rows):
    inside = (start + iota((rows, 1), 0)) < seq_ref[0]
    valid = jnp.where(inside, 1.0, 0.0)
    return valid, jnp.maximum(jnp.sum(valid, 0, keepdims=True), 1.0)


def head_mask(cols, shift, head):
    return jnp.where((iota((1, cols), 1) >> shift) == head, 1.0, 0.0)


def gate_rows(logits, group, heads, head_size, width):
    parts = [
        jnp.broadcast_to(
            logits[0:1, group * heads + head : group * heads + head + 1], (head_size, width)
        )
        for head in range(heads)
    ]
    return jnp.concatenate(parts, 0)


def prep_kernel(
    shift,
    seq_ref,
    x_ref,
    w_ref,
    conv_ref,
    gain_ref,
    gate_ref,
    pers_ref,
    q_ref,
    k_ref,
    v_ref,
    kt_ref,
    pre_ref,
    gp_ref,
    nl_ref,
    mean_ref,
    lg_ref,
    pers_out_ref,
    ext_ref,
):
    step = pl.program_id(0)
    rows, cols = q_ref.shape
    blocks = head_blocks(cols, shift)

    @pl.when(step == 0)
    def _():
        ext_ref[:, 0:HALO, :] = jnp.zeros((3, HALO, cols), F32)
        keys = pers_ref[0]
        keys = keys * lax.rsqrt(head_sum(keys * keys, blocks) + UNIT_EPS)
        pers_out_ref[0] = keys.astype(BF16)
        pers_out_ref[1] = pers_ref[1].astype(BF16)

    x = x_ref[...].astype(F32)
    scale = lax.rsqrt(jnp.mean(x * x, -1, keepdims=True) + NORM_EPS)
    normed = x * scale * gain_ref[0:1, :]
    low = normed.astype(BF16)
    nl_ref[...] = low
    valid, count = valid_column(seq_ref, step * rows, rows)
    mean = jnp.broadcast_to(
        jnp.sum(normed * valid, 0, keepdims=True) / count, (8, normed.shape[1])
    )
    mean_ref[...] = mean
    lg_ref[...] = dot_nt(mean, gate_ref[...], HIGH)
    gp_ref[...] = dot_nn(low, w_ref[3])
    for i in range(3):
        pre = dot_nn(low, w_ref[i])
        pre_ref[i] = pre
        ext_ref[i, HALO : HALO + rows, :] = pre
        conv = conv_ref[i, 0:1, :] * pre
        for j in range(1, conv_ref.shape[1]):
            conv = conv + conv_ref[i, j : j + 1, :] * ext_ref[i, HALO - j : HALO - j + rows, :]
        ext_ref[i, 0:HALO, :] = pre[rows - HALO :, :]
        act = conv * jax.nn.sigmoid(conv)
        if i < 2:
            act = act * lax.rsqrt(head_sum(act * act, blocks) + UNIT_EPS)
        act_low = act.astype(BF16)
        (q_ref, k_ref, v_ref)[i][...] = act_low
        if i == 1:
            kt_ref[...] = jnp.transpose(act_low.astype(F32)).astype(BF16)


def prep_call(seq, x, w, conv, gains, gate, pers, shift):
    rows, width = x.shape
    cols = w.shape[2]
    nb = rows // SPAN
    whole = lambda a: pl.BlockSpec(a.shape, lambda c, n=a.ndim: (0,) * n)
    row_cols = pl.BlockSpec((SPAN, cols), lambda c: (c, 0))
    return pl.pallas_call(
        functools.partial(prep_kernel, shift),
        grid=(nb,),
        in_specs=[
            pl.BlockSpec(memory_space=pltpu.SMEM),
            pl.BlockSpec((SPAN, width), lambda c: (c, 0)),
            whole(w),
            whole(conv),
            whole(gains),
            whole(gate),
            whole(pers),
        ],
        out_specs=[
            row_cols,
            row_cols,
            row_cols,
            pl.BlockSpec((cols, SPAN), lambda c: (0, c)),
            pl.BlockSpec((3, SPAN, cols), lambda c: (0, c, 0)),
            row_cols,
            pl.BlockSpec((SPAN, width), lambda c: (c, 0)),
            pl.BlockSpec((8, width), lambda c: (c, 0)),
            pl.BlockSpec((8, GATE_ROWS), lambda c: (c, 0)),
            whole(pers),
        ],
        out_shape=[
            jax.ShapeDtypeStruct((rows, cols), BF16),
            jax.ShapeDtypeStruct((rows, cols), BF16),
            jax.ShapeDtypeStruct((rows, cols), BF16),
            jax.ShapeDtypeStruct((cols, rows), BF16),
            jax.ShapeDtypeStruct((3, rows, cols), F32),
            jax.ShapeDtypeStruct((rows, cols), F32),
            jax.ShapeDtypeStruct((rows, width), BF16),
            jax.ShapeDtypeStruct((nb * 8, width), F32),
            jax.ShapeDtypeStruct((nb * 8, GATE_ROWS), F32),
            jax.ShapeDtypeStruct(pers.shape, BF16),
        ],
        scratch_shapes=[pltpu.VMEM((3, HALO + SPAN, cols), F32)],
        name="prep",
    )(seq, x, w, conv, gains, gate, pers)


def mix_kernel(block, blocks_all, shift, first, last, *refs):
    it = iter(refs)
    seq_ref, lg_ref, q_ref, k_ref, v_ref, kt_ref, pers_ref, gp_ref, a_ref, bt_ref = (
        next(it) for _ in range(10)
    )
    sa_ref, sbt_ref = (None, None) if first or last else (next(it), next(it))
    mixed_ref, tot_ref, att_ref, linv_ref = (next(it) for _ in range(4))
    if not last:
        a2_ref, bt2_ref, sa2_ref, sbt2_ref, ga_ref, gbt_ref = (next(it) for _ in range(6))
        z_ref, r_ref = next(it), next(it)
    rows, cols = q_ref.shape
    head_size = 1 << shift
    heads = cols // head_size
    a_low = a_ref[...].astype(BF16)
    bt_low = bt_ref[...].astype(BF16)
    valid, count = valid_column(seq_ref, block * rows, rows)
    weight = valid / count
    att_ref[...] = jnp.zeros((rows, cols), F32)
    linv_ref[...] = jnp.zeros((rows, cols), F32)
    tot_ref[...] = jnp.zeros((rows, cols), F32)
    if not last:
        r_ref[...] = jnp.zeros((rows, cols), F32)

    def one_head(head, carry):
        mask = head_mask(cols, shift, head)
        mask_low = mask.astype(BF16)
        ones_low = (1.0 - mask).astype(BF16)
        query = q_ref[...] * mask_low
        scaled = query * SCORE_SCALE
        raised = jnp.exp(dot_nt(scaled, pers_ref[0])).astype(BF16)
        total = dot_nn(raised, pers_ref[1] * mask_low + ones_low)
        for j in range(block + 1):
            span = slice(j * rows, (j + 1) * rows)
            raised = jnp.exp(dot_nt(scaled, k_ref[span, :]))
            if j == block:
                raised = jnp.where(
                    iota((rows, rows), 0) >= iota((rows, rows), 1), raised, 0.0
                )
            total = total + dot_nn(raised.astype(BF16), v_ref[span, :] * mask_low + ones_low)
        inverse = 1.0 / pltpu.roll(total, head_size, 1)
        inside = jnp.broadcast_to(mask, (rows, cols)) > 0.5
        linv_ref[...] = jnp.where(inside, inverse, linv_ref[...])
        attended = jnp.where(inside, total * inverse, 0.0)
        att_ref[...] = att_ref[...] + attended
        hid = dot_nn(query, a_low)
        hid = hid * jax.nn.sigmoid(hid)
        recalled = dot_nt(hid.astype(BF16), bt_low) * mask
        tot_ref[...] = tot_ref[...] + attended + recalled
        if not last:
            hid = dot_nn(k_ref[block * rows : (block + 1) * rows, :] * mask_low, a_low)
            sig = jax.nn.sigmoid(hid)
            act = (hid * sig).astype(BF16)
            z_ref[head] = act
            target = v_ref[block * rows : (block + 1) * rows, :].astype(F32)
            resid = (dot_nt(act, bt_low) - target) * mask * weight
            r_ref[...] = r_ref[...] + resid
            d_hid = dot_nn(resid.astype(BF16), bt_low) * (sig * (1.0 + hid * (1.0 - sig)))
            at = pl.ds(pl.multiple_of(head * head_size, head_size), head_size)
            ga_ref[at, :] = dot_nn(kt_ref[at, :], d_hid.astype(BF16))
        return carry

    lax.fori_loop(0, heads, one_head, 0)
    gate = jax.nn.sigmoid(gp_ref[...])
    mixed_ref[...] = (tot_ref[...] * gate).astype(BF16)
    if not last:
        resid_t = jnp.transpose(r_ref[...]).astype(BF16)
        for head in range(heads):
            at = slice(head * head_size, (head + 1) * head_size)
            gbt_ref[at, :] = dot_nn(resid_t[at, :], z_ref[head])
        width = a_ref.shape[1]
        logits = lg_ref[...]
        step = 0.2 * jax.nn.sigmoid(gate_rows(logits, 0, heads, head_size, width))
        keep = jax.nn.sigmoid(gate_rows(logits, 1, heads, head_size, width))
        stay = 1.0 - 0.5 * jax.nn.sigmoid(gate_rows(logits, 2, heads, head_size, width))
        moment_a = -step * ga_ref[...]
        moment_b = -step * gbt_ref[...]
        if not first:
            moment_a = moment_a + keep * sa_ref[...]
            moment_b = moment_b + keep * sbt_ref[...]
        sa2_ref[...] = moment_a
        sbt2_ref[...] = moment_b
        a2_ref[...] = stay * a_ref[...] + moment_a
        bt2_ref[...] = stay * bt_ref[...] + moment_b


def mix_call(block, nb, shift, seq, lg, q, k, v, kt, pers, gp, a, bt, sa, sbt):
    rows, cols = q.shape
    first, last = block == 0, block == nb - 1
    heads = cols >> shift
    whole = lambda s: pl.BlockSpec(s, lambda i, n=len(s): (0,) * n)
    at_block = pl.BlockSpec((SPAN, cols), lambda i: (block, 0))
    upto = pl.BlockSpec(((block + 1) * SPAN, cols), lambda i: (0, 0))
    state = whole(a.shape)
    ins = [seq, lg, q, k, v, kt, pers, gp, a, bt]
    in_specs = [
        pl.BlockSpec(memory_space=pltpu.SMEM),
        pl.BlockSpec((8, GATE_ROWS), lambda i: (block, 0)),
        at_block,
        upto,
        upto,
        pl.BlockSpec((cols, SPAN), lambda i: (0, block)),
        whole(pers.shape),
        at_block,
        state,
        state,
    ]
    if not (first or last):
        ins += [sa, sbt]
        in_specs += [state, state]
    row_spec = whole((SPAN, cols))
    outs = [jax.ShapeDtypeStruct((SPAN, cols), BF16)] + [
        jax.ShapeDtypeStruct((SPAN, cols), F32)
    ] * 3
    out_specs = [row_spec] * 4
    scratch = []
    if not last:
        outs += [jax.ShapeDtypeStruct(a.shape, F32)] * 6
        out_specs += [state] * 6
        scratch = [pltpu.VMEM((heads, SPAN, a.shape[1]), BF16), pltpu.VMEM((SPAN, cols), F32)]
    return pl.pallas_call(
        functools.partial(mix_kernel, block, nb, shift, first, last),
        grid=(1,),
        in_specs=in_specs,
        out_specs=out_specs,
        out_shape=outs,
        scratch_shapes=scratch,
        name=f"mix_{block}",
    )(*ins)


def ffn_kernel(
    peer_ref,
    x_ref,
    m0_ref,
    m1_ref,
    m2_ref,
    m3_ref,
    ow_ref,
    gain_ref,
    fin_ref,
    fout_ref,
    cot_ref,
    res_ref,
    nt_ref,
    hid_ref,
    dgu_ref,
    part_keep_ref,
    part_send_ref,
    dn_keep_ref,
    dn_send_ref,
    gg_ref,
    part_ref,
):
    rows, width = x_ref.shape
    cols = m0_ref.shape[1]
    shards = width // cols
    branch = None
    for j, m_ref in enumerate((m0_ref, m1_ref, m2_ref, m3_ref)):
        at = pl.ds(pl.multiple_of(peer_ref[j] * cols, cols), cols)
        weight = jnp.concatenate([ow_ref[p, at, :] for p in range(shards)], 1)
        term = dot_nn(m_ref[...], weight)
        branch = term if branch is None else branch + term
    residual = x_ref[...].astype(F32) + branch
    res_ref[...] = residual
    scale = lax.rsqrt(jnp.mean(residual * residual, -1, keepdims=True) + NORM_EPS)
    low = (residual * scale * gain_ref[1:2, :]).astype(BF16)
    nt_ref[...] = low
    gate_pre = dot_nn(low, fin_ref[0])
    up_pre = dot_nn(low, fin_ref[1])
    sig = jax.nn.sigmoid(gate_pre)
    silu = gate_pre * sig
    hidden = (silu * up_pre).astype(BF16)
    hid_ref[...] = hidden
    cot = jnp.concatenate([cot_ref[p] for p in range(shards)], 1)
    d_hidden = dot_nt(cot, fout_ref[...])
    slope = sig * (1.0 + gate_pre * (1.0 - sig))
    d_gate = (d_hidden * up_pre * slope).astype(BF16)
    d_up = (d_hidden * silu).astype(BF16)
    dgu_ref[0] = d_gate
    dgu_ref[1] = d_up
    d_normed = dot_nt(d_gate, fin_ref[0]) + dot_nt(d_up, fin_ref[1])
    gains = jnp.sum(d_normed * residual * scale, 0, keepdims=True)

    @pl.when(pl.program_id(0) == 0)
    def _():
        gg_ref[...] = jnp.zeros_like(gg_ref)

    gg_ref[...] = gg_ref[...] + jnp.broadcast_to(gains, gg_ref.shape)
    half = width // 2
    part_ref[...] = d_normed.astype(BF16)
    core = peer_ref[0] & 1
    dn_keep_ref[...] = part_ref[:, pl.ds(pl.multiple_of(core * half, half), half)]
    dn_send_ref[...] = part_ref[:, pl.ds(pl.multiple_of((1 - core) * half, half), half)]
    part_ref[...] = dot_nn(hidden, fout_ref[...]).astype(BF16)
    for slot, out_ref in ((0, part_keep_ref), (1, part_send_ref)):
        for n in range(2):
            start = pl.multiple_of(peer_ref[slot + 2 * n] * cols, cols)
            out_ref[n] = part_ref[:, pl.ds(start, cols)]


def ffn_call(block, peers, x, mixed, ow, gains, fin, fout, cot):
    width = x.shape[1]
    cols = mixed[0].shape[1]
    tile = SPAN // 2
    steps = SPAN // tile
    shards = width // cols
    hidden = fout.shape[0]
    whole = lambda a: pl.BlockSpec(a.shape, lambda i, n=a.ndim: (0,) * n)
    row = lambda n: pl.BlockSpec((tile, n), lambda i: (i, 0))
    stacked = lambda n, w: pl.BlockSpec((n, tile, w), lambda i: (0, i, 0))
    struct = jax.ShapeDtypeStruct
    return pl.pallas_call(
        ffn_kernel,
        grid=(steps,),
        in_specs=[
            pl.BlockSpec(memory_space=pltpu.SMEM),
            pl.BlockSpec((tile, width), lambda i: (block * steps + i, 0)),
            row(cols),
            row(cols),
            row(cols),
            row(cols),
            whole(ow),
            whole(gains),
            whole(fin),
            whole(fout),
            pl.BlockSpec((shards, tile, cols), lambda i: (0, block * steps + i, 0)),
        ],
        out_specs=[
            row(width),
            row(width),
            row(hidden),
            stacked(2, hidden),
            stacked(2, cols),
            stacked(2, cols),
            row(width // 2),
            row(width // 2),
            pl.BlockSpec((8, width), lambda i: (0, 0)),
        ],
        out_shape=[
            struct((SPAN, width), F32),
            struct((SPAN, width), BF16),
            struct((SPAN, hidden), BF16),
            struct((2, SPAN, hidden), BF16),
            struct((2, SPAN, cols), BF16),
            struct((2, SPAN, cols), BF16),
            struct((SPAN, width // 2), BF16),
            struct((SPAN, width // 2), BF16),
            struct((8, width), F32),
        ],
        scratch_shapes=[pltpu.VMEM((tile, width), BF16)],
        name=f"ffn_{block}",
    )(peers, x, *mixed, ow, gains, fin, fout, cot)


def turn_kernel(
    peer_ref,
    s1_ref,
    r2_ref,
    ps1_ref,
    pr2_ref,
    res_ref,
    cot_ref,
    ow_ref,
    gain_ref,
    gp_ref,
    tot_ref,
    dres_ref,
    rescol_ref,
    dbr_ref,
    dga_ref,
    dgp_ref,
    full_ref,
):
    rows, width = res_ref.shape
    cols = gp_ref.shape[1]
    shards = width // cols
    half = width // 2
    core = peer_ref[0] & 1
    at_own = pl.ds(pl.multiple_of(core * half, half), half)
    at_other = pl.ds(pl.multiple_of((1 - core) * half, half), half)
    full_ref[:, at_own] = s1_ref[...].astype(F32) + r2_ref[...].astype(F32)
    full_ref[:, at_other] = ps1_ref[...].astype(F32) + pr2_ref[...].astype(F32)
    residual = res_ref[...]
    scale = lax.rsqrt(jnp.mean(residual * residual, -1, keepdims=True) + NORM_EPS)
    gained = full_ref[...] * gain_ref[1:2, :]
    inner = jnp.sum(gained * residual, -1, keepdims=True) / width
    cot = jnp.concatenate([cot_ref[p].astype(F32) for p in range(shards)], 1)
    d_residual = cot + scale * gained - residual * (scale * scale * scale * inner)
    d_branch = d_residual.astype(BF16)
    own = pl.ds(pl.multiple_of(peer_ref[0] * cols, cols), cols)
    weight = jnp.concatenate([ow_ref[p, own, :] for p in range(shards)], 1)
    d_mixed = dot_nt(d_branch, weight)
    full_ref[...] = d_residual
    mine = full_ref[:, own]
    dres_ref[...] = mine
    dbr_ref[...] = mine.astype(BF16)
    rescol_ref[...] = res_ref[:, own]
    gate = jax.nn.sigmoid(gp_ref[...])
    d_gated = d_mixed * gate
    dga_ref[...] = d_gated.astype(BF16)
    dgp_ref[...] = (d_gated * tot_ref[...] * (1.0 - gate)).astype(BF16)


def turn_call(block, peers, pieces, res, cot, ow, gains, gp, tot):
    width = res.shape[1]
    cols = gp.shape[1]
    tile = SPAN // 2
    steps = SPAN // tile
    shards = width // cols
    whole = lambda a: pl.BlockSpec(a.shape, lambda i, n=a.ndim: (0,) * n)
    row = lambda n: pl.BlockSpec((tile, n), lambda i: (i, 0))
    struct = jax.ShapeDtypeStruct
    return pl.pallas_call(
        turn_kernel,
        grid=(steps,),
        in_specs=[
            pl.BlockSpec(memory_space=pltpu.SMEM),
            row(width // 2),
            row(width // 2),
            row(width // 2),
            row(width // 2),
            row(width),
            pl.BlockSpec((shards, tile, cols), lambda i: (0, block * steps + i, 0)),
            whole(ow),
            whole(gains),
            pl.BlockSpec((tile, cols), lambda i: (block * steps + i, 0)),
            row(cols),
        ],
        out_specs=[row(cols)] * 5,
        out_shape=[
            struct((SPAN, cols), F32),
            struct((SPAN, cols), F32),
            struct((SPAN, cols), BF16),
            struct((SPAN, cols), BF16),
            struct((SPAN, cols), BF16),
        ],
        scratch_shapes=[pltpu.VMEM((tile, width), F32)],
        name=f"turn_{block}",
    )(peers, *pieces, res, cot, ow, gains, gp, tot)


def back_kernel(block, nb, shift, *refs):
    it = iter(refs)
    take = lambda n: [next(it) for _ in range(n)]
    first, last = block == 0, block == nb - 1
    seq_ref, q_ref, k_ref, v_ref, kt_ref, pers_ref, dga_ref, att_ref, linv_ref = take(9)
    a_ref, bt_ref = take(2)
    if not last:
        dk_in_ref, dv_in_ref, dp_in_ref, lg_ref, ga_ref, gbt_ref, ab_in_ref, btb_in_ref = take(8)
        sab_in_ref, sbtb_in_ref = take(2) if block < nb - 2 else (None, None)
        sa_ref, sbt_ref = (None, None) if first else take(2)
    dq_ref, dk_ref, dv_ref, dp_ref, ab_ref, btb_ref = take(6)
    if not last:
        (dlg_ref,) = take(1)
        sab_ref, sbtb_ref = (None, None) if first else take(2)
    lt_ref, dt_ref, dqt_ref, qt_ref, dot_ref = take(5)
    if not last:
        z_ref, zd_ref, r_ref, y_ref, h_ref = take(5)
    rows, cols = q_ref.shape
    head_size = 1 << shift
    heads = cols // head_size
    own = slice(block * rows, (block + 1) * rows)
    a_low = a_ref[...].astype(BF16)
    bt_low = bt_ref[...].astype(BF16)
    if last:
        dk_ref[...] = jnp.zeros(dk_ref.shape, F32)
        dv_ref[...] = jnp.zeros(dv_ref.shape, F32)
        dp_ref[...] = jnp.zeros(dp_ref.shape, F32)
        ab_ref[...] = jnp.zeros(ab_ref.shape, F32)
        btb_ref[...] = jnp.zeros(btb_ref.shape, F32)
    else:
        dk_ref[...] = dk_in_ref[...]
        dv_ref[...] = dv_in_ref[...]
        dp_ref[...] = dp_in_ref[...]
    pick = (iota((8, cols), 1) >> shift) == iota((8, cols), 0)
    start = iota((8, cols), 1) == (iota((8, cols), 0) << shift)
    lt_ref[...] = dot_nt(jnp.where(start, 1.0, 0.0), linv_ref[...], HIGH)
    d_gated = dga_ref[...].astype(F32)
    dt_ref[...] = dot_nt(jnp.where(pick, 1.0, 0.0), d_gated * att_ref[...], HIGH)
    dq_ref[...] = jnp.zeros((rows, cols), F32)
    qt_ref[...] = jnp.transpose(q_ref[...].astype(F32)).astype(BF16)
    dot_ref[...] = jnp.transpose(d_gated).astype(BF16)
    if not last:
        valid, count = valid_column(seq_ref, block * rows, rows)
        weight = valid / count
        width = a_ref.shape[1]
        logits = lg_ref[...]
        sig_step = jax.nn.sigmoid(gate_rows(logits, 0, heads, head_size, width))
        keep = jax.nn.sigmoid(gate_rows(logits, 1, heads, head_size, width))
        sig_forget = jax.nn.sigmoid(gate_rows(logits, 2, heads, head_size, width))
        tot_a, tot_b = ab_in_ref[...], btb_in_ref[...]
        if sab_in_ref is not None:
            tot_a, tot_b = tot_a + sab_in_ref[...], tot_b + sbtb_in_ref[...]
        h_ref[0] = (-0.2 * sig_step * tot_a).astype(BF16)
        h_ref[1] = (-0.2 * sig_step * tot_b).astype(BF16)
        d_step = -(ga_ref[...] * tot_a + gbt_ref[...] * tot_b)
        groups = [d_step * (0.2 * sig_step * (1.0 - sig_step)), None, None]
        if not first:
            groups[1] = (sa_ref[...] * tot_a + sbt_ref[...] * tot_b) * (keep * (1.0 - keep))
        d_forget = -(a_ref[...] * ab_in_ref[...] + bt_ref[...] * btb_in_ref[...])
        groups[2] = d_forget * (0.5 * sig_forget * (1.0 - sig_forget))
        d_logits = jnp.zeros((8, GATE_ROWS), F32)
        for g, value in enumerate(groups):
            if value is None:
                continue
            for head in range(heads):
                part = value[head * head_size : (head + 1) * head_size, :]
                figure = jnp.sum(jnp.sum(part, 1, keepdims=True), 0, keepdims=True)
                here = iota((8, GATE_ROWS), 1) == g * heads + head
                d_logits = d_logits + jnp.where(here, 1.0, 0.0) * figure
        dlg_ref[...] = d_logits
        stay = 1.0 - 0.5 * sig_forget
        ab_ref[...] = stay * ab_in_ref[...]
        btb_ref[...] = stay * btb_in_ref[...]
        if not first:
            sab_ref[...] = keep * tot_a
            sbtb_ref[...] = keep * tot_b
        r_ref[...] = jnp.zeros((rows, cols), F32)
        y_ref[...] = jnp.zeros((rows, cols), F32)

    def one_head(head, carry):
        mask = head_mask(cols, shift, head)
        mask_low = mask.astype(BF16)
        query = q_ref[...] * mask_low
        scaled = query * SCORE_SCALE
        d_out = dga_ref[...] * mask_low
        at = pl.ds(pl.multiple_of(head * head_size, head_size), head_size)
        inverse = lt_ref[pl.ds(head, 1), :]
        delta = dt_ref[pl.ds(head, 1), :]
        probs = jnp.exp(dot_nt(pers_ref[0], scaled)) * inverse
        d_scores = (probs * (dot_nt(pers_ref[1], d_out) - delta)).astype(BF16)
        dp_ref[0] = dp_ref[0] + dot_nn(d_scores, scaled)
        dp_ref[1] = dp_ref[1] + dot_nn(probs.astype(BF16), d_out)
        d_query = lax.dot_general(
            d_scores, pers_ref[0], (((0,), (0,)), ((), ())), preferred_element_type=F32
        )
        d_query = d_query * SCORE_SCALE
        d_query_t = jnp.zeros((head_size, rows), F32)
        for j in range(block + 1):
            span = slice(j * rows, (j + 1) * rows)
            probs = jnp.exp(dot_nt(k_ref[span, :], scaled)) * inverse
            if j == block:
                probs = jnp.where(iota((rows, rows), 0) <= iota((rows, rows), 1), probs, 0.0)
            d_scores = (probs * (dot_nt(v_ref[span, :], d_out) - delta)).astype(BF16)
            dv_ref[span, :] = dv_ref[span, :] + dot_nn(probs.astype(BF16), d_out)
            dk_ref[span, :] = dk_ref[span, :] + dot_nn(d_scores, scaled)
            d_query_t = d_query_t + dot_nn(kt_ref[at, span], d_scores)
        dqt_ref[at, :] = d_query_t * SCORE_SCALE
        hid = dot_nn(query, a_low)
        sig = jax.nn.sigmoid(hid)
        d_hid = dot_nn(d_out, bt_low) * (sig * (1.0 + hid * (1.0 - sig)))
        d_hid = d_hid.astype(BF16)
        dq_ref[...] = dq_ref[...] + (d_query + dot_nt(d_hid, a_low)) * mask
        grad_a = dot_nn(qt_ref[at, :], d_hid)
        grad_b = dot_nn(dot_ref[at, :], (hid * sig).astype(BF16))
        if not last:
            key = k_ref[own, :] * mask_low
            hid = dot_nn(key, a_low)
            probe = dot_nn(key, h_ref[0])
            sig = jax.nn.sigmoid(hid)
            act = (hid * sig).astype(BF16)
            z_ref[head] = act
            slope = sig * (1.0 + hid * (1.0 - sig))
            curve = sig * (1.0 - sig) * (2.0 + hid * (1.0 - 2.0 * sig))
            target = v_ref[own, :].astype(F32)
            resid = (dot_nt(act, bt_low) - target) * mask * weight
            r_ref[...] = r_ref[...] + resid
            resid = resid.astype(BF16)
            d_act = dot_nn(resid, bt_low)
            d_slope = (probe * slope).astype(BF16)
            zd_ref[head] = d_slope
            d_net = (dot_nt(act, h_ref[1]) + dot_nt(d_slope, bt_low)) * mask * weight
            y_ref[...] = y_ref[...] + d_net
            back = dot_nn(resid, h_ref[1]) + dot_nn(d_net.astype(BF16), bt_low)
            d_hid = (probe * d_act * curve + back * slope).astype(BF16)
            direct = (d_act * slope).astype(BF16)
            d_key = (dot_nt(direct, h_ref[0]) + dot_nt(d_hid, a_low)) * mask
            dk_ref[own, :] = dk_ref[own, :] + d_key
            grad_a = grad_a + dot_nn(kt_ref[at, own], d_hid)
        ab_ref[at, :] = ab_ref[at, :] + grad_a
        btb_ref[at, :] = btb_ref[at, :] + grad_b
        return carry

    lax.fori_loop(0, heads, one_head, 0)
    dq_ref[...] = dq_ref[...] + jnp.transpose(dqt_ref[...])
    if not last:
        dv_ref[own, :] = dv_ref[own, :] - y_ref[...]
        resid_t = jnp.transpose(r_ref[...]).astype(BF16)
        net_t = jnp.transpose(y_ref[...]).astype(BF16)
        for head in range(heads):
            at = slice(head * head_size, (head + 1) * head_size)
            grad_b = dot_nn(resid_t[at, :], zd_ref[head]) + dot_nn(net_t[at, :], z_ref[head])
            btb_ref[at, :] = btb_ref[at, :] + grad_b


def back_call(block, nb, shift, seq, q, k, v, kt, pers, dga, att, linv, state, grads, adjoint):
    cols = q.shape[1]
    heads = cols >> shift
    first, last = block == 0, block == nb - 1
    done = (block + 1) * SPAN
    whole = lambda s: pl.BlockSpec(s, lambda i, n=len(s): (0,) * n)
    at_block = pl.BlockSpec((SPAN, cols), lambda i: (block, 0))
    upto = pl.BlockSpec((done, cols), lambda i: (0, 0))
    rows_spec = whole((SPAN, cols))
    square = state["a"].shape
    ins = [seq, q, k, v, kt, pers, dga, att, linv, state["a"], state["bt"]]
    in_specs = [
        pl.BlockSpec(memory_space=pltpu.SMEM),
        at_block,
        upto,
        upto,
        pl.BlockSpec((cols, done), lambda i: (0, 0)),
        whole(pers.shape),
        rows_spec,
        rows_spec,
        rows_spec,
        whole(square),
        whole(square),
    ]
    if not last:
        ins += [grads["dk"], grads["dv"], grads["dp"], state["lg"], state["ga"], state["gbt"]]
        ins += [adjoint["ab"], adjoint["btb"]]
        in_specs += [upto, upto, whole(pers.shape)]
        in_specs += [pl.BlockSpec((8, GATE_ROWS), lambda i: (block, 0))]
        in_specs += [whole(square)] * 4
        if block < nb - 2:
            ins += [adjoint["sab"], adjoint["sbtb"]]
            in_specs += [whole(square)] * 2
        if not first:
            ins += [state["sa"], state["sbt"]]
            in_specs += [whole(square)] * 2
    names = ["dq", "dk", "dv", "dp", "ab", "btb"]
    shapes = [(SPAN, cols), (done, cols), (done, cols), pers.shape, square, square]
    if not last:
        names.append("dlg")
        shapes.append((8, GATE_ROWS))
        if not first:
            names += ["sab", "sbtb"]
            shapes += [square, square]
    scratch = [
        pltpu.VMEM((8, SPAN), F32),
        pltpu.VMEM((8, SPAN), F32),
        pltpu.VMEM((cols, SPAN), F32),
        pltpu.VMEM((cols, SPAN), BF16),
        pltpu.VMEM((cols, SPAN), BF16),
    ]
    if not last:
        scratch += [
            pltpu.VMEM((heads, SPAN, square[1]), BF16),
            pltpu.VMEM((heads, SPAN, square[1]), BF16),
            pltpu.VMEM((SPAN, cols), F32),
            pltpu.VMEM((SPAN, cols), F32),
            pltpu.VMEM((2,) + square, BF16),
        ]
    outs = pl.pallas_call(
        functools.partial(back_kernel, block, nb, shift),
        grid=(1,),
        in_specs=in_specs,
        out_specs=[whole(s) for s in shapes],
        out_shape=[jax.ShapeDtypeStruct(s, F32) for s in shapes],
        scratch_shapes=scratch,
        name=f"back_{block}",
    )(*ins)
    return dict(zip(names, outs))


def unprep_kernel(block, nb, shift, *refs):
    it = iter(refs)
    take = lambda n: [next(it) for _ in range(n)]
    first, last = block == 0, block == nb - 1
    seq_ref, peer_ref, dq_ref, dk_ref, dv_ref, dgp_ref, pre_ref, w_ref, conv_ref = take(9)
    x_ref, gain_ref = take(2)
    (halo_ref,) = (None,) if first else take(1)
    next_ref, dlg_ref, gate_ref = (None, None, None) if last else take(3)
    dproj_ref, keep_ref, send_ref, inner_ref, cg_ref, gg_ref, edge_ref = take(7)
    ext_ref, dext_ref, low_ref = take(3)
    rows, cols = dq_ref.shape
    width = x_ref.shape[1]
    blocks = head_blocks(cols, shift)
    taps = conv_ref.shape[1]
    d_normed = dot_nt(dgp_ref[...], w_ref[3])
    dproj_ref[3] = dgp_ref[...]
    cg_ref[...] = jnp.zeros(cg_ref.shape, F32)
    for i in range(3):
        pre = pre_ref[i]
        ext_ref[0:HALO, :] = jnp.zeros((HALO, cols), F32) if first else halo_ref[i]
        ext_ref[HALO : HALO + rows, :] = pre
        shifted = [pre] + [ext_ref[HALO - j : HALO - j + rows, :] for j in range(1, taps)]
        conv = conv_ref[i, 0:1, :] * pre
        for j in range(1, taps):
            conv = conv + conv_ref[i, j : j + 1, :] * shifted[j]
        sig = jax.nn.sigmoid(conv)
        d_act = (dq_ref, dk_ref, dv_ref)[i][...]
        if i < 2:
            act = conv * sig
            scale = lax.rsqrt(head_sum(act * act, blocks) + UNIT_EPS)
            d_act = scale * (d_act - act * (scale * scale * head_sum(d_act * act, blocks)))
        d_conv = d_act * (sig * (1.0 + conv * (1.0 - sig)))
        edge_ref[i] = d_conv[0:HALO, :]
        dext_ref[0:rows, :] = d_conv
        dext_ref[rows : rows + HALO, :] = (
            jnp.zeros((HALO, cols), F32) if last else next_ref[i]
        )
        d_pre = conv_ref[i, 0:1, :] * d_conv
        for j in range(taps):
            if j:
                d_pre = d_pre + conv_ref[i, j : j + 1, :] * dext_ref[j : j + rows, :]
            cg_ref[i * taps + j : i * taps + j + 1, :] = jnp.sum(
                d_conv * shifted[j], 0, keepdims=True
            )
        d_low = d_pre.astype(BF16)
        dproj_ref[i] = d_low
        d_normed = d_normed + dot_nt(d_low, w_ref[i])
    if not last:
        valid, count = valid_column(seq_ref, block * rows, rows)
        d_mean = jnp.dot(
            dlg_ref[...], gate_ref[...], preferred_element_type=F32, precision=HIGH
        )
        d_normed = d_normed + (valid / count) * d_mean[0:1, :]
    x = x_ref[...].astype(F32)
    scale = lax.rsqrt(jnp.mean(x * x, -1, keepdims=True) + NORM_EPS)
    weighted = d_normed * x
    gg_ref[...] = jnp.broadcast_to(jnp.sum(weighted * scale, 0, keepdims=True), gg_ref.shape)
    ones = jnp.ones((8, width), BF16)
    high, rest = two_parts(weighted * gain_ref[0:1, :])
    inner_ref[...] = dot_nt(ones, high) + dot_nt(ones, rest)
    low_ref[...] = d_normed.astype(BF16)
    for slot, out_ref in ((0, keep_ref), (1, send_ref)):
        for n in range(2):
            start = pl.multiple_of(peer_ref[slot + 2 * n] * cols, cols)
            out_ref[n] = low_ref[:, pl.ds(start, cols)]


def unprep_call(block, nb, shift, seq, peers, back, dgp, pre, w, conv, x, gains, edge, gate):
    cols = dgp.shape[1]
    width = x.shape[1]
    first, last = block == 0, block == nb - 1
    whole = lambda a: pl.BlockSpec(a.shape, lambda i, n=a.ndim: (0,) * n)
    smem = pl.BlockSpec(memory_space=pltpu.SMEM)
    at_block = pl.BlockSpec((SPAN, cols), lambda i: (block, 0))
    ins = [seq, peers, back["dq"], back["dk"], back["dv"], dgp, pre, w, conv, x, gains]
    in_specs = [
        smem,
        smem,
        whole(back["dq"]),
        at_block,
        at_block,
        whole(dgp),
        pl.BlockSpec((3, SPAN, cols), lambda i: (0, block, 0)),
        whole(w),
        whole(conv),
        pl.BlockSpec((SPAN, width), lambda i: (block, 0)),
        whole(gains),
    ]
    if not first:
        ins.append(pre)
        in_specs.append(
            pl.BlockSpec((3, HALO, cols), lambda i: (0, block * (SPAN // HALO) - 1, 0))
        )
    if not last:
        ins += [edge, back["dlg"], gate]
        in_specs += [whole(edge), whole(back["dlg"]), whole(gate)]
    struct = jax.ShapeDtypeStruct
    outs = [
        struct((4, SPAN, cols), BF16),
        struct((2, SPAN, cols), BF16),
        struct((2, SPAN, cols), BF16),
        struct((8, SPAN), F32),
        struct((16, cols), F32),
        struct((8, width), F32),
        struct((3, HALO, cols), F32),
    ]
    names = ["dproj", "keep", "send", "inner", "cg", "gg", "edge"]
    got = pl.pallas_call(
        functools.partial(unprep_kernel, block, nb, shift),
        grid=(1,),
        in_specs=in_specs,
        out_specs=[pl.BlockSpec(s.shape, lambda i, n=len(s.shape): (0,) * n) for s in outs],
        out_shape=outs,
        scratch_shapes=[
            pltpu.VMEM((HALO + SPAN, cols), F32),
            pltpu.VMEM((SPAN + HALO, cols), F32),
            pltpu.VMEM((SPAN, width), BF16),
        ],
        name=f"unprep_{block}",
    )(*ins)
    return dict(zip(names, got))


def per_device(
    layer_input,
    proj_weight,
    conv_weight,
    persist_kv,
    memory_in,
    memory_out,
    memory_gate,
    out_weight,
    ffn_in,
    ffn_out,
    norm_gains,
    seq_len,
    out_grad,
):
    rows, width = layer_input.shape
    cols = proj_weight.shape[2]
    heads = persist_kv.shape[1]
    head_size = persist_kv.shape[3]
    shift = head_size.bit_length() - 1
    mem_hid = memory_in.shape[2]
    nb = rows // SPAN
    taps = conv_weight.shape[1]
    me = lax.axis_index("head")
    count = width // cols
    peers = jnp.stack([me, me ^ 1, me ^ 2, me ^ 3]).astype(jnp.int32)
    swap = lambda a, bit: lax.ppermute(a, "head", [(i, i ^ bit) for i in range(count)])
    ow = lax.all_gather(out_weight, "head", axis=0, tiled=False)
    cot = lax.all_gather(out_grad, "head", axis=0, tiled=False)
    gate = jnp.transpose(memory_gate, (1, 2, 0)).reshape(3 * heads, width)
    gate = jnp.pad(gate, ((0, GATE_ROWS - 3 * heads), (0, 0)))
    pers = jnp.transpose(persist_kv, (0, 2, 1, 3)).reshape(2, -1, cols)
    q, k, v, kt, pre, gp, nl, mean, lg, pers_low = prep_call(
        seq_len, layer_input, proj_weight, conv_weight, norm_gains, gate, pers, shift
    )
    a = memory_in.reshape(cols, mem_hid)
    bt = jnp.transpose(memory_out, (0, 2, 1)).reshape(cols, mem_hid)
    sa = sbt = None
    states, mixes = [], []
    for c in range(nb):
        state = dict(a=a, bt=bt, sa=sa, sbt=sbt, lg=lg)
        got = mix_call(c, nb, shift, seq_len, lg, q, k, v, kt, pers_low, gp, a, bt, sa, sbt)
        if c < nb - 1:
            a, bt, sa, sbt, state["ga"], state["gbt"] = got[4:]
        states.append(state)
        mixes.append(dict(mixed=got[0], tot=got[1], att=got[2], linv=got[3]))
    for mix in mixes:
        near, far = swap(mix["mixed"], 1), swap(mix["mixed"], 2)
        mix["all"] = (mix["mixed"], near, far, swap(far, 1))
    names = ["res", "nt", "hid", "dgu", "pkeep", "psend", "dkeep", "dsend", "gg"]
    ffns = []
    for c in range(nb):
        got = ffn_call(
            c, peers, layer_input, mixes[c]["all"], ow, norm_gains, ffn_in, ffn_out, cot
        )
        ffn = dict(zip(names, got))
        s1 = (ffn["dkeep"].astype(F32) + swap(ffn["dsend"], 1).astype(F32)).astype(BF16)
        r2 = swap(s1, 2)
        ffn["pieces"] = (s1, r2, swap(s1, 1), swap(r2, 1))
        part = (ffn["pkeep"].astype(F32) + swap(ffn["psend"], 1).astype(F32)).astype(BF16)
        ffn["out"] = part[0].astype(F32) + swap(part[1], 2).astype(F32)
        ffns.append(ffn)
    rows_of = lambda key, axis: jnp.concatenate([f[key] for f in ffns], axis)
    normed_two, hidden, dgu = rows_of("nt", 0), rows_of("hid", 0), rows_of("dgu", 1)
    cot_full = jnp.transpose(cot, (1, 0, 2)).reshape(rows, width)
    along_rows = (((0,), (0,)), ((), ()))
    ffn_out_grad = lax.dot_general(hidden, cot_full, along_rows, preferred_element_type=F32)
    ffn_in_grad = [
        lax.dot_general(normed_two, dgu[i], along_rows, preferred_element_type=F32)
        for i in range(2)
    ]
    ffn_grads = lax.psum(
        jnp.stack([ffn_in_grad[0], ffn_in_grad[1], ffn_out_grad]).astype(BF16), "dp"
    )
    grads = adjoint = edge = None
    turns, unpreps, dlgs = [None] * nb, [None] * nb, [None] * nb
    for c in reversed(range(nb)):
        dres, rescol, dbr, dga, dgp = turn_call(
            c, peers, ffns[c]["pieces"], ffns[c]["res"], cot, ow, norm_gains, gp, mixes[c]["tot"]
        )
        turns[c] = dict(dres=dres, rescol=rescol, dbr=dbr)
        back = back_call(
            c, nb, shift, seq_len, q, k, v, kt, pers_low, dga, mixes[c]["att"], mixes[c]["linv"],
            states[c], grads, adjoint,
        )
        grads = adjoint = back
        dlgs[c] = back.get("dlg")
        unpreps[c] = unprep_call(
            c, nb, shift, seq_len, peers, back, dgp, pre, proj_weight, conv_weight, layer_input,
            norm_gains, edge, gate,
        )
        edge = unpreps[c]["edge"]
    layer_output = jnp.concatenate(
        [(turns[c]["rescol"] + ffns[c]["out"]).astype(BF16) for c in range(nb)], 0
    )
    own_gain = lax.dynamic_slice_in_dim(norm_gains[0:1], me * cols, cols, 1)
    d_inputs = []
    for c in range(nb):
        up = unpreps[c]
        half = (up["keep"].astype(F32) + swap(up["send"], 1).astype(F32)).astype(BF16)
        d_normed = half[0].astype(F32) + swap(half[1], 2).astype(F32)
        inner = up["inner"]
        inner = inner + swap(inner, 1)
        inner = (inner + swap(inner, 2))[0][:, None]
        x = layer_input[c * SPAN : (c + 1) * SPAN].astype(F32)
        scale = lax.rsqrt(jnp.mean(x * x, -1, keepdims=True) + NORM_EPS)
        x_own = lax.dynamic_slice_in_dim(x, me * cols, cols, 1)
        d_one = scale * own_gain * d_normed - x_own * (scale * scale * scale * inner / width)
        d_inputs.append(turns[c]["dres"] + d_one)
    input_grad = jnp.concatenate(d_inputs, 0)
    dproj = jnp.concatenate([u["dproj"] for u in unpreps], 1)
    proj_grad = jnp.stack(
        [
            lax.dot_general(nl, dproj[i], along_rows, preferred_element_type=F32)
            for i in range(4)
        ]
    ).astype(BF16)
    dbr = jnp.concatenate([t["dbr"] for t in turns], 0)
    out_grads = jnp.zeros((width, cols), BF16)
    for j in range(4):
        piece = jnp.concatenate([m["all"][j] for m in mixes], 0)
        part = lax.dot_general(piece, dbr, along_rows, preferred_element_type=F32)
        out_grads = lax.dynamic_update_slice(out_grads, part.astype(BF16), (peers[j] * cols, 0))
    conv_grad = sum(u["cg"] for u in unpreps)[: 3 * taps]
    keys = pers[0].reshape(-1, heads, head_size)
    d_keys = grads["dp"][0].reshape(keys.shape)
    unit = lax.rsqrt(jnp.sum(keys * keys, -1, keepdims=True) + UNIT_EPS)
    d_keys = unit * (
        d_keys - keys * (unit * unit * jnp.sum(d_keys * keys, -1, keepdims=True))
    )
    d_pers = jnp.stack([d_keys.reshape(-1, cols), grads["dp"][1]])
    gate_grad = jnp.zeros((3 * heads, width), F32)
    for c in range(nb - 1):
        gate_grad = gate_grad + dlgs[c][0, : 3 * heads, None] * mean[8 * c][None, :]
    gains = jnp.stack(
        [sum(u["gg"][0] for u in unpreps), sum(f["gg"][0] for f in ffns)]
    )
    gains = gains + swap(gains, 1)
    gains = gains + swap(gains, 2)
    tail = [
        proj_grad,
        out_grads,
        grads["ab"].astype(BF16),
        grads["btb"].astype(BF16),
    ]
    small = jnp.concatenate(
        [g.reshape(-1, cols) for g in (gate_grad, conv_grad, d_pers, gains)], 0
    )
    tail = lax.psum(tail, "dp")
    small = lax.psum(small, "dp")
    sizes = [3 * heads * width, 3 * taps * cols, d_pers.size, 2 * width]
    cuts = [0]
    for size in sizes:
        cuts.append(cuts[-1] + size // cols)
    gate_grad, conv_grad, d_pers, gains = (small[b:e] for b, e in zip(cuts, cuts[1:]))
    return (
        layer_output,
        input_grad,
        tail[0].astype(F32),
        conv_grad.reshape(3, taps, cols),
        jnp.transpose(d_pers.reshape(2, -1, heads, head_size), (0, 2, 1, 3)),
        tail[2].astype(F32).reshape(memory_in.shape),
        jnp.transpose(tail[3].astype(F32).reshape(heads, head_size, mem_hid), (0, 2, 1)),
        jnp.transpose(gate_grad.reshape(3, heads, width), (2, 0, 1)),
        tail[1].astype(F32),
        ffn_grads[:2].astype(F32),
        ffn_grads[2].astype(F32),
        gains.reshape(2, width),
    )


def solution(mesh):
    in_specs = (
        P("dp", None),
        P(None, None, "head"),
        P(None, None, "head"),
        P(None, "head", None, None),
        P("head", None, None),
        P("head", None, None),
        P(None, None, "head"),
        P(None, "head"),
        P(None, None, "head"),
        P("head", None),
        P(),
        P("dp"),
        P("dp", "head"),
    )
    out_specs = (
        P("dp", "head"),
        P("dp", "head"),
        P(None, None, "head"),
        P(None, None, "head"),
        P(None, "head", None, None),
        P("head", None, None),
        P("head", None, None),
        P(None, None, "head"),
        P(None, "head"),
        P(None, None, "head"),
        P("head", None),
        P(),
    )
    return jax.shard_map(
        per_device, mesh=mesh, in_specs=in_specs, out_specs=out_specs, check_vma=False
    )
```

```python
import functools

import jax
import jax.numpy as jnp
from jax import lax
from jax.experimental import pallas as pl
from jax.experimental.pallas import tpu as pltpu
from jax.sharding import PartitionSpec as P

F32 = jnp.float32
BF16 = jnp.bfloat16
HIGH = lax.Precision.HIGHEST
NORM_EPS = 1e-05
UNIT_EPS = 1e-06
SCORE_SCALE = 8.0
SPAN = 512
HALO = 8
GATE_ROWS = 128
COST_UNIT = 1.5e8
SMALL_ROWS = 1024


def dot_nn(left, right):
    return jnp.dot(left, right, preferred_element_type=F32)


def dot_nt(left, right, precision=None):
    return lax.dot_general(
        left, right, (((1,), (1,)), ((), ())), preferred_element_type=F32, precision=precision
    )


def two_parts(value):
    high = value.astype(BF16)
    return high, (value - high.astype(F32)).astype(BF16)


def iota(shape, axis):
    return lax.broadcasted_iota(jnp.int32, shape, axis)


def cost(microseconds):
    return pl.CostEstimate(
        flops=int(microseconds * COST_UNIT), transcendentals=0, bytes_accessed=1 << 20
    )


def head_blocks(cols, shift):
    same = (iota((cols, cols), 0) >> shift) == (iota((cols, cols), 1) >> shift)
    return jnp.where(same, 1.0, 0.0).astype(BF16)


def head_sum(value, blocks):
    high, rest = two_parts(value)
    return dot_nn(high, blocks) + dot_nn(rest, blocks)


def valid_column(seq_ref, start, rows):
    inside = (start + iota((rows, 1), 0)) < seq_ref[0]
    valid = jnp.where(inside, 1.0, 0.0)
    return valid, jnp.maximum(jnp.sum(valid, 0, keepdims=True), 1.0)


def head_mask(cols, shift, head):
    return jnp.where((iota((1, cols), 1) >> shift) == head, 1.0, 0.0)


def gate_rows(logits, group, heads, head_size, width):
    parts = [
        jnp.broadcast_to(
            logits[0:1, group * heads + head : group * heads + head + 1], (head_size, width)
        )
        for head in range(heads)
    ]
    return jnp.concatenate(parts, 0)


def prep_kernel(
    shift,
    seq_ref,
    x_ref,
    w_ref,
    conv_ref,
    gain_ref,
    gate_ref,
    pers_ref,
    q_ref,
    k_ref,
    v_ref,
    kt_ref,
    pre_ref,
    gp_ref,
    nl_ref,
    mean_ref,
    lg_ref,
    pers_out_ref,
    ext_ref,
):
    step = pl.program_id(0)
    rows, cols = q_ref.shape
    blocks = head_blocks(cols, shift)

    @pl.when(step == 0)
    def _():
        ext_ref[:, 0:HALO, :] = jnp.zeros((3, HALO, cols), F32)
        keys = pers_ref[0]
        keys = keys * lax.rsqrt(head_sum(keys * keys, blocks) + UNIT_EPS)
        pers_out_ref[0] = keys.astype(BF16)
        pers_out_ref[1] = pers_ref[1].astype(BF16)

    x = x_ref[...].astype(F32)
    scale = lax.rsqrt(jnp.mean(x * x, -1, keepdims=True) + NORM_EPS)
    normed = x * scale * gain_ref[0:1, :]
    low = normed.astype(BF16)
    nl_ref[...] = low
    valid, count = valid_column(seq_ref, step * rows, rows)
    mean = jnp.broadcast_to(
        jnp.sum(normed * valid, 0, keepdims=True) / count, (8, normed.shape[1])
    )
    mean_ref[...] = mean
    lg_ref[...] = dot_nt(mean, gate_ref[...], HIGH)
    gp_ref[...] = dot_nn(low, w_ref[3])
    for i in range(3):
        pre = dot_nn(low, w_ref[i])
        pre_ref[i] = pre
        ext_ref[i, HALO : HALO + rows, :] = pre
        conv = conv_ref[i, 0:1, :] * pre
        for j in range(1, conv_ref.shape[1]):
            conv = conv + conv_ref[i, j : j + 1, :] * ext_ref[i, HALO - j : HALO - j + rows, :]
        ext_ref[i, 0:HALO, :] = pre[rows - HALO :, :]
        act = conv * jax.nn.sigmoid(conv)
        if i < 2:
            act = act * lax.rsqrt(head_sum(act * act, blocks) + UNIT_EPS)
        act_low = act.astype(BF16)
        (q_ref, k_ref, v_ref)[i][...] = act_low
        if i == 1:
            kt_ref[...] = jnp.transpose(act_low.astype(F32)).astype(BF16)


def prep_call(seq, x, w, conv, gains, gate, pers, shift):
    rows, width = x.shape
    cols = w.shape[2]
    nb = rows // SPAN
    whole = lambda a: pl.BlockSpec(a.shape, lambda c, n=a.ndim: (0,) * n)
    row_cols = pl.BlockSpec((SPAN, cols), lambda c: (c, 0))
    return pl.pallas_call(
        functools.partial(prep_kernel, shift),
        grid=(nb,),
        in_specs=[
            pl.BlockSpec(memory_space=pltpu.SMEM),
            pl.BlockSpec((SPAN, width), lambda c: (c, 0)),
            whole(w),
            whole(conv),
            whole(gains),
            whole(gate),
            whole(pers),
        ],
        out_specs=[
            row_cols,
            row_cols,
            row_cols,
            pl.BlockSpec((cols, SPAN), lambda c: (0, c)),
            pl.BlockSpec((3, SPAN, cols), lambda c: (0, c, 0)),
            row_cols,
            pl.BlockSpec((SPAN, width), lambda c: (c, 0)),
            pl.BlockSpec((8, width), lambda c: (c, 0)),
            pl.BlockSpec((8, GATE_ROWS), lambda c: (c, 0)),
            whole(pers),
        ],
        out_shape=[
            jax.ShapeDtypeStruct((rows, cols), BF16),
            jax.ShapeDtypeStruct((rows, cols), BF16),
            jax.ShapeDtypeStruct((rows, cols), BF16),
            jax.ShapeDtypeStruct((cols, rows), BF16),
            jax.ShapeDtypeStruct((3, rows, cols), F32),
            jax.ShapeDtypeStruct((rows, cols), F32),
            jax.ShapeDtypeStruct((rows, width), BF16),
            jax.ShapeDtypeStruct((nb * 8, width), F32),
            jax.ShapeDtypeStruct((nb * 8, GATE_ROWS), F32),
            jax.ShapeDtypeStruct(pers.shape, BF16),
        ],
        scratch_shapes=[pltpu.VMEM((3, HALO + SPAN, cols), F32)],
        cost_estimate=cost(15),
        name="prep",
    )(seq, x, w, conv, gains, gate, pers)


def mix_kernel(block, blocks_all, shift, first, last, *refs):
    it = iter(refs)
    seq_ref, lg_ref, q_ref, k_ref, v_ref, kt_ref, pers_ref, gp_ref, a_ref, bt_ref = (
        next(it) for _ in range(10)
    )
    sa_ref, sbt_ref = (None, None) if first or last else (next(it), next(it))
    mixed_ref, tot_ref, att_ref, linv_ref = (next(it) for _ in range(4))
    if not last:
        a2_ref, bt2_ref, sa2_ref, sbt2_ref, ga_ref, gbt_ref = (next(it) for _ in range(6))
        z_ref, r_ref = next(it), next(it)
    rows, cols = q_ref.shape
    head_size = 1 << shift
    heads = cols // head_size
    a_low = a_ref[...].astype(BF16)
    bt_low = bt_ref[...].astype(BF16)
    valid, count = valid_column(seq_ref, block * rows, rows)
    weight = valid / count
    att_ref[...] = jnp.zeros((rows, cols), F32)
    linv_ref[...] = jnp.zeros((rows, cols), F32)
    tot_ref[...] = jnp.zeros((rows, cols), F32)
    if not last:
        r_ref[...] = jnp.zeros((rows, cols), F32)

    def one_head(head, carry):
        mask = head_mask(cols, shift, head)
        mask_low = mask.astype(BF16)
        ones_low = (1.0 - mask).astype(BF16)
        query = q_ref[...] * mask_low
        scaled = query * SCORE_SCALE
        raised = jnp.exp(dot_nt(scaled, pers_ref[0])).astype(BF16)
        total = dot_nn(raised, pers_ref[1] * mask_low + ones_low)
        for j in range(block + 1):
            span = slice(j * rows, (j + 1) * rows)
            raised = jnp.exp(dot_nt(scaled, k_ref[span, :]))
            if j == block:
                raised = jnp.where(
                    iota((rows, rows), 0) >= iota((rows, rows), 1), raised, 0.0
                )
            total = total + dot_nn(raised.astype(BF16), v_ref[span, :] * mask_low + ones_low)
        inverse = 1.0 / pltpu.roll(total, head_size, 1)
        inside = jnp.broadcast_to(mask, (rows, cols)) > 0.5
        linv_ref[...] = jnp.where(inside, inverse, linv_ref[...])
        attended = jnp.where(inside, total * inverse, 0.0)
        att_ref[...] = att_ref[...] + attended
        hid = dot_nn(query, a_low)
        hid = hid * jax.nn.sigmoid(hid)
        recalled = dot_nt(hid.astype(BF16), bt_low) * mask
        tot_ref[...] = tot_ref[...] + attended + recalled
        if not last:
            hid = dot_nn(k_ref[block * rows : (block + 1) * rows, :] * mask_low, a_low)
            sig = jax.nn.sigmoid(hid)
            act = (hid * sig).astype(BF16)
            z_ref[head] = act
            target = v_ref[block * rows : (block + 1) * rows, :].astype(F32)
            resid = (dot_nt(act, bt_low) - target) * mask * weight
            r_ref[...] = r_ref[...] + resid
            d_hid = dot_nn(resid.astype(BF16), bt_low) * (sig * (1.0 + hid * (1.0 - sig)))
            at = pl.ds(pl.multiple_of(head * head_size, head_size), head_size)
            ga_ref[at, :] = dot_nn(kt_ref[at, :], d_hid.astype(BF16))
        return carry

    lax.fori_loop(0, heads, one_head, 0)
    gate = jax.nn.sigmoid(gp_ref[...])
    mixed_ref[...] = (tot_ref[...] * gate).astype(BF16)
    if not last:
        resid_t = jnp.transpose(r_ref[...]).astype(BF16)
        for head in range(heads):
            at = slice(head * head_size, (head + 1) * head_size)
            gbt_ref[at, :] = dot_nn(resid_t[at, :], z_ref[head])
        width = a_ref.shape[1]
        logits = lg_ref[...]
        step = 0.2 * jax.nn.sigmoid(gate_rows(logits, 0, heads, head_size, width))
        keep = jax.nn.sigmoid(gate_rows(logits, 1, heads, head_size, width))
        stay = 1.0 - 0.5 * jax.nn.sigmoid(gate_rows(logits, 2, heads, head_size, width))
        moment_a = -step * ga_ref[...]
        moment_b = -step * gbt_ref[...]
        if not first:
            moment_a = moment_a + keep * sa_ref[...]
            moment_b = moment_b + keep * sbt_ref[...]
        sa2_ref[...] = moment_a
        sbt2_ref[...] = moment_b
        a2_ref[...] = stay * a_ref[...] + moment_a
        bt2_ref[...] = stay * bt_ref[...] + moment_b


def mix_call(block, nb, shift, seq, lg, q, k, v, kt, pers, gp, a, bt, sa, sbt):
    rows, cols = q.shape
    first, last = block == 0, block == nb - 1
    heads = cols >> shift
    whole = lambda s: pl.BlockSpec(s, lambda i, n=len(s): (0,) * n)
    at_block = pl.BlockSpec((SPAN, cols), lambda i: (block, 0))
    upto = pl.BlockSpec(((block + 1) * SPAN, cols), lambda i: (0, 0))
    state = whole(a.shape)
    ins = [seq, lg, q, k, v, kt, pers, gp, a, bt]
    in_specs = [
        pl.BlockSpec(memory_space=pltpu.SMEM),
        pl.BlockSpec((8, GATE_ROWS), lambda i: (block, 0)),
        at_block,
        upto,
        upto,
        pl.BlockSpec((cols, SPAN), lambda i: (0, block)),
        whole(pers.shape),
        at_block,
        state,
        state,
    ]
    if not (first or last):
        ins += [sa, sbt]
        in_specs += [state, state]
    row_spec = whole((SPAN, cols))
    outs = [jax.ShapeDtypeStruct((SPAN, cols), BF16)] + [
        jax.ShapeDtypeStruct((SPAN, cols), F32)
    ] * 3
    out_specs = [row_spec] * 4
    scratch = []
    if not last:
        outs += [jax.ShapeDtypeStruct(a.shape, F32)] * 6
        out_specs += [state] * 6
        scratch = [pltpu.VMEM((heads, SPAN, a.shape[1]), BF16), pltpu.VMEM((SPAN, cols), F32)]
    return pl.pallas_call(
        functools.partial(mix_kernel, block, nb, shift, first, last),
        grid=(1,),
        in_specs=in_specs,
        out_specs=out_specs,
        out_shape=outs,
        scratch_shapes=scratch,
        cost_estimate=cost(9),
        name=f"mix_{block}",
    )(*ins)


def ffn_kernel(first_call, *refs):
    it = iter(refs)
    take = lambda n: [next(it) for _ in range(n)]
    peer_ref, x_ref, m0_ref, m1_ref, m2_ref, m3_ref = take(6)
    ow_ref, gain_ref, fin_ref, fout_ref, cot_ref = take(5)
    if not first_call:
        gg_in_ref = take(8)[0]
    gg_ref, nt_ref, hid_ref, dgu_ref, part_keep_ref, part_send_ref, cotf_ref, mfull_ref = take(8)
    res_ref, dn_keep_ref, dn_send_ref = take(3)
    if first_call:
        take(1)
    (part_ref,) = take(1)
    rows, width = x_ref.shape
    cols = m0_ref.shape[1]
    shards = width // cols
    branch = None
    for j, m_ref in enumerate((m0_ref, m1_ref, m2_ref, m3_ref)):
        at = pl.ds(pl.multiple_of(peer_ref[j] * cols, cols), cols)
        weight = jnp.concatenate([ow_ref[p, at, :] for p in range(shards)], 1)
        mfull_ref[:, at] = m_ref[...]
        term = dot_nn(m_ref[...], weight)
        branch = term if branch is None else branch + term
    residual = x_ref[...].astype(F32) + branch
    res_ref[...] = residual
    scale = lax.rsqrt(jnp.mean(residual * residual, -1, keepdims=True) + NORM_EPS)
    low = (residual * scale * gain_ref[1:2, :]).astype(BF16)
    nt_ref[...] = low
    gate_pre = dot_nn(low, fin_ref[0])
    up_pre = dot_nn(low, fin_ref[1])
    sig = jax.nn.sigmoid(gate_pre)
    silu = gate_pre * sig
    hidden = (silu * up_pre).astype(BF16)
    hid_ref[...] = hidden
    cot = jnp.concatenate([cot_ref[p] for p in range(shards)], 1)
    cotf_ref[...] = cot
    d_hidden = dot_nt(cot, fout_ref[...])
    slope = sig * (1.0 + gate_pre * (1.0 - sig))
    d_gate = (d_hidden * up_pre * slope).astype(BF16)
    d_up = (d_hidden * silu).astype(BF16)
    dgu_ref[0] = d_gate
    dgu_ref[1] = d_up
    d_normed = dot_nt(d_gate, fin_ref[0]) + dot_nt(d_up, fin_ref[1])
    gains = jnp.sum(d_normed * residual * scale, 0, keepdims=True)

    @pl.when(pl.program_id(0) == 0)
    def _():
        gg_ref[...] = jnp.zeros(gg_ref.shape, F32) if first_call else gg_in_ref[...]

    gg_ref[...] = gg_ref[...] + jnp.broadcast_to(gains, gg_ref.shape)
    half = width // 2
    part_ref[...] = d_normed.astype(BF16)
    core = peer_ref[0] & 1
    dn_keep_ref[...] = part_ref[:, pl.ds(pl.multiple_of(core * half, half), half)]
    dn_send_ref[...] = part_ref[:, pl.ds(pl.multiple_of((1 - core) * half, half), half)]
    part_ref[...] = dot_nn(hidden, fout_ref[...]).astype(BF16)
    for slot, out_ref in ((0, part_keep_ref), (1, part_send_ref)):
        for n in range(2):
            start = pl.multiple_of(peer_ref[slot + 2 * n] * cols, cols)
            out_ref[n] = part_ref[:, pl.ds(start, cols)]


def ffn_call(block, peers, x, mixed, ow, gains, fin, fout, cot, shared):
    rows, width = x.shape
    cols = mixed[0].shape[1]
    tile = SPAN // 2
    steps = SPAN // tile
    shards = width // cols
    hidden = fout.shape[0]
    whole = lambda a: pl.BlockSpec(a.shape, lambda i, n=a.ndim: (0,) * n)
    row = lambda n: pl.BlockSpec((tile, n), lambda i: (i, 0))
    at_rows = lambda n: pl.BlockSpec((tile, n), lambda i: (block * steps + i, 0))
    stacked = lambda n, w: pl.BlockSpec((n, tile, w), lambda i: (0, block * steps + i, 0))
    struct = jax.ShapeDtypeStruct
    ins = [peers, x, *mixed, ow, gains, fin, fout, cot]
    in_specs = [
        pl.BlockSpec(memory_space=pltpu.SMEM),
        at_rows(width),
        row(cols),
        row(cols),
        row(cols),
        row(cols),
        whole(ow),
        whole(gains),
        whole(fin),
        whole(fout),
        stacked(shards, cols),
    ]
    aliases = {}
    if shared is not None:
        aliases = {len(ins) + n: n for n in range(len(shared))}
        ins += shared
        in_specs += [pl.BlockSpec((8, width), lambda i: (0, 0))]
        in_specs += [pl.BlockSpec(memory_space=pl.ANY)] * (len(shared) - 1)
    room = [struct((3 * width, width), BF16)] if shared is None else []
    got = pl.pallas_call(
        functools.partial(ffn_kernel, shared is None),
        grid=(steps,),
        in_specs=in_specs,
        out_specs=[
            pl.BlockSpec((8, width), lambda i: (0, 0)),
            at_rows(width),
            at_rows(hidden),
            stacked(2, hidden),
            stacked(2, cols),
            stacked(2, cols),
            at_rows(width),
            at_rows(width),
            row(width),
            row(width // 2),
            row(width // 2),
        ]
        + [pl.BlockSpec(memory_space=pl.ANY)] * len(room),
        out_shape=[
            struct((8, width), F32),
            struct((rows, width), BF16),
            struct((rows, hidden), BF16),
            struct((2, rows, hidden), BF16),
            struct((2, rows, cols), BF16),
            struct((2, rows, cols), BF16),
            struct((rows, width), BF16),
            struct((rows, width), BF16),
            struct((SPAN, width), F32),
            struct((SPAN, width // 2), BF16),
            struct((SPAN, width // 2), BF16),
        ]
        + room,
        input_output_aliases=aliases,
        scratch_shapes=[pltpu.VMEM((tile, width), BF16)],
        cost_estimate=cost(15),
        name=f"ffn_{block}",
    )(*ins)
    return got[:8], got[8:]


def turn_kernel(first_call, *refs):
    it = iter(refs)
    take = lambda n: [next(it) for _ in range(n)]
    peer_ref, s1_ref, r2_ref, ps1_ref, pr2_ref, res_ref, cot_ref, ow_ref = take(8)
    gain_ref, gp_ref, tot_ref = take(3)
    if not first_call:
        take(4)
    dres_ref, rescol_ref, dbr_ref, dgall_ref, dga_ref, dgp_ref, full_ref = take(7)
    rows, width = res_ref.shape
    cols = gp_ref.shape[1]
    shards = width // cols
    half = width // 2
    core = peer_ref[0] & 1
    at_own = pl.ds(pl.multiple_of(core * half, half), half)
    at_other = pl.ds(pl.multiple_of((1 - core) * half, half), half)
    full_ref[:, at_own] = s1_ref[...].astype(F32) + r2_ref[...].astype(F32)
    full_ref[:, at_other] = ps1_ref[...].astype(F32) + pr2_ref[...].astype(F32)
    residual = res_ref[...]
    scale = lax.rsqrt(jnp.mean(residual * residual, -1, keepdims=True) + NORM_EPS)
    gained = full_ref[...] * gain_ref[1:2, :]
    inner = jnp.sum(gained * residual, -1, keepdims=True) / width
    cot = jnp.concatenate([cot_ref[p].astype(F32) for p in range(shards)], 1)
    d_residual = cot + scale * gained - residual * (scale * scale * scale * inner)
    d_branch = d_residual.astype(BF16)
    own = pl.ds(pl.multiple_of(peer_ref[0] * cols, cols), cols)
    weight = jnp.concatenate([ow_ref[p, own, :] for p in range(shards)], 1)
    d_mixed = dot_nt(d_branch, weight)
    full_ref[...] = d_residual
    mine = full_ref[:, own]
    dres_ref[...] = mine
    dbr_ref[...] = mine.astype(BF16)
    rescol_ref[...] = res_ref[:, own]
    gate = jax.nn.sigmoid(gp_ref[...])
    d_gated = d_mixed * gate
    dga_ref[...] = d_gated.astype(BF16)
    d_gate = (d_gated * tot_ref[...] * (1.0 - gate)).astype(BF16)
    dgp_ref[...] = d_gate
    dgall_ref[...] = d_gate


def turn_call(block, peers, pieces, res, cot, ow, gains, gp, tot, shared):
    width = res.shape[1]
    rows, cols = gp.shape
    tile = SPAN // 2
    steps = SPAN // tile
    shards = width // cols
    whole = lambda a: pl.BlockSpec(a.shape, lambda i, n=a.ndim: (0,) * n)
    row = lambda n: pl.BlockSpec((tile, n), lambda i: (i, 0))
    at_rows = lambda n: pl.BlockSpec((tile, n), lambda i: (block * steps + i, 0))
    struct = jax.ShapeDtypeStruct
    ins = [peers, *pieces, res, cot, ow, gains, gp, tot]
    in_specs = [
        pl.BlockSpec(memory_space=pltpu.SMEM),
        row(width // 2),
        row(width // 2),
        row(width // 2),
        row(width // 2),
        row(width),
        pl.BlockSpec((shards, tile, cols), lambda i: (0, block * steps + i, 0)),
        whole(ow),
        whole(gains),
        at_rows(cols),
        row(cols),
    ]
    aliases = {}
    if shared is not None:
        aliases = {len(ins) + n: n for n in range(len(shared))}
        ins += shared
        in_specs += [pl.BlockSpec(memory_space=pl.ANY)] * len(shared)
    got = pl.pallas_call(
        functools.partial(turn_kernel, shared is None),
        grid=(steps,),
        in_specs=in_specs,
        out_specs=[at_rows(cols)] * 4 + [row(cols)] * 2,
        out_shape=[
            struct((rows, cols), F32),
            struct((rows, cols), F32),
            struct((rows, cols), BF16),
            struct((rows, cols), BF16),
            struct((SPAN, cols), BF16),
            struct((SPAN, cols), BF16),
        ],
        input_output_aliases=aliases,
        scratch_shapes=[pltpu.VMEM((tile, width), F32)],
        cost_estimate=cost(5),
        name=f"turn_{block}",
    )(*ins)
    return got[:4], got[4:]


def back_kernel(block, nb, shift, *refs):
    it = iter(refs)
    take = lambda n: [next(it) for _ in range(n)]
    first, last = block == 0, block == nb - 1
    seq_ref, q_ref, k_ref, v_ref, kt_ref, pers_ref, dga_ref, att_ref, linv_ref = take(9)
    a_ref, bt_ref = take(2)
    if not last:
        dk_in_ref, dv_in_ref, dp_in_ref, lg_ref, ga_ref, gbt_ref, ab_in_ref, btb_in_ref = take(8)
        sab_in_ref, sbtb_in_ref = take(2) if block < nb - 2 else (None, None)
        sa_ref, sbt_ref = (None, None) if first else take(2)
    dq_ref, dk_ref, dv_ref, dp_ref, ab_ref, btb_ref = take(6)
    if not last:
        (dlg_ref,) = take(1)
        sab_ref, sbtb_ref = (None, None) if first else take(2)
    lt_ref, dt_ref, dqt_ref, qt_ref, dot_ref = take(5)
    if not last:
        z_ref, zd_ref, r_ref, y_ref, h_ref = take(5)
    rows, cols = q_ref.shape
    head_size = 1 << shift
    heads = cols // head_size
    own = slice(block * rows, (block + 1) * rows)
    a_low = a_ref[...].astype(BF16)
    bt_low = bt_ref[...].astype(BF16)
    if last:
        dk_ref[...] = jnp.zeros(dk_ref.shape, F32)
        dv_ref[...] = jnp.zeros(dv_ref.shape, F32)
        dp_ref[...] = jnp.zeros(dp_ref.shape, F32)
        ab_ref[...] = jnp.zeros(ab_ref.shape, F32)
        btb_ref[...] = jnp.zeros(btb_ref.shape, F32)
    else:
        dk_ref[...] = dk_in_ref[...]
        dv_ref[...] = dv_in_ref[...]
        dp_ref[...] = dp_in_ref[...]
    pick = (iota((8, cols), 1) >> shift) == iota((8, cols), 0)
    start = iota((8, cols), 1) == (iota((8, cols), 0) << shift)
    lt_ref[...] = dot_nt(jnp.where(start, 1.0, 0.0), linv_ref[...], HIGH)
    d_gated = dga_ref[...].astype(F32)
    dt_ref[...] = dot_nt(jnp.where(pick, 1.0, 0.0), d_gated * att_ref[...], HIGH)
    dq_ref[...] = jnp.zeros((rows, cols), F32)
    qt_ref[...] = jnp.transpose(q_ref[...].astype(F32)).astype(BF16)
    dot_ref[...] = jnp.transpose(d_gated).astype(BF16)
    if not last:
        valid, count = valid_column(seq_ref, block * rows, rows)
        weight = valid / count
        width = a_ref.shape[1]
        logits = lg_ref[...]
        sig_step = jax.nn.sigmoid(gate_rows(logits, 0, heads, head_size, width))
        keep = jax.nn.sigmoid(gate_rows(logits, 1, heads, head_size, width))
        sig_forget = jax.nn.sigmoid(gate_rows(logits, 2, heads, head_size, width))
        tot_a, tot_b = ab_in_ref[...], btb_in_ref[...]
        if sab_in_ref is not None:
            tot_a, tot_b = tot_a + sab_in_ref[...], tot_b + sbtb_in_ref[...]
        h_ref[0] = (-0.2 * sig_step * tot_a).astype(BF16)
        h_ref[1] = (-0.2 * sig_step * tot_b).astype(BF16)
        d_step = -(ga_ref[...] * tot_a + gbt_ref[...] * tot_b)
        groups = [d_step * (0.2 * sig_step * (1.0 - sig_step)), None, None]
        if not first:
            groups[1] = (sa_ref[...] * tot_a + sbt_ref[...] * tot_b) * (keep * (1.0 - keep))
        d_forget = -(a_ref[...] * ab_in_ref[...] + bt_ref[...] * btb_in_ref[...])
        groups[2] = d_forget * (0.5 * sig_forget * (1.0 - sig_forget))
        d_logits = jnp.zeros((8, GATE_ROWS), F32)
        for g, value in enumerate(groups):
            if value is None:
                continue
            for head in range(heads):
                part = value[head * head_size : (head + 1) * head_size, :]
                figure = jnp.sum(jnp.sum(part, 1, keepdims=True), 0, keepdims=True)
                here = iota((8, GATE_ROWS), 1) == g * heads + head
                d_logits = d_logits + jnp.where(here, 1.0, 0.0) * figure
        dlg_ref[...] = d_logits
        stay = 1.0 - 0.5 * sig_forget
        ab_ref[...] = stay * ab_in_ref[...]
        btb_ref[...] = stay * btb_in_ref[...]
        if not first:
            sab_ref[...] = keep * tot_a
            sbtb_ref[...] = keep * tot_b
        r_ref[...] = jnp.zeros((rows, cols), F32)
        y_ref[...] = jnp.zeros((rows, cols), F32)

    def one_head(head, carry):
        mask = head_mask(cols, shift, head)
        mask_low = mask.astype(BF16)
        query = q_ref[...] * mask_low
        scaled = query * SCORE_SCALE
        d_out = dga_ref[...] * mask_low
        at = pl.ds(pl.multiple_of(head * head_size, head_size), head_size)
        inverse = lt_ref[pl.ds(head, 1), :]
        delta = dt_ref[pl.ds(head, 1), :]
        probs = jnp.exp(dot_nt(pers_ref[0], scaled)) * inverse
        d_scores = (probs * (dot_nt(pers_ref[1], d_out) - delta)).astype(BF16)
        dp_ref[0] = dp_ref[0] + dot_nn(d_scores, scaled)
        dp_ref[1] = dp_ref[1] + dot_nn(probs.astype(BF16), d_out)
        d_query = lax.dot_general(
            d_scores, pers_ref[0], (((0,), (0,)), ((), ())), preferred_element_type=F32
        )
        d_query = d_query * SCORE_SCALE
        d_query_t = jnp.zeros((head_size, rows), F32)
        for j in range(block + 1):
            span = slice(j * rows, (j + 1) * rows)
            probs = jnp.exp(dot_nt(k_ref[span, :], scaled)) * inverse
            if j == block:
                probs = jnp.where(iota((rows, rows), 0) <= iota((rows, rows), 1), probs, 0.0)
            d_scores = (probs * (dot_nt(v_ref[span, :], d_out) - delta)).astype(BF16)
            dv_ref[span, :] = dv_ref[span, :] + dot_nn(probs.astype(BF16), d_out)
            dk_ref[span, :] = dk_ref[span, :] + dot_nn(d_scores, scaled)
            d_query_t = d_query_t + dot_nn(kt_ref[at, span], d_scores)
        dqt_ref[at, :] = d_query_t * SCORE_SCALE
        hid = dot_nn(query, a_low)
        sig = jax.nn.sigmoid(hid)
        d_hid = dot_nn(d_out, bt_low) * (sig * (1.0 + hid * (1.0 - sig)))
        d_hid = d_hid.astype(BF16)
        dq_ref[...] = dq_ref[...] + (d_query + dot_nt(d_hid, a_low)) * mask
        grad_a = dot_nn(qt_ref[at, :], d_hid)
        grad_b = dot_nn(dot_ref[at, :], (hid * sig).astype(BF16))
        if not last:
            key = k_ref[own, :] * mask_low
            hid = dot_nn(key, a_low)
            probe = dot_nn(key, h_ref[0])
            sig = jax.nn.sigmoid(hid)
            act = (hid * sig).astype(BF16)
            z_ref[head] = act
            slope = sig * (1.0 + hid * (1.0 - sig))
            curve = sig * (1.0 - sig) * (2.0 + hid * (1.0 - 2.0 * sig))
            target = v_ref[own, :].astype(F32)
            resid = (dot_nt(act, bt_low) - target) * mask * weight
            r_ref[...] = r_ref[...] + resid
            resid = resid.astype(BF16)
            d_act = dot_nn(resid, bt_low)
            d_slope = (probe * slope).astype(BF16)
            zd_ref[head] = d_slope
            d_net = (dot_nt(act, h_ref[1]) + dot_nt(d_slope, bt_low)) * mask * weight
            y_ref[...] = y_ref[...] + d_net
            back = dot_nn(resid, h_ref[1]) + dot_nn(d_net.astype(BF16), bt_low)
            d_hid = (probe * d_act * curve + back * slope).astype(BF16)
            direct = (d_act * slope).astype(BF16)
            d_key = (dot_nt(direct, h_ref[0]) + dot_nt(d_hid, a_low)) * mask
            dk_ref[own, :] = dk_ref[own, :] + d_key
            grad_a = grad_a + dot_nn(kt_ref[at, own], d_hid)
        ab_ref[at, :] = ab_ref[at, :] + grad_a
        btb_ref[at, :] = btb_ref[at, :] + grad_b
        return carry

    lax.fori_loop(0, heads, one_head, 0)
    dq_ref[...] = dq_ref[...] + jnp.transpose(dqt_ref[...])
    if not last:
        dv_ref[own, :] = dv_ref[own, :] - y_ref[...]
        resid_t = jnp.transpose(r_ref[...]).astype(BF16)
        net_t = jnp.transpose(y_ref[...]).astype(BF16)
        for head in range(heads):
            at = slice(head * head_size, (head + 1) * head_size)
            grad_b = dot_nn(resid_t[at, :], zd_ref[head]) + dot_nn(net_t[at, :], z_ref[head])
            btb_ref[at, :] = btb_ref[at, :] + grad_b


def back_call(block, nb, shift, seq, q, k, v, kt, pers, dga, att, linv, state, grads, adjoint):
    cols = q.shape[1]
    heads = cols >> shift
    first, last = block == 0, block == nb - 1
    done = (block + 1) * SPAN
    whole = lambda s: pl.BlockSpec(s, lambda i, n=len(s): (0,) * n)
    at_block = pl.BlockSpec((SPAN, cols), lambda i: (block, 0))
    upto = pl.BlockSpec((done, cols), lambda i: (0, 0))
    rows_spec = whole((SPAN, cols))
    square = state["a"].shape
    ins = [seq, q, k, v, kt, pers, dga, att, linv, state["a"], state["bt"]]
    in_specs = [
        pl.BlockSpec(memory_space=pltpu.SMEM),
        at_block,
        upto,
        upto,
        pl.BlockSpec((cols, done), lambda i: (0, 0)),
        whole(pers.shape),
        rows_spec,
        rows_spec,
        rows_spec,
        whole(square),
        whole(square),
    ]
    if not last:
        ins += [grads["dk"], grads["dv"], grads["dp"], state["lg"], state["ga"], state["gbt"]]
        ins += [adjoint["ab"], adjoint["btb"]]
        in_specs += [upto, upto, whole(pers.shape)]
        in_specs += [pl.BlockSpec((8, GATE_ROWS), lambda i: (block, 0))]
        in_specs += [whole(square)] * 4
        if block < nb - 2:
            ins += [adjoint["sab"], adjoint["sbtb"]]
            in_specs += [whole(square)] * 2
        if not first:
            ins += [state["sa"], state["sbt"]]
            in_specs += [whole(square)] * 2
    names = ["dq", "dk", "dv", "dp", "ab", "btb"]
    shapes = [(SPAN, cols), (done, cols), (done, cols), pers.shape, square, square]
    if not last:
        names.append("dlg")
        shapes.append((8, GATE_ROWS))
        if not first:
            names += ["sab", "sbtb"]
            shapes += [square, square]
    scratch = [
        pltpu.VMEM((8, SPAN), F32),
        pltpu.VMEM((8, SPAN), F32),
        pltpu.VMEM((cols, SPAN), F32),
        pltpu.VMEM((cols, SPAN), BF16),
        pltpu.VMEM((cols, SPAN), BF16),
    ]
    if not last:
        scratch += [
            pltpu.VMEM((heads, SPAN, square[1]), BF16),
            pltpu.VMEM((heads, SPAN, square[1]), BF16),
            pltpu.VMEM((SPAN, cols), F32),
            pltpu.VMEM((SPAN, cols), F32),
            pltpu.VMEM((2,) + square, BF16),
        ]
    outs = pl.pallas_call(
        functools.partial(back_kernel, block, nb, shift),
        grid=(1,),
        in_specs=in_specs,
        out_specs=[whole(s) for s in shapes],
        out_shape=[jax.ShapeDtypeStruct(s, F32) for s in shapes],
        scratch_shapes=scratch,
        cost_estimate=cost(17),
        name=f"back_{block}",
    )(*ins)
    return dict(zip(names, outs))


def unprep_kernel(block, nb, shift, *refs):
    it = iter(refs)
    take = lambda n: [next(it) for _ in range(n)]
    first, last = block == 0, block == nb - 1
    seq_ref, peer_ref, dq_ref, dk_ref, dv_ref, dgp_ref, pre_ref, w_ref, conv_ref = take(9)
    x_ref, gain_ref = take(2)
    halo_ref = None if first else take(1)[0]
    dp_ref, pers_ref, ab_ref, btb_ref, gain_two_ref = take(5) if first else [None] * 5
    if not last:
        edge_in_ref, dlg_ref, gate_ref, mean_ref = take(4)
        cg_in_ref, gg_in_ref, gate_in_ref = take(7)[:3]
    cg_ref, gg_ref, gate_out_ref = take(3)
    dproj_ref, keep_ref, send_ref, inner_ref, edge_ref = take(5)
    small_ref, gains_ref = take(2) if first else (None, None)
    ext_ref, dext_ref, low_ref = take(3)
    rows, cols = dq_ref.shape
    width = x_ref.shape[1]
    blocks = head_blocks(cols, shift)
    taps = conv_ref.shape[1]
    d_normed = dot_nt(dgp_ref[...], w_ref[3])
    dproj_ref[3] = dgp_ref[...]
    if last:
        cg_ref[...] = jnp.zeros(cg_ref.shape, F32)
        gg_ref[...] = jnp.zeros(gg_ref.shape, F32)
        gate_out_ref[...] = jnp.zeros(gate_out_ref.shape, F32)
    else:
        cg_ref[...] = cg_in_ref[...]
        gg_ref[...] = gg_in_ref[...]
    for i in range(3):
        pre = pre_ref[i]
        ext_ref[0:HALO, :] = jnp.zeros((HALO, cols), F32) if first else halo_ref[i]
        ext_ref[HALO : HALO + rows, :] = pre
        shifted = [pre] + [ext_ref[HALO - j : HALO - j + rows, :] for j in range(1, taps)]
        conv = conv_ref[i, 0:1, :] * pre
        for j in range(1, taps):
            conv = conv + conv_ref[i, j : j + 1, :] * shifted[j]
        sig = jax.nn.sigmoid(conv)
        d_act = (dq_ref, dk_ref, dv_ref)[i][...]
        if i < 2:
            act = conv * sig
            scale = lax.rsqrt(head_sum(act * act, blocks) + UNIT_EPS)
            d_act = scale * (d_act - act * (scale * scale * head_sum(d_act * act, blocks)))
        d_conv = d_act * (sig * (1.0 + conv * (1.0 - sig)))
        edge_ref[i] = d_conv[0:HALO, :]
        dext_ref[0:rows, :] = d_conv
        dext_ref[rows : rows + HALO, :] = (
            jnp.zeros((HALO, cols), F32) if last else edge_in_ref[i]
        )
        d_pre = conv_ref[i, 0:1, :] * d_conv
        for j in range(taps):
            if j:
                d_pre = d_pre + conv_ref[i, j : j + 1, :] * dext_ref[j : j + rows, :]
            at = slice(i * taps + j, i * taps + j + 1)
            cg_ref[at, :] = cg_ref[at, :] + jnp.sum(d_conv * shifted[j], 0, keepdims=True)
        d_low = d_pre.astype(BF16)
        dproj_ref[i] = d_low
        d_normed = d_normed + dot_nt(d_low, w_ref[i])
    if not last:
        valid, count = valid_column(seq_ref, block * rows, rows)
        d_mean = jnp.dot(
            dlg_ref[...], gate_ref[...], preferred_element_type=F32, precision=HIGH
        )
        d_normed = d_normed + (valid / count) * d_mean[0:1, :]
        outer = lax.dot_general(
            dlg_ref[...] * 0.125,
            mean_ref[...],
            (((0,), (0,)), ((), ())),
            preferred_element_type=F32,
            precision=HIGH,
        )
        gate_out_ref[...] = gate_in_ref[...] + outer[0 : gate_out_ref.shape[0], :]
    x = x_ref[...].astype(F32)
    scale = lax.rsqrt(jnp.mean(x * x, -1, keepdims=True) + NORM_EPS)
    weighted = d_normed * x
    gains = jnp.sum(weighted * scale, 0, keepdims=True)
    gg_ref[...] = gg_ref[...] + jnp.broadcast_to(gains, gg_ref.shape)
    ones = jnp.ones((8, width), BF16)
    high, rest = two_parts(weighted * gain_ref[0:1, :])
    inner_ref[...] = dot_nt(ones, high) + dot_nt(ones, rest)
    low_ref[...] = d_normed.astype(BF16)
    for slot, out_ref in ((0, keep_ref), (1, send_ref)):
        for n in range(2):
            start = pl.multiple_of(peer_ref[slot + 2 * n] * cols, cols)
            out_ref[n] = low_ref[:, pl.ds(start, cols)]
    if first:
        keys = pers_ref[0]
        d_keys = dp_ref[0]
        scale = lax.rsqrt(head_sum(keys * keys, blocks) + UNIT_EPS)
        along = head_sum(d_keys * keys, blocks)
        d_keys = scale * (d_keys - keys * (scale * scale * along))
        across = lambda a: [a[:, n : n + cols] for n in range(0, width, cols)]
        parts = [ab_ref[...], btb_ref[...], *across(gate_out_ref[...]), cg_ref[...]]
        parts += [d_keys, dp_ref[1]]
        at = 0
        for part in parts:
            small_ref[at : at + part.shape[0], :] = part.astype(BF16)
            at += part.shape[0]
        gains_ref[0:1, :] = gg_ref[0:1, :]
        gains_ref[1:2, :] = gain_two_ref[0:1, :]
        small_ref[at:, :] = jnp.zeros((small_ref.shape[0] - at, cols), BF16)


def unprep_call(
    block, nb, shift, seq, peers, back, dgp, pre, w, conv, x, gains, gate, mean, pers, gain_two,
    shared,
):
    rows, width = x.shape
    cols = dgp.shape[1]
    first, last = block == 0, block == nb - 1
    whole = lambda a: pl.BlockSpec(a.shape, lambda i, n=len(a.shape): (0,) * n)
    smem = pl.BlockSpec(memory_space=pltpu.SMEM)
    at_block = pl.BlockSpec((SPAN, cols), lambda i: (block, 0))
    stacked = lambda n: pl.BlockSpec((n, SPAN, cols), lambda i: (0, block, 0))
    struct = jax.ShapeDtypeStruct
    gate_rows_out = 16
    names = ["cg", "gg", "gate", "dproj", "keep", "send", "inner", "edge"]
    outs = [
        struct((16, cols), F32),
        struct((8, width), F32),
        struct((gate_rows_out, width), F32),
        struct((4, rows, cols), BF16),
        struct((2, rows, cols), BF16),
        struct((2, rows, cols), BF16),
        struct((8, rows), F32),
        struct((3, HALO, cols), F32),
    ]
    out_specs = [whole(a) for a in outs[:3]]
    out_specs += [
        stacked(4),
        stacked(2),
        stacked(2),
        pl.BlockSpec((8, SPAN), lambda i: (0, block)),
        whole(outs[7]),
    ]
    ins = [seq, peers, back["dq"], back["dk"], back["dv"], dgp, pre, w, conv, x, gains]
    in_specs = [
        smem,
        smem,
        whole(back["dq"]),
        at_block,
        at_block,
        whole(dgp),
        stacked(3),
        whole(w),
        whole(conv),
        pl.BlockSpec((SPAN, width), lambda i: (block, 0)),
        whole(gains),
    ]
    aliases = {}
    if not first:
        ins.append(pre)
        in_specs.append(
            pl.BlockSpec((3, HALO, cols), lambda i: (0, block * (SPAN // HALO) - 1, 0))
        )
    else:
        others = [back["dp"], pers, back["ab"], back["btb"], gain_two]
        ins += others
        in_specs += [whole(a) for a in others]
        names += ["small", "gains"]
        ahead = 5 * width // SMALL_ROWS
        outs.append(struct(((ahead + 1) * SMALL_ROWS, cols), BF16))
        out_specs.append(pl.BlockSpec((SMALL_ROWS, cols), lambda i: (ahead, 0)))
        outs.append(struct((2, width), F32))
        out_specs.append(whole(outs[-1]))
    if not last:
        ins += [shared["edge"], back["dlg"], gate, mean]
        in_specs += [whole(shared["edge"]), whole(back["dlg"]), whole(gate)]
        in_specs.append(pl.BlockSpec((8, width), lambda i: (block, 0)))
        aliases = {len(ins) + n: n for n in range(7)}
        ins += [shared[name] for name in names[:7]]
        in_specs += [whole(a) for a in outs[:3]] + [pl.BlockSpec(memory_space=pl.ANY)] * 4
    got = pl.pallas_call(
        functools.partial(unprep_kernel, block, nb, shift),
        grid=(1,),
        in_specs=in_specs,
        out_specs=out_specs,
        out_shape=outs,
        input_output_aliases=aliases,
        scratch_shapes=[
            pltpu.VMEM((HALO + SPAN, cols), F32),
            pltpu.VMEM((SPAN + HALO, cols), F32),
            pltpu.VMEM((SPAN, width), BF16),
        ],
        cost_estimate=cost(10),
        name=f"unprep_{block}",
    )(*ins)
    return dict(zip(names, got))


def finish_kernel(peer_ref, x_ref, dres_ref, half_ref, far_ref, i0_ref, i1_ref, gain_ref, out_ref):
    rows, width = x_ref.shape
    cols = out_ref.shape[1]
    own = pl.ds(pl.multiple_of(peer_ref[0] * cols, cols), cols)
    x = x_ref[...].astype(F32)
    scale = lax.rsqrt(jnp.mean(x * x, -1, keepdims=True) + NORM_EPS)
    inner = jnp.transpose(i0_ref[...] + i1_ref[...])[:, 0:1] / width
    d_normed = half_ref[0].astype(F32) + far_ref[...].astype(F32)
    d_normed = d_normed * gain_ref[0:1, own]
    x_own = x_ref[:, own].astype(F32)
    out_ref[...] = dres_ref[...] + scale * d_normed - x_own * (scale * scale * scale * inner)


def finish_call(peers, x, dres, half, far, inner, inner_far, gains):
    rows, width = x.shape
    cols = dres.shape[1]
    row = lambda n: pl.BlockSpec((SPAN, n), lambda i: (i, 0))
    across = pl.BlockSpec((8, SPAN), lambda i: (0, i))
    return pl.pallas_call(
        finish_kernel,
        grid=(rows // SPAN,),
        in_specs=[
            pl.BlockSpec(memory_space=pltpu.SMEM),
            row(width),
            row(cols),
            pl.BlockSpec((1, SPAN, cols), lambda i: (0, i, 0)),
            row(cols),
            across,
            across,
            pl.BlockSpec(gains.shape, lambda i: (0, 0)),
        ],
        out_specs=row(cols),
        out_shape=jax.ShapeDtypeStruct((rows, cols), F32),
        cost_estimate=cost(4),
        name="finish",
    )(peers, x, dres, half, far, inner, inner_far, gains)


def ring_of(size):
    return [list(range(0, size, 2)) + list(range(size - 1 - size % 2, 0, -2))]


def ring_scatter(payload, axis, size):
    return lax.psum_scatter(
        payload, axis, scatter_dimension=0, axis_index_groups=ring_of(size), tiled=True
    )


def ring_gather(part, axis, size):
    return lax.all_gather(part, axis, axis=0, axis_index_groups=ring_of(size), tiled=True)


def stacked_rows(pieces, full):
    at = 0
    for piece in pieces:
        full = lax.dynamic_update_slice(full, piece, (at, 0))
        at += piece.shape[0]
    return full


def after(value, *others):
    return lax.optimization_barrier((value, *others))[0]


def per_device(
    ring_size,
    layer_input,
    proj_weight,
    conv_weight,
    persist_kv,
    memory_in,
    memory_out,
    memory_gate,
    out_weight,
    ffn_in,
    ffn_out,
    norm_gains,
    seq_len,
    out_grad,
):
    rows, width = layer_input.shape
    cols = proj_weight.shape[2]
    heads = persist_kv.shape[1]
    head_size = persist_kv.shape[3]
    shift = head_size.bit_length() - 1
    mem_hid = memory_in.shape[2]
    nb = rows // SPAN
    taps = conv_weight.shape[1]
    me = lax.axis_index("head")
    count = width // cols
    peers = jnp.stack([me, me ^ 1, me ^ 2, me ^ 3]).astype(jnp.int32)
    swap = lambda a, bit: lax.ppermute(a, "head", [(i, i ^ bit) for i in range(count)])
    ow = lax.all_gather(out_weight, "head", axis=0, tiled=False)
    cot = lax.all_gather(out_grad, "head", axis=0, tiled=False)
    gate = jnp.transpose(memory_gate, (1, 2, 0)).reshape(3 * heads, width)
    gate = jnp.pad(gate, ((0, GATE_ROWS - 3 * heads), (0, 0)))
    pers = jnp.transpose(persist_kv, (0, 2, 1, 3)).reshape(2, -1, cols)
    q, k, v, kt, pre, gp, nl, mean, lg, pers_low = prep_call(
        seq_len, layer_input, proj_weight, conv_weight, norm_gains, gate, pers, shift
    )
    a = memory_in.reshape(cols, mem_hid)
    bt = jnp.transpose(memory_out, (0, 2, 1)).reshape(cols, mem_hid)
    sa = sbt = None
    states, mixes = [], []
    for c in range(nb):
        if c > 1:
            a = after(a, *mixes[c - 2]["pieces"][1:3])
        state = dict(a=a, bt=bt, sa=sa, sbt=sbt, lg=lg)
        got = mix_call(c, nb, shift, seq_len, lg, q, k, v, kt, pers_low, gp, a, bt, sa, sbt)
        if c < nb - 1:
            a, bt, sa, sbt, state["ga"], state["gbt"] = got[4:]
        states.append(state)
        far = swap(got[0], 2)
        other = swap(got[0], 3) if c == nb - 1 else swap(far, 1)
        pieces = (got[0], swap(got[0], 1), far, other)
        mixes.append(dict(pieces=pieces, tot=got[1], att=got[2], linv=got[3]))
    shared = None
    ffns = [None] * nb
    wait = [mixes[-1]["pieces"][0]]
    if nb > 1:
        wait += mixes[-2]["pieces"][1:3]
    order = [0] + list(range(nb - 1, 0, -1))
    for n, c in enumerate(order):
        if n > 1:
            wait = [ffns[order[n - 2]]["s1"]]
        x = after(layer_input, *wait) if wait else layer_input
        wait = []
        shared, (res, keep, send, *room) = ffn_call(
            c, peers, x, mixes[c]["pieces"], ow, norm_gains, ffn_in, ffn_out, cot, shared
        )
        ffns[c] = dict(res=res)
        grads_room = room[0] if room else grads_room
        if c and c < nb - 1:
            keep = after(keep, ffns[nb - 1]["r2"])
        ffns[c]["s1"] = (keep.astype(F32) + swap(send, 1).astype(F32)).astype(BF16)
        ffns[c]["r2"] = swap(ffns[c]["s1"], 2)
    gain_two, normed_two, hidden, dgu, part_keep, part_send, cot_full, mixed_full = shared
    along_rows = (((0,), (0,)), ((), ()))
    outer = lambda left, right: lax.dot_general(
        left, right, along_rows, preferred_element_type=F32
    ).astype(BF16)
    lead = ffns[nb - 1]
    part = (part_keep.astype(F32) + swap(part_send, 1).astype(F32)).astype(BF16)
    ffn_grads = stacked_rows(
        [
            outer(after(normed_two, lead["s1"], ffns[0]["r2"]), dgu[0]),
            outer(after(normed_two, lead["r2"]), dgu[1]),
            outer(after(hidden, part), cot_full),
        ],
        grads_room,
    )
    tie = (ffn_grads,)
    ffn_part = ring_scatter(ffn_grads, "dp", ring_size)
    back = unprep = None
    gated = [None] * nb

    def turn(c, turned, ties, relay_ties):
        s1, r2 = ffns[c]["s1"], ffns[c]["r2"]
        pieces = (s1, r2, swap(after(s1, *relay_ties), 1), swap(after(r2, *relay_ties), 1))
        turned, gated[c] = turn_call(
            c, peers, pieces, after(ffns[c]["res"], *ties), cot, ow, norm_gains, gp,
            mixes[c]["tot"], turned,
        )
        return turned

    turned = turn(nb - 1, None, tie, (lead["r2"],))
    ffn_wait = max(nb - 2, 0)
    part_far = swap(part[1], 2)
    tie = ()
    for c in reversed(range(nb)):
        back = back_call(
            c, nb, shift, seq_len, q, k, v, kt, pers_low, after(gated[c][0], *tie),
            mixes[c]["att"], mixes[c]["linv"], states[c], back, back,
        )
        if c == nb - 1:
            relay_ties = (back["dq"],)
            back["dq"] = after(back["dq"], part_far)
        if c == ffn_wait:
            back["dq"], ffn_part = lax.optimization_barrier((back["dq"], ffn_part))
            ffn_grads = ring_gather(ffn_part, "dp", ring_size)
        unprep = unprep_call(
            c, nb, shift, seq_len, peers, back, gated[c][1], pre, proj_weight, conv_weight,
            layer_input, norm_gains, gate, mean, pers, gain_two, unprep,
        )
        tie = (unprep["edge"],)
        if c == nb - 1:
            for other in reversed(range(c)):
                turned = turn(other, turned, tie, relay_ties)
                tie = ()
            d_res, res_cols, d_branch, d_gate_all = turned
            tie = (d_branch,)
    gains = unprep["gains"]
    gains = gains + sum(swap(gains, bit) for bit in (1, 2, 3))
    cuts = [4 * width, width, 2 * cols, 16 * width // cols, 16, pers.shape[1] * 2]
    cuts.append(2 * width // cols)
    payload = stacked_rows(
        [outer(nl, unprep["dproj"][i]) for i in range(4)]
        + [outer(mixed_full, d_branch)],
        unprep["small"],
    )
    payload = lax.dynamic_update_slice(
        payload, gains.reshape(-1, cols).astype(BF16), (sum(cuts[:-1]), 0)
    )
    layer_output = (res_cols + part[0].astype(F32) + part_far.astype(F32)).astype(BF16)
    tie = (payload,)
    payload, ffn_grads = lax.optimization_barrier((payload, ffn_grads))
    ffn_in_grad = ffn_grads[: 2 * width].astype(F32).reshape(2, width, -1)
    ffn_out_grad = ffn_grads[2 * width :].astype(F32)
    payload = ring_scatter(payload, "dp", ring_size)
    half = (
        unprep["keep"].astype(F32) + swap(after(unprep["send"], *tie), 1).astype(F32)
    ).astype(BF16)
    inner = unprep["inner"] + swap(unprep["inner"], 1)
    far = swap(half[1], 2)
    input_grad = finish_call(
        peers, layer_input, d_res, half, far, inner, swap(inner, 2), norm_gains
    )
    payload, input_grad, ffn_in_grad, ffn_out_grad, layer_output = lax.optimization_barrier(
        (payload, input_grad, ffn_in_grad, ffn_out_grad, layer_output)
    )
    payload = ring_gather(payload, "dp", ring_size)
    got, at = [], 0
    for cut in cuts:
        got.append(payload[at : at + cut].astype(F32))
        at += cut
    gains = got[6].reshape(2, width)
    d_gate = jnp.concatenate(jnp.split(got[3], width // cols, 0), 1)[: 3 * heads]
    d_pers = got[5].reshape(2, -1, heads, head_size)
    return (
        layer_output,
        input_grad,
        got[0].reshape(4, width, cols),
        got[4][: 3 * taps].reshape(3, taps, cols),
        jnp.transpose(d_pers, (0, 2, 1, 3)),
        got[2][:cols].reshape(memory_in.shape),
        jnp.transpose(got[2][cols:].reshape(heads, head_size, mem_hid), (0, 2, 1)),
        jnp.transpose(d_gate.reshape(3, heads, width), (2, 0, 1)),
        got[1],
        ffn_in_grad,
        ffn_out_grad,
        gains,
    )


def solution(mesh):
    in_specs = (
        P("dp", None),
        P(None, None, "head"),
        P(None, None, "head"),
        P(None, "head", None, None),
        P("head", None, None),
        P("head", None, None),
        P(None, None, "head"),
        P(None, "head"),
        P(None, None, "head"),
        P("head", None),
        P(),
        P("dp"),
        P("dp", "head"),
    )
    out_specs = (
        P("dp", "head"),
        P("dp", "head"),
        P(None, None, "head"),
        P(None, None, "head"),
        P(None, "head", None, None),
        P("head", None, None),
        P("head", None, None),
        P(None, None, "head"),
        P(None, "head"),
        P(None, None, "head"),
        P("head", None),
        P(),
    )
    body = functools.partial(per_device, mesh.shape["dp"])
    return jax.shard_map(
        body, mesh=mesh, in_specs=in_specs, out_specs=out_specs, check_vma=False
    )
```

```python
import functools

import jax
import jax.numpy as jnp
from jax import lax
from jax.experimental import pallas as pl
from jax.experimental.pallas import tpu as pltpu
from jax.sharding import PartitionSpec as P

F32 = jnp.float32
BF16 = jnp.bfloat16
HIGH = lax.Precision.HIGHEST
NORM_EPS = 1e-05
UNIT_EPS = 1e-06
SCORE_SCALE = 8.0
SPAN = 512
HALO = 8
COST_UNIT = 1.5e8
SMALL_ROWS = 640


def dot_nn(left, right):
    return jnp.dot(left, right, preferred_element_type=F32)


def dot_nt(left, right, precision=None):
    return lax.dot_general(
        left, right, (((1,), (1,)), ((), ())), preferred_element_type=F32, precision=precision
    )


def iota(shape, axis):
    return lax.broadcasted_iota(jnp.int32, shape, axis)


def cost(microseconds):
    return pl.CostEstimate(
        flops=int(microseconds * COST_UNIT), transcendentals=0, bytes_accessed=1 << 20
    )


def head_blocks(cols, shift):
    same = (iota((cols, cols), 0) >> shift) == (iota((cols, cols), 1) >> shift)
    return jnp.where(same, 1.0, 0.0).astype(BF16)


def head_sum(value, blocks):
    return dot_nn(value.astype(BF16), blocks)


def valid_column(seq_ref, start, rows):
    inside = (start + iota((rows, 1), 0)) < seq_ref[0]
    valid = jnp.where(inside, 1.0, 0.0)
    return valid, jnp.maximum(jnp.sum(valid, 0, keepdims=True), 1.0)


def head_mask(cols, shift, head):
    return jnp.where((iota((1, cols), 1) >> shift) == head, 1.0, 0.0)


def gate_rows(logits, group, heads, head_size, width):
    parts = [
        jnp.broadcast_to(
            logits[0:1, group * heads + head : group * heads + head + 1], (head_size, width)
        )
        for head in range(heads)
    ]
    return jnp.concatenate(parts, 0)


def prep_kernel(
    shift,
    seq_ref,
    x_ref,
    w_ref,
    conv_ref,
    gain_ref,
    gate_ref,
    pers_ref,
    q_ref,
    k_ref,
    v_ref,
    kt_ref,
    pre_ref,
    gp_ref,
    nl_ref,
    mean_ref,
    lg_ref,
    pers_out_ref,
    ext_ref,
):
    step = pl.program_id(0)
    rows, cols = q_ref.shape
    blocks = head_blocks(cols, shift)

    @pl.when(step == 0)
    def _():
        ext_ref[:, 0:HALO, :] = jnp.zeros((3, HALO, cols), F32)
        keys = pers_ref[0]
        keys = keys * lax.rsqrt(head_sum(keys * keys, blocks) + UNIT_EPS)
        pers_out_ref[0] = keys.astype(BF16)
        pers_out_ref[1] = pers_ref[1].astype(BF16)

    x = x_ref[...].astype(F32)
    scale = lax.rsqrt(jnp.mean(x * x, -1, keepdims=True) + NORM_EPS)
    normed = x * scale * gain_ref[0:1, :]
    low = normed.astype(BF16)
    nl_ref[...] = low
    inside = (step * rows + iota((8, rows), 1)) < seq_ref[0]
    valid = jnp.where(inside, 1.0, 0.0)
    count = jnp.maximum(jnp.sum(valid, 1, keepdims=True), 1.0)
    mean = dot_nn(valid.astype(BF16), low) / count
    mean_ref[...] = mean
    lg_ref[...] = dot_nt(mean, gate_ref[...], HIGH)
    gp_ref[...] = dot_nn(low, w_ref[3])
    for i in range(3):
        pre = dot_nn(low, w_ref[i])
        pre_ref[i] = pre
        ext_ref[i, HALO : HALO + rows, :] = pre
        conv = conv_ref[i, 0:1, :] * pre
        for j in range(1, conv_ref.shape[1]):
            conv = conv + conv_ref[i, j : j + 1, :] * ext_ref[i, HALO - j : HALO - j + rows, :]
        ext_ref[i, 0:HALO, :] = pre[rows - HALO :, :]
        act = conv * jax.nn.sigmoid(conv)
        if i < 2:
            act = act * lax.rsqrt(head_sum(act * act, blocks) + UNIT_EPS)
        act_low = act.astype(BF16)
        (q_ref, k_ref, v_ref)[i][...] = act_low
        if i == 1:
            kt_ref[...] = jnp.transpose(act_low.astype(F32)).astype(BF16)


def prep_call(seq, x, w, conv, gains, gate, pers, shift):
    gates = gate.shape[0]
    rows, width = x.shape
    cols = w.shape[2]
    nb = rows // SPAN
    whole = lambda a: pl.BlockSpec(a.shape, lambda c, n=a.ndim: (0,) * n)
    row_cols = pl.BlockSpec((SPAN, cols), lambda c: (c, 0))
    return pl.pallas_call(
        functools.partial(prep_kernel, shift),
        grid=(nb,),
        in_specs=[
            pl.BlockSpec(memory_space=pltpu.SMEM),
            pl.BlockSpec((SPAN, width), lambda c: (c, 0)),
            whole(w),
            whole(conv),
            whole(gains),
            whole(gate),
            whole(pers),
        ],
        out_specs=[
            row_cols,
            row_cols,
            row_cols,
            pl.BlockSpec((cols, SPAN), lambda c: (0, c)),
            pl.BlockSpec((3, SPAN, cols), lambda c: (0, c, 0)),
            row_cols,
            pl.BlockSpec((SPAN, width), lambda c: (c, 0)),
            pl.BlockSpec((8, width), lambda c: (c, 0)),
            pl.BlockSpec((8, gates), lambda c: (c, 0)),
            whole(pers),
        ],
        out_shape=[
            jax.ShapeDtypeStruct((rows, cols), BF16),
            jax.ShapeDtypeStruct((rows, cols), BF16),
            jax.ShapeDtypeStruct((rows, cols), BF16),
            jax.ShapeDtypeStruct((cols, rows), BF16),
            jax.ShapeDtypeStruct((3, rows, cols), F32),
            jax.ShapeDtypeStruct((rows, cols), F32),
            jax.ShapeDtypeStruct((rows, width), BF16),
            jax.ShapeDtypeStruct((nb * 8, width), F32),
            jax.ShapeDtypeStruct((nb * 8, gates), F32),
            jax.ShapeDtypeStruct(pers.shape, BF16),
        ],
        scratch_shapes=[pltpu.VMEM((3, HALO + SPAN, cols), F32)],
        cost_estimate=cost(15),
        name="prep",
    )(seq, x, w, conv, gains, gate, pers)


def mix_kernel(block, blocks_all, shift, first, last, *refs):
    it = iter(refs)
    seq_ref, lg_ref, q_ref, k_ref, v_ref, kt_ref, pers_ref, gp_ref, a_ref, bt_ref = (
        next(it) for _ in range(10)
    )
    sa_ref, sbt_ref = (None, None) if first or last else (next(it), next(it))
    mixed_ref, tot_ref, att_ref, linv_ref = (next(it) for _ in range(4))
    if not last:
        a2_ref, bt2_ref, sa2_ref, sbt2_ref, ga_ref, gbt_ref = (next(it) for _ in range(6))
        z_ref, r_ref = next(it), next(it)
    rows, cols = q_ref.shape
    head_size = 1 << shift
    heads = cols // head_size
    a_low = a_ref[...].astype(BF16)
    bt_low = bt_ref[...].astype(BF16)
    valid, count = valid_column(seq_ref, block * rows, rows)
    weight = valid / count
    att_ref[...] = jnp.zeros((rows, cols), F32)
    linv_ref[...] = jnp.zeros((rows, cols), F32)
    tot_ref[...] = jnp.zeros((rows, cols), F32)
    if not last:
        r_ref[...] = jnp.zeros((rows, cols), F32)

    def one_head(head, carry):
        mask = head_mask(cols, shift, head)
        mask_low = mask.astype(BF16)
        ones_low = (1.0 - mask).astype(BF16)
        query = q_ref[...] * mask_low
        scaled = query * SCORE_SCALE
        raised = jnp.exp(dot_nt(scaled, pers_ref[0])).astype(BF16)
        total = dot_nn(raised, pers_ref[1] * mask_low + ones_low)
        for j in range(block + 1):
            span = slice(j * rows, (j + 1) * rows)
            raised = jnp.exp(dot_nt(scaled, k_ref[span, :]))
            if j == block:
                raised = jnp.where(
                    iota((rows, rows), 0) >= iota((rows, rows), 1), raised, 0.0
                )
            total = total + dot_nn(raised.astype(BF16), v_ref[span, :] * mask_low + ones_low)
        inverse = 1.0 / pltpu.roll(total, head_size, 1)
        inside = jnp.broadcast_to(mask, (rows, cols)) > 0.5
        linv_ref[...] = jnp.where(inside, inverse, linv_ref[...])
        attended = jnp.where(inside, total * inverse, 0.0)
        att_ref[...] = att_ref[...] + attended
        hid = dot_nn(query, a_low)
        hid = hid * jax.nn.sigmoid(hid)
        recalled = dot_nt(hid.astype(BF16), bt_low) * mask
        tot_ref[...] = tot_ref[...] + attended + recalled
        if not last:
            hid = dot_nn(k_ref[block * rows : (block + 1) * rows, :] * mask_low, a_low)
            sig = jax.nn.sigmoid(hid)
            act = (hid * sig).astype(BF16)
            z_ref[head] = act
            target = v_ref[block * rows : (block + 1) * rows, :].astype(F32)
            resid = (dot_nt(act, bt_low) - target) * mask * weight
            r_ref[...] = r_ref[...] + resid
            d_hid = dot_nn(resid.astype(BF16), bt_low) * (sig * (1.0 + hid * (1.0 - sig)))
            at = pl.ds(pl.multiple_of(head * head_size, head_size), head_size)
            ga_ref[at, :] = dot_nn(kt_ref[at, :], d_hid.astype(BF16))
        return carry

    lax.fori_loop(0, heads, one_head, 0)
    gate = jax.nn.sigmoid(gp_ref[...])
    mixed_ref[...] = (tot_ref[...] * gate).astype(BF16)
    if not last:
        resid_t = jnp.transpose(r_ref[...]).astype(BF16)
        for head in range(heads):
            at = slice(head * head_size, (head + 1) * head_size)
            gbt_ref[at, :] = dot_nn(resid_t[at, :], z_ref[head])
        width = a_ref.shape[1]
        logits = lg_ref[...]
        step = 0.2 * jax.nn.sigmoid(gate_rows(logits, 0, heads, head_size, width))
        keep = jax.nn.sigmoid(gate_rows(logits, 1, heads, head_size, width))
        stay = 1.0 - 0.5 * jax.nn.sigmoid(gate_rows(logits, 2, heads, head_size, width))
        moment_a = -step * ga_ref[...]
        moment_b = -step * gbt_ref[...]
        if not first:
            moment_a = moment_a + keep * sa_ref[...]
            moment_b = moment_b + keep * sbt_ref[...]
        sa2_ref[...] = moment_a
        sbt2_ref[...] = moment_b
        a2_ref[...] = stay * a_ref[...] + moment_a
        bt2_ref[...] = stay * bt_ref[...] + moment_b


def mix_call(block, nb, shift, seq, lg, q, k, v, kt, pers, gp, a, bt, sa, sbt):
    rows, cols = q.shape
    first, last = block == 0, block == nb - 1
    heads = cols >> shift
    whole = lambda s: pl.BlockSpec(s, lambda i, n=len(s): (0,) * n)
    at_block = pl.BlockSpec((SPAN, cols), lambda i: (block, 0))
    upto = pl.BlockSpec(((block + 1) * SPAN, cols), lambda i: (0, 0))
    state = whole(a.shape)
    ins = [seq, lg, q, k, v, kt, pers, gp, a, bt]
    in_specs = [
        pl.BlockSpec(memory_space=pltpu.SMEM),
        pl.BlockSpec((8, lg.shape[1]), lambda i: (block, 0)),
        at_block,
        upto,
        upto,
        pl.BlockSpec((cols, SPAN), lambda i: (0, block)),
        whole(pers.shape),
        at_block,
        state,
        state,
    ]
    if not (first or last):
        ins += [sa, sbt]
        in_specs += [state, state]
    row_spec = whole((SPAN, cols))
    outs = [jax.ShapeDtypeStruct((SPAN, cols), BF16)] + [
        jax.ShapeDtypeStruct((SPAN, cols), F32)
    ] * 3
    out_specs = [row_spec] * 4
    scratch = []
    if not last:
        outs += [jax.ShapeDtypeStruct(a.shape, F32)] * 6
        out_specs += [state] * 6
        scratch = [pltpu.VMEM((heads, SPAN, a.shape[1]), BF16), pltpu.VMEM((SPAN, cols), F32)]
    return pl.pallas_call(
        functools.partial(mix_kernel, block, nb, shift, first, last),
        grid=(1,),
        in_specs=in_specs,
        out_specs=out_specs,
        out_shape=outs,
        scratch_shapes=scratch,
        cost_estimate=cost(9),
        name=f"mix_{block}",
    )(*ins)


def ffn_kernel(nb, first_call, *refs):
    it = iter(refs)
    take = lambda n: [next(it) for _ in range(n)]
    peer_ref, x_ref = take(2)
    piece_refs = [take(4) for _ in range(nb)]
    gain_ref, fin_ref, fout_ref = take(3)
    ow_refs, cot_refs = take(4), take(4)
    if not first_call:
        take(6)
    nt_ref, hid_ref, dgu_ref, cotf_ref, mfull_ref, res_ref = take(6)
    if first_call:
        take(1)
    (m_ref,) = take(1)
    step = pl.program_id(0)
    cols = m_ref.shape[2]
    for block in range(nb):

        @pl.when(step == block)
        def _(block=block):
            for j in range(4):
                m_ref[j] = piece_refs[block][j][...]

    spots = [pl.ds(pl.multiple_of(peer_ref[j] * cols, cols), cols) for j in range(4)]
    for j in range(4):
        mfull_ref[:, spots[j]] = m_ref[j]
        cotf_ref[:, spots[j]] = cot_refs[j][...]
    mixed = mfull_ref[...]
    for j in range(4):
        branch = dot_nn(mixed, ow_refs[j][...])
        res_ref[:, spots[j]] = x_ref[:, spots[j]].astype(F32) + branch
    residual = res_ref[...]
    scale = lax.rsqrt(jnp.mean(residual * residual, -1, keepdims=True) + NORM_EPS)
    low = (residual * scale * gain_ref[1:2, :]).astype(BF16)
    nt_ref[...] = low
    d_hidden = dot_nt(cotf_ref[...], fout_ref[...])
    gate_pre = dot_nn(low, fin_ref[0])
    up_pre = dot_nn(low, fin_ref[1])
    sig = jax.nn.sigmoid(gate_pre)
    silu = gate_pre * sig
    hid_ref[...] = (silu * up_pre).astype(BF16)
    slope = sig * (1.0 + gate_pre * (1.0 - sig))
    dgu_ref[0] = (d_hidden * up_pre * slope).astype(BF16)
    dgu_ref[1] = (d_hidden * silu).astype(BF16)


def ffn_call(blocks, peers, x, pieces, ow, gains, fin, fout, cot, shared):
    rows, width = x.shape
    cols = pieces[0][0].shape[1]
    nb = len(blocks)
    low = blocks[0]
    hidden = fout.shape[0]
    once = pl.Buffered(1)
    whole = lambda a: pl.BlockSpec(a.shape, lambda i, n=a.ndim: (0,) * n, pipeline_mode=once)
    at_rows = lambda n: pl.BlockSpec((SPAN, n), lambda i: (low + i, 0))
    anywhere = pl.BlockSpec(memory_space=pl.ANY)
    struct = jax.ShapeDtypeStruct
    ins = [peers, x, *[piece for block in pieces for piece in block], gains, fin, fout]
    ins += [*ow, *cot]
    in_specs = [pl.BlockSpec(memory_space=pltpu.SMEM), at_rows(width)]
    in_specs += [whole(piece) for block in pieces for piece in block]
    in_specs += [whole(gains), whole(fin), whole(fout)]
    in_specs += [whole(piece) for piece in ow] + [at_rows(cols)] * 4
    room = [] if shared else [struct((3 * width, width), BF16)]
    aliases = {}
    if shared:
        aliases = {len(ins) + n: n for n in range(len(shared))}
        ins += shared
        in_specs += [anywhere] * len(shared)
    got = pl.pallas_call(
        functools.partial(ffn_kernel, nb, not shared),
        grid=(nb,),
        in_specs=in_specs,
        out_specs=[
            at_rows(width),
            at_rows(hidden),
            pl.BlockSpec((2, SPAN, hidden), lambda i: (0, low + i, 0)),
            at_rows(width),
            at_rows(width),
            at_rows(width),
        ]
        + [anywhere] * len(room),
        out_shape=[
            struct((rows, width), BF16),
            struct((rows, hidden), BF16),
            struct((2, rows, hidden), BF16),
            struct((rows, width), BF16),
            struct((rows, width), BF16),
            struct((rows, width), F32),
        ]
        + room,
        input_output_aliases=aliases,
        scratch_shapes=[pltpu.VMEM((4, SPAN, cols), BF16)],
        cost_estimate=cost(8 * nb),
        name=f"ffn_{low}",
    )(*ins)
    return got[:6], got[6:]


def ffn_back_kernel(first_call, *refs):
    it = iter(refs)
    take = lambda n: [next(it) for _ in range(n)]
    peer_ref, dgu_ref, fin_ref, res_ref = take(4)
    gg_in_ref = None if first_call else take(1)[0]
    gg_ref, keep_ref, send_ref, part_ref = take(4)
    width = res_ref.shape[1]
    residual = res_ref[...]
    scale = lax.rsqrt(jnp.mean(residual * residual, -1, keepdims=True) + NORM_EPS)
    d_normed = dot_nt(dgu_ref[0], fin_ref[0]) + dot_nt(dgu_ref[1], fin_ref[1])
    gains = jnp.sum(d_normed * residual * scale, 0, keepdims=True)

    @pl.when(pl.program_id(0) == 0)
    def _():
        gg_ref[...] = jnp.zeros(gg_ref.shape, F32) if first_call else gg_in_ref[...]

    gg_ref[...] = gg_ref[...] + jnp.broadcast_to(gains, gg_ref.shape)
    half = width // 2
    part_ref[...] = d_normed.astype(BF16)
    core = peer_ref[0] & 1
    keep_ref[...] = part_ref[:, pl.ds(pl.multiple_of(core * half, half), half)]
    send_ref[...] = part_ref[:, pl.ds(pl.multiple_of((1 - core) * half, half), half)]


def ffn_back_call(blocks, peers, dgu, fin, res, gains):
    width = res.shape[1]
    tile = SPAN // 2
    steps = SPAN // tile
    low = blocks[0] * steps
    lines = len(blocks) * SPAN
    gain_spec = pl.BlockSpec((8, width), lambda i: (0, 0))
    row = pl.BlockSpec((tile, width // 2), lambda i: (i, 0))
    struct = jax.ShapeDtypeStruct
    return pl.pallas_call(
        functools.partial(ffn_back_kernel, gains is None),
        grid=(len(blocks) * steps,),
        in_specs=[
            pl.BlockSpec(memory_space=pltpu.SMEM),
            pl.BlockSpec((2, tile, dgu.shape[2]), lambda i: (0, low + i, 0)),
            pl.BlockSpec(fin.shape, lambda i: (0, 0, 0), pipeline_mode=pl.Buffered(1)),
            pl.BlockSpec((tile, width), lambda i: (low + i, 0)),
        ]
        + ([] if gains is None else [gain_spec]),
        out_specs=[gain_spec, row, row],
        out_shape=[
            struct((8, width), F32),
            struct((lines, width // 2), BF16),
            struct((lines, width // 2), BF16),
        ],
        scratch_shapes=[pltpu.VMEM((tile, width), BF16)],
        cost_estimate=cost(4 * len(blocks)),
        name=f"ffn_back_{blocks[0]}",
    )(peers, dgu, fin, res, *([] if gains is None else [gains]))


def down_kernel(peer_ref, hid_ref, fout_ref, keep_ref, send_ref, part_ref):
    cols = keep_ref.shape[2]
    part_ref[...] = dot_nn(hid_ref[...], fout_ref[...]).astype(BF16)
    for slot, out_ref in ((0, keep_ref), (1, send_ref)):
        for n in range(2):
            start = pl.multiple_of(peer_ref[slot + 2 * n] * cols, cols)
            out_ref[n] = part_ref[:, pl.ds(start, cols)]


def down_call(peers, hid, fout, cols):
    rows, hidden = hid.shape
    width = fout.shape[1]
    stacked = pl.BlockSpec((2, SPAN, cols), lambda i: (0, i, 0))
    return pl.pallas_call(
        down_kernel,
        grid=(rows // SPAN,),
        in_specs=[
            pl.BlockSpec(memory_space=pltpu.SMEM),
            pl.BlockSpec((SPAN, hidden), lambda i: (i, 0)),
            pl.BlockSpec(fout.shape, lambda i: (0, 0), pipeline_mode=pl.Buffered(1)),
        ],
        out_specs=[stacked, stacked],
        out_shape=[jax.ShapeDtypeStruct((2, rows, cols), BF16)] * 2,
        scratch_shapes=[pltpu.VMEM((SPAN, width), BF16)],
        cost_estimate=cost(6),
        name="down",
    )(peers, hid, fout)


def turn_kernel(blocks, steps, first_call, *refs):
    it = iter(refs)
    take = lambda n: [next(it) for _ in range(n)]
    peer_ref, s1_ref, r2_ref, ps1_ref, pr2_ref, res_ref, cot_ref = take(7)
    gain_ref, gp_ref = take(2)
    ow_refs = take(4)
    tot_refs = take(blocks)
    if not first_call:
        take(4)
    dres_ref, rescol_ref, dbr_ref, dgall_ref, dga_ref, dgp_ref, full_ref = take(7)
    rows, width = res_ref.shape
    cols = gp_ref.shape[1]
    half = width // 2
    core = peer_ref[0] & 1
    at_own = pl.ds(pl.multiple_of(core * half, half), half)
    at_other = pl.ds(pl.multiple_of((1 - core) * half, half), half)
    full_ref[:, at_own] = s1_ref[...].astype(F32) + r2_ref[...].astype(F32)
    full_ref[:, at_other] = ps1_ref[...].astype(F32) + pr2_ref[...].astype(F32)
    residual = res_ref[...]
    scale = lax.rsqrt(jnp.mean(residual * residual, -1, keepdims=True) + NORM_EPS)
    gained = full_ref[...] * gain_ref[1:2, :]
    inner = jnp.sum(gained * residual, -1, keepdims=True) / width
    d_residual = cot_ref[...].astype(F32) + scale * gained - residual * (scale * scale * scale * inner)
    own = pl.ds(pl.multiple_of(peer_ref[0] * cols, cols), cols)
    full_ref[...] = d_residual
    d_mixed = None
    for j in range(4):
        at = pl.ds(pl.multiple_of(peer_ref[j] * cols, cols), cols)
        term = dot_nt(full_ref[:, at].astype(BF16), ow_refs[j][own, :])
        d_mixed = term if d_mixed is None else d_mixed + term
    mine = full_ref[:, own]
    dres_ref[...] = mine
    dbr_ref[...] = mine.astype(BF16)
    rescol_ref[...] = res_ref[:, own]
    gate = jax.nn.sigmoid(gp_ref[...])
    d_gated = d_mixed * gate
    dga_ref[...] = d_gated.astype(BF16)
    total = tot_refs[0][...]
    for n in range(1, blocks):
        total = jnp.where(pl.program_id(0) >= n * steps, tot_refs[n][...], total)
    d_gate = (d_gated * total * (1.0 - gate)).astype(BF16)
    dgp_ref[...] = d_gate
    dgall_ref[...] = d_gate


def turn_call(blocks, peers, pieces, res, cot, ow, gains, gp, tots, shared):
    rows, cols = gp.shape
    width = res.shape[1]
    tile = SPAN // 2
    steps = SPAN // tile
    low = blocks[0] * steps
    count = len(blocks) * steps
    whole = lambda a: pl.BlockSpec(a.shape, lambda i, n=a.ndim: (0,) * n)
    row = lambda n: pl.BlockSpec((tile, n), lambda i: (i, 0))
    at_rows = lambda n: pl.BlockSpec((tile, n), lambda i: (low + i, 0))
    struct = jax.ShapeDtypeStruct
    ins = [peers, *pieces, res, cot, gains, gp, *ow, *tots]
    in_specs = [
        pl.BlockSpec(memory_space=pltpu.SMEM),
        row(width // 2),
        row(width // 2),
        row(width // 2),
        row(width // 2),
        at_rows(width),
        at_rows(width),
        whole(gains),
        at_rows(cols),
    ] + [whole(piece) for piece in ow]
    for n in range(len(blocks)):
        spot = lambda i, n=n: (jnp.clip(i - n * steps, 0, steps - 1), 0)
        in_specs.append(pl.BlockSpec((tile, cols), spot))
    aliases = {}
    if shared is not None:
        aliases = {len(ins) + n: n for n in range(len(shared))}
        ins += shared
        in_specs += [pl.BlockSpec(memory_space=pl.ANY)] * len(shared)
    got = pl.pallas_call(
        functools.partial(turn_kernel, len(blocks), steps, shared is None),
        grid=(count,),
        in_specs=in_specs,
        out_specs=[at_rows(cols)] * 4 + [row(cols)] * 2,
        out_shape=[
            struct((rows, cols), F32),
            struct((rows, cols), F32),
            struct((rows, cols), BF16),
            struct((rows, cols), BF16),
            struct((len(blocks) * SPAN, cols), BF16),
            struct((len(blocks) * SPAN, cols), BF16),
        ],
        input_output_aliases=aliases,
        scratch_shapes=[pltpu.VMEM((tile, width), F32)],
        cost_estimate=cost(5 * len(blocks)),
        name=f"turn_{blocks[0]}",
    )(*ins)
    return got[:4], got[4:]


def back_kernel(block, nb, shift, *refs):
    it = iter(refs)
    take = lambda n: [next(it) for _ in range(n)]
    first, last = block == 0, block == nb - 1
    seq_ref, q_ref, k_ref, v_ref, kt_ref, pers_ref, dga_ref, att_ref, linv_ref = take(9)
    a_ref, bt_ref = take(2)
    if not last:
        dk_in_ref, dv_in_ref, dp_in_ref, lg_ref, ga_ref, gbt_ref, ab_in_ref, btb_in_ref = take(8)
        sab_in_ref, sbtb_in_ref = take(2) if block < nb - 2 else (None, None)
        sa_ref, sbt_ref = (None, None) if first else take(2)
    dq_ref, dk_ref, dv_ref, dp_ref, ab_ref, btb_ref = take(6)
    if not last:
        (dlg_ref,) = take(1)
        sab_ref, sbtb_ref = (None, None) if first else take(2)
    lt_ref, dt_ref, dqt_ref, qt_ref, dot_ref = take(5)
    if not last:
        z_ref, zd_ref, r_ref, y_ref, h_ref = take(5)
    rows, cols = q_ref.shape
    head_size = 1 << shift
    heads = cols // head_size
    own = slice(block * rows, (block + 1) * rows)
    a_low = a_ref[...].astype(BF16)
    bt_low = bt_ref[...].astype(BF16)
    if last:
        dk_ref[...] = jnp.zeros(dk_ref.shape, F32)
        dv_ref[...] = jnp.zeros(dv_ref.shape, F32)
        dp_ref[...] = jnp.zeros(dp_ref.shape, F32)
        ab_ref[...] = jnp.zeros(ab_ref.shape, F32)
        btb_ref[...] = jnp.zeros(btb_ref.shape, F32)
    else:
        dk_ref[...] = dk_in_ref[...]
        dv_ref[...] = dv_in_ref[...]
        dp_ref[...] = dp_in_ref[...]
    pick = (iota((8, cols), 1) >> shift) == iota((8, cols), 0)
    start = iota((8, cols), 1) == (iota((8, cols), 0) << shift)
    lt_ref[...] = dot_nt(jnp.where(start, 1.0, 0.0), linv_ref[...], HIGH)
    d_gated = dga_ref[...].astype(F32)
    dt_ref[...] = dot_nt(jnp.where(pick, 1.0, 0.0), d_gated * att_ref[...], HIGH)
    dq_ref[...] = jnp.zeros((rows, cols), F32)
    qt_ref[...] = jnp.transpose(q_ref[...].astype(F32)).astype(BF16)
    dot_ref[...] = jnp.transpose(d_gated).astype(BF16)
    if not last:
        valid, count = valid_column(seq_ref, block * rows, rows)
        weight = valid / count
        width = a_ref.shape[1]
        logits = lg_ref[...]
        sig_step = jax.nn.sigmoid(gate_rows(logits, 0, heads, head_size, width))
        keep = jax.nn.sigmoid(gate_rows(logits, 1, heads, head_size, width))
        sig_forget = jax.nn.sigmoid(gate_rows(logits, 2, heads, head_size, width))
        tot_a, tot_b = ab_in_ref[...], btb_in_ref[...]
        if sab_in_ref is not None:
            tot_a, tot_b = tot_a + sab_in_ref[...], tot_b + sbtb_in_ref[...]
        h_ref[0] = (-0.2 * sig_step * tot_a).astype(BF16)
        h_ref[1] = (-0.2 * sig_step * tot_b).astype(BF16)
        d_step = -(ga_ref[...] * tot_a + gbt_ref[...] * tot_b)
        groups = [d_step * (0.2 * sig_step * (1.0 - sig_step)), None, None]
        if not first:
            groups[1] = (sa_ref[...] * tot_a + sbt_ref[...] * tot_b) * (keep * (1.0 - keep))
        d_forget = -(a_ref[...] * ab_in_ref[...] + bt_ref[...] * btb_in_ref[...])
        groups[2] = d_forget * (0.5 * sig_forget * (1.0 - sig_forget))
        d_logits = jnp.zeros(dlg_ref.shape, F32)
        for g, value in enumerate(groups):
            if value is None:
                continue
            for head in range(heads):
                part = value[head * head_size : (head + 1) * head_size, :]
                figure = jnp.sum(jnp.sum(part, 1, keepdims=True), 0, keepdims=True)
                here = iota(dlg_ref.shape, 1) == g * heads + head
                d_logits = d_logits + jnp.where(here, 1.0, 0.0) * figure
        dlg_ref[...] = d_logits
        stay = 1.0 - 0.5 * sig_forget
        ab_ref[...] = stay * ab_in_ref[...]
        btb_ref[...] = stay * btb_in_ref[...]
        if not first:
            sab_ref[...] = keep * tot_a
            sbtb_ref[...] = keep * tot_b
        r_ref[...] = jnp.zeros((rows, cols), F32)
        y_ref[...] = jnp.zeros((rows, cols), F32)

    def one_head(head, carry):
        mask = head_mask(cols, shift, head)
        mask_low = mask.astype(BF16)
        query = q_ref[...] * mask_low
        scaled = query * SCORE_SCALE
        d_out = dga_ref[...] * mask_low
        at = pl.ds(pl.multiple_of(head * head_size, head_size), head_size)
        inverse = lt_ref[pl.ds(head, 1), :]
        delta = dt_ref[pl.ds(head, 1), :]
        probs = jnp.exp(dot_nt(pers_ref[0], scaled)) * inverse
        d_scores = (probs * (dot_nt(pers_ref[1], d_out) - delta)).astype(BF16)
        dp_ref[0] = dp_ref[0] + dot_nn(d_scores, scaled)
        dp_ref[1] = dp_ref[1] + dot_nn(probs.astype(BF16), d_out)
        d_query = lax.dot_general(
            d_scores, pers_ref[0], (((0,), (0,)), ((), ())), preferred_element_type=F32
        )
        d_query = d_query * SCORE_SCALE
        d_query_t = jnp.zeros((head_size, rows), F32)
        for j in range(block + 1):
            span = slice(j * rows, (j + 1) * rows)
            probs = jnp.exp(dot_nt(k_ref[span, :], scaled)) * inverse
            if j == block:
                probs = jnp.where(iota((rows, rows), 0) <= iota((rows, rows), 1), probs, 0.0)
            d_scores = (probs * (dot_nt(v_ref[span, :], d_out) - delta)).astype(BF16)
            dv_ref[span, :] = dv_ref[span, :] + dot_nn(probs.astype(BF16), d_out)
            dk_ref[span, :] = dk_ref[span, :] + dot_nn(d_scores, scaled)
            d_query_t = d_query_t + dot_nn(kt_ref[at, span], d_scores)
        dqt_ref[at, :] = d_query_t * SCORE_SCALE
        hid = dot_nn(query, a_low)
        sig = jax.nn.sigmoid(hid)
        d_hid = dot_nn(d_out, bt_low) * (sig * (1.0 + hid * (1.0 - sig)))
        d_hid = d_hid.astype(BF16)
        dq_ref[...] = dq_ref[...] + (d_query + dot_nt(d_hid, a_low)) * mask
        grad_a = dot_nn(qt_ref[at, :], d_hid)
        grad_b = dot_nn(dot_ref[at, :], (hid * sig).astype(BF16))
        if not last:
            key = k_ref[own, :] * mask_low
            hid = dot_nn(key, a_low)
            probe = dot_nn(key, h_ref[0])
            sig = jax.nn.sigmoid(hid)
            act = (hid * sig).astype(BF16)
            z_ref[head] = act
            slope = sig * (1.0 + hid * (1.0 - sig))
            curve = sig * (1.0 - sig) * (2.0 + hid * (1.0 - 2.0 * sig))
            target = v_ref[own, :].astype(F32)
            resid = (dot_nt(act, bt_low) - target) * mask * weight
            r_ref[...] = r_ref[...] + resid
            resid = resid.astype(BF16)
            d_act = dot_nn(resid, bt_low)
            d_slope = (probe * slope).astype(BF16)
            zd_ref[head] = d_slope
            d_net = (dot_nt(act, h_ref[1]) + dot_nt(d_slope, bt_low)) * mask * weight
            y_ref[...] = y_ref[...] + d_net
            back = dot_nn(resid, h_ref[1]) + dot_nn(d_net.astype(BF16), bt_low)
            d_hid = (probe * d_act * curve + back * slope).astype(BF16)
            direct = (d_act * slope).astype(BF16)
            d_key = (dot_nt(direct, h_ref[0]) + dot_nt(d_hid, a_low)) * mask
            dk_ref[own, :] = dk_ref[own, :] + d_key
            grad_a = grad_a + dot_nn(kt_ref[at, own], d_hid)
        ab_ref[at, :] = ab_ref[at, :] + grad_a
        btb_ref[at, :] = btb_ref[at, :] + grad_b
        return carry

    lax.fori_loop(0, heads, one_head, 0)
    dq_ref[...] = dq_ref[...] + jnp.transpose(dqt_ref[...])
    if not last:
        dv_ref[own, :] = dv_ref[own, :] - y_ref[...]
        resid_t = jnp.transpose(r_ref[...]).astype(BF16)
        net_t = jnp.transpose(y_ref[...]).astype(BF16)
        for head in range(heads):
            at = slice(head * head_size, (head + 1) * head_size)
            grad_b = dot_nn(resid_t[at, :], zd_ref[head]) + dot_nn(net_t[at, :], z_ref[head])
            btb_ref[at, :] = btb_ref[at, :] + grad_b


def back_call(block, nb, shift, seq, q, k, v, kt, pers, dga, att, linv, state, grads, adjoint):
    dga, spot = dga
    cols = q.shape[1]
    heads = cols >> shift
    first, last = block == 0, block == nb - 1
    done = (block + 1) * SPAN
    whole = lambda s: pl.BlockSpec(s, lambda i, n=len(s): (0,) * n)
    at_block = pl.BlockSpec((SPAN, cols), lambda i: (block, 0))
    upto = pl.BlockSpec((done, cols), lambda i: (0, 0))
    rows_spec = whole((SPAN, cols))
    square = state["a"].shape
    ins = [seq, q, k, v, kt, pers, dga, att, linv, state["a"], state["bt"]]
    in_specs = [
        pl.BlockSpec(memory_space=pltpu.SMEM),
        at_block,
        upto,
        upto,
        pl.BlockSpec((cols, done), lambda i: (0, 0)),
        whole(pers.shape),
        pl.BlockSpec((SPAN, cols), lambda i: (spot, 0)),
        rows_spec,
        rows_spec,
        whole(square),
        whole(square),
    ]
    if not last:
        ins += [grads["dk"], grads["dv"], grads["dp"], state["lg"], state["ga"], state["gbt"]]
        ins += [adjoint["ab"], adjoint["btb"]]
        in_specs += [upto, upto, whole(pers.shape)]
        in_specs += [pl.BlockSpec((8, state["lg"].shape[1]), lambda i: (block, 0))]
        in_specs += [whole(square)] * 4
        if block < nb - 2:
            ins += [adjoint["sab"], adjoint["sbtb"]]
            in_specs += [whole(square)] * 2
        if not first:
            ins += [state["sa"], state["sbt"]]
            in_specs += [whole(square)] * 2
    names = ["dq", "dk", "dv", "dp", "ab", "btb"]
    shapes = [(SPAN, cols), (done, cols), (done, cols), pers.shape, square, square]
    if not last:
        names.append("dlg")
        shapes.append((8, state["lg"].shape[1]))
        if not first:
            names += ["sab", "sbtb"]
            shapes += [square, square]
    scratch = [
        pltpu.VMEM((8, SPAN), F32),
        pltpu.VMEM((8, SPAN), F32),
        pltpu.VMEM((cols, SPAN), F32),
        pltpu.VMEM((cols, SPAN), BF16),
        pltpu.VMEM((cols, SPAN), BF16),
    ]
    if not last:
        scratch += [
            pltpu.VMEM((heads, SPAN, square[1]), BF16),
            pltpu.VMEM((heads, SPAN, square[1]), BF16),
            pltpu.VMEM((SPAN, cols), F32),
            pltpu.VMEM((SPAN, cols), F32),
            pltpu.VMEM((2,) + square, BF16),
        ]
    outs = pl.pallas_call(
        functools.partial(back_kernel, block, nb, shift),
        grid=(1,),
        in_specs=in_specs,
        out_specs=[whole(s) for s in shapes],
        out_shape=[jax.ShapeDtypeStruct(s, F32) for s in shapes],
        scratch_shapes=scratch,
        cost_estimate=cost(17),
        name=f"back_{block}",
    )(*ins)
    return dict(zip(names, outs))


def unprep_kernel(block, nb, shift, *refs):
    it = iter(refs)
    take = lambda n: [next(it) for _ in range(n)]
    first, last = block == 0, block == nb - 1
    seq_ref, peer_ref, dq_ref, dk_ref, dv_ref, dgp_ref, pre_ref, w_ref, conv_ref = take(9)
    x_ref, gain_ref = take(2)
    halo_ref = None if first else take(1)[0]
    dp_ref, pers_ref, ab_ref, btb_ref, gain_two_ref = take(5) if first else [None] * 5
    if not last:
        edge_in_ref, dlg_ref, gate_ref, mean_ref = take(4)
        cg_in_ref, gg_in_ref, gate_in_ref = take(7)[:3]
    cg_ref, gg_ref, gate_out_ref = take(3)
    dproj_ref, keep_ref, send_ref, inner_ref, edge_ref = take(5)
    small_ref, gains_ref = take(2) if first else (None, None)
    ext_ref, dext_ref, low_ref = take(3)
    rows, cols = dq_ref.shape
    width = x_ref.shape[1]
    blocks = head_blocks(cols, shift)
    taps = conv_ref.shape[1]
    d_normed = dot_nt(dgp_ref[...], w_ref[3])
    dproj_ref[3] = dgp_ref[...]
    if last:
        cg_ref[...] = jnp.zeros(cg_ref.shape, F32)
        gg_ref[...] = jnp.zeros(gg_ref.shape, F32)
        gate_out_ref[...] = jnp.zeros(gate_out_ref.shape, F32)
    else:
        cg_ref[...] = cg_in_ref[...]
        gg_ref[...] = gg_in_ref[...]
    for i in range(3):
        pre = pre_ref[i]
        ext_ref[0:HALO, :] = jnp.zeros((HALO, cols), F32) if first else halo_ref[i]
        ext_ref[HALO : HALO + rows, :] = pre
        shifted = [pre] + [ext_ref[HALO - j : HALO - j + rows, :] for j in range(1, taps)]
        conv = conv_ref[i, 0:1, :] * pre
        for j in range(1, taps):
            conv = conv + conv_ref[i, j : j + 1, :] * shifted[j]
        sig = jax.nn.sigmoid(conv)
        d_act = (dq_ref, dk_ref, dv_ref)[i][...]
        if i < 2:
            act = conv * sig
            scale = lax.rsqrt(head_sum(act * act, blocks) + UNIT_EPS)
            d_act = scale * (d_act - act * (scale * scale * head_sum(d_act * act, blocks)))
        d_conv = d_act * (sig * (1.0 + conv * (1.0 - sig)))
        edge_ref[i] = d_conv[0:HALO, :]
        dext_ref[0:rows, :] = d_conv
        dext_ref[rows : rows + HALO, :] = (
            jnp.zeros((HALO, cols), F32) if last else edge_in_ref[i]
        )
        d_pre = conv_ref[i, 0:1, :] * d_conv
        for j in range(taps):
            if j:
                d_pre = d_pre + conv_ref[i, j : j + 1, :] * dext_ref[j : j + rows, :]
            at = slice(i * taps + j, i * taps + j + 1)
            cg_ref[at, :] = cg_ref[at, :] + jnp.sum(d_conv * shifted[j], 0, keepdims=True)
        d_low = d_pre.astype(BF16)
        dproj_ref[i] = d_low
        d_normed = d_normed + dot_nt(d_low, w_ref[i])
    if not last:
        valid, count = valid_column(seq_ref, block * rows, rows)
        d_mean = jnp.dot(
            dlg_ref[...], gate_ref[...], preferred_element_type=F32, precision=HIGH
        )
        d_normed = d_normed + (valid / count) * d_mean[0:1, :]
        outer = lax.dot_general(
            dlg_ref[...] * 0.125,
            mean_ref[...],
            (((0,), (0,)), ((), ())),
            preferred_element_type=F32,
            precision=HIGH,
        )
        gate_out_ref[...] = gate_in_ref[...]
        at = slice(0, outer.shape[0])
        gate_out_ref[at, :] = gate_in_ref[at, :] + outer
    x = x_ref[...].astype(F32)
    scale = lax.rsqrt(jnp.mean(x * x, -1, keepdims=True) + NORM_EPS)
    weighted = d_normed * x
    gains = jnp.sum(weighted * scale, 0, keepdims=True)
    gg_ref[...] = gg_ref[...] + jnp.broadcast_to(gains, gg_ref.shape)
    gained = jnp.broadcast_to(gain_ref[0:1, :], (8, width))
    inner_ref[...] = dot_nt(gained.astype(BF16), weighted.astype(BF16))
    low_ref[...] = d_normed.astype(BF16)
    for slot, out_ref in ((0, keep_ref), (1, send_ref)):
        for n in range(2):
            start = pl.multiple_of(peer_ref[slot + 2 * n] * cols, cols)
            out_ref[n] = low_ref[:, pl.ds(start, cols)]
    if first:
        keys = pers_ref[0]
        d_keys = dp_ref[0]
        scale = lax.rsqrt(head_sum(keys * keys, blocks) + UNIT_EPS)
        along = head_sum(d_keys * keys, blocks)
        d_keys = scale * (d_keys - keys * (scale * scale * along))
        across = lambda a: [a[:, n : n + cols] for n in range(0, width, cols)]
        parts = [ab_ref[...], btb_ref[...], *across(gate_out_ref[...]), cg_ref[...]]
        parts += [d_keys, dp_ref[1]]
        at = 0
        for part in parts:
            small_ref[at : at + part.shape[0], :] = part.astype(BF16)
            at += part.shape[0]
        gains_ref[0:1, :] = gg_ref[0:1, :]
        gains_ref[1:2, :] = gain_two_ref[0:1, :]
        small_ref[at:, :] = jnp.zeros((small_ref.shape[0] - at, cols), BF16)


def unprep_call(
    block, nb, shift, seq, peers, back, dgp, pre, w, conv, x, gains, gate, mean, pers, gain_two,
    shared,
):
    dgp, spot = dgp
    rows, width = x.shape
    cols = dgp.shape[1]
    first, last = block == 0, block == nb - 1
    whole = lambda a: pl.BlockSpec(a.shape, lambda i, n=len(a.shape): (0,) * n)
    smem = pl.BlockSpec(memory_space=pltpu.SMEM)
    at_block = pl.BlockSpec((SPAN, cols), lambda i: (block, 0))
    stacked = lambda n: pl.BlockSpec((n, SPAN, cols), lambda i: (0, block, 0))
    struct = jax.ShapeDtypeStruct
    gate_rows_out = 16
    names = ["cg", "gg", "gate", "dproj", "keep", "send", "inner", "edge"]
    outs = [
        struct((16, cols), F32),
        struct((8, width), F32),
        struct((gate_rows_out, width), F32),
        struct((4, rows, cols), BF16),
        struct((2, rows, cols), BF16),
        struct((2, rows, cols), BF16),
        struct((8, rows), F32),
        struct((3, HALO, cols), F32),
    ]
    out_specs = [whole(a) for a in outs[:3]]
    out_specs += [
        stacked(4),
        stacked(2),
        stacked(2),
        pl.BlockSpec((8, SPAN), lambda i: (0, block)),
        whole(outs[7]),
    ]
    ins = [seq, peers, back["dq"], back["dk"], back["dv"], dgp, pre, w, conv, x, gains]
    in_specs = [
        smem,
        smem,
        whole(back["dq"]),
        at_block,
        at_block,
        pl.BlockSpec((SPAN, cols), lambda i: (spot, 0)),
        stacked(3),
        whole(w),
        whole(conv),
        pl.BlockSpec((SPAN, width), lambda i: (block, 0)),
        whole(gains),
    ]
    aliases = {}
    if not first:
        ins.append(pre)
        in_specs.append(
            pl.BlockSpec((3, HALO, cols), lambda i: (0, block * (SPAN // HALO) - 1, 0))
        )
    else:
        others = [back["dp"], pers, back["ab"], back["btb"], gain_two]
        ins += others
        in_specs += [whole(a) for a in others]
        names += ["small", "gains"]
        ahead = 5 * width // SMALL_ROWS
        outs.append(struct(((ahead + 1) * SMALL_ROWS, cols), BF16))
        out_specs.append(pl.BlockSpec((SMALL_ROWS, cols), lambda i: (ahead, 0)))
        outs.append(struct((2, width), F32))
        out_specs.append(whole(outs[-1]))
    if not last:
        ins += [shared["edge"], back["dlg"], gate, mean]
        in_specs += [whole(shared["edge"]), whole(back["dlg"]), whole(gate)]
        in_specs.append(pl.BlockSpec((8, width), lambda i: (block, 0)))
        aliases = {len(ins) + n: n for n in range(7)}
        ins += [shared[name] for name in names[:7]]
        in_specs += [whole(a) for a in outs[:3]] + [pl.BlockSpec(memory_space=pl.ANY)] * 4
    got = pl.pallas_call(
        functools.partial(unprep_kernel, block, nb, shift),
        grid=(1,),
        in_specs=in_specs,
        out_specs=out_specs,
        out_shape=outs,
        input_output_aliases=aliases,
        scratch_shapes=[
            pltpu.VMEM((HALO + SPAN, cols), F32),
            pltpu.VMEM((SPAN + HALO, cols), F32),
            pltpu.VMEM((SPAN, width), BF16),
        ],
        cost_estimate=cost(10),
        name=f"unprep_{block}",
    )(*ins)
    return dict(zip(names, got))


def finish_kernel(peer_ref, x_ref, dres_ref, half_ref, far_ref, i0_ref, i1_ref, gain_ref, out_ref):
    rows, width = x_ref.shape
    cols = out_ref.shape[1]
    own = pl.ds(pl.multiple_of(peer_ref[0] * cols, cols), cols)
    x = x_ref[...].astype(F32)
    scale = lax.rsqrt(jnp.mean(x * x, -1, keepdims=True) + NORM_EPS)
    inner = jnp.transpose(i0_ref[...] + i1_ref[...])[:, 0:1] / width
    d_normed = half_ref[0].astype(F32) + far_ref[...].astype(F32)
    d_normed = d_normed * gain_ref[0:1, own]
    x_own = x_ref[:, own].astype(F32)
    out_ref[...] = dres_ref[...] + scale * d_normed - x_own * (scale * scale * scale * inner)


def finish_call(peers, x, dres, half, far, inner, inner_far, gains):
    rows, width = x.shape
    cols = dres.shape[1]
    row = lambda n: pl.BlockSpec((SPAN, n), lambda i: (i, 0))
    across = pl.BlockSpec((8, SPAN), lambda i: (0, i))
    return pl.pallas_call(
        finish_kernel,
        grid=(rows // SPAN,),
        in_specs=[
            pl.BlockSpec(memory_space=pltpu.SMEM),
            row(width),
            row(cols),
            pl.BlockSpec((1, SPAN, cols), lambda i: (0, i, 0)),
            row(cols),
            across,
            across,
            pl.BlockSpec(gains.shape, lambda i: (0, 0)),
        ],
        out_specs=row(cols),
        out_shape=jax.ShapeDtypeStruct((rows, cols), F32),
        cost_estimate=cost(4),
        name="finish",
    )(peers, x, dres, half, far, inner, inner_far, gains)


def unpack_kernel(shift, main_ref, small_ref, proj_ref, out_ref, a_ref, b_ref, gate_ref, conv_ref,
                  pers_ref, gain_ref):
    step = pl.program_id(0)
    cols = main_ref.shape[1]
    head_size = 1 << shift
    heads = cols // head_size
    last = pl.num_programs(0) - 1

    @pl.when(step < last)
    def _():
        proj_ref[0] = main_ref[...].astype(F32)

    @pl.when(step == last)
    def _():
        out_ref[...] = main_ref[...].astype(F32)

    @pl.when(step == 0)
    def _():
        small = small_ref[...].astype(F32)
        at = 2 * cols
        for h in range(heads):
            rows = slice(h * head_size, (h + 1) * head_size)
            a_ref[h] = small[rows, :]
            b_ref[h] = jnp.transpose(small[cols : 2 * cols][rows, :])
        lanes = gain_ref.shape[1] // cols
        for n in range(lanes):
            gate_ref[:, n * cols : (n + 1) * cols] = small[at + 16 * n : at + 16 * (n + 1), :]
        at += 16 * lanes
        taps = conv_ref.shape[1]
        for i in range(3):
            conv_ref[i] = small[at + i * taps : at + (i + 1) * taps, :]
        at += 16
        count = pers_ref.shape[2]
        for i in range(2):
            for h in range(heads):
                spot = slice(h * head_size, (h + 1) * head_size)
                pers_ref[i, h] = small[at + i * count : at + (i + 1) * count, spot]
        at += 2 * count
        for i in range(2):
            for n in range(lanes):
                row = at + i * lanes + n
                gain_ref[i : i + 1, n * cols : (n + 1) * cols] = small[row : row + 1, :]


def unpack_call(payload, shift, width, mem_hid, taps, persist_rows):
    cols = payload.shape[1]
    heads = cols >> shift
    head_size = 1 << shift
    ahead = 5 * width // SMALL_ROWS
    struct = jax.ShapeDtypeStruct
    outs = [
        struct((4, width, cols), F32),
        struct((width, cols), F32),
        struct((heads, head_size, mem_hid), F32),
        struct((heads, mem_hid, head_size), F32),
        struct((16, width), F32),
        struct((3, taps, cols), F32),
        struct((2, heads, persist_rows, head_size), F32),
        struct((2, width), F32),
    ]
    whole = lambda a: pl.BlockSpec(a.shape, lambda i, n=len(a.shape): (0,) * n)
    return pl.pallas_call(
        functools.partial(unpack_kernel, shift),
        grid=(5,),
        in_specs=[
            pl.BlockSpec((width, cols), lambda i: (i, 0)),
            pl.BlockSpec((SMALL_ROWS, cols), lambda i: (ahead, 0)),
        ],
        out_specs=[pl.BlockSpec((1, width, cols), lambda i: (jnp.minimum(i, 3), 0, 0))]
        + [whole(a) for a in outs[1:]],
        out_shape=outs,
        cost_estimate=cost(4),
        name="unpack",
    )(payload, payload)


def ring_of(size):
    return [list(range(0, size, 2)) + list(range(size - 1 - size % 2, 0, -2))]


def ring_scatter(payload, axis, size):
    return lax.psum_scatter(
        payload, axis, scatter_dimension=0, axis_index_groups=ring_of(size), tiled=True
    )


def ring_gather(part, axis, size):
    return lax.all_gather(part, axis, axis=0, axis_index_groups=ring_of(size), tiled=True)


def stacked_rows(pieces, full):
    at = 0
    for piece in pieces:
        full = lax.dynamic_update_slice(full, piece, (at, 0))
        at += piece.shape[0]
    return full


def after(value, *others):
    return lax.optimization_barrier((value, *others))[0]


def per_device(
    ring_size,
    layer_input,
    proj_weight,
    conv_weight,
    persist_kv,
    memory_in,
    memory_out,
    memory_gate,
    out_weight,
    ffn_in,
    ffn_out,
    norm_gains,
    seq_len,
    out_grad,
):
    rows, width = layer_input.shape
    cols = proj_weight.shape[2]
    heads = persist_kv.shape[1]
    head_size = persist_kv.shape[3]
    shift = head_size.bit_length() - 1
    mem_hid = memory_in.shape[2]
    nb = rows // SPAN
    taps = conv_weight.shape[1]
    me = lax.axis_index("head")
    count = width // cols
    peers = jnp.stack([me, me ^ 1, me ^ 2, me ^ 3]).astype(jnp.int32)
    swap = lambda a, bit: lax.ppermute(a, "head", [(i, i ^ bit) for i in range(count)])
    far_weight, far_cot = swap(out_weight, 2), swap(out_grad, 2)
    near_weight, near_cot = swap(out_weight, 1), swap(out_grad, 1)
    gate = jnp.transpose(memory_gate, (1, 2, 0)).reshape(3 * heads, width)
    pers = jnp.transpose(persist_kv, (0, 2, 1, 3)).reshape(2, -1, cols)
    q, k, v, kt, pre, gp, nl, mean, lg, pers_low = prep_call(
        seq_len, layer_input, proj_weight, conv_weight, norm_gains, gate, pers, shift
    )
    a = memory_in.reshape(cols, mem_hid)
    bt = jnp.transpose(memory_out, (0, 2, 1)).reshape(cols, mem_hid)
    sa = sbt = None
    ow = (out_weight, near_weight, far_weight, swap(after(far_weight, q), 1))
    states, mixes = [], []
    for c in range(nb):
        if c == 1:
            a = after(a, far_weight)
        if c == min(2, nb - 1):
            cot = (out_grad, near_cot, far_cot, swap(after(far_cot, mixes[c - 1]["tot"]), 1))
            a = after(a, far_cot)
        if c > 1:
            a = after(a, *mixes[c - 2]["pieces"][1:3])
        state = dict(a=a, bt=bt, sa=sa, sbt=sbt, lg=lg)
        got = mix_call(c, nb, shift, seq_len, lg, q, k, v, kt, pers_low, gp, a, bt, sa, sbt)
        if c < nb - 1:
            a, bt, sa, sbt, state["ga"], state["gbt"] = got[4:]
        states.append(state)
        pieces = [got[0], swap(got[0], 1), swap(got[0], 2)]
        if c:
            pieces.append(swap(got[0], 3))
        mixes.append(dict(pieces=pieces, tot=got[1], att=got[2], linv=got[3]))
    pieces = mixes[0]["pieces"]
    pieces.append(swap(after(pieces[2], mixes[min(1, nb - 1)]["pieces"][0]), 1))
    groups = [list(range(nb - 1)), [nb - 1]] if nb > 1 else [[0]]
    shared = None
    for n, blocks in enumerate(groups):
        x = after(layer_input, mixes[-1]["pieces"][0]) if n == 0 else layer_input
        shared, room = ffn_call(
            blocks, peers, x, [mixes[c]["pieces"] for c in blocks], ow, norm_gains, ffn_in,
            ffn_out, cot, shared,
        )
        grads_room = room[0] if room else grads_room
    normed_two, hidden, dgu, cot_full, mixed_full, residual = shared
    along_rows = (((0,), (0,)), ((), ()))
    outer = lambda left, right: lax.dot_general(
        left, right, along_rows, preferred_element_type=F32
    ).astype(BF16)
    ffn_grads = stacked_rows(
        [outer(normed_two, dgu[0]), outer(normed_two, dgu[1]), outer(hidden, cot_full)],
        grads_room,
    )
    ffn_part = ring_scatter(ffn_grads, "dp", ring_size)
    s1, r2, gain_two = [], [], None
    tie = (ffn_grads,)
    for n, blocks in enumerate(reversed(groups)):
        gain_two, keep, send = ffn_back_call(
            blocks, peers, after(dgu, *tie), ffn_in, residual, gain_two
        )
        s1.append((keep.astype(F32) + swap(send, 1).astype(F32)).astype(BF16))
        r2.append(swap(after(s1[n], *r2), 2))
        tie = (s1[0],)
    part_keep, part_send = down_call(peers, after(hidden, gain_two, r2[0]), ffn_out, cols)
    tie = (part_keep,)
    back = unprep = None
    gated = [None] * nb

    def turn(n, blocks, turned, ties, relay_ties):
        pieces = (
            s1[n], r2[n], swap(after(s1[n], *relay_ties), 1), swap(after(r2[n], *relay_ties), 1)
        )
        turned, (d_gated, d_gates) = turn_call(
            blocks, peers, pieces, after(residual, *ties), cot_full, ow, norm_gains, gp,
            [mixes[c]["tot"] for c in blocks], turned,
        )
        for spot, c in enumerate(blocks):
            gated[c] = (d_gated, spot), (d_gates, spot)
        return turned

    turned = turn(0, [nb - 1], None, tie, (r2[0],))
    part_keep = after(part_keep, gated[nb - 1][0][0])
    part = (part_keep.astype(F32) + swap(part_send, 1).astype(F32)).astype(BF16)
    part_far = swap(part[1], 2)
    tie = (part,)
    for c in reversed(range(nb)):
        back = back_call(
            c, nb, shift, seq_len, after(q, *tie, *([part_far] if c == 0 else [])), k, v, kt,
            pers_low, gated[c][0],
            mixes[c]["att"], mixes[c]["linv"], states[c], back, back,
        )
        if c == nb - 1:
            relay_ties = (back["dq"],)
        unprep = unprep_call(
            c, nb, shift, seq_len, peers, back, gated[c][1], pre, proj_weight, conv_weight,
            layer_input, norm_gains, gate, mean, pers, gain_two, unprep,
        )
        tie = (unprep["edge"],)
        if c == nb - 1:
            if c:
                turned = turn(1, list(range(c)), turned, tie, relay_ties)
            d_res, res_cols, d_branch, d_gate_all = turned
            d_branch, ffn_part = lax.optimization_barrier((d_branch, ffn_part))
            ffn_grads = ring_gather(ffn_part, "dp", ring_size)
            tie = (d_branch,)
    gains = unprep["gains"]
    gains = gains + sum(swap(gains, bit) for bit in (1, 2, 3))
    cuts = [4 * width, width, 2 * cols, 16 * width // cols, 16, pers.shape[1] * 2]
    cuts.append(2 * width // cols)
    payload = stacked_rows(
        [outer(nl, unprep["dproj"][i]) for i in range(4)]
        + [outer(mixed_full, d_branch)],
        unprep["small"],
    )
    payload = lax.dynamic_update_slice(
        payload, gains.reshape(-1, cols).astype(BF16), (sum(cuts[:-1]), 0)
    )
    layer_output = (res_cols + part[0].astype(F32) + part_far.astype(F32)).astype(BF16)
    tie = (payload,)
    payload, ffn_grads = lax.optimization_barrier((payload, ffn_grads))
    ffn_in_grad = ffn_grads[: 2 * width].astype(F32).reshape(2, width, -1)
    ffn_out_grad = ffn_grads[2 * width :].astype(F32)
    payload = ring_scatter(payload, "dp", ring_size)
    half = (
        unprep["keep"].astype(F32) + swap(after(unprep["send"], *tie), 1).astype(F32)
    ).astype(BF16)
    inner = unprep["inner"] + swap(unprep["inner"], 1)
    far = swap(half[1], 2)
    input_grad = finish_call(
        peers, layer_input, d_res, half, far, inner, swap(inner, 2), norm_gains
    )
    payload, input_grad, ffn_in_grad, ffn_out_grad, layer_output = lax.optimization_barrier(
        (payload, input_grad, ffn_in_grad, ffn_out_grad, layer_output)
    )
    payload = ring_gather(payload, "dp", ring_size)
    proj_grad, out_grads, a_grad, b_grad, gate_grad, conv_grad, pers_grad, gains = unpack_call(
        payload, shift, width, mem_hid, taps, persist_kv.shape[2]
    )
    gate_grad = gate_grad[: 3 * heads].reshape(3, heads, width)
    return (
        layer_output,
        input_grad,
        proj_grad,
        conv_grad,
        pers_grad,
        a_grad,
        b_grad,
        jnp.transpose(gate_grad, (2, 0, 1)),
        out_grads,
        ffn_in_grad,
        ffn_out_grad,
        gains,
    )


def solution(mesh):
    in_specs = (
        P("dp", None),
        P(None, None, "head"),
        P(None, None, "head"),
        P(None, "head", None, None),
        P("head", None, None),
        P("head", None, None),
        P(None, None, "head"),
        P(None, "head"),
        P(None, None, "head"),
        P("head", None),
        P(),
        P("dp"),
        P("dp", "head"),
    )
    out_specs = (
        P("dp", "head"),
        P("dp", "head"),
        P(None, None, "head"),
        P(None, None, "head"),
        P(None, "head", None, None),
        P("head", None, None),
        P("head", None, None),
        P(None, None, "head"),
        P(None, "head"),
        P(None, None, "head"),
        P("head", None),
        P(),
    )
    body = functools.partial(per_device, mesh.shape["dp"])
    return jax.shard_map(
        body, mesh=mesh, in_specs=in_specs, out_specs=out_specs, check_vma=False
    )
```

```python
import functools

import jax
import jax.numpy as jnp
from jax import lax
from jax.experimental import pallas as pl
from jax.experimental.pallas import tpu as pltpu
from jax.sharding import PartitionSpec as P

F32 = jnp.float32
BF16 = jnp.bfloat16
HIGH = lax.Precision.HIGHEST
NORM_EPS = 1e-05
UNIT_EPS = 1e-06
SCORE_SCALE = 8.0
SPAN = 512
HALO = 8
COST_UNIT = 1.5e8
SMALL_ROWS = 640


def dot_nn(left, right):
    return jnp.dot(left, right, preferred_element_type=F32)


def dot_nt(left, right, precision=None):
    return lax.dot_general(
        left, right, (((1,), (1,)), ((), ())), preferred_element_type=F32, precision=precision
    )


def iota(shape, axis):
    return lax.broadcasted_iota(jnp.int32, shape, axis)


def cost(microseconds):
    return pl.CostEstimate(
        flops=int(microseconds * COST_UNIT), transcendentals=0, bytes_accessed=1 << 20
    )


def head_blocks(cols, shift):
    same = (iota((cols, cols), 0) >> shift) == (iota((cols, cols), 1) >> shift)
    return jnp.where(same, 1.0, 0.0).astype(BF16)


def head_sum(value, blocks):
    return dot_nn(value.astype(BF16), blocks)


def valid_column(seq_ref, start, rows):
    inside = (start + iota((rows, 1), 0)) < seq_ref[0]
    valid = jnp.where(inside, 1.0, 0.0)
    return valid, jnp.maximum(jnp.sum(valid, 0, keepdims=True), 1.0)


def head_mask(cols, shift, head):
    return jnp.where((iota((1, cols), 1) >> shift) == head, 1.0, 0.0)


def gate_rows(logits, group, heads, head_size, width):
    parts = [
        jnp.broadcast_to(
            logits[0:1, group * heads + head : group * heads + head + 1], (head_size, width)
        )
        for head in range(heads)
    ]
    return jnp.concatenate(parts, 0)


def prep_kernel(
    shift,
    seq_ref,
    x_ref,
    w_ref,
    conv_ref,
    gain_ref,
    gate_ref,
    pers_ref,
    q_ref,
    k_ref,
    v_ref,
    kt_ref,
    pre_ref,
    gp_ref,
    nl_ref,
    mean_ref,
    lg_ref,
    pers_out_ref,
    flat_ref,
    ext_ref,
):
    step = pl.program_id(0)
    rows, cols = q_ref.shape
    blocks = head_blocks(cols, shift)

    @pl.when(step == 0)
    def _():
        ext_ref[:, 0:HALO, :] = jnp.zeros((3, HALO, cols), F32)
        keys = pers_ref[0]
        keys = keys * lax.rsqrt(head_sum(keys * keys, blocks) + UNIT_EPS)
        pers_out_ref[0] = keys.astype(BF16)
        pers_out_ref[1] = pers_ref[1].astype(BF16)
        heads = gate_ref.shape[1]
        for g in range(3):
            flat_ref[g * heads : (g + 1) * heads, :] = gate_ref[g]

    x = x_ref[...].astype(F32)
    scale = lax.rsqrt(jnp.mean(x * x, -1, keepdims=True) + NORM_EPS)
    normed = x * scale * gain_ref[0:1, :]
    low = normed.astype(BF16)
    nl_ref[...] = low
    inside = (step * rows + iota((8, rows), 1)) < seq_ref[0]
    valid = jnp.where(inside, 1.0, 0.0)
    count = jnp.maximum(jnp.sum(valid, 1, keepdims=True), 1.0)
    mean = dot_nn(valid.astype(BF16), low) / count
    mean_ref[...] = mean
    lg_ref[...] = dot_nt(mean, flat_ref[...], HIGH)
    gp_ref[...] = dot_nn(low, w_ref[3])
    for i in range(3):
        pre = dot_nn(low, w_ref[i])
        pre_ref[i] = pre
        ext_ref[i, HALO : HALO + rows, :] = pre
        conv = conv_ref[i, 0:1, :] * pre
        for j in range(1, conv_ref.shape[1]):
            conv = conv + conv_ref[i, j : j + 1, :] * ext_ref[i, HALO - j : HALO - j + rows, :]
        ext_ref[i, 0:HALO, :] = pre[rows - HALO :, :]
        act = conv * jax.nn.sigmoid(conv)
        if i < 2:
            act = act * lax.rsqrt(head_sum(act * act, blocks) + UNIT_EPS)
        act_low = act.astype(BF16)
        (q_ref, k_ref, v_ref)[i][...] = act_low
        if i == 1:
            kt_ref[...] = jnp.transpose(act_low.astype(F32)).astype(BF16)


def prep_call(seq, x, w, conv, gains, gate, pers, shift):
    gates = 3 * gate.shape[1]
    rows, width = x.shape
    cols = w.shape[2]
    nb = rows // SPAN
    whole = lambda a: pl.BlockSpec(a.shape, lambda c, n=a.ndim: (0,) * n)
    row_cols = pl.BlockSpec((SPAN, cols), lambda c: (c, 0))
    return pl.pallas_call(
        functools.partial(prep_kernel, shift),
        grid=(nb,),
        in_specs=[
            pl.BlockSpec(memory_space=pltpu.SMEM),
            pl.BlockSpec((SPAN, width), lambda c: (c, 0)),
            whole(w),
            whole(conv),
            whole(gains),
            whole(gate),
            whole(pers),
        ],
        out_specs=[
            row_cols,
            row_cols,
            row_cols,
            pl.BlockSpec((cols, SPAN), lambda c: (0, c)),
            pl.BlockSpec((3, SPAN, cols), lambda c: (0, c, 0)),
            row_cols,
            pl.BlockSpec((SPAN, width), lambda c: (c, 0)),
            pl.BlockSpec((8, width), lambda c: (c, 0)),
            pl.BlockSpec((8, gates), lambda c: (c, 0)),
            whole(pers),
            pl.BlockSpec((gates, width), lambda c: (0, 0)),
        ],
        out_shape=[
            jax.ShapeDtypeStruct((rows, cols), BF16),
            jax.ShapeDtypeStruct((rows, cols), BF16),
            jax.ShapeDtypeStruct((rows, cols), BF16),
            jax.ShapeDtypeStruct((cols, rows), BF16),
            jax.ShapeDtypeStruct((3, rows, cols), F32),
            jax.ShapeDtypeStruct((rows, cols), F32),
            jax.ShapeDtypeStruct((rows, width), BF16),
            jax.ShapeDtypeStruct((nb * 8, width), F32),
            jax.ShapeDtypeStruct((nb * 8, gates), F32),
            jax.ShapeDtypeStruct(pers.shape, BF16),
            jax.ShapeDtypeStruct((gates, width), F32),
        ],
        scratch_shapes=[pltpu.VMEM((3, HALO + SPAN, cols), F32)],
        cost_estimate=cost(15),
        name="prep",
    )(seq, x, w, conv, gains, gate, pers)


def mix_kernel(block, blocks_all, shift, first, last, *refs):
    it = iter(refs)
    seq_ref, lg_ref, q_ref, k_ref, v_ref, kt_ref, pers_ref, gp_ref, a_ref, bt_ref = (
        next(it) for _ in range(10)
    )
    sa_ref, sbt_ref = (None, None) if first or last else (next(it), next(it))
    mixed_ref, tot_ref, att_ref, linv_ref = (next(it) for _ in range(4))
    if not last:
        a2_ref, bt2_ref, sa2_ref, sbt2_ref, ga_ref, gbt_ref = (next(it) for _ in range(6))
        z_ref, r_ref = next(it), next(it)
    rows, cols = q_ref.shape
    head_size = 1 << shift
    heads = cols // head_size
    a_low = a_ref[...].astype(BF16)
    bt_low = bt_ref[...].astype(BF16)
    valid, count = valid_column(seq_ref, block * rows, rows)
    weight = valid / count
    att_ref[...] = jnp.zeros((rows, cols), F32)
    linv_ref[...] = jnp.zeros((rows, cols), F32)
    tot_ref[...] = jnp.zeros((rows, cols), F32)
    if not last:
        r_ref[...] = jnp.zeros((rows, cols), F32)

    def one_head(head, carry):
        mask = head_mask(cols, shift, head)
        mask_low = mask.astype(BF16)
        ones_low = (1.0 - mask).astype(BF16)
        query = q_ref[...] * mask_low
        scaled = query * SCORE_SCALE
        raised = jnp.exp(dot_nt(scaled, pers_ref[0])).astype(BF16)
        total = dot_nn(raised, pers_ref[1] * mask_low + ones_low)
        for j in range(block + 1):
            span = slice(j * rows, (j + 1) * rows)
            raised = jnp.exp(dot_nt(scaled, k_ref[span, :]))
            if j == block:
                raised = jnp.where(
                    iota((rows, rows), 0) >= iota((rows, rows), 1), raised, 0.0
                )
            total = total + dot_nn(raised.astype(BF16), v_ref[span, :] * mask_low + ones_low)
        inverse = 1.0 / pltpu.roll(total, head_size, 1)
        inside = jnp.broadcast_to(mask, (rows, cols)) > 0.5
        linv_ref[...] = jnp.where(inside, inverse, linv_ref[...])
        attended = jnp.where(inside, total * inverse, 0.0)
        att_ref[...] = att_ref[...] + attended
        hid = dot_nn(query, a_low)
        hid = hid * jax.nn.sigmoid(hid)
        recalled = dot_nt(hid.astype(BF16), bt_low) * mask
        tot_ref[...] = tot_ref[...] + attended + recalled
        if not last:
            hid = dot_nn(k_ref[block * rows : (block + 1) * rows, :] * mask_low, a_low)
            sig = jax.nn.sigmoid(hid)
            act = (hid * sig).astype(BF16)
            z_ref[head] = act
            target = v_ref[block * rows : (block + 1) * rows, :].astype(F32)
            resid = (dot_nt(act, bt_low) - target) * mask * weight
            r_ref[...] = r_ref[...] + resid
            d_hid = dot_nn(resid.astype(BF16), bt_low) * (sig * (1.0 + hid * (1.0 - sig)))
            at = pl.ds(pl.multiple_of(head * head_size, head_size), head_size)
            ga_ref[at, :] = dot_nn(kt_ref[at, :], d_hid.astype(BF16))
        return carry

    lax.fori_loop(0, heads, one_head, 0)
    gate = jax.nn.sigmoid(gp_ref[...])
    mixed_ref[...] = (tot_ref[...] * gate).astype(BF16)
    if not last:
        resid_t = jnp.transpose(r_ref[...]).astype(BF16)
        for head in range(heads):
            at = slice(head * head_size, (head + 1) * head_size)
            gbt_ref[at, :] = dot_nn(resid_t[at, :], z_ref[head])
        width = a_ref.shape[1]
        logits = lg_ref[...]
        step = 0.2 * jax.nn.sigmoid(gate_rows(logits, 0, heads, head_size, width))
        keep = jax.nn.sigmoid(gate_rows(logits, 1, heads, head_size, width))
        stay = 1.0 - 0.5 * jax.nn.sigmoid(gate_rows(logits, 2, heads, head_size, width))
        moment_a = -step * ga_ref[...]
        moment_b = -step * gbt_ref[...]
        if not first:
            moment_a = moment_a + keep * sa_ref[...]
            moment_b = moment_b + keep * sbt_ref[...]
        sa2_ref[...] = moment_a
        sbt2_ref[...] = moment_b
        a2_ref[...] = stay * a_ref[...] + moment_a
        bt2_ref[...] = stay * bt_ref[...] + moment_b


def mix_call(block, nb, shift, seq, lg, q, k, v, kt, pers, gp, a, bt, sa, sbt):
    rows, cols = q.shape
    first, last = block == 0, block == nb - 1
    heads = cols >> shift
    whole = lambda s: pl.BlockSpec(s, lambda i, n=len(s): (0,) * n)
    at_block = pl.BlockSpec((SPAN, cols), lambda i: (block, 0))
    upto = pl.BlockSpec(((block + 1) * SPAN, cols), lambda i: (0, 0))
    state = whole(a.shape)
    ins = [seq, lg, q, k, v, kt, pers, gp, a, bt]
    in_specs = [
        pl.BlockSpec(memory_space=pltpu.SMEM),
        pl.BlockSpec((8, lg.shape[1]), lambda i: (block, 0)),
        at_block,
        upto,
        upto,
        pl.BlockSpec((cols, SPAN), lambda i: (0, block)),
        whole(pers.shape),
        at_block,
        state,
        state,
    ]
    if not (first or last):
        ins += [sa, sbt]
        in_specs += [state, state]
    row_spec = whole((SPAN, cols))
    outs = [jax.ShapeDtypeStruct((SPAN, cols), BF16)] + [
        jax.ShapeDtypeStruct((SPAN, cols), F32)
    ] * 3
    out_specs = [row_spec] * 4
    scratch = []
    if not last:
        outs += [jax.ShapeDtypeStruct(a.shape, F32)] * 6
        out_specs += [state] * 6
        scratch = [pltpu.VMEM((heads, SPAN, a.shape[1]), BF16), pltpu.VMEM((SPAN, cols), F32)]
    return pl.pallas_call(
        functools.partial(mix_kernel, block, nb, shift, first, last),
        grid=(1,),
        in_specs=in_specs,
        out_specs=out_specs,
        out_shape=outs,
        scratch_shapes=scratch,
        cost_estimate=cost(9),
        name=f"mix_{block}",
    )(*ins)


def ffn_kernel(nb, first_call, *refs):
    it = iter(refs)
    take = lambda n: [next(it) for _ in range(n)]
    peer_ref, x_ref = take(2)
    piece_refs = [take(4) for _ in range(nb)]
    gain_ref, fin_ref, fout_ref = take(3)
    ow_refs, cot_refs = take(4), take(4)
    if not first_call:
        take(6)
    nt_ref, hid_ref, dgu_ref, cotf_ref, mfull_ref, res_ref = take(6)
    if first_call:
        take(1)
    (m_ref,) = take(1)
    step = pl.program_id(0)
    cols = m_ref.shape[2]
    for block in range(nb):

        @pl.when(step == block)
        def _(block=block):
            for j in range(4):
                m_ref[j] = piece_refs[block][j][...]

    spots = [pl.ds(pl.multiple_of(peer_ref[j] * cols, cols), cols) for j in range(4)]
    for j in range(4):
        mfull_ref[:, spots[j]] = m_ref[j]
        cotf_ref[:, spots[j]] = cot_refs[j][...]
    mixed = mfull_ref[...]
    for j in range(4):
        branch = dot_nn(mixed, ow_refs[j][...])
        res_ref[:, spots[j]] = x_ref[:, spots[j]].astype(F32) + branch
    residual = res_ref[...]
    scale = lax.rsqrt(jnp.mean(residual * residual, -1, keepdims=True) + NORM_EPS)
    low = (residual * scale * gain_ref[1:2, :]).astype(BF16)
    nt_ref[...] = low
    d_hidden = dot_nt(cotf_ref[...], fout_ref[...])
    gate_pre = dot_nn(low, fin_ref[0])
    up_pre = dot_nn(low, fin_ref[1])
    sig = jax.nn.sigmoid(gate_pre)
    silu = gate_pre * sig
    hid_ref[...] = (silu * up_pre).astype(BF16)
    slope = sig * (1.0 + gate_pre * (1.0 - sig))
    dgu_ref[0] = (d_hidden * up_pre * slope).astype(BF16)
    dgu_ref[1] = (d_hidden * silu).astype(BF16)


def ffn_call(blocks, peers, x, pieces, packs, gains, fin, fout, shared):
    rows, width = x.shape
    cols = pieces[0][0].shape[1]
    nb = len(blocks)
    low = blocks[0]
    hidden = fout.shape[0]
    once = pl.Buffered(1)
    whole = lambda a: pl.BlockSpec(a.shape, lambda i, n=a.ndim: (0,) * n, pipeline_mode=once)
    at_rows = lambda n: pl.BlockSpec((SPAN, n), lambda i: (low + i, 0))
    anywhere = pl.BlockSpec(memory_space=pl.ANY)
    struct = jax.ShapeDtypeStruct
    ins = [peers, x, *[piece for block in pieces for piece in block], gains, fin, fout]
    ins += [*packs, *packs]
    in_specs = [pl.BlockSpec(memory_space=pltpu.SMEM), at_rows(width)]
    in_specs += [whole(piece) for block in pieces for piece in block]
    in_specs += [whole(gains), whole(fin), whole(fout)]
    ahead = width // SPAN
    in_specs += [pl.BlockSpec((width, cols), lambda i: (0, 0), pipeline_mode=once)] * 4
    in_specs += [pl.BlockSpec((SPAN, cols), lambda i: (ahead + low + i, 0))] * 4
    room = [] if shared else [struct((3 * width, width), BF16)]
    aliases = {}
    if shared:
        aliases = {len(ins) + n: n for n in range(len(shared))}
        ins += shared
        in_specs += [anywhere] * len(shared)
    got = pl.pallas_call(
        functools.partial(ffn_kernel, nb, not shared),
        grid=(nb,),
        in_specs=in_specs,
        out_specs=[
            at_rows(width),
            at_rows(hidden),
            pl.BlockSpec((2, SPAN, hidden), lambda i: (0, low + i, 0)),
            at_rows(width),
            at_rows(width),
            at_rows(width),
        ]
        + [anywhere] * len(room),
        out_shape=[
            struct((rows, width), BF16),
            struct((rows, hidden), BF16),
            struct((2, rows, hidden), BF16),
            struct((rows, width), BF16),
            struct((rows, width), BF16),
            struct((rows, width), F32),
        ]
        + room,
        input_output_aliases=aliases,
        scratch_shapes=[pltpu.VMEM((4, SPAN, cols), BF16)],
        cost_estimate=cost(8 * nb),
        name=f"ffn_{low}",
    )(*ins)
    return got[:6], got[6:]


def ffn_back_kernel(first_call, *refs):
    it = iter(refs)
    take = lambda n: [next(it) for _ in range(n)]
    peer_ref, dgu_ref, fin_ref, res_ref = take(4)
    gg_in_ref = None if first_call else take(1)[0]
    gg_ref, keep_ref, send_ref, part_ref = take(4)
    width = res_ref.shape[1]
    residual = res_ref[...]
    scale = lax.rsqrt(jnp.mean(residual * residual, -1, keepdims=True) + NORM_EPS)
    d_normed = dot_nt(dgu_ref[0], fin_ref[0]) + dot_nt(dgu_ref[1], fin_ref[1])
    gains = jnp.sum(d_normed * residual * scale, 0, keepdims=True)

    @pl.when(pl.program_id(0) == 0)
    def _():
        gg_ref[...] = jnp.zeros(gg_ref.shape, F32) if first_call else gg_in_ref[...]

    gg_ref[...] = gg_ref[...] + jnp.broadcast_to(gains, gg_ref.shape)
    half = width // 2
    part_ref[...] = d_normed.astype(BF16)
    core = peer_ref[0] & 1
    keep_ref[...] = part_ref[:, pl.ds(pl.multiple_of(core * half, half), half)]
    send_ref[...] = part_ref[:, pl.ds(pl.multiple_of((1 - core) * half, half), half)]


def ffn_back_call(blocks, peers, dgu, fin, res, gains):
    width = res.shape[1]
    tile = SPAN // 2
    steps = SPAN // tile
    low = blocks[0] * steps
    lines = len(blocks) * SPAN
    gain_spec = pl.BlockSpec((8, width), lambda i: (0, 0))
    row = pl.BlockSpec((tile, width // 2), lambda i: (i, 0))
    struct = jax.ShapeDtypeStruct
    return pl.pallas_call(
        functools.partial(ffn_back_kernel, gains is None),
        grid=(len(blocks) * steps,),
        in_specs=[
            pl.BlockSpec(memory_space=pltpu.SMEM),
            pl.BlockSpec((2, tile, dgu.shape[2]), lambda i: (0, low + i, 0)),
            pl.BlockSpec(fin.shape, lambda i: (0, 0, 0), pipeline_mode=pl.Buffered(1)),
            pl.BlockSpec((tile, width), lambda i: (low + i, 0)),
        ]
        + ([] if gains is None else [gain_spec]),
        out_specs=[gain_spec, row, row],
        out_shape=[
            struct((8, width), F32),
            struct((lines, width // 2), BF16),
            struct((lines, width // 2), BF16),
        ],
        scratch_shapes=[pltpu.VMEM((tile, width), BF16)],
        cost_estimate=cost(4 * len(blocks)),
        name=f"ffn_back_{blocks[0]}",
    )(peers, dgu, fin, res, *([] if gains is None else [gains]))


def down_kernel(peer_ref, hid_ref, fout_ref, keep_ref, send_ref, part_ref):
    cols = keep_ref.shape[2]
    part_ref[...] = dot_nn(hid_ref[...], fout_ref[...]).astype(BF16)
    for slot, out_ref in ((0, keep_ref), (1, send_ref)):
        for n in range(2):
            start = pl.multiple_of(peer_ref[slot + 2 * n] * cols, cols)
            out_ref[n] = part_ref[:, pl.ds(start, cols)]


def down_call(peers, hid, fout, cols):
    rows, hidden = hid.shape
    width = fout.shape[1]
    stacked = pl.BlockSpec((2, SPAN, cols), lambda i: (0, i, 0))
    return pl.pallas_call(
        down_kernel,
        grid=(rows // SPAN,),
        in_specs=[
            pl.BlockSpec(memory_space=pltpu.SMEM),
            pl.BlockSpec((SPAN, hidden), lambda i: (i, 0)),
            pl.BlockSpec(fout.shape, lambda i: (0, 0), pipeline_mode=pl.Buffered(1)),
        ],
        out_specs=[stacked, stacked],
        out_shape=[jax.ShapeDtypeStruct((2, rows, cols), BF16)] * 2,
        scratch_shapes=[pltpu.VMEM((SPAN, width), BF16)],
        cost_estimate=cost(6),
        name="down",
    )(peers, hid, fout)


def turn_kernel(blocks, steps, first_call, *refs):
    it = iter(refs)
    take = lambda n: [next(it) for _ in range(n)]
    peer_ref, s1_ref, r2_ref, ps1_ref, pr2_ref, res_ref, cot_ref = take(7)
    gain_ref, gp_ref = take(2)
    ow_refs = take(4)
    tot_refs = take(blocks)
    if not first_call:
        take(4)
    dres_ref, rescol_ref, dbr_ref, dgall_ref, dga_ref, dgp_ref, full_ref = take(7)
    rows, width = res_ref.shape
    cols = gp_ref.shape[1]
    half = width // 2
    core = peer_ref[0] & 1
    at_own = pl.ds(pl.multiple_of(core * half, half), half)
    at_other = pl.ds(pl.multiple_of((1 - core) * half, half), half)
    full_ref[:, at_own] = s1_ref[...].astype(F32) + r2_ref[...].astype(F32)
    full_ref[:, at_other] = ps1_ref[...].astype(F32) + pr2_ref[...].astype(F32)
    residual = res_ref[...]
    scale = lax.rsqrt(jnp.mean(residual * residual, -1, keepdims=True) + NORM_EPS)
    gained = full_ref[...] * gain_ref[1:2, :]
    inner = jnp.sum(gained * residual, -1, keepdims=True) / width
    d_residual = cot_ref[...].astype(F32) + scale * gained - residual * (scale * scale * scale * inner)
    own = pl.ds(pl.multiple_of(peer_ref[0] * cols, cols), cols)
    full_ref[...] = d_residual
    d_mixed = None
    for j in range(4):
        at = pl.ds(pl.multiple_of(peer_ref[j] * cols, cols), cols)
        term = dot_nt(full_ref[:, at].astype(BF16), ow_refs[j][own, :])
        d_mixed = term if d_mixed is None else d_mixed + term
    mine = full_ref[:, own]
    dres_ref[...] = mine
    dbr_ref[...] = mine.astype(BF16)
    rescol_ref[...] = res_ref[:, own]
    gate = jax.nn.sigmoid(gp_ref[...])
    d_gated = d_mixed * gate
    dga_ref[...] = d_gated.astype(BF16)
    total = tot_refs[0][...]
    for n in range(1, blocks):
        total = jnp.where(pl.program_id(0) >= n * steps, tot_refs[n][...], total)
    d_gate = (d_gated * total * (1.0 - gate)).astype(BF16)
    dgp_ref[...] = d_gate
    dgall_ref[...] = d_gate


def turn_call(blocks, peers, pieces, res, cot, ow, gains, gp, tots, shared):
    rows, cols = gp.shape
    width = res.shape[1]
    tile = SPAN // 2
    steps = SPAN // tile
    low = blocks[0] * steps
    count = len(blocks) * steps
    whole = lambda a: pl.BlockSpec(a.shape, lambda i, n=a.ndim: (0,) * n)
    row = lambda n: pl.BlockSpec((tile, n), lambda i: (i, 0))
    at_rows = lambda n: pl.BlockSpec((tile, n), lambda i: (low + i, 0))
    struct = jax.ShapeDtypeStruct
    ins = [peers, *pieces, res, cot, gains, gp, *ow, *tots]
    in_specs = [
        pl.BlockSpec(memory_space=pltpu.SMEM),
        row(width // 2),
        row(width // 2),
        row(width // 2),
        row(width // 2),
        at_rows(width),
        at_rows(width),
        whole(gains),
        at_rows(cols),
    ] + [pl.BlockSpec((width, cols), lambda i: (0, 0))] * 4
    for n in range(len(blocks)):
        spot = lambda i, n=n: (jnp.clip(i - n * steps, 0, steps - 1), 0)
        in_specs.append(pl.BlockSpec((tile, cols), spot))
    aliases = {}
    if shared is not None:
        aliases = {len(ins) + n: n for n in range(len(shared))}
        ins += shared
        in_specs += [pl.BlockSpec(memory_space=pl.ANY)] * len(shared)
    got = pl.pallas_call(
        functools.partial(turn_kernel, len(blocks), steps, shared is None),
        grid=(count,),
        in_specs=in_specs,
        out_specs=[at_rows(cols)] * 4 + [row(cols)] * 2,
        out_shape=[
            struct((rows, cols), F32),
            struct((rows, cols), F32),
            struct((rows, cols), BF16),
            struct((rows, cols), BF16),
            struct((len(blocks) * SPAN, cols), BF16),
            struct((len(blocks) * SPAN, cols), BF16),
        ],
        input_output_aliases=aliases,
        scratch_shapes=[pltpu.VMEM((tile, width), F32)],
        cost_estimate=cost(5 * len(blocks)),
        name=f"turn_{blocks[0]}",
    )(*ins)
    return got[:4], got[4:]


def back_kernel(block, nb, shift, *refs):
    it = iter(refs)
    take = lambda n: [next(it) for _ in range(n)]
    first, last = block == 0, block == nb - 1
    seq_ref, q_ref, k_ref, v_ref, kt_ref, pers_ref, dga_ref, att_ref, linv_ref = take(9)
    a_ref, bt_ref = take(2)
    if not last:
        dk_in_ref, dv_in_ref, dp_in_ref, lg_ref, ga_ref, gbt_ref, ab_in_ref, btb_in_ref = take(8)
        sab_in_ref, sbtb_in_ref = take(2) if block < nb - 2 else (None, None)
        sa_ref, sbt_ref = (None, None) if first else take(2)
    dq_ref, dk_ref, dv_ref, dp_ref, ab_ref, btb_ref = take(6)
    if not last:
        (dlg_ref,) = take(1)
        sab_ref, sbtb_ref = (None, None) if first else take(2)
    lt_ref, dt_ref, dqt_ref, qt_ref, dot_ref = take(5)
    if not last:
        z_ref, zd_ref, r_ref, y_ref, h_ref = take(5)
    rows, cols = q_ref.shape
    head_size = 1 << shift
    heads = cols // head_size
    own = slice(block * rows, (block + 1) * rows)
    a_low = a_ref[...].astype(BF16)
    bt_low = bt_ref[...].astype(BF16)
    if last:
        dk_ref[...] = jnp.zeros(dk_ref.shape, F32)
        dv_ref[...] = jnp.zeros(dv_ref.shape, F32)
        dp_ref[...] = jnp.zeros(dp_ref.shape, F32)
        ab_ref[...] = jnp.zeros(ab_ref.shape, F32)
        btb_ref[...] = jnp.zeros(btb_ref.shape, F32)
    else:
        dk_ref[...] = dk_in_ref[...]
        dv_ref[...] = dv_in_ref[...]
        dp_ref[...] = dp_in_ref[...]
    pick = (iota((8, cols), 1) >> shift) == iota((8, cols), 0)
    start = iota((8, cols), 1) == (iota((8, cols), 0) << shift)
    lt_ref[...] = dot_nt(jnp.where(start, 1.0, 0.0), linv_ref[...], HIGH)
    d_gated = dga_ref[...].astype(F32)
    dt_ref[...] = dot_nt(jnp.where(pick, 1.0, 0.0), d_gated * att_ref[...], HIGH)
    dq_ref[...] = jnp.zeros((rows, cols), F32)
    qt_ref[...] = jnp.transpose(q_ref[...].astype(F32)).astype(BF16)
    dot_ref[...] = jnp.transpose(d_gated).astype(BF16)
    if not last:
        valid, count = valid_column(seq_ref, block * rows, rows)
        weight = valid / count
        width = a_ref.shape[1]
        logits = lg_ref[...]
        sig_step = jax.nn.sigmoid(gate_rows(logits, 0, heads, head_size, width))
        keep = jax.nn.sigmoid(gate_rows(logits, 1, heads, head_size, width))
        sig_forget = jax.nn.sigmoid(gate_rows(logits, 2, heads, head_size, width))
        tot_a, tot_b = ab_in_ref[...], btb_in_ref[...]
        if sab_in_ref is not None:
            tot_a, tot_b = tot_a + sab_in_ref[...], tot_b + sbtb_in_ref[...]
        h_ref[0] = (-0.2 * sig_step * tot_a).astype(BF16)
        h_ref[1] = (-0.2 * sig_step * tot_b).astype(BF16)
        d_step = -(ga_ref[...] * tot_a + gbt_ref[...] * tot_b)
        groups = [d_step * (0.2 * sig_step * (1.0 - sig_step)), None, None]
        if not first:
            groups[1] = (sa_ref[...] * tot_a + sbt_ref[...] * tot_b) * (keep * (1.0 - keep))
        d_forget = -(a_ref[...] * ab_in_ref[...] + bt_ref[...] * btb_in_ref[...])
        groups[2] = d_forget * (0.5 * sig_forget * (1.0 - sig_forget))
        d_logits = jnp.zeros(dlg_ref.shape, F32)
        for g, value in enumerate(groups):
            if value is None:
                continue
            for head in range(heads):
                part = value[head * head_size : (head + 1) * head_size, :]
                figure = jnp.sum(jnp.sum(part, 1, keepdims=True), 0, keepdims=True)
                here = iota(dlg_ref.shape, 1) == g * heads + head
                d_logits = d_logits + jnp.where(here, 1.0, 0.0) * figure
        dlg_ref[...] = d_logits
        stay = 1.0 - 0.5 * sig_forget
        ab_ref[...] = stay * ab_in_ref[...]
        btb_ref[...] = stay * btb_in_ref[...]
        if not first:
            sab_ref[...] = keep * tot_a
            sbtb_ref[...] = keep * tot_b
        r_ref[...] = jnp.zeros((rows, cols), F32)
        y_ref[...] = jnp.zeros((rows, cols), F32)

    def one_head(head, carry):
        mask = head_mask(cols, shift, head)
        mask_low = mask.astype(BF16)
        query = q_ref[...] * mask_low
        scaled = query * SCORE_SCALE
        d_out = dga_ref[...] * mask_low
        at = pl.ds(pl.multiple_of(head * head_size, head_size), head_size)
        inverse = lt_ref[pl.ds(head, 1), :]
        delta = dt_ref[pl.ds(head, 1), :]
        probs = jnp.exp(dot_nt(pers_ref[0], scaled)) * inverse
        d_scores = (probs * (dot_nt(pers_ref[1], d_out) - delta)).astype(BF16)
        dp_ref[0] = dp_ref[0] + dot_nn(d_scores, scaled)
        dp_ref[1] = dp_ref[1] + dot_nn(probs.astype(BF16), d_out)
        d_query = lax.dot_general(
            d_scores, pers_ref[0], (((0,), (0,)), ((), ())), preferred_element_type=F32
        )
        d_query = d_query * SCORE_SCALE
        d_query_t = jnp.zeros((head_size, rows), F32)
        for j in range(block + 1):
            span = slice(j * rows, (j + 1) * rows)
            probs = jnp.exp(dot_nt(k_ref[span, :], scaled)) * inverse
            if j == block:
                probs = jnp.where(iota((rows, rows), 0) <= iota((rows, rows), 1), probs, 0.0)
            d_scores = (probs * (dot_nt(v_ref[span, :], d_out) - delta)).astype(BF16)
            dv_ref[span, :] = dv_ref[span, :] + dot_nn(probs.astype(BF16), d_out)
            dk_ref[span, :] = dk_ref[span, :] + dot_nn(d_scores, scaled)
            d_query_t = d_query_t + dot_nn(kt_ref[at, span], d_scores)
        dqt_ref[at, :] = d_query_t * SCORE_SCALE
        hid = dot_nn(query, a_low)
        sig = jax.nn.sigmoid(hid)
        d_hid = dot_nn(d_out, bt_low) * (sig * (1.0 + hid * (1.0 - sig)))
        d_hid = d_hid.astype(BF16)
        dq_ref[...] = dq_ref[...] + (d_query + dot_nt(d_hid, a_low)) * mask
        grad_a = dot_nn(qt_ref[at, :], d_hid)
        grad_b = dot_nn(dot_ref[at, :], (hid * sig).astype(BF16))
        if not last:
            key = k_ref[own, :] * mask_low
            hid = dot_nn(key, a_low)
            probe = dot_nn(key, h_ref[0])
            sig = jax.nn.sigmoid(hid)
            act = (hid * sig).astype(BF16)
            z_ref[head] = act
            slope = sig * (1.0 + hid * (1.0 - sig))
            curve = sig * (1.0 - sig) * (2.0 + hid * (1.0 - 2.0 * sig))
            target = v_ref[own, :].astype(F32)
            resid = (dot_nt(act, bt_low) - target) * mask * weight
            r_ref[...] = r_ref[...] + resid
            resid = resid.astype(BF16)
            d_act = dot_nn(resid, bt_low)
            d_slope = (probe * slope).astype(BF16)
            zd_ref[head] = d_slope
            d_net = (dot_nt(act, h_ref[1]) + dot_nt(d_slope, bt_low)) * mask * weight
            y_ref[...] = y_ref[...] + d_net
            back = dot_nn(resid, h_ref[1]) + dot_nn(d_net.astype(BF16), bt_low)
            d_hid = (probe * d_act * curve + back * slope).astype(BF16)
            direct = (d_act * slope).astype(BF16)
            d_key = (dot_nt(direct, h_ref[0]) + dot_nt(d_hid, a_low)) * mask
            dk_ref[own, :] = dk_ref[own, :] + d_key
            grad_a = grad_a + dot_nn(kt_ref[at, own], d_hid)
        ab_ref[at, :] = ab_ref[at, :] + grad_a
        btb_ref[at, :] = btb_ref[at, :] + grad_b
        return carry

    lax.fori_loop(0, heads, one_head, 0)
    dq_ref[...] = dq_ref[...] + jnp.transpose(dqt_ref[...])
    if not last:
        dv_ref[own, :] = dv_ref[own, :] - y_ref[...]
        resid_t = jnp.transpose(r_ref[...]).astype(BF16)
        net_t = jnp.transpose(y_ref[...]).astype(BF16)
        for head in range(heads):
            at = slice(head * head_size, (head + 1) * head_size)
            grad_b = dot_nn(resid_t[at, :], zd_ref[head]) + dot_nn(net_t[at, :], z_ref[head])
            btb_ref[at, :] = btb_ref[at, :] + grad_b


def back_call(block, nb, shift, seq, q, k, v, kt, pers, dga, att, linv, state, grads, adjoint):
    dga, spot = dga
    cols = q.shape[1]
    heads = cols >> shift
    first, last = block == 0, block == nb - 1
    done = (block + 1) * SPAN
    whole = lambda s: pl.BlockSpec(s, lambda i, n=len(s): (0,) * n)
    at_block = pl.BlockSpec((SPAN, cols), lambda i: (block, 0))
    upto = pl.BlockSpec((done, cols), lambda i: (0, 0))
    rows_spec = whole((SPAN, cols))
    square = state["a"].shape
    ins = [seq, q, k, v, kt, pers, dga, att, linv, state["a"], state["bt"]]
    in_specs = [
        pl.BlockSpec(memory_space=pltpu.SMEM),
        at_block,
        upto,
        upto,
        pl.BlockSpec((cols, done), lambda i: (0, 0)),
        whole(pers.shape),
        pl.BlockSpec((SPAN, cols), lambda i: (spot, 0)),
        rows_spec,
        rows_spec,
        whole(square),
        whole(square),
    ]
    if not last:
        ins += [grads["dk"], grads["dv"], grads["dp"], state["lg"], state["ga"], state["gbt"]]
        ins += [adjoint["ab"], adjoint["btb"]]
        in_specs += [upto, upto, whole(pers.shape)]
        in_specs += [pl.BlockSpec((8, state["lg"].shape[1]), lambda i: (block, 0))]
        in_specs += [whole(square)] * 4
        if block < nb - 2:
            ins += [adjoint["sab"], adjoint["sbtb"]]
            in_specs += [whole(square)] * 2
        if not first:
            ins += [state["sa"], state["sbt"]]
            in_specs += [whole(square)] * 2
    names = ["dq", "dk", "dv", "dp", "ab", "btb"]
    shapes = [(SPAN, cols), (done, cols), (done, cols), pers.shape, square, square]
    if not last:
        names.append("dlg")
        shapes.append((8, state["lg"].shape[1]))
        if not first:
            names += ["sab", "sbtb"]
            shapes += [square, square]
    scratch = [
        pltpu.VMEM((8, SPAN), F32),
        pltpu.VMEM((8, SPAN), F32),
        pltpu.VMEM((cols, SPAN), F32),
        pltpu.VMEM((cols, SPAN), BF16),
        pltpu.VMEM((cols, SPAN), BF16),
    ]
    if not last:
        scratch += [
            pltpu.VMEM((heads, SPAN, square[1]), BF16),
            pltpu.VMEM((heads, SPAN, square[1]), BF16),
            pltpu.VMEM((SPAN, cols), F32),
            pltpu.VMEM((SPAN, cols), F32),
            pltpu.VMEM((2,) + square, BF16),
        ]
    outs = pl.pallas_call(
        functools.partial(back_kernel, block, nb, shift),
        grid=(1,),
        in_specs=in_specs,
        out_specs=[whole(s) for s in shapes],
        out_shape=[jax.ShapeDtypeStruct(s, F32) for s in shapes],
        scratch_shapes=scratch,
        cost_estimate=cost(17),
        name=f"back_{block}",
    )(*ins)
    return dict(zip(names, outs))


def unprep_kernel(block, nb, shift, *refs):
    it = iter(refs)
    take = lambda n: [next(it) for _ in range(n)]
    first, last = block == 0, block == nb - 1
    seq_ref, peer_ref, dq_ref, dk_ref, dv_ref, dgp_ref, pre_ref, w_ref, conv_ref = take(9)
    x_ref, gain_ref = take(2)
    halo_ref = None if first else take(1)[0]
    dp_ref, pers_ref, ab_ref, btb_ref, gain_two_ref = take(5) if first else [None] * 5
    if not last:
        edge_in_ref, dlg_ref, gate_ref, mean_ref = take(4)
        cg_in_ref, gg_in_ref, gate_in_ref = take(7)[:3]
    cg_ref, gg_ref, gate_out_ref = take(3)
    dproj_ref, keep_ref, send_ref, inner_ref, edge_ref = take(5)
    small_ref, gains_ref = take(2) if first else (None, None)
    ext_ref, dext_ref, low_ref = take(3)
    rows, cols = dq_ref.shape
    width = x_ref.shape[1]
    blocks = head_blocks(cols, shift)
    taps = conv_ref.shape[1]
    d_normed = dot_nt(dgp_ref[...], w_ref[3])
    dproj_ref[3] = dgp_ref[...]
    if last:
        cg_ref[...] = jnp.zeros(cg_ref.shape, F32)
        gg_ref[...] = jnp.zeros(gg_ref.shape, F32)
        gate_out_ref[...] = jnp.zeros(gate_out_ref.shape, F32)
    else:
        cg_ref[...] = cg_in_ref[...]
        gg_ref[...] = gg_in_ref[...]
    for i in range(3):
        pre = pre_ref[i]
        ext_ref[0:HALO, :] = jnp.zeros((HALO, cols), F32) if first else halo_ref[i]
        ext_ref[HALO : HALO + rows, :] = pre
        shifted = [pre] + [ext_ref[HALO - j : HALO - j + rows, :] for j in range(1, taps)]
        conv = conv_ref[i, 0:1, :] * pre
        for j in range(1, taps):
            conv = conv + conv_ref[i, j : j + 1, :] * shifted[j]
        sig = jax.nn.sigmoid(conv)
        d_act = (dq_ref, dk_ref, dv_ref)[i][...]
        if i < 2:
            act = conv * sig
            scale = lax.rsqrt(head_sum(act * act, blocks) + UNIT_EPS)
            d_act = scale * (d_act - act * (scale * scale * head_sum(d_act * act, blocks)))
        d_conv = d_act * (sig * (1.0 + conv * (1.0 - sig)))
        edge_ref[i] = d_conv[0:HALO, :]
        dext_ref[0:rows, :] = d_conv
        dext_ref[rows : rows + HALO, :] = (
            jnp.zeros((HALO, cols), F32) if last else edge_in_ref[i]
        )
        d_pre = conv_ref[i, 0:1, :] * d_conv
        for j in range(taps):
            if j:
                d_pre = d_pre + conv_ref[i, j : j + 1, :] * dext_ref[j : j + rows, :]
            at = slice(i * taps + j, i * taps + j + 1)
            cg_ref[at, :] = cg_ref[at, :] + jnp.sum(d_conv * shifted[j], 0, keepdims=True)
        d_low = d_pre.astype(BF16)
        dproj_ref[i] = d_low
        d_normed = d_normed + dot_nt(d_low, w_ref[i])
    if not last:
        valid, count = valid_column(seq_ref, block * rows, rows)
        d_mean = jnp.dot(
            dlg_ref[...], gate_ref[...], preferred_element_type=F32, precision=HIGH
        )
        d_normed = d_normed + (valid / count) * d_mean[0:1, :]
        outer = lax.dot_general(
            dlg_ref[...] * 0.125,
            mean_ref[...],
            (((0,), (0,)), ((), ())),
            preferred_element_type=F32,
            precision=HIGH,
        )
        gate_out_ref[...] = gate_in_ref[...]
        at = slice(0, outer.shape[0])
        gate_out_ref[at, :] = gate_in_ref[at, :] + outer
    x = x_ref[...].astype(F32)
    scale = lax.rsqrt(jnp.mean(x * x, -1, keepdims=True) + NORM_EPS)
    weighted = d_normed * x
    gains = jnp.sum(weighted * scale, 0, keepdims=True)
    gg_ref[...] = gg_ref[...] + jnp.broadcast_to(gains, gg_ref.shape)
    gained = jnp.broadcast_to(gain_ref[0:1, :], (8, width))
    inner_ref[...] = dot_nt(gained.astype(BF16), weighted.astype(BF16))
    low_ref[...] = d_normed.astype(BF16)
    for slot, out_ref in ((0, keep_ref), (1, send_ref)):
        for n in range(2):
            start = pl.multiple_of(peer_ref[slot + 2 * n] * cols, cols)
            out_ref[n] = low_ref[:, pl.ds(start, cols)]
    if first:
        keys = pers_ref[0]
        d_keys = dp_ref[0]
        scale = lax.rsqrt(head_sum(keys * keys, blocks) + UNIT_EPS)
        along = head_sum(d_keys * keys, blocks)
        d_keys = scale * (d_keys - keys * (scale * scale * along))
        across = lambda a: [a[:, n : n + cols] for n in range(0, width, cols)]
        parts = [ab_ref[...], btb_ref[...], *across(gate_out_ref[...]), cg_ref[...]]
        parts += [d_keys, dp_ref[1]]
        at = 0
        for part in parts:
            small_ref[at : at + part.shape[0], :] = part.astype(BF16)
            at += part.shape[0]
        gains_ref[0:1, :] = gg_ref[0:1, :]
        gains_ref[1:2, :] = gain_two_ref[0:1, :]
        small_ref[at:, :] = jnp.zeros((small_ref.shape[0] - at, cols), BF16)


def unprep_call(
    block, nb, shift, seq, peers, back, dgp, pre, w, conv, x, gains, gate, mean, pers, gain_two,
    shared,
):
    dgp, spot = dgp
    rows, width = x.shape
    cols = dgp.shape[1]
    first, last = block == 0, block == nb - 1
    whole = lambda a: pl.BlockSpec(a.shape, lambda i, n=len(a.shape): (0,) * n)
    smem = pl.BlockSpec(memory_space=pltpu.SMEM)
    at_block = pl.BlockSpec((SPAN, cols), lambda i: (block, 0))
    stacked = lambda n: pl.BlockSpec((n, SPAN, cols), lambda i: (0, block, 0))
    struct = jax.ShapeDtypeStruct
    gate_rows_out = 16
    names = ["cg", "gg", "gate", "dproj", "keep", "send", "inner", "edge"]
    outs = [
        struct((16, cols), F32),
        struct((8, width), F32),
        struct((gate_rows_out, width), F32),
        struct((4, rows, cols), BF16),
        struct((2, rows, cols), BF16),
        struct((2, rows, cols), BF16),
        struct((8, rows), F32),
        struct((3, HALO, cols), F32),
    ]
    out_specs = [whole(a) for a in outs[:3]]
    out_specs += [
        stacked(4),
        stacked(2),
        stacked(2),
        pl.BlockSpec((8, SPAN), lambda i: (0, block)),
        whole(outs[7]),
    ]
    ins = [seq, peers, back["dq"], back["dk"], back["dv"], dgp, pre, w, conv, x, gains]
    in_specs = [
        smem,
        smem,
        whole(back["dq"]),
        at_block,
        at_block,
        pl.BlockSpec((SPAN, cols), lambda i: (spot, 0)),
        stacked(3),
        whole(w),
        whole(conv),
        pl.BlockSpec((SPAN, width), lambda i: (block, 0)),
        whole(gains),
    ]
    aliases = {}
    if not first:
        ins.append(pre)
        in_specs.append(
            pl.BlockSpec((3, HALO, cols), lambda i: (0, block * (SPAN // HALO) - 1, 0))
        )
    else:
        others = [back["dp"], pers, back["ab"], back["btb"], gain_two]
        ins += others
        in_specs += [whole(a) for a in others]
        names += ["small", "gains"]
        ahead = 5 * width // SMALL_ROWS
        outs.append(struct(((ahead + 1) * SMALL_ROWS, cols), BF16))
        out_specs.append(pl.BlockSpec((SMALL_ROWS, cols), lambda i: (ahead, 0)))
        outs.append(struct((2, width), F32))
        out_specs.append(whole(outs[-1]))
    if not last:
        ins += [shared["edge"], back["dlg"], gate, mean]
        in_specs += [whole(shared["edge"]), whole(back["dlg"]), whole(gate)]
        in_specs.append(pl.BlockSpec((8, width), lambda i: (block, 0)))
        aliases = {len(ins) + n: n for n in range(7)}
        ins += [shared[name] for name in names[:7]]
        in_specs += [whole(a) for a in outs[:3]] + [pl.BlockSpec(memory_space=pl.ANY)] * 4
    got = pl.pallas_call(
        functools.partial(unprep_kernel, block, nb, shift),
        grid=(1,),
        in_specs=in_specs,
        out_specs=out_specs,
        out_shape=outs,
        input_output_aliases=aliases,
        scratch_shapes=[
            pltpu.VMEM((HALO + SPAN, cols), F32),
            pltpu.VMEM((SPAN + HALO, cols), F32),
            pltpu.VMEM((SPAN, width), BF16),
        ],
        cost_estimate=cost(10),
        name=f"unprep_{block}",
    )(*ins)
    return dict(zip(names, got))


def finish_kernel(peer_ref, x_ref, dres_ref, half_ref, far_ref, i0_ref, i1_ref, gain_ref, out_ref):
    rows, width = x_ref.shape
    cols = out_ref.shape[1]
    own = pl.ds(pl.multiple_of(peer_ref[0] * cols, cols), cols)
    x = x_ref[...].astype(F32)
    scale = lax.rsqrt(jnp.mean(x * x, -1, keepdims=True) + NORM_EPS)
    inner = jnp.transpose(i0_ref[...] + i1_ref[...])[:, 0:1] / width
    d_normed = half_ref[0].astype(F32) + far_ref[...].astype(F32)
    d_normed = d_normed * gain_ref[0:1, own]
    x_own = x_ref[:, own].astype(F32)
    out_ref[...] = dres_ref[...] + scale * d_normed - x_own * (scale * scale * scale * inner)


def finish_call(peers, x, dres, half, far, inner, inner_far, gains):
    rows, width = x.shape
    cols = dres.shape[1]
    row = lambda n: pl.BlockSpec((SPAN, n), lambda i: (i, 0))
    across = pl.BlockSpec((8, SPAN), lambda i: (0, i))
    return pl.pallas_call(
        finish_kernel,
        grid=(rows // SPAN,),
        in_specs=[
            pl.BlockSpec(memory_space=pltpu.SMEM),
            row(width),
            row(cols),
            pl.BlockSpec((1, SPAN, cols), lambda i: (0, i, 0)),
            row(cols),
            across,
            across,
            pl.BlockSpec(gains.shape, lambda i: (0, 0)),
        ],
        out_specs=row(cols),
        out_shape=jax.ShapeDtypeStruct((rows, cols), F32),
        cost_estimate=cost(4),
        name="finish",
    )(peers, x, dres, half, far, inner, inner_far, gains)


def unpack_kernel(shift, main_ref, small_ref, proj_ref, out_ref, a_ref, b_ref, gate_ref, conv_ref,
                  pers_ref, gain_ref):
    step = pl.program_id(0)
    cols = main_ref.shape[1]
    head_size = 1 << shift
    heads = cols // head_size
    last = pl.num_programs(0) - 1

    @pl.when(step < last)
    def _():
        proj_ref[0] = main_ref[...].astype(F32)

    @pl.when(step == last)
    def _():
        out_ref[...] = main_ref[...].astype(F32)

    @pl.when(step == 0)
    def _():
        small = small_ref[...].astype(F32)
        at = 2 * cols
        for h in range(heads):
            rows = slice(h * head_size, (h + 1) * head_size)
            a_ref[h] = small[rows, :]
            b_ref[h] = small[cols : 2 * cols][rows, :]
        lanes = gain_ref.shape[1] // cols
        for n in range(lanes):
            for g in range(3):
                row = at + 16 * n + g * heads
                gate_ref[g, :, n * cols : (n + 1) * cols] = small[row : row + heads, :]
        at += 16 * lanes
        taps = conv_ref.shape[1]
        for i in range(3):
            conv_ref[i] = small[at + i * taps : at + (i + 1) * taps, :]
        at += 16
        count = pers_ref.shape[2]
        for i in range(2):
            for h in range(heads):
                spot = slice(h * head_size, (h + 1) * head_size)
                pers_ref[i, h] = small[at + i * count : at + (i + 1) * count, spot]
        at += 2 * count
        for i in range(2):
            for n in range(lanes):
                row = at + i * lanes + n
                gain_ref[i : i + 1, n * cols : (n + 1) * cols] = small[row : row + 1, :]


def unpack_call(payload, shift, width, mem_hid, taps, persist_rows):
    cols = payload.shape[1]
    heads = cols >> shift
    head_size = 1 << shift
    ahead = 5 * width // SMALL_ROWS
    struct = jax.ShapeDtypeStruct
    outs = [
        struct((4, width, cols), F32),
        struct((width, cols), F32),
        struct((heads, head_size, mem_hid), F32),
        struct((heads, head_size, mem_hid), F32),
        struct((3, heads, width), F32),
        struct((3, taps, cols), F32),
        struct((2, heads, persist_rows, head_size), F32),
        struct((2, width), F32),
    ]
    whole = lambda a: pl.BlockSpec(a.shape, lambda i, n=len(a.shape): (0,) * n)
    return pl.pallas_call(
        functools.partial(unpack_kernel, shift),
        grid=(5,),
        in_specs=[
            pl.BlockSpec((width, cols), lambda i: (i, 0)),
            pl.BlockSpec((SMALL_ROWS, cols), lambda i: (ahead, 0)),
        ],
        out_specs=[pl.BlockSpec((1, width, cols), lambda i: (jnp.minimum(i, 3), 0, 0))]
        + [whole(a) for a in outs[1:]],
        out_shape=outs,
        cost_estimate=cost(4),
        name="unpack",
    )(payload, payload)


def ring_of(size):
    return [list(range(0, size, 2)) + list(range(size - 1 - size % 2, 0, -2))]


def ring_scatter(payload, axis, size):
    return lax.psum_scatter(
        payload, axis, scatter_dimension=0, axis_index_groups=ring_of(size), tiled=True
    )


def ring_gather(part, axis, size):
    return lax.all_gather(part, axis, axis=0, axis_index_groups=ring_of(size), tiled=True)


def stacked_rows(pieces, full):
    at = 0
    for piece in pieces:
        full = lax.dynamic_update_slice(full, piece, (at, 0))
        at += piece.shape[0]
    return full


def after(value, *others):
    return lax.optimization_barrier((value, *others))[0]


def per_device(
    ring_size,
    layer_input,
    proj_weight,
    conv_weight,
    persist_kv,
    memory_in,
    memory_out,
    memory_gate,
    out_weight,
    ffn_in,
    ffn_out,
    norm_gains,
    seq_len,
    out_grad,
):
    rows, width = layer_input.shape
    cols = proj_weight.shape[2]
    heads = persist_kv.shape[1]
    head_size = persist_kv.shape[3]
    shift = head_size.bit_length() - 1
    mem_hid = memory_in.shape[2]
    nb = rows // SPAN
    taps = conv_weight.shape[1]
    me = lax.axis_index("head")
    count = width // cols
    peers = jnp.stack([me, me ^ 1, me ^ 2, me ^ 3]).astype(jnp.int32)
    swap = lambda a, bit: lax.ppermute(a, "head", [(i, i ^ bit) for i in range(count)])
    packed = jnp.concatenate([out_weight, out_grad], 0)
    far_pack, near_pack = swap(packed, 2), swap(packed, 1)
    pers = jnp.transpose(persist_kv, (0, 2, 1, 3)).reshape(2, -1, cols)
    q, k, v, kt, pre, gp, nl, mean, lg, pers_low, gate = prep_call(
        seq_len, layer_input, proj_weight, conv_weight, norm_gains,
        jnp.transpose(memory_gate, (1, 2, 0)), pers, shift,
    )
    a = memory_in.reshape(cols, mem_hid)
    bt = jnp.transpose(memory_out, (0, 2, 1)).reshape(cols, mem_hid)
    sa = sbt = None
    states, mixes = [], []
    for c in range(nb):
        if c == 1:
            a = after(a, near_pack)
        if c == min(2, nb - 1):
            a = after(a, far_pack)
            packs = (packed, near_pack, far_pack, swap(after(far_pack, mixes[c - 1]["tot"]), 1))
        state = dict(a=a, bt=bt, sa=sa, sbt=sbt, lg=lg)
        got = mix_call(c, nb, shift, seq_len, lg, q, k, v, kt, pers_low, gp, a, bt, sa, sbt)
        if c < nb - 1:
            a, bt, sa, sbt, state["ga"], state["gbt"] = got[4:]
        states.append(state)
        pieces = [got[0], swap(got[0], 1), swap(got[0], 2)]
        if c == nb - 1:
            pieces.append(swap(got[0], 3))
        mixes.append(dict(pieces=pieces, tot=got[1], att=got[2], linv=got[3]))
    for c in range(nb - 1):
        pieces = mixes[c]["pieces"]
        pieces.append(swap(after(pieces[2], mixes[-1]["pieces"][0]), 1))
    groups = [list(range(nb - 1)), [nb - 1]] if nb > 1 else [[0]]
    shared = None
    for n, blocks in enumerate(groups):
        x = after(layer_input, mixes[-1]["pieces"][0]) if n == 0 else layer_input
        shared, room = ffn_call(
            blocks, peers, x, [mixes[c]["pieces"] for c in blocks], packs, norm_gains, ffn_in,
            ffn_out, shared,
        )
        grads_room = room[0] if room else grads_room
    normed_two, hidden, dgu, cot_full, mixed_full, residual = shared
    along_rows = (((0,), (0,)), ((), ()))
    outer = lambda left, right: lax.dot_general(
        left, right, along_rows, preferred_element_type=F32
    ).astype(BF16)
    ffn_grads = stacked_rows(
        [outer(normed_two, dgu[0]), outer(normed_two, dgu[1]), outer(hidden, cot_full)],
        grads_room,
    )
    ffn_part = ring_scatter(ffn_grads, "dp", ring_size)
    s1, r2, gain_two = [], [], None
    tie = (ffn_grads,)
    for n, blocks in enumerate(reversed(groups)):
        gain_two, keep, send = ffn_back_call(
            blocks, peers, after(dgu, *tie), ffn_in, residual, gain_two
        )
        send = after(send, *r2) if r2 else send
        s1.append((keep.astype(F32) + swap(send, 1).astype(F32)).astype(BF16))
        r2.append(swap(s1[n], 2))
        tie = (s1[0],)
    tie = (gain_two,)
    back = unprep = None
    gated = [None] * nb

    def turn(n, blocks, turned, ties, relay_ties):
        pieces = (
            s1[n], r2[n], swap(after(s1[n], *relay_ties), 1), swap(after(r2[n], *relay_ties), 1)
        )
        turned, (d_gated, d_gates) = turn_call(
            blocks, peers, pieces, after(residual, *ties), cot_full, packs, norm_gains, gp,
            [mixes[c]["tot"] for c in blocks], turned,
        )
        for spot, c in enumerate(blocks):
            gated[c] = (d_gated, spot), (d_gates, spot)
        return turned

    turned = turn(0, [nb - 1], None, tie, (r2[0],))
    tie = tuple(s1[1:])
    for c in reversed(range(nb)):
        back = back_call(
            c, nb, shift, seq_len, after(q, *tie), k, v, kt,
            pers_low, gated[c][0],
            mixes[c]["att"], mixes[c]["linv"], states[c], back, back,
        )
        if c == nb - 1:
            relay_ties = (back["dq"],)
        unprep = unprep_call(
            c, nb, shift, seq_len, peers, back, gated[c][1], pre, proj_weight, conv_weight,
            layer_input, norm_gains, gate, mean, pers, gain_two, unprep,
        )
        tie = (unprep["edge"],)
        if c == nb - 1:
            if c:
                turned = turn(1, list(range(c)), turned, tie, relay_ties)
            d_res, res_cols, d_branch, d_gate_all = turned
            d_branch, ffn_part = lax.optimization_barrier((d_branch, ffn_part))
            ffn_grads = ring_gather(ffn_part, "dp", ring_size)
            tie = (d_branch,)
    gains = unprep["gains"]
    gains = gains + sum(swap(gains, bit) for bit in (1, 2, 3))
    cuts = [4 * width, width, 2 * cols, 16 * width // cols, 16, pers.shape[1] * 2]
    cuts.append(2 * width // cols)
    payload = stacked_rows(
        [outer(nl, unprep["dproj"][i]) for i in range(4)]
        + [outer(mixed_full, d_branch)],
        unprep["small"],
    )
    payload = lax.dynamic_update_slice(
        payload, gains.reshape(-1, cols).astype(BF16), (sum(cuts[:-1]), 0)
    )
    tie = (payload,)
    payload, ffn_grads = lax.optimization_barrier((payload, ffn_grads))
    ffn_in_grad = ffn_grads[: 2 * width].astype(F32).reshape(2, width, -1)
    ffn_out_grad = ffn_grads[2 * width :].astype(F32)
    payload = ring_scatter(payload, "dp", ring_size)
    half = (
        unprep["keep"].astype(F32) + swap(after(unprep["send"], *tie), 1).astype(F32)
    ).astype(BF16)
    inner = unprep["inner"] + swap(unprep["inner"], 1)
    far = swap(half[1], 2)
    input_grad = finish_call(
        peers, layer_input, d_res, half, far, inner, swap(inner, 2), norm_gains
    )
    part_keep, part_send = down_call(peers, after(hidden, half), ffn_out, cols)
    payload, input_grad, ffn_in_grad, ffn_out_grad, part_keep, part_send = (
        lax.optimization_barrier(
            (payload, input_grad, ffn_in_grad, ffn_out_grad, part_keep, part_send)
        )
    )
    payload = ring_gather(payload, "dp", ring_size)
    part = (part_keep.astype(F32) + swap(part_send, 1).astype(F32)).astype(BF16)
    layer_output = res_cols + part[0].astype(F32) + swap(part[1], 2).astype(F32)
    layer_output = layer_output.astype(BF16)
    proj_grad, out_grads, a_grad, b_grad, gate_grad, conv_grad, pers_grad, gains = unpack_call(
        payload, shift, width, mem_hid, taps, persist_kv.shape[2]
    )
    return (
        layer_output,
        input_grad,
        proj_grad,
        conv_grad,
        pers_grad,
        a_grad,
        jnp.transpose(b_grad, (0, 2, 1)),
        jnp.transpose(gate_grad, (2, 0, 1)),
        out_grads,
        ffn_in_grad,
        ffn_out_grad,
        gains,
    )


def solution(mesh):
    in_specs = (
        P("dp", None),
        P(None, None, "head"),
        P(None, None, "head"),
        P(None, "head", None, None),
        P("head", None, None),
        P("head", None, None),
        P(None, None, "head"),
        P(None, "head"),
        P(None, None, "head"),
        P("head", None),
        P(),
        P("dp"),
        P("dp", "head"),
    )
    out_specs = (
        P("dp", "head"),
        P("dp", "head"),
        P(None, None, "head"),
        P(None, None, "head"),
        P(None, "head", None, None),
        P("head", None, None),
        P("head", None, None),
        P(None, None, "head"),
        P(None, "head"),
        P(None, None, "head"),
        P("head", None),
        P(),
    )
    body = functools.partial(per_device, mesh.shape["dp"])
    return jax.shard_map(
        body, mesh=mesh, in_specs=in_specs, out_specs=out_specs, check_vma=False
    )
```

```python
import functools

import jax
import jax.numpy as jnp
from jax import lax
from jax.experimental import pallas as pl
from jax.experimental.pallas import tpu as pltpu
from jax.sharding import PartitionSpec as P

F32 = jnp.float32
BF16 = jnp.bfloat16
HIGH = lax.Precision.HIGHEST
NORM_EPS = 1e-05
UNIT_EPS = 1e-06
SCORE_SCALE = 8.0
SPAN = 512
HALO = 8
COST_UNIT = 1.5e8
SMALL_ROWS = 640


def dot_nn(left, right):
    return jnp.dot(left, right, preferred_element_type=F32)


def dot_nt(left, right, precision=None):
    return lax.dot_general(
        left, right, (((1,), (1,)), ((), ())), preferred_element_type=F32, precision=precision
    )


def iota(shape, axis):
    return lax.broadcasted_iota(jnp.int32, shape, axis)


def cost(microseconds):
    return pl.CostEstimate(
        flops=int(microseconds * COST_UNIT), transcendentals=0, bytes_accessed=1 << 20
    )


def head_blocks(cols, shift):
    same = (iota((cols, cols), 0) >> shift) == (iota((cols, cols), 1) >> shift)
    return jnp.where(same, 1.0, 0.0).astype(BF16)


def head_sum(value, blocks):
    return dot_nn(value.astype(BF16), blocks)


def valid_column(seq_ref, start, rows):
    inside = (start + iota((rows, 1), 0)) < seq_ref[0]
    valid = jnp.where(inside, 1.0, 0.0)
    return valid, jnp.maximum(jnp.sum(valid, 0, keepdims=True), 1.0)


def head_mask(cols, shift, head):
    return jnp.where((iota((1, cols), 1) >> shift) == head, 1.0, 0.0)


def gate_rows(logits, group, heads, head_size, width):
    parts = [
        jnp.broadcast_to(
            logits[0:1, group * heads + head : group * heads + head + 1], (head_size, width)
        )
        for head in range(heads)
    ]
    return jnp.concatenate(parts, 0)


def prep_kernel(
    shift,
    seq_ref,
    x_ref,
    w_ref,
    conv_ref,
    gain_ref,
    gate_ref,
    pers_ref,
    q_ref,
    k_ref,
    v_ref,
    kt_ref,
    pre_ref,
    gp_ref,
    nl_ref,
    mean_ref,
    lg_ref,
    pers_out_ref,
    flat_ref,
    ext_ref,
):
    step = pl.program_id(0)
    rows, cols = q_ref.shape
    blocks = head_blocks(cols, shift)

    @pl.when(step == 0)
    def _():
        ext_ref[:, 0:HALO, :] = jnp.zeros((3, HALO, cols), F32)
        keys = pers_ref[0]
        keys = keys * lax.rsqrt(head_sum(keys * keys, blocks) + UNIT_EPS)
        pers_out_ref[0] = keys.astype(BF16)
        pers_out_ref[1] = pers_ref[1].astype(BF16)
        heads = gate_ref.shape[1]
        for g in range(3):
            flat_ref[g * heads : (g + 1) * heads, :] = gate_ref[g]

    x = x_ref[...].astype(F32)
    scale = lax.rsqrt(jnp.mean(x * x, -1, keepdims=True) + NORM_EPS)
    normed = x * scale * gain_ref[0:1, :]
    low = normed.astype(BF16)
    nl_ref[...] = low
    inside = (step * rows + iota((8, rows), 1)) < seq_ref[0]
    valid = jnp.where(inside, 1.0, 0.0)
    count = jnp.maximum(jnp.sum(valid, 1, keepdims=True), 1.0)
    mean = dot_nn(valid.astype(BF16), low) / count
    mean_ref[...] = mean
    lg_ref[...] = dot_nt(mean, flat_ref[...], HIGH)
    gp_ref[...] = dot_nn(low, w_ref[3]).astype(BF16)
    for i in range(3):
        pre = dot_nn(low, w_ref[i])
        pre_ref[i] = pre.astype(BF16)
        ext_ref[i, HALO : HALO + rows, :] = pre
        conv = conv_ref[i, 0:1, :] * pre
        for j in range(1, conv_ref.shape[1]):
            conv = conv + conv_ref[i, j : j + 1, :] * ext_ref[i, HALO - j : HALO - j + rows, :]
        ext_ref[i, 0:HALO, :] = pre[rows - HALO :, :]
        act = conv * jax.nn.sigmoid(conv)
        if i < 2:
            act = act * lax.rsqrt(head_sum(act * act, blocks) + UNIT_EPS)
        act_low = act.astype(BF16)
        (q_ref, k_ref, v_ref)[i][...] = act_low
        if i == 1:
            kt_ref[...] = jnp.transpose(act_low.astype(F32)).astype(BF16)


def prep_call(seq, x, w, conv, gains, gate, pers, shift):
    gates = 3 * gate.shape[1]
    rows, width = x.shape
    cols = w.shape[2]
    nb = rows // SPAN
    whole = lambda a: pl.BlockSpec(a.shape, lambda c, n=a.ndim: (0,) * n)
    row_cols = pl.BlockSpec((SPAN, cols), lambda c: (c, 0))
    return pl.pallas_call(
        functools.partial(prep_kernel, shift),
        grid=(nb,),
        in_specs=[
            pl.BlockSpec(memory_space=pltpu.SMEM),
            pl.BlockSpec((SPAN, width), lambda c: (c, 0)),
            whole(w),
            whole(conv),
            whole(gains),
            whole(gate),
            whole(pers),
        ],
        out_specs=[
            row_cols,
            row_cols,
            row_cols,
            pl.BlockSpec((cols, SPAN), lambda c: (0, c)),
            pl.BlockSpec((3, SPAN, cols), lambda c: (0, c, 0)),
            row_cols,
            pl.BlockSpec((SPAN, width), lambda c: (c, 0)),
            pl.BlockSpec((8, width), lambda c: (c, 0)),
            pl.BlockSpec((8, gates), lambda c: (c, 0)),
            whole(pers),
            pl.BlockSpec((gates, width), lambda c: (0, 0)),
        ],
        out_shape=[
            jax.ShapeDtypeStruct((rows, cols), BF16),
            jax.ShapeDtypeStruct((rows, cols), BF16),
            jax.ShapeDtypeStruct((rows, cols), BF16),
            jax.ShapeDtypeStruct((cols, rows), BF16),
            jax.ShapeDtypeStruct((3, rows, cols), BF16),
            jax.ShapeDtypeStruct((rows, cols), BF16),
            jax.ShapeDtypeStruct((rows, width), BF16),
            jax.ShapeDtypeStruct((nb * 8, width), F32),
            jax.ShapeDtypeStruct((nb * 8, gates), F32),
            jax.ShapeDtypeStruct(pers.shape, BF16),
            jax.ShapeDtypeStruct((gates, width), F32),
        ],
        scratch_shapes=[pltpu.VMEM((3, HALO + SPAN, cols), F32)],
        cost_estimate=cost(15),
        name="prep",
    )(seq, x, w, conv, gains, gate, pers)


def mix_kernel(block, blocks_all, shift, first, last, *refs):
    it = iter(refs)
    seq_ref, lg_ref, q_ref, k_ref, v_ref, kt_ref, pers_ref, gp_ref, a_ref, bt_ref = (
        next(it) for _ in range(10)
    )
    sa_ref, sbt_ref = (None, None) if first or last else (next(it), next(it))
    mixed_ref, tot_out_ref, att_out_ref, lt_ref = (next(it) for _ in range(4))
    if not last:
        a2_ref, bt2_ref, sa2_ref, sbt2_ref, ga_ref, gbt_ref = (next(it) for _ in range(6))
    tot_ref, att_ref, linv_ref = (next(it) for _ in range(3))
    if not last:
        z_ref, r_ref = next(it), next(it)
    rows, cols = q_ref.shape
    head_size = 1 << shift
    heads = cols // head_size
    a_low = a_ref[...].astype(BF16)
    bt_low = bt_ref[...].astype(BF16)
    valid, count = valid_column(seq_ref, block * rows, rows)
    weight = valid / count
    att_ref[...] = jnp.zeros((rows, cols), F32)
    linv_ref[...] = jnp.zeros((rows, cols), F32)
    tot_ref[...] = jnp.zeros((rows, cols), F32)
    if not last:
        r_ref[...] = jnp.zeros((rows, cols), F32)

    def one_head(head, carry):
        mask = head_mask(cols, shift, head)
        mask_low = mask.astype(BF16)
        ones_low = (1.0 - mask).astype(BF16)
        query = q_ref[...] * mask_low
        scaled = query * SCORE_SCALE
        raised = jnp.exp(dot_nt(scaled, pers_ref[0])).astype(BF16)
        total = dot_nn(raised, pers_ref[1] * mask_low + ones_low)
        for j in range(block + 1):
            span = slice(j * rows, (j + 1) * rows)
            raised = jnp.exp(dot_nt(scaled, k_ref[span, :]))
            if j == block:
                raised = jnp.where(
                    iota((rows, rows), 0) >= iota((rows, rows), 1), raised, 0.0
                )
            total = total + dot_nn(raised.astype(BF16), v_ref[span, :] * mask_low + ones_low)
        inverse = 1.0 / pltpu.roll(total, head_size, 1)
        inside = jnp.broadcast_to(mask, (rows, cols)) > 0.5
        linv_ref[...] = jnp.where(inside, inverse, linv_ref[...])
        attended = jnp.where(inside, total * inverse, 0.0)
        att_ref[...] = att_ref[...] + attended
        hid = dot_nn(query, a_low)
        hid = hid * jax.nn.sigmoid(hid)
        recalled = dot_nt(hid.astype(BF16), bt_low) * mask
        tot_ref[...] = tot_ref[...] + attended + recalled
        if not last:
            hid = dot_nn(k_ref[block * rows : (block + 1) * rows, :] * mask_low, a_low)
            sig = jax.nn.sigmoid(hid)
            act = (hid * sig).astype(BF16)
            z_ref[head] = act
            target = v_ref[block * rows : (block + 1) * rows, :].astype(F32)
            resid = (dot_nt(act, bt_low) - target) * mask * weight
            r_ref[...] = r_ref[...] + resid
            d_hid = dot_nn(resid.astype(BF16), bt_low) * (sig * (1.0 + hid * (1.0 - sig)))
            at = pl.ds(pl.multiple_of(head * head_size, head_size), head_size)
            ga_ref[at, :] = dot_nn(kt_ref[at, :], d_hid.astype(BF16))
        return carry

    lax.fori_loop(0, heads, one_head, 0)
    gate = jax.nn.sigmoid(gp_ref[...].astype(F32))
    mixed_ref[...] = (tot_ref[...] * gate).astype(BF16)
    tot_out_ref[...] = tot_ref[...].astype(BF16)
    att_out_ref[...] = att_ref[...].astype(BF16)
    start = iota((8, cols), 1) == (iota((8, cols), 0) << shift)
    lt_ref[...] = dot_nt(jnp.where(start, 1.0, 0.0), linv_ref[...], HIGH)
    if not last:
        resid_t = jnp.transpose(r_ref[...]).astype(BF16)
        for head in range(heads):
            at = slice(head * head_size, (head + 1) * head_size)
            gbt_ref[at, :] = dot_nn(resid_t[at, :], z_ref[head])
        width = a_ref.shape[1]
        logits = lg_ref[...]
        step = 0.2 * jax.nn.sigmoid(gate_rows(logits, 0, heads, head_size, width))
        keep = jax.nn.sigmoid(gate_rows(logits, 1, heads, head_size, width))
        stay = 1.0 - 0.5 * jax.nn.sigmoid(gate_rows(logits, 2, heads, head_size, width))
        moment_a = -step * ga_ref[...]
        moment_b = -step * gbt_ref[...]
        if not first:
            moment_a = moment_a + keep * sa_ref[...]
            moment_b = moment_b + keep * sbt_ref[...]
        sa2_ref[...] = moment_a
        sbt2_ref[...] = moment_b
        a2_ref[...] = stay * a_ref[...] + moment_a
        bt2_ref[...] = stay * bt_ref[...] + moment_b


def mix_call(block, nb, shift, seq, lg, q, k, v, kt, pers, gp, a, bt, sa, sbt):
    rows, cols = q.shape
    first, last = block == 0, block == nb - 1
    heads = cols >> shift
    whole = lambda s: pl.BlockSpec(s, lambda i, n=len(s): (0,) * n)
    at_block = pl.BlockSpec((SPAN, cols), lambda i: (block, 0))
    upto = pl.BlockSpec(((block + 1) * SPAN, cols), lambda i: (0, 0))
    state = whole(a.shape)
    ins = [seq, lg, q, k, v, kt, pers, gp, a, bt]
    in_specs = [
        pl.BlockSpec(memory_space=pltpu.SMEM),
        pl.BlockSpec((8, lg.shape[1]), lambda i: (block, 0)),
        at_block,
        upto,
        upto,
        pl.BlockSpec((cols, SPAN), lambda i: (0, block)),
        whole(pers.shape),
        at_block,
        state,
        state,
    ]
    if not (first or last):
        ins += [sa, sbt]
        in_specs += [state, state]
    row_spec = whole((SPAN, cols))
    outs = [jax.ShapeDtypeStruct((SPAN, cols), BF16)] * 3
    outs.append(jax.ShapeDtypeStruct((8, SPAN), F32))
    out_specs = [row_spec] * 3 + [whole((8, SPAN))]
    scratch = [pltpu.VMEM((SPAN, cols), F32)] * 3
    if not last:
        outs += [jax.ShapeDtypeStruct(a.shape, F32)] * 6
        out_specs += [state] * 6
        scratch += [pltpu.VMEM((heads, SPAN, a.shape[1]), BF16), pltpu.VMEM((SPAN, cols), F32)]
    return pl.pallas_call(
        functools.partial(mix_kernel, block, nb, shift, first, last),
        grid=(1,),
        in_specs=in_specs,
        out_specs=out_specs,
        out_shape=outs,
        scratch_shapes=scratch,
        cost_estimate=cost(9),
        name=f"mix_{block}",
    )(*ins)


def ffn_kernel(nb, low, first_call, *refs):
    it = iter(refs)
    take = lambda n: [next(it) for _ in range(n)]
    peer_ref, x_ref = take(2)
    piece_refs = [take(4) for _ in range(nb)]
    (gain_ref,) = take(1)
    weights = take(6)
    cot_refs = take(4)
    if not first_call:
        take(6)
    nt_out, hid_ref, dgu_ref, cotf_out, mfull_out, res_out = take(6)
    if first_call:
        take(1)
    held = take(6)
    nt_ref, cotf_ref, mfull_ref, res_ref = take(4)
    weight_sems, out_sems = take(2)
    step = pl.program_id(0)
    rows, cols = cot_refs[0].shape
    loads = [
        pltpu.make_async_copy(source, target, weight_sems.at[n])
        for n, (source, target) in enumerate(zip(weights, held))
    ]
    fin_ref, fout_ref, ow_refs = held[5], held[4], held[:4]
    mine = pl.ds(pl.multiple_of((low + step) * rows, rows), rows)
    stores = [
        pltpu.make_async_copy(source, target.at[mine, :], out_sems.at[n])
        for n, (source, target) in enumerate(
            ((mfull_ref, mfull_out), (cotf_ref, cotf_out), (res_ref, res_out), (nt_ref, nt_out))
        )
    ]

    @pl.when(step == 0)
    def _():
        for load in loads:
            load.start()

    def ready(some):
        @pl.when(step == 0)
        def _():
            for load in some:
                load.wait()

    if nb > 1:

        @pl.when(step > 0)
        def _():
            for store in stores:
                store.wait()

    spots = [pl.ds(pl.multiple_of(peer_ref[j] * cols, cols), cols) for j in range(4)]
    for j in range(4):
        cotf_ref[:, spots[j]] = cot_refs[j][...]
    for block in range(nb):

        @pl.when(step == block)
        def _(block=block):
            for j in range(4):
                mfull_ref[:, spots[j]] = piece_refs[block][j][...]

    stores[0].start()
    stores[1].start()
    ready(loads[:4])
    mixed = mfull_ref[...]
    for j in range(4):
        branch = dot_nn(mixed, ow_refs[j][...])
        res_ref[:, spots[j]] = x_ref[:, spots[j]].astype(F32) + branch
    stores[2].start()
    residual = res_ref[...]
    scale = lax.rsqrt(jnp.mean(residual * residual, -1, keepdims=True) + NORM_EPS)
    low_rows = (residual * scale * gain_ref[1:2, :]).astype(BF16)
    nt_ref[...] = low_rows
    stores[3].start()
    ready(loads[4:])
    d_hidden = dot_nt(cotf_ref[...], fout_ref[...])
    gate_pre = dot_nn(low_rows, fin_ref[0])
    up_pre = dot_nn(low_rows, fin_ref[1])
    sig = jax.nn.sigmoid(gate_pre)
    silu = gate_pre * sig
    hid_ref[...] = (silu * up_pre).astype(BF16)
    slope = sig * (1.0 + gate_pre * (1.0 - sig))
    dgu_ref[0] = (d_hidden * up_pre * slope).astype(BF16)
    dgu_ref[1] = (d_hidden * silu).astype(BF16)

    @pl.when(step == nb - 1)
    def _():
        for store in stores:
            store.wait()


def ffn_call(blocks, peers, x, pieces, ow, gains, fin, fout, cot, shared):
    rows, width = x.shape
    cols = pieces[0][0].shape[1]
    nb = len(blocks)
    low = blocks[0]
    hidden = fout.shape[0]
    once = pl.Buffered(1)
    whole = lambda a: pl.BlockSpec(a.shape, lambda i, n=a.ndim: (0,) * n, pipeline_mode=once)
    at_rows = lambda n: pl.BlockSpec((SPAN, n), lambda i: (low + i, 0))
    anywhere = pl.BlockSpec(memory_space=pl.ANY)
    struct = jax.ShapeDtypeStruct
    ins = [peers, x, *[piece for block in pieces for piece in block], gains]
    ins += [*ow, fout, fin, *cot]
    in_specs = [pl.BlockSpec(memory_space=pltpu.SMEM), at_rows(width)]
    in_specs += [whole(piece) for block in pieces for piece in block]
    in_specs += [whole(gains)] + [anywhere] * 6 + [at_rows(cols)] * 4
    spare = [] if shared else [struct((3 * width, width), BF16)]
    aliases = {}
    if shared:
        aliases = {len(ins) + n: n for n in range(len(shared))}
        ins += shared
        in_specs += [anywhere] * len(shared)
    got = pl.pallas_call(
        functools.partial(ffn_kernel, nb, low, not shared),
        grid=(nb,),
        in_specs=in_specs,
        out_specs=[
            anywhere,
            at_rows(hidden),
            pl.BlockSpec((2, SPAN, hidden), lambda i: (0, low + i, 0)),
            anywhere,
            anywhere,
            anywhere,
        ]
        + [anywhere] * len(spare),
        out_shape=[
            struct((rows, width), BF16),
            struct((rows, hidden), BF16),
            struct((2, rows, hidden), BF16),
            struct((rows, width), BF16),
            struct((rows, width), BF16),
            struct((rows, width), F32),
        ]
        + spare,
        input_output_aliases=aliases,
        scratch_shapes=[pltpu.VMEM(piece.shape, BF16) for piece in (*ow, fout, fin)]
        + [pltpu.VMEM((SPAN, width), BF16)] * 3
        + [pltpu.VMEM((SPAN, width), F32)]
        + [pltpu.SemaphoreType.DMA((6,)), pltpu.SemaphoreType.DMA((4,))],
        cost_estimate=cost(8 * nb),
        name=f"ffn_{low}",
    )(*ins)
    return got[:6], got[6:]


def ffn_back_kernel(first_call, *refs):
    it = iter(refs)
    take = lambda n: [next(it) for _ in range(n)]
    peer_ref, dgu_ref, fin_ref, res_ref = take(4)
    gg_in_ref = None if first_call else take(1)[0]
    gg_ref, keep_ref, send_ref, part_ref = take(4)
    width = res_ref.shape[1]
    residual = res_ref[...]
    scale = lax.rsqrt(jnp.mean(residual * residual, -1, keepdims=True) + NORM_EPS)
    d_normed = dot_nt(dgu_ref[0], fin_ref[0]) + dot_nt(dgu_ref[1], fin_ref[1])
    gains = jnp.sum(d_normed * residual * scale, 0, keepdims=True)

    @pl.when(pl.program_id(0) == 0)
    def _():
        gg_ref[...] = jnp.zeros(gg_ref.shape, F32) if first_call else gg_in_ref[...]

    gg_ref[...] = gg_ref[...] + jnp.broadcast_to(gains, gg_ref.shape)
    half = width // 2
    part_ref[...] = d_normed.astype(BF16)
    core = peer_ref[0] & 1
    keep_ref[...] = part_ref[:, pl.ds(pl.multiple_of(core * half, half), half)]
    send_ref[...] = part_ref[:, pl.ds(pl.multiple_of((1 - core) * half, half), half)]


def ffn_back_call(blocks, peers, dgu, fin, res, gains):
    width = res.shape[1]
    tile = SPAN // 2
    steps = SPAN // tile
    low = blocks[0] * steps
    lines = len(blocks) * SPAN
    gain_spec = pl.BlockSpec((8, width), lambda i: (0, 0))
    row = pl.BlockSpec((tile, width // 2), lambda i: (i, 0))
    struct = jax.ShapeDtypeStruct
    return pl.pallas_call(
        functools.partial(ffn_back_kernel, gains is None),
        grid=(len(blocks) * steps,),
        in_specs=[
            pl.BlockSpec(memory_space=pltpu.SMEM),
            pl.BlockSpec((2, tile, dgu.shape[2]), lambda i: (0, low + i, 0)),
            pl.BlockSpec(fin.shape, lambda i: (0, 0, 0), pipeline_mode=pl.Buffered(1)),
            pl.BlockSpec((tile, width), lambda i: (low + i, 0)),
        ]
        + ([] if gains is None else [gain_spec]),
        out_specs=[gain_spec, row, row],
        out_shape=[
            struct((8, width), F32),
            struct((lines, width // 2), BF16),
            struct((lines, width // 2), BF16),
        ],
        scratch_shapes=[pltpu.VMEM((tile, width), BF16)],
        cost_estimate=cost(4 * len(blocks)),
        name=f"ffn_back_{blocks[0]}",
    )(peers, dgu, fin, res, *([] if gains is None else [gains]))


def down_kernel(peer_ref, hid_ref, fout_ref, keep_ref, send_ref, part_ref):
    cols = keep_ref.shape[2]
    part_ref[...] = dot_nn(hid_ref[...], fout_ref[...]).astype(BF16)
    for slot, out_ref in ((0, keep_ref), (1, send_ref)):
        for n in range(2):
            start = pl.multiple_of(peer_ref[slot + 2 * n] * cols, cols)
            out_ref[n] = part_ref[:, pl.ds(start, cols)]


def down_call(peers, hid, fout, cols):
    rows, hidden = hid.shape
    width = fout.shape[1]
    stacked = pl.BlockSpec((2, SPAN, cols), lambda i: (0, i, 0))
    return pl.pallas_call(
        down_kernel,
        grid=(rows // SPAN,),
        in_specs=[
            pl.BlockSpec(memory_space=pltpu.SMEM),
            pl.BlockSpec((SPAN, hidden), lambda i: (i, 0)),
            pl.BlockSpec(fout.shape, lambda i: (0, 0), pipeline_mode=pl.Buffered(1)),
        ],
        out_specs=[stacked, stacked],
        out_shape=[jax.ShapeDtypeStruct((2, rows, cols), BF16)] * 2,
        scratch_shapes=[pltpu.VMEM((SPAN, width), BF16)],
        cost_estimate=cost(6),
        name="down",
    )(peers, hid, fout)


def turn_kernel(blocks, steps, first_call, *refs):
    it = iter(refs)
    take = lambda n: [next(it) for _ in range(n)]
    peer_ref, s1_ref, r2_ref, ps1_ref, pr2_ref, res_ref, cot_ref = take(7)
    gain_ref, gp_ref = take(2)
    ow_refs = take(4)
    tot_refs = take(blocks)
    if not first_call:
        take(4)
    dres_ref, rescol_ref, dbr_ref, dgall_ref, dga_ref, dgp_ref, full_ref = take(7)
    rows, width = res_ref.shape
    cols = gp_ref.shape[1]
    half = width // 2
    core = peer_ref[0] & 1
    at_own = pl.ds(pl.multiple_of(core * half, half), half)
    at_other = pl.ds(pl.multiple_of((1 - core) * half, half), half)
    full_ref[:, at_own] = s1_ref[...].astype(F32) + r2_ref[...].astype(F32)
    full_ref[:, at_other] = ps1_ref[...].astype(F32) + pr2_ref[...].astype(F32)
    residual = res_ref[...]
    scale = lax.rsqrt(jnp.mean(residual * residual, -1, keepdims=True) + NORM_EPS)
    gained = full_ref[...] * gain_ref[1:2, :]
    inner = jnp.sum(gained * residual, -1, keepdims=True) / width
    d_residual = cot_ref[...].astype(F32) + scale * gained - residual * (scale * scale * scale * inner)
    own = pl.ds(pl.multiple_of(peer_ref[0] * cols, cols), cols)
    full_ref[...] = d_residual
    d_mixed = None
    for j in range(4):
        at = pl.ds(pl.multiple_of(peer_ref[j] * cols, cols), cols)
        term = dot_nt(full_ref[:, at].astype(BF16), ow_refs[j][own, :])
        d_mixed = term if d_mixed is None else d_mixed + term
    mine = full_ref[:, own]
    dres_ref[...] = mine
    dbr_ref[...] = mine.astype(BF16)
    rescol_ref[...] = res_ref[:, own]
    gate = jax.nn.sigmoid(gp_ref[...].astype(F32))
    d_gated = d_mixed * gate
    dga_ref[...] = d_gated.astype(BF16)
    total = tot_refs[0][...]
    for n in range(1, blocks):
        total = jnp.where(pl.program_id(0) >= n * steps, tot_refs[n][...], total)
    d_gate = (d_gated * total.astype(F32) * (1.0 - gate)).astype(BF16)
    dgp_ref[...] = d_gate
    dgall_ref[...] = d_gate


def turn_call(blocks, peers, pieces, res, cot, ow, gains, gp, tots, shared):
    rows, cols = gp.shape
    width = res.shape[1]
    tile = SPAN // 2
    steps = SPAN // tile
    low = blocks[0] * steps
    count = len(blocks) * steps
    whole = lambda a: pl.BlockSpec(a.shape, lambda i, n=a.ndim: (0,) * n)
    row = lambda n: pl.BlockSpec((tile, n), lambda i: (i, 0))
    at_rows = lambda n: pl.BlockSpec((tile, n), lambda i: (low + i, 0))
    struct = jax.ShapeDtypeStruct
    ins = [peers, *pieces, res, cot, gains, gp, *ow, *tots]
    in_specs = [
        pl.BlockSpec(memory_space=pltpu.SMEM),
        row(width // 2),
        row(width // 2),
        row(width // 2),
        row(width // 2),
        at_rows(width),
        at_rows(width),
        whole(gains),
        at_rows(cols),
    ] + [pl.BlockSpec((width, cols), lambda i: (0, 0))] * 4
    for n in range(len(blocks)):
        spot = lambda i, n=n: (jnp.clip(i - n * steps, 0, steps - 1), 0)
        in_specs.append(pl.BlockSpec((tile, cols), spot))
    aliases = {}
    if shared is not None:
        aliases = {len(ins) + n: n for n in range(len(shared))}
        ins += shared
        in_specs += [pl.BlockSpec(memory_space=pl.ANY)] * len(shared)
    got = pl.pallas_call(
        functools.partial(turn_kernel, len(blocks), steps, shared is None),
        grid=(count,),
        in_specs=in_specs,
        out_specs=[at_rows(cols)] * 4 + [row(cols)] * 2,
        out_shape=[
            struct((rows, cols), F32),
            struct((rows, cols), F32),
            struct((rows, cols), BF16),
            struct((rows, cols), BF16),
            struct((len(blocks) * SPAN, cols), BF16),
            struct((len(blocks) * SPAN, cols), BF16),
        ],
        input_output_aliases=aliases,
        scratch_shapes=[pltpu.VMEM((tile, width), F32)],
        cost_estimate=cost(5 * len(blocks)),
        name=f"turn_{blocks[0]}",
    )(*ins)
    return got[:4], got[4:]


def back_kernel(block, nb, shift, *refs):
    it = iter(refs)
    take = lambda n: [next(it) for _ in range(n)]
    first, last = block == 0, block == nb - 1
    seq_ref, q_ref, k_ref, v_ref, kt_ref, pers_ref, dga_ref, att_ref, lt_ref = take(9)
    a_ref, bt_ref = take(2)
    if not last:
        dk_in_ref, dv_in_ref, dp_in_ref, lg_ref, ga_ref, gbt_ref, ab_in_ref, btb_in_ref = take(8)
        sab_in_ref, sbtb_in_ref = take(2) if block < nb - 2 else (None, None)
        sa_ref, sbt_ref = (None, None) if first else take(2)
    dq_ref, dk_ref, dv_ref, dp_ref, ab_ref, btb_ref = take(6)
    if not last:
        (dlg_ref,) = take(1)
        sab_ref, sbtb_ref = (None, None) if first else take(2)
    dt_ref, dqt_ref, qt_ref, dot_ref = take(4)
    if not last:
        z_ref, zd_ref, r_ref, y_ref, h_ref = take(5)
    rows, cols = q_ref.shape
    head_size = 1 << shift
    heads = cols // head_size
    own = slice(block * rows, (block + 1) * rows)
    a_low = a_ref[...].astype(BF16)
    bt_low = bt_ref[...].astype(BF16)
    if last:
        dk_ref[...] = jnp.zeros(dk_ref.shape, F32)
        dv_ref[...] = jnp.zeros(dv_ref.shape, F32)
        dp_ref[...] = jnp.zeros(dp_ref.shape, F32)
        ab_ref[...] = jnp.zeros(ab_ref.shape, F32)
        btb_ref[...] = jnp.zeros(btb_ref.shape, F32)
    else:
        dk_ref[...] = dk_in_ref[...]
        dv_ref[...] = dv_in_ref[...]
        dp_ref[...] = dp_in_ref[...]
    pick = (iota((8, cols), 1) >> shift) == iota((8, cols), 0)
    d_gated = dga_ref[...].astype(F32)
    dt_ref[...] = dot_nt(jnp.where(pick, 1.0, 0.0), d_gated * att_ref[...].astype(F32), HIGH)
    dq_ref[...] = jnp.zeros((rows, cols), F32)
    qt_ref[...] = jnp.transpose(q_ref[...].astype(F32)).astype(BF16)
    dot_ref[...] = jnp.transpose(d_gated).astype(BF16)
    if not last:
        valid, count = valid_column(seq_ref, block * rows, rows)
        weight = valid / count
        width = a_ref.shape[1]
        logits = lg_ref[...]
        sig_step = jax.nn.sigmoid(gate_rows(logits, 0, heads, head_size, width))
        keep = jax.nn.sigmoid(gate_rows(logits, 1, heads, head_size, width))
        sig_forget = jax.nn.sigmoid(gate_rows(logits, 2, heads, head_size, width))
        tot_a, tot_b = ab_in_ref[...], btb_in_ref[...]
        if sab_in_ref is not None:
            tot_a, tot_b = tot_a + sab_in_ref[...], tot_b + sbtb_in_ref[...]
        h_ref[0] = (-0.2 * sig_step * tot_a).astype(BF16)
        h_ref[1] = (-0.2 * sig_step * tot_b).astype(BF16)
        d_step = -(ga_ref[...] * tot_a + gbt_ref[...] * tot_b)
        groups = [d_step * (0.2 * sig_step * (1.0 - sig_step)), None, None]
        if not first:
            groups[1] = (sa_ref[...] * tot_a + sbt_ref[...] * tot_b) * (keep * (1.0 - keep))
        d_forget = -(a_ref[...] * ab_in_ref[...] + bt_ref[...] * btb_in_ref[...])
        groups[2] = d_forget * (0.5 * sig_forget * (1.0 - sig_forget))
        d_logits = jnp.zeros(dlg_ref.shape, F32)
        for g, value in enumerate(groups):
            if value is None:
                continue
            for head in range(heads):
                part = value[head * head_size : (head + 1) * head_size, :]
                figure = jnp.sum(jnp.sum(part, 1, keepdims=True), 0, keepdims=True)
                here = iota(dlg_ref.shape, 1) == g * heads + head
                d_logits = d_logits + jnp.where(here, 1.0, 0.0) * figure
        dlg_ref[...] = d_logits
        stay = 1.0 - 0.5 * sig_forget
        ab_ref[...] = stay * ab_in_ref[...]
        btb_ref[...] = stay * btb_in_ref[...]
        if not first:
            sab_ref[...] = keep * tot_a
            sbtb_ref[...] = keep * tot_b
        r_ref[...] = jnp.zeros((rows, cols), F32)
        y_ref[...] = jnp.zeros((rows, cols), F32)

    def one_head(head, carry):
        mask = head_mask(cols, shift, head)
        mask_low = mask.astype(BF16)
        query = q_ref[...] * mask_low
        scaled = query * SCORE_SCALE
        d_out = dga_ref[...] * mask_low
        at = pl.ds(pl.multiple_of(head * head_size, head_size), head_size)
        inverse = lt_ref[pl.ds(head, 1), :]
        delta = dt_ref[pl.ds(head, 1), :]
        probs = jnp.exp(dot_nt(pers_ref[0], scaled)) * inverse
        d_scores = (probs * (dot_nt(pers_ref[1], d_out) - delta)).astype(BF16)
        dp_ref[0] = dp_ref[0] + dot_nn(d_scores, scaled)
        dp_ref[1] = dp_ref[1] + dot_nn(probs.astype(BF16), d_out)
        d_query = lax.dot_general(
            d_scores, pers_ref[0], (((0,), (0,)), ((), ())), preferred_element_type=F32
        )
        d_query = d_query * SCORE_SCALE
        d_query_t = jnp.zeros((head_size, rows), F32)
        for j in range(block + 1):
            span = slice(j * rows, (j + 1) * rows)
            probs = jnp.exp(dot_nt(k_ref[span, :], scaled)) * inverse
            if j == block:
                probs = jnp.where(iota((rows, rows), 0) <= iota((rows, rows), 1), probs, 0.0)
            d_scores = (probs * (dot_nt(v_ref[span, :], d_out) - delta)).astype(BF16)
            dv_ref[span, :] = dv_ref[span, :] + dot_nn(probs.astype(BF16), d_out)
            dk_ref[span, :] = dk_ref[span, :] + dot_nn(d_scores, scaled)
            d_query_t = d_query_t + dot_nn(kt_ref[at, span], d_scores)
        dqt_ref[at, :] = d_query_t * SCORE_SCALE
        hid = dot_nn(query, a_low)
        sig = jax.nn.sigmoid(hid)
        d_hid = dot_nn(d_out, bt_low) * (sig * (1.0 + hid * (1.0 - sig)))
        d_hid = d_hid.astype(BF16)
        dq_ref[...] = dq_ref[...] + (d_query + dot_nt(d_hid, a_low)) * mask
        grad_a = dot_nn(qt_ref[at, :], d_hid)
        grad_b = dot_nn(dot_ref[at, :], (hid * sig).astype(BF16))
        if not last:
            key = k_ref[own, :] * mask_low
            hid = dot_nn(key, a_low)
            probe = dot_nn(key, h_ref[0])
            sig = jax.nn.sigmoid(hid)
            act = (hid * sig).astype(BF16)
            z_ref[head] = act
            slope = sig * (1.0 + hid * (1.0 - sig))
            curve = sig * (1.0 - sig) * (2.0 + hid * (1.0 - 2.0 * sig))
            target = v_ref[own, :].astype(F32)
            resid = (dot_nt(act, bt_low) - target) * mask * weight
            r_ref[...] = r_ref[...] + resid
            resid = resid.astype(BF16)
            d_act = dot_nn(resid, bt_low)
            d_slope = (probe * slope).astype(BF16)
            zd_ref[head] = d_slope
            d_net = (dot_nt(act, h_ref[1]) + dot_nt(d_slope, bt_low)) * mask * weight
            y_ref[...] = y_ref[...] + d_net
            back = dot_nn(resid, h_ref[1]) + dot_nn(d_net.astype(BF16), bt_low)
            d_hid = (probe * d_act * curve + back * slope).astype(BF16)
            direct = (d_act * slope).astype(BF16)
            d_key = (dot_nt(direct, h_ref[0]) + dot_nt(d_hid, a_low)) * mask
            dk_ref[own, :] = dk_ref[own, :] + d_key
            grad_a = grad_a + dot_nn(kt_ref[at, own], d_hid)
        ab_ref[at, :] = ab_ref[at, :] + grad_a
        btb_ref[at, :] = btb_ref[at, :] + grad_b
        return carry

    lax.fori_loop(0, heads, one_head, 0)
    dq_ref[...] = dq_ref[...] + jnp.transpose(dqt_ref[...])
    if not last:
        dv_ref[own, :] = dv_ref[own, :] - y_ref[...]
        resid_t = jnp.transpose(r_ref[...]).astype(BF16)
        net_t = jnp.transpose(y_ref[...]).astype(BF16)
        for head in range(heads):
            at = slice(head * head_size, (head + 1) * head_size)
            grad_b = dot_nn(resid_t[at, :], zd_ref[head]) + dot_nn(net_t[at, :], z_ref[head])
            btb_ref[at, :] = btb_ref[at, :] + grad_b


def back_call(block, nb, shift, seq, q, k, v, kt, pers, dga, att, linv, state, grads, adjoint):
    dga, spot = dga
    cols = q.shape[1]
    heads = cols >> shift
    first, last = block == 0, block == nb - 1
    done = (block + 1) * SPAN
    whole = lambda s: pl.BlockSpec(s, lambda i, n=len(s): (0,) * n)
    at_block = pl.BlockSpec((SPAN, cols), lambda i: (block, 0))
    upto = pl.BlockSpec((done, cols), lambda i: (0, 0))
    rows_spec = whole((SPAN, cols))
    square = state["a"].shape
    ins = [seq, q, k, v, kt, pers, dga, att, linv, state["a"], state["bt"]]
    in_specs = [
        pl.BlockSpec(memory_space=pltpu.SMEM),
        at_block,
        upto,
        upto,
        pl.BlockSpec((cols, done), lambda i: (0, 0)),
        whole(pers.shape),
        pl.BlockSpec((SPAN, cols), lambda i: (spot, 0)),
        rows_spec,
        whole((8, SPAN)),
        whole(square),
        whole(square),
    ]
    if not last:
        ins += [grads["dk"], grads["dv"], grads["dp"], state["lg"], state["ga"], state["gbt"]]
        ins += [adjoint["ab"], adjoint["btb"]]
        in_specs += [upto, upto, whole(pers.shape)]
        in_specs += [pl.BlockSpec((8, state["lg"].shape[1]), lambda i: (block, 0))]
        in_specs += [whole(square)] * 4
        if block < nb - 2:
            ins += [adjoint["sab"], adjoint["sbtb"]]
            in_specs += [whole(square)] * 2
        if not first:
            ins += [state["sa"], state["sbt"]]
            in_specs += [whole(square)] * 2
    names = ["dq", "dk", "dv", "dp", "ab", "btb"]
    shapes = [(SPAN, cols), (done, cols), (done, cols), pers.shape, square, square]
    if not last:
        names.append("dlg")
        shapes.append((8, state["lg"].shape[1]))
        if not first:
            names += ["sab", "sbtb"]
            shapes += [square, square]
    scratch = [
        pltpu.VMEM((8, SPAN), F32),
        pltpu.VMEM((cols, SPAN), F32),
        pltpu.VMEM((cols, SPAN), BF16),
        pltpu.VMEM((cols, SPAN), BF16),
    ]
    if not last:
        scratch += [
            pltpu.VMEM((heads, SPAN, square[1]), BF16),
            pltpu.VMEM((heads, SPAN, square[1]), BF16),
            pltpu.VMEM((SPAN, cols), F32),
            pltpu.VMEM((SPAN, cols), F32),
            pltpu.VMEM((2,) + square, BF16),
        ]
    outs = pl.pallas_call(
        functools.partial(back_kernel, block, nb, shift),
        grid=(1,),
        in_specs=in_specs,
        out_specs=[whole(s) for s in shapes],
        out_shape=[jax.ShapeDtypeStruct(s, F32) for s in shapes],
        scratch_shapes=scratch,
        cost_estimate=cost(17),
        name=f"back_{block}",
    )(*ins)
    return dict(zip(names, outs))


def unprep_kernel(block, nb, shift, *refs):
    it = iter(refs)
    take = lambda n: [next(it) for _ in range(n)]
    first, last = block == 0, block == nb - 1
    seq_ref, peer_ref, dq_ref, dk_ref, dv_ref, dgp_ref, pre_ref, w_ref, conv_ref = take(9)
    x_ref, gain_ref = take(2)
    halo_ref = None if first else take(1)[0]
    dp_ref, pers_ref, ab_ref, btb_ref, gain_two_ref = take(5) if first else [None] * 5
    if not last:
        edge_in_ref, dlg_ref, gate_ref, mean_ref = take(4)
        cg_in_ref, gg_in_ref, gate_in_ref = take(7)[:3]
    cg_ref, gg_ref, gate_out_ref = take(3)
    dproj_ref, keep_ref, send_ref, inner_ref, edge_ref = take(5)
    small_ref, gains_ref = take(2) if first else (None, None)
    ext_ref, dext_ref, low_ref = take(3)
    rows, cols = dq_ref.shape
    width = x_ref.shape[1]
    blocks = head_blocks(cols, shift)
    taps = conv_ref.shape[1]
    d_normed = dot_nt(dgp_ref[...], w_ref[3])
    dproj_ref[3] = dgp_ref[...]
    if last:
        cg_ref[...] = jnp.zeros(cg_ref.shape, F32)
        gg_ref[...] = jnp.zeros(gg_ref.shape, F32)
        gate_out_ref[...] = jnp.zeros(gate_out_ref.shape, F32)
    else:
        cg_ref[...] = cg_in_ref[...]
        gg_ref[...] = gg_in_ref[...]
    for i in range(3):
        pre = pre_ref[i].astype(F32)
        ext_ref[0:HALO, :] = jnp.zeros((HALO, cols), F32) if first else halo_ref[i, HALO:, :].astype(F32)
        ext_ref[HALO : HALO + rows, :] = pre
        shifted = [pre] + [ext_ref[HALO - j : HALO - j + rows, :] for j in range(1, taps)]
        conv = conv_ref[i, 0:1, :] * pre
        for j in range(1, taps):
            conv = conv + conv_ref[i, j : j + 1, :] * shifted[j]
        sig = jax.nn.sigmoid(conv)
        d_act = (dq_ref, dk_ref, dv_ref)[i][...]
        if i < 2:
            act = conv * sig
            scale = lax.rsqrt(head_sum(act * act, blocks) + UNIT_EPS)
            d_act = scale * (d_act - act * (scale * scale * head_sum(d_act * act, blocks)))
        d_conv = d_act * (sig * (1.0 + conv * (1.0 - sig)))
        edge_ref[i] = d_conv[0:HALO, :]
        dext_ref[0:rows, :] = d_conv
        dext_ref[rows : rows + HALO, :] = (
            jnp.zeros((HALO, cols), F32) if last else edge_in_ref[i]
        )
        d_pre = conv_ref[i, 0:1, :] * d_conv
        for j in range(taps):
            if j:
                d_pre = d_pre + conv_ref[i, j : j + 1, :] * dext_ref[j : j + rows, :]
            at = slice(i * taps + j, i * taps + j + 1)
            cg_ref[at, :] = cg_ref[at, :] + jnp.sum(d_conv * shifted[j], 0, keepdims=True)
        d_low = d_pre.astype(BF16)
        dproj_ref[i] = d_low
        d_normed = d_normed + dot_nt(d_low, w_ref[i])
    if not last:
        valid, count = valid_column(seq_ref, block * rows, rows)
        d_mean = jnp.dot(
            dlg_ref[...], gate_ref[...], preferred_element_type=F32, precision=HIGH
        )
        d_normed = d_normed + (valid / count) * d_mean[0:1, :]
        outer = lax.dot_general(
            dlg_ref[...] * 0.125,
            mean_ref[...],
            (((0,), (0,)), ((), ())),
            preferred_element_type=F32,
            precision=HIGH,
        )
        gate_out_ref[...] = gate_in_ref[...]
        at = slice(0, outer.shape[0])
        gate_out_ref[at, :] = gate_in_ref[at, :] + outer
    x = x_ref[...].astype(F32)
    scale = lax.rsqrt(jnp.mean(x * x, -1, keepdims=True) + NORM_EPS)
    weighted = d_normed * x
    gains = jnp.sum(weighted * scale, 0, keepdims=True)
    gg_ref[...] = gg_ref[...] + jnp.broadcast_to(gains, gg_ref.shape)
    gained = jnp.broadcast_to(gain_ref[0:1, :], (8, width))
    inner_ref[...] = dot_nt(gained.astype(BF16), weighted.astype(BF16))
    low_ref[...] = d_normed.astype(BF16)
    for slot, out_ref in ((0, keep_ref), (1, send_ref)):
        for n in range(2):
            start = pl.multiple_of(peer_ref[slot + 2 * n] * cols, cols)
            out_ref[n] = low_ref[:, pl.ds(start, cols)]
    if first:
        keys = pers_ref[0]
        d_keys = dp_ref[0]
        scale = lax.rsqrt(head_sum(keys * keys, blocks) + UNIT_EPS)
        along = head_sum(d_keys * keys, blocks)
        d_keys = scale * (d_keys - keys * (scale * scale * along))
        across = lambda a: [a[:, n : n + cols] for n in range(0, width, cols)]
        parts = [ab_ref[...], btb_ref[...], *across(gate_out_ref[...]), cg_ref[...]]
        parts += [d_keys, dp_ref[1]]
        at = 0
        for part in parts:
            small_ref[at : at + part.shape[0], :] = part.astype(BF16)
            at += part.shape[0]
        gains_ref[0:1, :] = gg_ref[0:1, :]
        gains_ref[1:2, :] = gain_two_ref[0:1, :]
        small_ref[at:, :] = jnp.zeros((small_ref.shape[0] - at, cols), BF16)


def unprep_call(
    block, nb, shift, seq, peers, back, dgp, pre, w, conv, x, gains, gate, mean, pers, gain_two,
    shared,
):
    dgp, spot = dgp
    rows, width = x.shape
    cols = dgp.shape[1]
    first, last = block == 0, block == nb - 1
    whole = lambda a: pl.BlockSpec(a.shape, lambda i, n=len(a.shape): (0,) * n)
    smem = pl.BlockSpec(memory_space=pltpu.SMEM)
    at_block = pl.BlockSpec((SPAN, cols), lambda i: (block, 0))
    stacked = lambda n: pl.BlockSpec((n, SPAN, cols), lambda i: (0, block, 0))
    struct = jax.ShapeDtypeStruct
    gate_rows_out = 16
    names = ["cg", "gg", "gate", "dproj", "keep", "send", "inner", "edge"]
    outs = [
        struct((16, cols), F32),
        struct((8, width), F32),
        struct((gate_rows_out, width), F32),
        struct((4, rows, cols), BF16),
        struct((2, rows, cols), BF16),
        struct((2, rows, cols), BF16),
        struct((8, rows), F32),
        struct((3, HALO, cols), F32),
    ]
    out_specs = [whole(a) for a in outs[:3]]
    out_specs += [
        stacked(4),
        stacked(2),
        stacked(2),
        pl.BlockSpec((8, SPAN), lambda i: (0, block)),
        whole(outs[7]),
    ]
    ins = [seq, peers, back["dq"], back["dk"], back["dv"], dgp, pre, w, conv, x, gains]
    in_specs = [
        smem,
        smem,
        whole(back["dq"]),
        at_block,
        at_block,
        pl.BlockSpec((SPAN, cols), lambda i: (spot, 0)),
        stacked(3),
        whole(w),
        whole(conv),
        pl.BlockSpec((SPAN, width), lambda i: (block, 0)),
        whole(gains),
    ]
    aliases = {}
    if not first:
        ins.append(pre)
        in_specs.append(
            pl.BlockSpec((3, 2 * HALO, cols), lambda i: (0, block * (SPAN // HALO // 2) - 1, 0))
        )
    else:
        others = [back["dp"], pers, back["ab"], back["btb"], gain_two]
        ins += others
        in_specs += [whole(a) for a in others]
        names += ["small", "gains"]
        ahead = 5 * width // SMALL_ROWS
        outs.append(struct(((ahead + 1) * SMALL_ROWS, cols), BF16))
        out_specs.append(pl.BlockSpec((SMALL_ROWS, cols), lambda i: (ahead, 0)))
        outs.append(struct((2, width), F32))
        out_specs.append(whole(outs[-1]))
    if not last:
        ins += [shared["edge"], back["dlg"], gate, mean]
        in_specs += [whole(shared["edge"]), whole(back["dlg"]), whole(gate)]
        in_specs.append(pl.BlockSpec((8, width), lambda i: (block, 0)))
        aliases = {len(ins) + n: n for n in range(7)}
        ins += [shared[name] for name in names[:7]]
        in_specs += [whole(a) for a in outs[:3]] + [pl.BlockSpec(memory_space=pl.ANY)] * 4
    got = pl.pallas_call(
        functools.partial(unprep_kernel, block, nb, shift),
        grid=(1,),
        in_specs=in_specs,
        out_specs=out_specs,
        out_shape=outs,
        input_output_aliases=aliases,
        scratch_shapes=[
            pltpu.VMEM((HALO + SPAN, cols), F32),
            pltpu.VMEM((SPAN + HALO, cols), F32),
            pltpu.VMEM((SPAN, width), BF16),
        ],
        cost_estimate=cost(10),
        name=f"unprep_{block}",
    )(*ins)
    return dict(zip(names, got))


def finish_kernel(peer_ref, x_ref, dres_ref, half_ref, far_ref, i0_ref, i1_ref, gain_ref, out_ref):
    rows, width = x_ref.shape
    cols = out_ref.shape[1]
    own = pl.ds(pl.multiple_of(peer_ref[0] * cols, cols), cols)
    x = x_ref[...].astype(F32)
    scale = lax.rsqrt(jnp.mean(x * x, -1, keepdims=True) + NORM_EPS)
    inner = jnp.transpose(i0_ref[...] + i1_ref[...])[:, 0:1] / width
    d_normed = half_ref[0].astype(F32) + far_ref[...].astype(F32)
    d_normed = d_normed * gain_ref[0:1, own]
    x_own = x_ref[:, own].astype(F32)
    out_ref[...] = dres_ref[...] + scale * d_normed - x_own * (scale * scale * scale * inner)


def finish_call(peers, x, dres, half, far, inner, inner_far, gains):
    rows, width = x.shape
    cols = dres.shape[1]
    row = lambda n: pl.BlockSpec((SPAN, n), lambda i: (i, 0))
    across = pl.BlockSpec((8, SPAN), lambda i: (0, i))
    return pl.pallas_call(
        finish_kernel,
        grid=(rows // SPAN,),
        in_specs=[
            pl.BlockSpec(memory_space=pltpu.SMEM),
            row(width),
            row(cols),
            pl.BlockSpec((1, SPAN, cols), lambda i: (0, i, 0)),
            row(cols),
            across,
            across,
            pl.BlockSpec(gains.shape, lambda i: (0, 0)),
        ],
        out_specs=row(cols),
        out_shape=jax.ShapeDtypeStruct((rows, cols), F32),
        cost_estimate=cost(4),
        name="finish",
    )(peers, x, dres, half, far, inner, inner_far, gains)


def unpack_kernel(shift, main_ref, small_ref, proj_ref, out_ref, a_ref, b_ref, gate_ref, conv_ref,
                  pers_ref, gain_ref):
    step = pl.program_id(0)
    cols = main_ref.shape[1]
    head_size = 1 << shift
    heads = cols // head_size
    last = pl.num_programs(0) - 1

    @pl.when(step < last)
    def _():
        proj_ref[0] = main_ref[...].astype(F32)

    @pl.when(step == last)
    def _():
        out_ref[...] = main_ref[...].astype(F32)

    @pl.when(step == 0)
    def _():
        small = small_ref[...].astype(F32)
        at = 2 * cols
        for h in range(heads):
            rows = slice(h * head_size, (h + 1) * head_size)
            a_ref[h] = small[rows, :]
            b_ref[h] = small[cols : 2 * cols][rows, :]
        lanes = gain_ref.shape[1] // cols
        for n in range(lanes):
            for g in range(3):
                row = at + 16 * n + g * heads
                gate_ref[g, :, n * cols : (n + 1) * cols] = small[row : row + heads, :]
        at += 16 * lanes
        taps = conv_ref.shape[1]
        for i in range(3):
            conv_ref[i] = small[at + i * taps : at + (i + 1) * taps, :]
        at += 16
        count = pers_ref.shape[2]
        for i in range(2):
            for h in range(heads):
                spot = slice(h * head_size, (h + 1) * head_size)
                pers_ref[i, h] = small[at + i * count : at + (i + 1) * count, spot]
        at += 2 * count
        for i in range(2):
            for n in range(lanes):
                row = at + i * lanes + n
                gain_ref[i : i + 1, n * cols : (n + 1) * cols] = small[row : row + 1, :]


def unpack_call(payload, shift, width, mem_hid, taps, persist_rows):
    cols = payload.shape[1]
    heads = cols >> shift
    head_size = 1 << shift
    ahead = 5 * width // SMALL_ROWS
    struct = jax.ShapeDtypeStruct
    outs = [
        struct((4, width, cols), F32),
        struct((width, cols), F32),
        struct((heads, head_size, mem_hid), F32),
        struct((heads, head_size, mem_hid), F32),
        struct((3, heads, width), F32),
        struct((3, taps, cols), F32),
        struct((2, heads, persist_rows, head_size), F32),
        struct((2, width), F32),
    ]
    whole = lambda a: pl.BlockSpec(a.shape, lambda i, n=len(a.shape): (0,) * n)
    return pl.pallas_call(
        functools.partial(unpack_kernel, shift),
        grid=(5,),
        in_specs=[
            pl.BlockSpec((width, cols), lambda i: (i, 0)),
            pl.BlockSpec((SMALL_ROWS, cols), lambda i: (ahead, 0)),
        ],
        out_specs=[pl.BlockSpec((1, width, cols), lambda i: (jnp.minimum(i, 3), 0, 0))]
        + [whole(a) for a in outs[1:]],
        out_shape=outs,
        cost_estimate=cost(4),
        name="unpack",
    )(payload, payload)


def ring_of(size):
    return [list(range(0, size, 2)) + list(range(size - 1 - size % 2, 0, -2))]


def ring_scatter(payload, axis, size):
    return lax.psum_scatter(
        payload, axis, scatter_dimension=0, axis_index_groups=ring_of(size), tiled=True
    )


def ring_gather(part, axis, size):
    return lax.all_gather(part, axis, axis=0, axis_index_groups=ring_of(size), tiled=True)


def stacked_rows(pieces, full):
    at = 0
    for piece in pieces:
        full = lax.dynamic_update_slice(full, piece, (at, 0))
        at += piece.shape[0]
    return full


def after(value, *others):
    return lax.optimization_barrier((value, *others))[0]


def per_device(
    ring_size,
    layer_input,
    proj_weight,
    conv_weight,
    persist_kv,
    memory_in,
    memory_out,
    memory_gate,
    out_weight,
    ffn_in,
    ffn_out,
    norm_gains,
    seq_len,
    out_grad,
):
    rows, width = layer_input.shape
    cols = proj_weight.shape[2]
    heads = persist_kv.shape[1]
    head_size = persist_kv.shape[3]
    shift = head_size.bit_length() - 1
    mem_hid = memory_in.shape[2]
    nb = rows // SPAN
    taps = conv_weight.shape[1]
    me = lax.axis_index("head")
    count = width // cols
    peers = jnp.stack([me, me ^ 1, me ^ 2, me ^ 3]).astype(jnp.int32)
    swap = lambda a, bit: lax.ppermute(a, "head", [(i, i ^ bit) for i in range(count)])
    far_weight, far_cot = swap(out_weight, 2), swap(out_grad, 2)
    near_weight, near_cot = swap(out_weight, 1), swap(out_grad, 1)
    pers = jnp.transpose(persist_kv, (0, 2, 1, 3)).reshape(2, -1, cols)
    q, k, v, kt, pre, gp, nl, mean, lg, pers_low, gate = prep_call(
        seq_len, layer_input, proj_weight, conv_weight, norm_gains,
        jnp.transpose(memory_gate, (1, 2, 0)), pers, shift,
    )
    a = memory_in.reshape(cols, mem_hid)
    bt = jnp.transpose(memory_out, (0, 2, 1)).reshape(cols, mem_hid)
    sa = sbt = None
    states, mixes = [], []
    relay = lambda far, *ties: swap(after(far, *ties), 1)
    gathered = earlier = [near_weight, near_cot, far_weight]
    for c in range(nb):
        if c:
            a = after(a, *earlier)
        earlier = gathered
        state = dict(a=a, bt=bt, sa=sa, sbt=sbt, lg=lg)
        got = mix_call(c, nb, shift, seq_len, lg, q, k, v, kt, pers_low, gp, a, bt, sa, sbt)
        if c < nb - 1:
            a, bt, sa, sbt, state["ga"], state["gbt"] = got[4:]
        states.append(state)
        mixed = after(got[0], *gathered)
        pieces = [got[0], swap(mixed, 1), swap(mixed, 2)]
        if c or nb == 1:
            pieces.append(swap(mixed, 3))
        gathered = pieces[1:]
        mixes.append(dict(pieces=pieces, tot=got[1], att=got[2], linv=got[3]))
        if c == 0:
            last_weight = relay(far_weight, mixed)
            gathered = gathered + [last_weight, far_cot]
        if c == min(1, nb - 1):
            last_cot = relay(far_cot, mixed)
            if c:
                first = mixes[0]["pieces"]
                first.append(relay(first[2], mixed))
                gathered = gathered + [first[3]]
            gathered = gathered + [last_cot]
    ow = (out_weight, near_weight, far_weight, last_weight)
    cot = (out_grad, near_cot, far_cot, last_cot)
    groups = [list(range(nb - 1)), [nb - 1]] if nb > 1 else [[0]]
    shared = None
    for n, blocks in enumerate(groups):
        x = layer_input
        if n == 0:
            x = after(x, mixes[-1]["pieces"][0], *earlier)
        shared, room = ffn_call(
            blocks, peers, x, [mixes[c]["pieces"] for c in blocks], ow, norm_gains, ffn_in,
            ffn_out, cot, shared,
        )
        grads_room = room[0] if room else grads_room
    normed_two, hidden, dgu, cot_full, mixed_full, residual = shared
    along_rows = (((0,), (0,)), ((), ()))
    outer = lambda left, right: lax.dot_general(
        left, right, along_rows, preferred_element_type=F32
    ).astype(BF16)
    ffn_grads = stacked_rows(
        [outer(normed_two, dgu[0]), outer(normed_two, dgu[1]), outer(hidden, cot_full)],
        grads_room,
    )
    ffn_part = ring_scatter(ffn_grads, "dp", ring_size)
    s1, r2, gain_two = [], [], None
    tie = (ffn_grads,)
    for n, blocks in enumerate(reversed(groups)):
        gain_two, keep, send = ffn_back_call(
            blocks, peers, after(dgu, *tie), ffn_in, residual, gain_two
        )
        send = after(send, *r2) if r2 else send
        s1.append((keep.astype(F32) + swap(send, 1).astype(F32)).astype(BF16))
        r2.append(swap(s1[n], 2))
        tie = (s1[0],)
    tie = (gain_two,)
    back = unprep = None
    gated = [None] * nb

    def turn(n, blocks, turned, ties, relay_ties):
        pieces = (
            s1[n], r2[n], swap(after(s1[n], *relay_ties), 1), swap(after(r2[n], *relay_ties), 1)
        )
        turned, (d_gated, d_gates) = turn_call(
            blocks, peers, pieces, after(residual, *ties), cot_full, ow, norm_gains, gp,
            [mixes[c]["tot"] for c in blocks], turned,
        )
        for spot, c in enumerate(blocks):
            gated[c] = (d_gated, spot), (d_gates, spot)
        return turned

    turned = turn(0, [nb - 1], None, tie, (r2[0],))
    tie = tuple(s1[1:])
    for c in reversed(range(nb)):
        back = back_call(
            c, nb, shift, seq_len, after(q, *tie), k, v, kt,
            pers_low, gated[c][0],
            mixes[c]["att"], mixes[c]["linv"], states[c], back, back,
        )
        if c == nb - 1:
            relay_ties = (back["dq"],)
        unprep = unprep_call(
            c, nb, shift, seq_len, peers, back, gated[c][1], pre, proj_weight, conv_weight,
            layer_input, norm_gains, gate, mean, pers, gain_two, unprep,
        )
        tie = (unprep["edge"],)
        if c == nb - 1:
            if c:
                turned = turn(1, list(range(c)), turned, tie, relay_ties)
            d_res, res_cols, d_branch, d_gate_all = turned
            d_branch, ffn_part = lax.optimization_barrier((d_branch, ffn_part))
            ffn_grads = ring_gather(ffn_part, "dp", ring_size)
            tie = (d_branch,)
    gains = unprep["gains"]
    gains = gains + sum(swap(gains, bit) for bit in (1, 2, 3))
    cuts = [4 * width, width, 2 * cols, 16 * width // cols, 16, pers.shape[1] * 2]
    cuts.append(2 * width // cols)
    payload = stacked_rows(
        [outer(nl, unprep["dproj"][i]) for i in range(4)]
        + [outer(mixed_full, d_branch)],
        unprep["small"],
    )
    payload = lax.dynamic_update_slice(
        payload, gains.reshape(-1, cols).astype(BF16), (sum(cuts[:-1]), 0)
    )
    tie = (payload,)
    payload, ffn_grads = lax.optimization_barrier((payload, ffn_grads))
    ffn_in_grad = ffn_grads[: 2 * width].astype(F32).reshape(2, width, -1)
    ffn_out_grad = ffn_grads[2 * width :].astype(F32)
    payload = ring_scatter(payload, "dp", ring_size)
    half = (
        unprep["keep"].astype(F32) + swap(after(unprep["send"], *tie), 1).astype(F32)
    ).astype(BF16)
    inner = unprep["inner"] + swap(unprep["inner"], 1)
    far = swap(half[1], 2)
    input_grad = finish_call(
        peers, layer_input, d_res, half, far, inner, swap(inner, 2), norm_gains
    )
    part_keep, part_send = down_call(peers, after(hidden, half), ffn_out, cols)
    payload, input_grad, ffn_in_grad, ffn_out_grad, part_keep, part_send = (
        lax.optimization_barrier(
            (payload, input_grad, ffn_in_grad, ffn_out_grad, part_keep, part_send)
        )
    )
    payload = ring_gather(payload, "dp", ring_size)
    part = (part_keep.astype(F32) + swap(part_send, 1).astype(F32)).astype(BF16)
    layer_output = res_cols + part[0].astype(F32) + swap(part[1], 2).astype(F32)
    layer_output = layer_output.astype(BF16)
    proj_grad, out_grads, a_grad, b_grad, gate_grad, conv_grad, pers_grad, gains = unpack_call(
        payload, shift, width, mem_hid, taps, persist_kv.shape[2]
    )
    return (
        layer_output,
        input_grad,
        proj_grad,
        conv_grad,
        pers_grad,
        a_grad,
        jnp.transpose(b_grad, (0, 2, 1)),
        jnp.transpose(gate_grad, (2, 0, 1)),
        out_grads,
        ffn_in_grad,
        ffn_out_grad,
        gains,
    )


def solution(mesh):
    in_specs = (
        P("dp", None),
        P(None, None, "head"),
        P(None, None, "head"),
        P(None, "head", None, None),
        P("head", None, None),
        P("head", None, None),
        P(None, None, "head"),
        P(None, "head"),
        P(None, None, "head"),
        P("head", None),
        P(),
        P("dp"),
        P("dp", "head"),
    )
    out_specs = (
        P("dp", "head"),
        P("dp", "head"),
        P(None, None, "head"),
        P(None, None, "head"),
        P(None, "head", None, None),
        P("head", None, None),
        P("head", None, None),
        P(None, None, "head"),
        P(None, "head"),
        P(None, None, "head"),
        P("head", None),
        P(),
    )
    body = functools.partial(per_device, mesh.shape["dp"])
    return jax.shard_map(
        body, mesh=mesh, in_specs=in_specs, out_specs=out_specs, check_vma=False
    )
```

```python
import functools

import jax
import jax.numpy as jnp
from jax import lax
from jax.experimental import pallas as pl
from jax.experimental.pallas import tpu as pltpu
from jax.sharding import PartitionSpec as P

F32 = jnp.float32
BF16 = jnp.bfloat16
HIGH = lax.Precision.HIGHEST
NORM_EPS = 1e-05
UNIT_EPS = 1e-06
SCORE_SCALE = 8.0
SPAN = 512
HALO = 8
COST_UNIT = 1.5e8
SMALL_ROWS = 640


def dot_nn(left, right):
    return jnp.dot(left, right, preferred_element_type=F32)


def dot_nt(left, right, precision=None):
    return lax.dot_general(
        left, right, (((1,), (1,)), ((), ())), preferred_element_type=F32, precision=precision
    )


def iota(shape, axis):
    return lax.broadcasted_iota(jnp.int32, shape, axis)


def cost(microseconds):
    return pl.CostEstimate(
        flops=int(microseconds * COST_UNIT), transcendentals=0, bytes_accessed=1 << 20
    )


def head_blocks(cols, shift):
    same = (iota((cols, cols), 0) >> shift) == (iota((cols, cols), 1) >> shift)
    return jnp.where(same, 1.0, 0.0).astype(BF16)


def head_sum(value, blocks):
    return dot_nn(value.astype(BF16), blocks)


def valid_column(seq_ref, start, rows):
    inside = (start + iota((rows, 1), 0)) < seq_ref[0]
    valid = jnp.where(inside, 1.0, 0.0)
    return valid, jnp.maximum(jnp.sum(valid, 0, keepdims=True), 1.0)


def head_mask(cols, shift, head):
    return jnp.where((iota((1, cols), 1) >> shift) == head, 1.0, 0.0)


def gate_rows(logits, group, heads, head_size, width):
    parts = [
        jnp.broadcast_to(
            logits[0:1, group * heads + head : group * heads + head + 1], (head_size, width)
        )
        for head in range(heads)
    ]
    return jnp.concatenate(parts, 0)


def prep_kernel(
    shift,
    low_block,
    seq_ref,
    x_ref,
    w_ref,
    conv_ref,
    gain_ref,
    gate_ref,
    pers_ref,
    edge_ref,
    q_ref,
    k_ref,
    v_ref,
    kt_ref,
    pre_ref,
    gp_ref,
    nl_ref,
    mean_ref,
    lg_ref,
    pers_out_ref,
    flat_ref,
    ext_ref,
):
    step = pl.program_id(0)
    rows, cols = q_ref.shape
    blocks = head_blocks(cols, shift)

    @pl.when(step == 0)
    def _():
        ext_ref[:, 0:HALO, :] = (
            jnp.zeros((3, HALO, cols), F32) if edge_ref is None else edge_ref[...]
        )
        keys = pers_ref[0]
        keys = keys * lax.rsqrt(head_sum(keys * keys, blocks) + UNIT_EPS)
        pers_out_ref[0] = keys.astype(BF16)
        pers_out_ref[1] = pers_ref[1].astype(BF16)
        heads = gate_ref.shape[1]
        for g in range(3):
            flat_ref[g * heads : (g + 1) * heads, :] = gate_ref[g]

    x = x_ref[...].astype(F32)
    scale = lax.rsqrt(jnp.mean(x * x, -1, keepdims=True) + NORM_EPS)
    normed = x * scale * gain_ref[0:1, :]
    low = normed.astype(BF16)
    nl_ref[...] = low
    inside = ((low_block + step) * rows + iota((8, rows), 1)) < seq_ref[0]
    valid = jnp.where(inside, 1.0, 0.0)
    count = jnp.maximum(jnp.sum(valid, 1, keepdims=True), 1.0)
    mean = dot_nn(valid.astype(BF16), low) / count
    mean_ref[...] = mean
    lg_ref[...] = dot_nt(mean, flat_ref[...], HIGH)
    gp_ref[...] = dot_nn(low, w_ref[3]).astype(BF16)
    for i in range(3):
        pre = dot_nn(low, w_ref[i])
        pre_ref[i] = pre.astype(BF16)
        ext_ref[i, HALO : HALO + rows, :] = pre
        conv = conv_ref[i, 0:1, :] * pre
        for j in range(1, conv_ref.shape[1]):
            conv = conv + conv_ref[i, j : j + 1, :] * ext_ref[i, HALO - j : HALO - j + rows, :]
        ext_ref[i, 0:HALO, :] = pre[rows - HALO :, :]
        act = conv * jax.nn.sigmoid(conv)
        if i < 2:
            act = act * lax.rsqrt(head_sum(act * act, blocks) + UNIT_EPS)
        act_low = act.astype(BF16)
        (q_ref, k_ref, v_ref)[i][...] = act_low
        if i == 1:
            kt_ref[...] = jnp.transpose(act_low.astype(F32)).astype(BF16)


def mix_kernel(block, blocks_all, shift, first, last, *refs):
    it = iter(refs)
    seq_ref, lg_ref, q_ref, k_ref, v_ref, kt_ref, pers_ref, gp_ref, a_ref, bt_ref = (
        next(it) for _ in range(10)
    )
    sa_ref, sbt_ref = (None, None) if first or last else (next(it), next(it))
    mixed_ref, tot_out_ref, att_out_ref, lt_ref = (next(it) for _ in range(4))
    if not last:
        a2_ref, bt2_ref, sa2_ref, sbt2_ref, ga_ref, gbt_ref = (next(it) for _ in range(6))
    tot_ref, att_ref, linv_ref = (next(it) for _ in range(3))
    if not last:
        z_ref, r_ref = next(it), next(it)
    rows, cols = q_ref.shape
    head_size = 1 << shift
    heads = cols // head_size
    a_low = a_ref[...].astype(BF16)
    bt_low = bt_ref[...].astype(BF16)
    valid, count = valid_column(seq_ref, block * rows, rows)
    weight = valid / count
    att_ref[...] = jnp.zeros((rows, cols), F32)
    linv_ref[...] = jnp.zeros((rows, cols), F32)
    tot_ref[...] = jnp.zeros((rows, cols), F32)
    if not last:
        r_ref[...] = jnp.zeros((rows, cols), F32)

    def one_head(head, carry):
        mask = head_mask(cols, shift, head)
        mask_low = mask.astype(BF16)
        ones_low = (1.0 - mask).astype(BF16)
        query = q_ref[...] * mask_low
        scaled = query * SCORE_SCALE
        raised = jnp.exp(dot_nt(scaled, pers_ref[0])).astype(BF16)
        total = dot_nn(raised, pers_ref[1] * mask_low + ones_low)
        for j in range(block + 1):
            span = slice(j * rows, (j + 1) * rows)
            raised = jnp.exp(dot_nt(scaled, k_ref[span, :]))
            if j == block:
                raised = jnp.where(
                    iota((rows, rows), 0) >= iota((rows, rows), 1), raised, 0.0
                )
            total = total + dot_nn(raised.astype(BF16), v_ref[span, :] * mask_low + ones_low)
        inverse = 1.0 / pltpu.roll(total, head_size, 1)
        inside = jnp.broadcast_to(mask, (rows, cols)) > 0.5
        linv_ref[...] = jnp.where(inside, inverse, linv_ref[...])
        attended = jnp.where(inside, total * inverse, 0.0)
        att_ref[...] = att_ref[...] + attended
        hid = dot_nn(query, a_low)
        hid = hid * jax.nn.sigmoid(hid)
        recalled = dot_nt(hid.astype(BF16), bt_low) * mask
        tot_ref[...] = tot_ref[...] + attended + recalled
        if not last:
            hid = dot_nn(k_ref[block * rows : (block + 1) * rows, :] * mask_low, a_low)
            sig = jax.nn.sigmoid(hid)
            act = (hid * sig).astype(BF16)
            z_ref[head] = act
            target = v_ref[block * rows : (block + 1) * rows, :].astype(F32)
            resid = (dot_nt(act, bt_low) - target) * mask * weight
            r_ref[...] = r_ref[...] + resid
            d_hid = dot_nn(resid.astype(BF16), bt_low) * (sig * (1.0 + hid * (1.0 - sig)))
            at = pl.ds(pl.multiple_of(head * head_size, head_size), head_size)
            ga_ref[at, :] = dot_nn(kt_ref[at, :], d_hid.astype(BF16))
        return carry

    lax.fori_loop(0, heads, one_head, 0)
    gate = jax.nn.sigmoid(gp_ref[...].astype(F32))
    mixed_ref[...] = (tot_ref[...] * gate).astype(BF16)
    tot_out_ref[...] = tot_ref[...].astype(BF16)
    att_out_ref[...] = att_ref[...].astype(BF16)
    start = iota((8, cols), 1) == (iota((8, cols), 0) << shift)
    lt_ref[...] = dot_nt(jnp.where(start, 1.0, 0.0), linv_ref[...], HIGH)
    if not last:
        resid_t = jnp.transpose(r_ref[...]).astype(BF16)
        for head in range(heads):
            at = slice(head * head_size, (head + 1) * head_size)
            gbt_ref[at, :] = dot_nn(resid_t[at, :], z_ref[head])
        width = a_ref.shape[1]
        logits = lg_ref[...]
        step = 0.2 * jax.nn.sigmoid(gate_rows(logits, 0, heads, head_size, width))
        keep = jax.nn.sigmoid(gate_rows(logits, 1, heads, head_size, width))
        stay = 1.0 - 0.5 * jax.nn.sigmoid(gate_rows(logits, 2, heads, head_size, width))
        moment_a = -step * ga_ref[...]
        moment_b = -step * gbt_ref[...]
        if not first:
            moment_a = moment_a + keep * sa_ref[...]
            moment_b = moment_b + keep * sbt_ref[...]
        sa2_ref[...] = moment_a
        sbt2_ref[...] = moment_b
        a2_ref[...] = stay * a_ref[...] + moment_a
        bt2_ref[...] = stay * bt_ref[...] + moment_b


def lead_kernel(low, count, nb, shift, *refs):
    it = iter(refs)
    take = lambda n: [next(it) for _ in range(n)]
    final = low + count == nb
    prep_in = take(7)
    k_in_ref, v_in_ref, edge_in_ref = take(3) if low else [None] * 3
    state = take(4 if 0 < low < nb - 1 else 2)
    if low:
        take(12)
    prep_out, kept, (mixed_ref, pers_ref, flat_ref) = take(9), take(3), take(3)
    blocks = range(low, low + count)
    squares = [take(6) if block < nb - 1 else [] for block in blocks]
    k_out_ref, v_out_ref, edge_out_ref = [None] * 3 if final else take(3)
    ext_ref, k_all_ref, v_all_ref = take(3)
    room, more = take(3), take(0 if low == nb - 1 else 2)
    step = pl.program_id(0)
    q_ref, k_ref, v_ref, kt_ref, _, gp_ref, _, _, lg_ref = prep_out
    rows = q_ref.shape[0]
    prep_kernel(shift, low, *prep_in, edge_in_ref, *prep_out, pers_ref, flat_ref, ext_ref)
    for i, block in enumerate(blocks):

        @pl.when(step == i)
        def _(i=i, block=block):
            if low and i == 0:
                k_all_ref[0 : low * rows, :] = k_in_ref[...]
                v_all_ref[0 : low * rows, :] = v_in_ref[...]
            own = slice(block * rows, (block + 1) * rows)
            k_all_ref[own, :] = k_ref[...]
            v_all_ref[own, :] = v_ref[...]
            first, last = block == 0, block == nb - 1
            now = squares[i - 1][:4] if i else state
            now = now[:2] if first or last else now
            mix_kernel(
                block, nb, shift, first, last, prep_in[0], lg_ref, q_ref, k_all_ref, v_all_ref,
                kt_ref, pers_ref, gp_ref, *now, mixed_ref, *kept, *squares[i], *room,
                *([] if last else more),
            )
            if i == count - 1 and not final:
                done = (low + count) * rows
                k_out_ref[...] = k_all_ref[0:done, :]
                v_out_ref[...] = v_all_ref[0:done, :]
                edge_out_ref[...] = ext_ref[:, 0:HALO, :]


def lead_call(blocks, nb, shift, seq, x, w, conv, gains, gate, pers, state, carried, shared):
    rows, width = x.shape
    cols = w.shape[2]
    low, count = blocks[0], len(blocks)
    final = low + count == nb
    gates = 3 * gate.shape[1]
    mem_hid = state[0].shape[1]
    square = (cols, mem_hid)
    once = pl.Buffered(1)
    fixed = lambda a: pl.BlockSpec(a.shape, lambda c, n=len(a.shape): (0,) * n, pipeline_mode=once)
    whole = lambda a: pl.BlockSpec(a.shape, lambda c, n=len(a.shape): (0,) * n)
    at_rows = lambda n: pl.BlockSpec((SPAN, n), lambda c: (low + c, 0))
    eight = lambda n: pl.BlockSpec((8, n), lambda c: (low + c, 0))
    struct = jax.ShapeDtypeStruct
    ins = [seq, x, w, conv, gains, gate, pers, *carried, *state]
    in_specs = [pl.BlockSpec(memory_space=pltpu.SMEM), at_rows(width)]
    in_specs += [fixed(a) for a in ins[2:]]
    aliases = {}
    if shared:
        aliases = {len(ins) + n: n for n in range(len(shared))}
        ins += shared
        in_specs += [pl.BlockSpec(memory_space=pl.ANY)] * len(shared)
    outs = [struct((rows, cols), BF16)] * 3 + [
        struct((cols, rows), BF16),
        struct((3, rows, cols), BF16),
        struct((rows, cols), BF16),
        struct((rows, width), BF16),
        struct((nb * 8, width), F32),
        struct((nb * 8, gates), F32),
        struct((rows, cols), BF16),
        struct((rows, cols), BF16),
        struct((8, rows), F32),
        struct((count * SPAN, cols), BF16),
        struct(pers.shape, BF16),
        struct((gates, width), F32),
    ]
    out_specs = [at_rows(cols)] * 3 + [
        pl.BlockSpec((cols, SPAN), lambda c: (0, low + c)),
        pl.BlockSpec((3, SPAN, cols), lambda c: (0, low + c, 0)),
        at_rows(cols),
        at_rows(width),
        eight(width),
        eight(gates),
        at_rows(cols),
        at_rows(cols),
        pl.BlockSpec((8, SPAN), lambda c: (0, low + c)),
        pl.BlockSpec((SPAN, cols), lambda c: (c, 0)),
        whole(pers),
        pl.BlockSpec((gates, width), lambda c: (0, 0)),
    ]
    updates = [block for block in blocks if block < nb - 1]
    more = [struct(square, F32)] * (6 * len(updates))
    if not final:
        done = ((low + count) * SPAN, cols)
        more += [struct(done, BF16), struct(done, BF16), struct((3, HALO, cols), F32)]
    scratch = [
        pltpu.VMEM((3, HALO + SPAN, cols), F32),
        pltpu.VMEM((rows, cols), BF16),
        pltpu.VMEM((rows, cols), BF16),
    ] + [pltpu.VMEM((SPAN, cols), F32)] * 3
    if updates:
        heads = cols >> shift
        scratch += [pltpu.VMEM((heads, SPAN, mem_hid), BF16), pltpu.VMEM((SPAN, cols), F32)]
    got = pl.pallas_call(
        functools.partial(lead_kernel, low, count, nb, shift),
        grid=(count,),
        in_specs=in_specs,
        out_specs=out_specs + [whole(a) for a in more],
        out_shape=outs + more,
        input_output_aliases=aliases,
        scratch_shapes=scratch,
        cost_estimate=cost(11 * count),
        name=f"lead_{low}",
    )(*ins)
    at = 15 + 6 * len(updates)
    squares = [got[n : n + 6] for n in range(15, at, 6)]
    return got[:12], got[12:15], squares, got[at:]


def cot_kernel(peer_ref, c0_ref, c1_ref, c2_ref, c3_ref, fout_ref, full_ref, dh_ref):
    cols = c0_ref.shape[1]
    for j, piece_ref in enumerate((c0_ref, c1_ref, c2_ref, c3_ref)):
        at = pl.ds(pl.multiple_of(peer_ref[j] * cols, cols), cols)
        full_ref[:, at] = piece_ref[...]
    dh_ref[...] = dot_nt(full_ref[...], fout_ref[...]).astype(BF16)


def cot_call(peers, cot, fout):
    rows, cols = cot[0].shape
    hidden, width = fout.shape
    row = lambda n: pl.BlockSpec((SPAN, n), lambda i: (i, 0))
    return pl.pallas_call(
        cot_kernel,
        grid=(rows // SPAN,),
        in_specs=[pl.BlockSpec(memory_space=pltpu.SMEM)]
        + [row(cols)] * 4
        + [pl.BlockSpec(fout.shape, lambda i: (0, 0), pipeline_mode=pl.Buffered(1))],
        out_specs=[row(width), row(hidden)],
        out_shape=[
            jax.ShapeDtypeStruct((rows, width), BF16),
            jax.ShapeDtypeStruct((rows, hidden), BF16),
        ],
        cost_estimate=cost(6),
        name="cot",
    )(peers, *cot, fout)


def ffn_kernel(groups, *refs):
    it = iter(refs)
    take = lambda n: [next(it) for _ in range(n)]
    peer_ref, x_ref = take(2)
    piece_refs = [take(4) for _ in groups]
    gain_ref, dh_ref = take(2)
    weights = take(5)
    nt_out, hid_ref, dgu_ref, mfull_out, res_out, _ = take(6)
    held = take(5)
    nt_ref, mfull_ref, res_ref = take(3)
    weight_sems, out_sems = take(2)
    step = pl.program_id(0)
    rows, cols = piece_refs[0][0].shape
    loads = [
        pltpu.make_async_copy(source, target, weight_sems.at[n])
        for n, (source, target) in enumerate(zip(weights, held))
    ]
    fin_ref, ow_refs = held[4], held[:4]
    mine = pl.ds(pl.multiple_of(step * rows, rows), rows)
    stores = [
        pltpu.make_async_copy(source, target.at[mine, :], out_sems.at[n])
        for n, (source, target) in enumerate(
            ((mfull_ref, mfull_out), (res_ref, res_out), (nt_ref, nt_out))
        )
    ]

    @pl.when(step == 0)
    def _():
        for load in loads:
            load.start()

    def ready(some):
        @pl.when(step == 0)
        def _():
            for load in some:
                load.wait()

    @pl.when(step > 0)
    def _():
        for store in stores:
            store.wait()

    spots = [pl.ds(pl.multiple_of(peer_ref[j] * cols, cols), cols) for j in range(4)]
    for n, blocks in enumerate(groups):

        @pl.when((step >= blocks[0]) & (step <= blocks[-1]))
        def _(n=n):
            for j in range(4):
                mfull_ref[:, spots[j]] = piece_refs[n][j][...]

    stores[0].start()
    ready(loads[:4])
    mixed = mfull_ref[...]
    for j in range(4):
        branch = dot_nn(mixed, ow_refs[j][...])
        res_ref[:, spots[j]] = x_ref[:, spots[j]].astype(F32) + branch
    stores[1].start()
    residual = res_ref[...]
    scale = lax.rsqrt(jnp.mean(residual * residual, -1, keepdims=True) + NORM_EPS)
    low_rows = (residual * scale * gain_ref[1:2, :]).astype(BF16)
    nt_ref[...] = low_rows
    stores[2].start()
    ready(loads[4:])
    gate_pre = dot_nn(low_rows, fin_ref[0])
    up_pre = dot_nn(low_rows, fin_ref[1])
    sig = jax.nn.sigmoid(gate_pre)
    silu = gate_pre * sig
    hid_ref[...] = (silu * up_pre).astype(BF16)
    slope = sig * (1.0 + gate_pre * (1.0 - sig))
    d_hidden = dh_ref[...].astype(F32)
    dgu_ref[0] = (d_hidden * up_pre * slope).astype(BF16)
    dgu_ref[1] = (d_hidden * silu).astype(BF16)

    @pl.when(step == pl.num_programs(0) - 1)
    def _():
        for store in stores:
            store.wait()


def ffn_call(groups, peers, x, pieces, ow, gains, fin, dh):
    rows, width = x.shape
    cols = pieces[0][0].shape[1]
    hidden = dh.shape[1]
    at_rows = lambda n: pl.BlockSpec((SPAN, n), lambda i: (i, 0))
    anywhere = pl.BlockSpec(memory_space=pl.ANY)
    struct = jax.ShapeDtypeStruct
    ins = [peers, x, *[piece for group in pieces for piece in group], gains, dh, *ow, fin]
    in_specs = [pl.BlockSpec(memory_space=pltpu.SMEM), at_rows(width)]
    for blocks in groups:
        spot = lambda i, low=blocks[0], n=len(blocks): (jnp.clip(i - low, 0, n - 1), 0)
        in_specs += [pl.BlockSpec((SPAN, cols), spot)] * 4
    in_specs += [pl.BlockSpec(gains.shape, lambda i: (0, 0)), at_rows(hidden)] + [anywhere] * 5
    return pl.pallas_call(
        functools.partial(ffn_kernel, groups),
        grid=(rows // SPAN,),
        in_specs=in_specs,
        out_specs=[
            anywhere,
            at_rows(hidden),
            pl.BlockSpec((2, SPAN, hidden), lambda i: (0, i, 0)),
            anywhere,
            anywhere,
            anywhere,
        ],
        out_shape=[
            struct((rows, width), BF16),
            struct((rows, hidden), BF16),
            struct((2, rows, hidden), BF16),
            struct((rows, width), BF16),
            struct((rows, width), F32),
            struct((3 * width, width), BF16),
        ],
        scratch_shapes=[pltpu.VMEM(piece.shape, BF16) for piece in (*ow, fin)]
        + [pltpu.VMEM((SPAN, width), BF16)] * 2
        + [pltpu.VMEM((SPAN, width), F32)]
        + [pltpu.SemaphoreType.DMA((5,)), pltpu.SemaphoreType.DMA((3,))],
        cost_estimate=cost(22),
        name="ffn",
    )(*ins)


def ffn_back_kernel(first_call, *refs):
    it = iter(refs)
    take = lambda n: [next(it) for _ in range(n)]
    peer_ref, dgu_ref, fin_ref, res_ref = take(4)
    gg_in_ref = None if first_call else take(1)[0]
    gg_ref, keep_ref, send_ref, part_ref = take(4)
    width = res_ref.shape[1]
    residual = res_ref[...]
    scale = lax.rsqrt(jnp.mean(residual * residual, -1, keepdims=True) + NORM_EPS)
    d_normed = dot_nt(dgu_ref[0], fin_ref[0]) + dot_nt(dgu_ref[1], fin_ref[1])
    gains = jnp.sum(d_normed * residual * scale, 0, keepdims=True)

    @pl.when(pl.program_id(0) == 0)
    def _():
        gg_ref[...] = jnp.zeros(gg_ref.shape, F32) if first_call else gg_in_ref[...]

    gg_ref[...] = gg_ref[...] + jnp.broadcast_to(gains, gg_ref.shape)
    half = width // 2
    part_ref[...] = d_normed.astype(BF16)
    core = peer_ref[0] & 1
    keep_ref[...] = part_ref[:, pl.ds(pl.multiple_of(core * half, half), half)]
    send_ref[...] = part_ref[:, pl.ds(pl.multiple_of((1 - core) * half, half), half)]


def ffn_back_call(blocks, peers, dgu, fin, res, gains):
    width = res.shape[1]
    tile = SPAN // 2
    steps = SPAN // tile
    low = blocks[0] * steps
    lines = len(blocks) * SPAN
    gain_spec = pl.BlockSpec((8, width), lambda i: (0, 0))
    row = pl.BlockSpec((tile, width // 2), lambda i: (i, 0))
    struct = jax.ShapeDtypeStruct
    return pl.pallas_call(
        functools.partial(ffn_back_kernel, gains is None),
        grid=(len(blocks) * steps,),
        in_specs=[
            pl.BlockSpec(memory_space=pltpu.SMEM),
            pl.BlockSpec((2, tile, dgu.shape[2]), lambda i: (0, low + i, 0)),
            pl.BlockSpec(fin.shape, lambda i: (0, 0, 0), pipeline_mode=pl.Buffered(1)),
            pl.BlockSpec((tile, width), lambda i: (low + i, 0)),
        ]
        + ([] if gains is None else [gain_spec]),
        out_specs=[gain_spec, row, row],
        out_shape=[
            struct((8, width), F32),
            struct((lines, width // 2), BF16),
            struct((lines, width // 2), BF16),
        ],
        scratch_shapes=[pltpu.VMEM((tile, width), BF16)],
        cost_estimate=cost(4 * len(blocks)),
        name=f"ffn_back_{blocks[0]}",
    )(peers, dgu, fin, res, *([] if gains is None else [gains]))


def down_kernel(peer_ref, hid_ref, fout_ref, keep_ref, send_ref, part_ref):
    cols = keep_ref.shape[2]
    part_ref[...] = dot_nn(hid_ref[...], fout_ref[...]).astype(BF16)
    for slot, out_ref in ((0, keep_ref), (1, send_ref)):
        for n in range(2):
            start = pl.multiple_of(peer_ref[slot + 2 * n] * cols, cols)
            out_ref[n] = part_ref[:, pl.ds(start, cols)]


def down_call(peers, hid, fout, cols):
    rows, hidden = hid.shape
    width = fout.shape[1]
    stacked = pl.BlockSpec((2, SPAN, cols), lambda i: (0, i, 0))
    return pl.pallas_call(
        down_kernel,
        grid=(rows // SPAN,),
        in_specs=[
            pl.BlockSpec(memory_space=pltpu.SMEM),
            pl.BlockSpec((SPAN, hidden), lambda i: (i, 0)),
            pl.BlockSpec(fout.shape, lambda i: (0, 0), pipeline_mode=pl.Buffered(1)),
        ],
        out_specs=[stacked, stacked],
        out_shape=[jax.ShapeDtypeStruct((2, rows, cols), BF16)] * 2,
        scratch_shapes=[pltpu.VMEM((SPAN, width), BF16)],
        cost_estimate=cost(6),
        name="down",
    )(peers, hid, fout)


def turn_kernel(first_call, *refs):
    it = iter(refs)
    take = lambda n: [next(it) for _ in range(n)]
    peer_ref, s1_ref, r2_ref, ps1_ref, pr2_ref, res_ref, cot_ref = take(7)
    gain_ref, gp_ref = take(2)
    ow_refs = take(4)
    (tot_ref,) = take(1)
    if not first_call:
        take(4)
    dres_ref, rescol_ref, dbr_ref, dgall_ref, dga_ref, dgp_ref, full_ref = take(7)
    rows, width = res_ref.shape
    cols = gp_ref.shape[1]
    half = width // 2
    core = peer_ref[0] & 1
    at_own = pl.ds(pl.multiple_of(core * half, half), half)
    at_other = pl.ds(pl.multiple_of((1 - core) * half, half), half)
    full_ref[:, at_own] = s1_ref[...].astype(F32) + r2_ref[...].astype(F32)
    full_ref[:, at_other] = ps1_ref[...].astype(F32) + pr2_ref[...].astype(F32)
    residual = res_ref[...]
    scale = lax.rsqrt(jnp.mean(residual * residual, -1, keepdims=True) + NORM_EPS)
    gained = full_ref[...] * gain_ref[1:2, :]
    inner = jnp.sum(gained * residual, -1, keepdims=True) / width
    d_residual = cot_ref[...].astype(F32) + scale * gained - residual * (scale * scale * scale * inner)
    own = pl.ds(pl.multiple_of(peer_ref[0] * cols, cols), cols)
    full_ref[...] = d_residual
    d_mixed = None
    for j in range(4):
        at = pl.ds(pl.multiple_of(peer_ref[j] * cols, cols), cols)
        term = dot_nt(full_ref[:, at].astype(BF16), ow_refs[j][own, :])
        d_mixed = term if d_mixed is None else d_mixed + term
    mine = full_ref[:, own]
    dres_ref[...] = mine
    dbr_ref[...] = mine.astype(BF16)
    rescol_ref[...] = res_ref[:, own]
    gate = jax.nn.sigmoid(gp_ref[...].astype(F32))
    d_gated = d_mixed * gate
    dga_ref[...] = d_gated.astype(BF16)
    d_gate = (d_gated * tot_ref[...].astype(F32) * (1.0 - gate)).astype(BF16)
    dgp_ref[...] = d_gate
    dgall_ref[...] = d_gate


def turn_call(blocks, peers, pieces, res, cot, ow, gains, gp, tot, shared):
    rows, cols = gp.shape
    width = res.shape[1]
    tile = SPAN // 2
    steps = SPAN // tile
    low = blocks[0] * steps
    count = len(blocks) * steps
    whole = lambda a: pl.BlockSpec(a.shape, lambda i, n=a.ndim: (0,) * n)
    row = lambda n: pl.BlockSpec((tile, n), lambda i: (i, 0))
    at_rows = lambda n: pl.BlockSpec((tile, n), lambda i: (low + i, 0))
    struct = jax.ShapeDtypeStruct
    ins = [peers, *pieces, res, cot, gains, gp, *ow, tot]
    in_specs = [
        pl.BlockSpec(memory_space=pltpu.SMEM),
        row(width // 2),
        row(width // 2),
        row(width // 2),
        row(width // 2),
        at_rows(width),
        at_rows(width),
        whole(gains),
        at_rows(cols),
    ] + [pl.BlockSpec((width, cols), lambda i: (0, 0))] * 4
    in_specs.append(at_rows(cols))
    aliases = {}
    if shared is not None:
        aliases = {len(ins) + n: n for n in range(len(shared))}
        ins += shared
        in_specs += [pl.BlockSpec(memory_space=pl.ANY)] * len(shared)
    got = pl.pallas_call(
        functools.partial(turn_kernel, shared is None),
        grid=(count,),
        in_specs=in_specs,
        out_specs=[at_rows(cols)] * 4 + [row(cols)] * 2,
        out_shape=[
            struct((rows, cols), F32),
            struct((rows, cols), F32),
            struct((rows, cols), BF16),
            struct((rows, cols), BF16),
            struct((len(blocks) * SPAN, cols), BF16),
            struct((len(blocks) * SPAN, cols), BF16),
        ],
        input_output_aliases=aliases,
        scratch_shapes=[pltpu.VMEM((tile, width), F32)],
        cost_estimate=cost(5 * len(blocks)),
        name=f"turn_{blocks[0]}",
    )(*ins)
    return got[:4], got[4:]


def back_kernel(block, nb, shift, *refs):
    it = iter(refs)
    take = lambda n: [next(it) for _ in range(n)]
    first, last = block == 0, block == nb - 1
    seq_ref, q_ref, k_ref, v_ref, kt_ref, pers_ref, dga_ref, att_ref, lt_ref = take(9)
    a_ref, bt_ref = take(2)
    if not last:
        dk_in_ref, dv_in_ref, dp_in_ref, lg_ref, ga_ref, gbt_ref, ab_in_ref, btb_in_ref = take(8)
        sab_in_ref, sbtb_in_ref = take(2) if block < nb - 2 else (None, None)
        sa_ref, sbt_ref = (None, None) if first else take(2)
    dq_ref, dk_ref, dv_ref, dp_ref, ab_ref, btb_ref = take(6)
    if not last:
        (dlg_ref,) = take(1)
        sab_ref, sbtb_ref = (None, None) if first else take(2)
    dt_ref, dqt_ref, qt_ref, dot_ref = take(4)
    if not last:
        z_ref, zd_ref, r_ref, y_ref, h_ref = take(5)
    rows, cols = q_ref.shape
    head_size = 1 << shift
    heads = cols // head_size
    own = slice(block * rows, (block + 1) * rows)
    a_low = a_ref[...].astype(BF16)
    bt_low = bt_ref[...].astype(BF16)
    if last:
        dk_ref[...] = jnp.zeros(dk_ref.shape, F32)
        dv_ref[...] = jnp.zeros(dv_ref.shape, F32)
        dp_ref[...] = jnp.zeros(dp_ref.shape, F32)
        ab_ref[...] = jnp.zeros(ab_ref.shape, F32)
        btb_ref[...] = jnp.zeros(btb_ref.shape, F32)
    else:
        dk_ref[...] = dk_in_ref[...]
        dv_ref[...] = dv_in_ref[...]
        dp_ref[...] = dp_in_ref[...]
    pick = (iota((8, cols), 1) >> shift) == iota((8, cols), 0)
    d_gated = dga_ref[...].astype(F32)
    dt_ref[...] = dot_nt(jnp.where(pick, 1.0, 0.0), d_gated * att_ref[...].astype(F32), HIGH)
    dq_ref[...] = jnp.zeros((rows, cols), F32)
    qt_ref[...] = jnp.transpose(q_ref[...].astype(F32)).astype(BF16)
    dot_ref[...] = jnp.transpose(d_gated).astype(BF16)
    if not last:
        valid, count = valid_column(seq_ref, block * rows, rows)
        weight = valid / count
        width = a_ref.shape[1]
        logits = lg_ref[...]
        sig_step = jax.nn.sigmoid(gate_rows(logits, 0, heads, head_size, width))
        keep = jax.nn.sigmoid(gate_rows(logits, 1, heads, head_size, width))
        sig_forget = jax.nn.sigmoid(gate_rows(logits, 2, heads, head_size, width))
        tot_a, tot_b = ab_in_ref[...], btb_in_ref[...]
        if sab_in_ref is not None:
            tot_a, tot_b = tot_a + sab_in_ref[...], tot_b + sbtb_in_ref[...]
        h_ref[0] = (-0.2 * sig_step * tot_a).astype(BF16)
        h_ref[1] = (-0.2 * sig_step * tot_b).astype(BF16)
        d_step = -(ga_ref[...] * tot_a + gbt_ref[...] * tot_b)
        groups = [d_step * (0.2 * sig_step * (1.0 - sig_step)), None, None]
        if not first:
            groups[1] = (sa_ref[...] * tot_a + sbt_ref[...] * tot_b) * (keep * (1.0 - keep))
        d_forget = -(a_ref[...] * ab_in_ref[...] + bt_ref[...] * btb_in_ref[...])
        groups[2] = d_forget * (0.5 * sig_forget * (1.0 - sig_forget))
        d_logits = jnp.zeros(dlg_ref.shape, F32)
        for g, value in enumerate(groups):
            if value is None:
                continue
            for head in range(heads):
                part = value[head * head_size : (head + 1) * head_size, :]
                figure = jnp.sum(jnp.sum(part, 1, keepdims=True), 0, keepdims=True)
                here = iota(dlg_ref.shape, 1) == g * heads + head
                d_logits = d_logits + jnp.where(here, 1.0, 0.0) * figure
        dlg_ref[...] = d_logits
        stay = 1.0 - 0.5 * sig_forget
        ab_ref[...] = stay * ab_in_ref[...]
        btb_ref[...] = stay * btb_in_ref[...]
        if not first:
            sab_ref[...] = keep * tot_a
            sbtb_ref[...] = keep * tot_b
        r_ref[...] = jnp.zeros((rows, cols), F32)
        y_ref[...] = jnp.zeros((rows, cols), F32)

    def one_head(head, carry):
        mask = head_mask(cols, shift, head)
        mask_low = mask.astype(BF16)
        query = q_ref[...] * mask_low
        scaled = query * SCORE_SCALE
        d_out = dga_ref[...] * mask_low
        at = pl.ds(pl.multiple_of(head * head_size, head_size), head_size)
        inverse = lt_ref[pl.ds(head, 1), :]
        delta = dt_ref[pl.ds(head, 1), :]
        probs = jnp.exp(dot_nt(pers_ref[0], scaled)) * inverse
        d_scores = (probs * (dot_nt(pers_ref[1], d_out) - delta)).astype(BF16)
        dp_ref[0] = dp_ref[0] + dot_nn(d_scores, scaled)
        dp_ref[1] = dp_ref[1] + dot_nn(probs.astype(BF16), d_out)
        d_query = lax.dot_general(
            d_scores, pers_ref[0], (((0,), (0,)), ((), ())), preferred_element_type=F32
        )
        d_query = d_query * SCORE_SCALE
        d_query_t = jnp.zeros((head_size, rows), F32)
        for j in range(block + 1):
            span = slice(j * rows, (j + 1) * rows)
            probs = jnp.exp(dot_nt(k_ref[span, :], scaled)) * inverse
            if j == block:
                probs = jnp.where(iota((rows, rows), 0) <= iota((rows, rows), 1), probs, 0.0)
            d_scores = (probs * (dot_nt(v_ref[span, :], d_out) - delta)).astype(BF16)
            dv_ref[span, :] = dv_ref[span, :] + dot_nn(probs.astype(BF16), d_out)
            dk_ref[span, :] = dk_ref[span, :] + dot_nn(d_scores, scaled)
            d_query_t = d_query_t + dot_nn(kt_ref[at, span], d_scores)
        dqt_ref[at, :] = d_query_t * SCORE_SCALE
        hid = dot_nn(query, a_low)
        sig = jax.nn.sigmoid(hid)
        d_hid = dot_nn(d_out, bt_low) * (sig * (1.0 + hid * (1.0 - sig)))
        d_hid = d_hid.astype(BF16)
        dq_ref[...] = dq_ref[...] + (d_query + dot_nt(d_hid, a_low)) * mask
        grad_a = dot_nn(qt_ref[at, :], d_hid)
        grad_b = dot_nn(dot_ref[at, :], (hid * sig).astype(BF16))
        if not last:
            key = k_ref[own, :] * mask_low
            hid = dot_nn(key, a_low)
            probe = dot_nn(key, h_ref[0])
            sig = jax.nn.sigmoid(hid)
            act = (hid * sig).astype(BF16)
            z_ref[head] = act
            slope = sig * (1.0 + hid * (1.0 - sig))
            curve = sig * (1.0 - sig) * (2.0 + hid * (1.0 - 2.0 * sig))
            target = v_ref[own, :].astype(F32)
            resid = (dot_nt(act, bt_low) - target) * mask * weight
            r_ref[...] = r_ref[...] + resid
            resid = resid.astype(BF16)
            d_act = dot_nn(resid, bt_low)
            d_slope = (probe * slope).astype(BF16)
            zd_ref[head] = d_slope
            d_net = (dot_nt(act, h_ref[1]) + dot_nt(d_slope, bt_low)) * mask * weight
            y_ref[...] = y_ref[...] + d_net
            back = dot_nn(resid, h_ref[1]) + dot_nn(d_net.astype(BF16), bt_low)
            d_hid = (probe * d_act * curve + back * slope).astype(BF16)
            direct = (d_act * slope).astype(BF16)
            d_key = (dot_nt(direct, h_ref[0]) + dot_nt(d_hid, a_low)) * mask
            dk_ref[own, :] = dk_ref[own, :] + d_key
            grad_a = grad_a + dot_nn(kt_ref[at, own], d_hid)
        ab_ref[at, :] = ab_ref[at, :] + grad_a
        btb_ref[at, :] = btb_ref[at, :] + grad_b
        return carry

    lax.fori_loop(0, heads, one_head, 0)
    dq_ref[...] = dq_ref[...] + jnp.transpose(dqt_ref[...])
    if not last:
        dv_ref[own, :] = dv_ref[own, :] - y_ref[...]
        resid_t = jnp.transpose(r_ref[...]).astype(BF16)
        net_t = jnp.transpose(y_ref[...]).astype(BF16)
        for head in range(heads):
            at = slice(head * head_size, (head + 1) * head_size)
            grad_b = dot_nn(resid_t[at, :], zd_ref[head]) + dot_nn(net_t[at, :], z_ref[head])
            btb_ref[at, :] = btb_ref[at, :] + grad_b


def back_call(block, nb, shift, seq, q, k, v, kt, pers, dga, att, linv, state, grads, adjoint):
    dga, spot = dga
    cols = q.shape[1]
    heads = cols >> shift
    first, last = block == 0, block == nb - 1
    done = (block + 1) * SPAN
    whole = lambda s: pl.BlockSpec(s, lambda i, n=len(s): (0,) * n)
    at_block = pl.BlockSpec((SPAN, cols), lambda i: (block, 0))
    upto = pl.BlockSpec((done, cols), lambda i: (0, 0))
    square = state["a"].shape
    ins = [seq, q, k, v, kt, pers, dga, att, linv, state["a"], state["bt"]]
    in_specs = [
        pl.BlockSpec(memory_space=pltpu.SMEM),
        at_block,
        upto,
        upto,
        pl.BlockSpec((cols, done), lambda i: (0, 0)),
        whole(pers.shape),
        pl.BlockSpec((SPAN, cols), lambda i: (spot, 0)),
        at_block,
        pl.BlockSpec((8, SPAN), lambda i: (0, block)),
        whole(square),
        whole(square),
    ]
    if not last:
        ins += [grads["dk"], grads["dv"], grads["dp"], state["lg"], state["ga"], state["gbt"]]
        ins += [adjoint["ab"], adjoint["btb"]]
        in_specs += [upto, upto, whole(pers.shape)]
        in_specs += [pl.BlockSpec((8, state["lg"].shape[1]), lambda i: (block, 0))]
        in_specs += [whole(square)] * 4
        if block < nb - 2:
            ins += [adjoint["sab"], adjoint["sbtb"]]
            in_specs += [whole(square)] * 2
        if not first:
            ins += [state["sa"], state["sbt"]]
            in_specs += [whole(square)] * 2
    names = ["dq", "dk", "dv", "dp", "ab", "btb"]
    shapes = [(SPAN, cols), (done, cols), (done, cols), pers.shape, square, square]
    if not last:
        names.append("dlg")
        shapes.append((8, state["lg"].shape[1]))
        if not first:
            names += ["sab", "sbtb"]
            shapes += [square, square]
    scratch = [
        pltpu.VMEM((8, SPAN), F32),
        pltpu.VMEM((cols, SPAN), F32),
        pltpu.VMEM((cols, SPAN), BF16),
        pltpu.VMEM((cols, SPAN), BF16),
    ]
    if not last:
        scratch += [
            pltpu.VMEM((heads, SPAN, square[1]), BF16),
            pltpu.VMEM((heads, SPAN, square[1]), BF16),
            pltpu.VMEM((SPAN, cols), F32),
            pltpu.VMEM((SPAN, cols), F32),
            pltpu.VMEM((2,) + square, BF16),
        ]
    outs = pl.pallas_call(
        functools.partial(back_kernel, block, nb, shift),
        grid=(1,),
        in_specs=in_specs,
        out_specs=[whole(s) for s in shapes],
        out_shape=[jax.ShapeDtypeStruct(s, F32) for s in shapes],
        scratch_shapes=scratch,
        cost_estimate=cost(17),
        name=f"back_{block}",
    )(*ins)
    return dict(zip(names, outs))


def unprep_kernel(block, nb, shift, *refs):
    it = iter(refs)
    take = lambda n: [next(it) for _ in range(n)]
    first, last = block == 0, block == nb - 1
    seq_ref, peer_ref, dq_ref, dk_ref, dv_ref, dgp_ref, pre_ref, w_ref, conv_ref = take(9)
    x_ref, gain_ref = take(2)
    halo_ref = None if first else take(1)[0]
    dp_ref, pers_ref, ab_ref, btb_ref, gain_two_ref = take(5) if first else [None] * 5
    if not last:
        edge_in_ref, dlg_ref, gate_ref, mean_ref = take(4)
        cg_in_ref, gg_in_ref, gate_in_ref = take(7)[:3]
    cg_ref, gg_ref, gate_out_ref = take(3)
    dproj_ref, keep_ref, send_ref, inner_ref, edge_ref = take(5)
    small_ref, gains_ref = take(2) if first else (None, None)
    ext_ref, dext_ref, low_ref = take(3)
    rows, cols = dq_ref.shape
    width = x_ref.shape[1]
    blocks = head_blocks(cols, shift)
    taps = conv_ref.shape[1]
    d_normed = dot_nt(dgp_ref[...], w_ref[3])
    dproj_ref[3] = dgp_ref[...]
    if last:
        cg_ref[...] = jnp.zeros(cg_ref.shape, F32)
        gg_ref[...] = jnp.zeros(gg_ref.shape, F32)
        gate_out_ref[...] = jnp.zeros(gate_out_ref.shape, F32)
    else:
        cg_ref[...] = cg_in_ref[...]
        gg_ref[...] = gg_in_ref[...]
    for i in range(3):
        pre = pre_ref[i].astype(F32)
        ext_ref[0:HALO, :] = jnp.zeros((HALO, cols), F32) if first else halo_ref[i, HALO:, :].astype(F32)
        ext_ref[HALO : HALO + rows, :] = pre
        shifted = [pre] + [ext_ref[HALO - j : HALO - j + rows, :] for j in range(1, taps)]
        conv = conv_ref[i, 0:1, :] * pre
        for j in range(1, taps):
            conv = conv + conv_ref[i, j : j + 1, :] * shifted[j]
        sig = jax.nn.sigmoid(conv)
        d_act = (dq_ref, dk_ref, dv_ref)[i][...]
        if i < 2:
            act = conv * sig
            scale = lax.rsqrt(head_sum(act * act, blocks) + UNIT_EPS)
            d_act = scale * (d_act - act * (scale * scale * head_sum(d_act * act, blocks)))
        d_conv = d_act * (sig * (1.0 + conv * (1.0 - sig)))
        edge_ref[i] = d_conv[0:HALO, :]
        dext_ref[0:rows, :] = d_conv
        dext_ref[rows : rows + HALO, :] = (
            jnp.zeros((HALO, cols), F32) if last else edge_in_ref[i]
        )
        d_pre = conv_ref[i, 0:1, :] * d_conv
        for j in range(taps):
            if j:
                d_pre = d_pre + conv_ref[i, j : j + 1, :] * dext_ref[j : j + rows, :]
            at = slice(i * taps + j, i * taps + j + 1)
            cg_ref[at, :] = cg_ref[at, :] + jnp.sum(d_conv * shifted[j], 0, keepdims=True)
        d_low = d_pre.astype(BF16)
        dproj_ref[i] = d_low
        d_normed = d_normed + dot_nt(d_low, w_ref[i])
    if not last:
        valid, count = valid_column(seq_ref, block * rows, rows)
        d_mean = jnp.dot(
            dlg_ref[...], gate_ref[...], preferred_element_type=F32, precision=HIGH
        )
        d_normed = d_normed + (valid / count) * d_mean[0:1, :]
        outer = lax.dot_general(
            dlg_ref[...] * 0.125,
            mean_ref[...],
            (((0,), (0,)), ((), ())),
            preferred_element_type=F32,
            precision=HIGH,
        )
        gate_out_ref[...] = gate_in_ref[...]
        at = slice(0, outer.shape[0])
        gate_out_ref[at, :] = gate_in_ref[at, :] + outer
    x = x_ref[...].astype(F32)
    scale = lax.rsqrt(jnp.mean(x * x, -1, keepdims=True) + NORM_EPS)
    weighted = d_normed * x
    gains = jnp.sum(weighted * scale, 0, keepdims=True)
    gg_ref[...] = gg_ref[...] + jnp.broadcast_to(gains, gg_ref.shape)
    gained = jnp.broadcast_to(gain_ref[0:1, :], (8, width))
    inner_ref[...] = dot_nt(gained.astype(BF16), weighted.astype(BF16))
    low_ref[...] = d_normed.astype(BF16)
    for slot, out_ref in ((0, keep_ref), (1, send_ref)):
        for n in range(2):
            start = pl.multiple_of(peer_ref[slot + 2 * n] * cols, cols)
            out_ref[n] = low_ref[:, pl.ds(start, cols)]
    if first:
        keys = pers_ref[0]
        d_keys = dp_ref[0]
        scale = lax.rsqrt(head_sum(keys * keys, blocks) + UNIT_EPS)
        along = head_sum(d_keys * keys, blocks)
        d_keys = scale * (d_keys - keys * (scale * scale * along))
        across = lambda a: [a[:, n : n + cols] for n in range(0, width, cols)]
        parts = [ab_ref[...], btb_ref[...], *across(gate_out_ref[...]), cg_ref[...]]
        parts += [d_keys, dp_ref[1]]
        at = 0
        for part in parts:
            small_ref[at : at + part.shape[0], :] = part.astype(BF16)
            at += part.shape[0]
        gains_ref[0:1, :] = gg_ref[0:1, :]
        gains_ref[1:2, :] = gain_two_ref[0:1, :]
        small_ref[at:, :] = jnp.zeros((small_ref.shape[0] - at, cols), BF16)


def unprep_call(
    block, nb, shift, seq, peers, back, dgp, pre, w, conv, x, gains, gate, mean, pers, gain_two,
    shared,
):
    dgp, spot = dgp
    rows, width = x.shape
    cols = dgp.shape[1]
    first, last = block == 0, block == nb - 1
    whole = lambda a: pl.BlockSpec(a.shape, lambda i, n=len(a.shape): (0,) * n)
    smem = pl.BlockSpec(memory_space=pltpu.SMEM)
    at_block = pl.BlockSpec((SPAN, cols), lambda i: (block, 0))
    stacked = lambda n: pl.BlockSpec((n, SPAN, cols), lambda i: (0, block, 0))
    struct = jax.ShapeDtypeStruct
    gate_rows_out = 16
    names = ["cg", "gg", "gate", "dproj", "keep", "send", "inner", "edge"]
    outs = [
        struct((16, cols), F32),
        struct((8, width), F32),
        struct((gate_rows_out, width), F32),
        struct((4, rows, cols), BF16),
        struct((2, rows, cols), BF16),
        struct((2, rows, cols), BF16),
        struct((8, rows), F32),
        struct((3, HALO, cols), F32),
    ]
    out_specs = [whole(a) for a in outs[:3]]
    out_specs += [
        stacked(4),
        stacked(2),
        stacked(2),
        pl.BlockSpec((8, SPAN), lambda i: (0, block)),
        whole(outs[7]),
    ]
    ins = [seq, peers, back["dq"], back["dk"], back["dv"], dgp, pre, w, conv, x, gains]
    in_specs = [
        smem,
        smem,
        whole(back["dq"]),
        at_block,
        at_block,
        pl.BlockSpec((SPAN, cols), lambda i: (spot, 0)),
        stacked(3),
        whole(w),
        whole(conv),
        pl.BlockSpec((SPAN, width), lambda i: (block, 0)),
        whole(gains),
    ]
    aliases = {}
    if not first:
        ins.append(pre)
        in_specs.append(
            pl.BlockSpec((3, 2 * HALO, cols), lambda i: (0, block * (SPAN // HALO // 2) - 1, 0))
        )
    else:
        others = [back["dp"], pers, back["ab"], back["btb"], gain_two]
        ins += others
        in_specs += [whole(a) for a in others]
        names += ["small", "gains"]
        ahead = 5 * width // SMALL_ROWS
        outs.append(struct(((ahead + 1) * SMALL_ROWS, cols), BF16))
        out_specs.append(pl.BlockSpec((SMALL_ROWS, cols), lambda i: (ahead, 0)))
        outs.append(struct((2, width), F32))
        out_specs.append(whole(outs[-1]))
    if not last:
        ins += [shared["edge"], back["dlg"], gate, mean]
        in_specs += [whole(shared["edge"]), whole(back["dlg"]), whole(gate)]
        in_specs.append(pl.BlockSpec((8, width), lambda i: (block, 0)))
        aliases = {len(ins) + n: n for n in range(7)}
        ins += [shared[name] for name in names[:7]]
        in_specs += [whole(a) for a in outs[:3]] + [pl.BlockSpec(memory_space=pl.ANY)] * 4
    got = pl.pallas_call(
        functools.partial(unprep_kernel, block, nb, shift),
        grid=(1,),
        in_specs=in_specs,
        out_specs=out_specs,
        out_shape=outs,
        input_output_aliases=aliases,
        scratch_shapes=[
            pltpu.VMEM((HALO + SPAN, cols), F32),
            pltpu.VMEM((SPAN + HALO, cols), F32),
            pltpu.VMEM((SPAN, width), BF16),
        ],
        cost_estimate=cost(10),
        name=f"unprep_{block}",
    )(*ins)
    return dict(zip(names, got))


def finish_kernel(peer_ref, x_ref, dres_ref, half_ref, far_ref, i0_ref, i1_ref, gain_ref, out_ref):
    rows, width = x_ref.shape
    cols = out_ref.shape[1]
    own = pl.ds(pl.multiple_of(peer_ref[0] * cols, cols), cols)
    x = x_ref[...].astype(F32)
    scale = lax.rsqrt(jnp.mean(x * x, -1, keepdims=True) + NORM_EPS)
    inner = jnp.transpose(i0_ref[...] + i1_ref[...])[:, 0:1] / width
    d_normed = half_ref[0].astype(F32) + far_ref[...].astype(F32)
    d_normed = d_normed * gain_ref[0:1, own]
    x_own = x_ref[:, own].astype(F32)
    out_ref[...] = dres_ref[...] + scale * d_normed - x_own * (scale * scale * scale * inner)


def finish_call(peers, x, dres, half, far, inner, inner_far, gains):
    rows, width = x.shape
    cols = dres.shape[1]
    row = lambda n: pl.BlockSpec((SPAN, n), lambda i: (i, 0))
    across = pl.BlockSpec((8, SPAN), lambda i: (0, i))
    return pl.pallas_call(
        finish_kernel,
        grid=(rows // SPAN,),
        in_specs=[
            pl.BlockSpec(memory_space=pltpu.SMEM),
            row(width),
            row(cols),
            pl.BlockSpec((1, SPAN, cols), lambda i: (0, i, 0)),
            row(cols),
            across,
            across,
            pl.BlockSpec(gains.shape, lambda i: (0, 0)),
        ],
        out_specs=row(cols),
        out_shape=jax.ShapeDtypeStruct((rows, cols), F32),
        cost_estimate=cost(4),
        name="finish",
    )(peers, x, dres, half, far, inner, inner_far, gains)


def unpack_kernel(shift, main_ref, small_ref, proj_ref, out_ref, a_ref, b_ref, gate_ref, conv_ref,
                  pers_ref, gain_ref):
    step = pl.program_id(0)
    cols = main_ref.shape[1]
    head_size = 1 << shift
    heads = cols // head_size
    last = pl.num_programs(0) - 1

    @pl.when(step < last)
    def _():
        proj_ref[0] = main_ref[...].astype(F32)

    @pl.when(step == last)
    def _():
        out_ref[...] = main_ref[...].astype(F32)

    @pl.when(step == 0)
    def _():
        small = small_ref[...].astype(F32)
        at = 2 * cols
        for h in range(heads):
            rows = slice(h * head_size, (h + 1) * head_size)
            a_ref[h] = small[rows, :]
            b_ref[h] = small[cols : 2 * cols][rows, :]
        lanes = gain_ref.shape[1] // cols
        for n in range(lanes):
            for g in range(3):
                row = at + 16 * n + g * heads
                gate_ref[g, :, n * cols : (n + 1) * cols] = small[row : row + heads, :]
        at += 16 * lanes
        taps = conv_ref.shape[1]
        for i in range(3):
            conv_ref[i] = small[at + i * taps : at + (i + 1) * taps, :]
        at += 16
        count = pers_ref.shape[2]
        for i in range(2):
            for h in range(heads):
                spot = slice(h * head_size, (h + 1) * head_size)
                pers_ref[i, h] = small[at + i * count : at + (i + 1) * count, spot]
        at += 2 * count
        for i in range(2):
            for n in range(lanes):
                row = at + i * lanes + n
                gain_ref[i : i + 1, n * cols : (n + 1) * cols] = small[row : row + 1, :]


def unpack_call(payload, shift, width, mem_hid, taps, persist_rows):
    cols = payload.shape[1]
    heads = cols >> shift
    head_size = 1 << shift
    ahead = 5 * width // SMALL_ROWS
    struct = jax.ShapeDtypeStruct
    outs = [
        struct((4, width, cols), F32),
        struct((width, cols), F32),
        struct((heads, head_size, mem_hid), F32),
        struct((heads, head_size, mem_hid), F32),
        struct((3, heads, width), F32),
        struct((3, taps, cols), F32),
        struct((2, heads, persist_rows, head_size), F32),
        struct((2, width), F32),
    ]
    whole = lambda a: pl.BlockSpec(a.shape, lambda i, n=len(a.shape): (0,) * n)
    return pl.pallas_call(
        functools.partial(unpack_kernel, shift),
        grid=(5,),
        in_specs=[
            pl.BlockSpec((width, cols), lambda i: (i, 0)),
            pl.BlockSpec((SMALL_ROWS, cols), lambda i: (ahead, 0)),
        ],
        out_specs=[pl.BlockSpec((1, width, cols), lambda i: (jnp.minimum(i, 3), 0, 0))]
        + [whole(a) for a in outs[1:]],
        out_shape=outs,
        cost_estimate=cost(4),
        name="unpack",
    )(payload, payload)


def ring_of(size):
    return [list(range(0, size, 2)) + list(range(size - 1 - size % 2, 0, -2))]


def ring_scatter(payload, axis, size):
    return lax.psum_scatter(
        payload, axis, scatter_dimension=0, axis_index_groups=ring_of(size), tiled=True
    )


def ring_gather(part, axis, size):
    return lax.all_gather(part, axis, axis=0, axis_index_groups=ring_of(size), tiled=True)


def stacked_rows(pieces, full):
    at = 0
    for piece in pieces:
        full = lax.dynamic_update_slice(full, piece, (at, 0))
        at += piece.shape[0]
    return full


def after(value, *others):
    return lax.optimization_barrier((value, *others))[0]


def per_device(
    ring_size,
    layer_input,
    proj_weight,
    conv_weight,
    persist_kv,
    memory_in,
    memory_out,
    memory_gate,
    out_weight,
    ffn_in,
    ffn_out,
    norm_gains,
    seq_len,
    out_grad,
):
    rows, width = layer_input.shape
    cols = proj_weight.shape[2]
    heads = persist_kv.shape[1]
    head_size = persist_kv.shape[3]
    shift = head_size.bit_length() - 1
    mem_hid = memory_in.shape[2]
    nb = rows // SPAN
    taps = conv_weight.shape[1]
    me = lax.axis_index("head")
    count = width // cols
    peers = jnp.stack([me, me ^ 1, me ^ 2, me ^ 3]).astype(jnp.int32)
    swap = lambda a, bit: lax.ppermute(a, "head", [(i, i ^ bit) for i in range(count)])
    far_weight, far_cot = swap(out_weight, 2), swap(out_grad, 2)
    near_weight, near_cot = swap(out_weight, 1), swap(out_grad, 1)
    pers = jnp.transpose(persist_kv, (0, 2, 1, 3)).reshape(2, -1, cols)
    gate = jnp.transpose(memory_gate, (1, 2, 0))
    groups = [list(range(nb - 1)), [nb - 1]] if nb > 1 else [[0]]
    state = [memory_in.reshape(cols, mem_hid)]
    state.append(jnp.transpose(memory_out, (0, 2, 1)).reshape(cols, mem_hid))
    states = [dict(a=state[0], bt=state[1], sa=None, sbt=None)]
    earlier = gathered = [near_weight, near_cot, far_weight]
    shared, carried, pieces = None, [], []
    for n, blocks in enumerate(groups):
        if n:
            state = [after(state[0], *earlier), *state[1:]]
        shared, (mixed, pers_low, flat), squares, carried = lead_call(
            blocks, nb, shift, seq_len, layer_input, proj_weight, conv_weight, norm_gains, gate,
            pers, state, carried, shared,
        )
        for a, bt, sa, sbt, ga, gbt in squares:
            states[-1].update(ga=ga, gbt=gbt)
            states.append(dict(a=a, bt=bt, sa=sa, sbt=sbt))
            state = [a, bt] if blocks[-1] + 1 == nb - 1 else [a, bt, sa, sbt]
        sent = after(mixed, *gathered)
        pieces.append([mixed, swap(sent, 1), swap(sent, 2)])
        gathered = pieces[n][1:]
        if n == 0:
            last_weight = swap(after(far_weight, sent), 1)
            last_cot = swap(after(far_cot, sent), 1)
            gathered = gathered + [last_weight, last_cot]
    q, k, v, kt, pre, gp, nl, mean, lg, tot, att, lt = shared
    for state in states:
        state["lg"] = lg
    gate = flat
    ow = (out_weight, near_weight, far_weight, last_weight)
    if nb > 1:
        pieces[0].append(swap(after(pieces[0][2], pieces[1][0]), 1))
    fout = after(ffn_out, pieces[-1][0])
    cot_full, d_hidden = cot_call(peers, (out_grad, near_cot, far_cot, last_cot), fout)
    pieces[-1].append(swap(after(pieces[-1][2], cot_full), 1))
    normed_two, hidden, dgu, mixed_full, residual, grads_room = ffn_call(
        groups, peers, after(layer_input, cot_full), pieces, ow, norm_gains, ffn_in, d_hidden
    )
    along_rows = (((0,), (0,)), ((), ()))
    outer = lambda left, right: lax.dot_general(
        left, right, along_rows, preferred_element_type=F32
    ).astype(BF16)
    out_part = outer(hidden, cot_full)
    ffn_grads = stacked_rows(
        [out_part, outer(after(normed_two, out_part), dgu[0]), outer(normed_two, dgu[1])],
        grads_room,
    )
    ffn_part = ring_scatter(ffn_grads, "dp", ring_size)
    s1, r2, gain_two = [], [], None
    tie = (ffn_grads,)
    for n, blocks in enumerate(reversed(groups)):
        gain_two, keep, send = ffn_back_call(
            blocks, peers, after(dgu, *tie), ffn_in, residual, gain_two
        )
        send = after(send, *r2) if r2 else send
        s1.append((keep.astype(F32) + swap(send, 1).astype(F32)).astype(BF16))
        r2.append(swap(s1[n], 2))
        tie = (s1[0],)
    tie = (gain_two,)
    back = unprep = None
    gated = [None] * nb

    def turn(n, blocks, turned, ties, relay_ties):
        pieces = (
            s1[n], r2[n], swap(after(s1[n], *relay_ties), 1), swap(after(r2[n], *relay_ties), 1)
        )
        turned, (d_gated, d_gates) = turn_call(
            blocks, peers, pieces, after(residual, *ties), cot_full, ow, norm_gains, gp,
            tot, turned,
        )
        for spot, c in enumerate(blocks):
            gated[c] = (d_gated, spot), (d_gates, spot)
        return turned

    turned = turn(0, [nb - 1], None, tie, (r2[0],))
    tie = tuple(s1[1:])
    for c in reversed(range(nb)):
        back = back_call(
            c, nb, shift, seq_len, after(q, *tie), k, v, kt,
            pers_low, gated[c][0],
            att, lt, states[c], back, back,
        )
        if c == nb - 1:
            relay_ties = (back["dq"],)
        unprep = unprep_call(
            c, nb, shift, seq_len, peers, back, gated[c][1], pre, proj_weight, conv_weight,
            layer_input, norm_gains, gate, mean, pers, gain_two, unprep,
        )
        tie = (unprep["edge"],)
        if c == nb - 1:
            if c:
                turned = turn(1, list(range(c)), turned, tie, relay_ties)
            d_res, res_cols, d_branch, d_gate_all = turned
            d_branch, ffn_part = lax.optimization_barrier((d_branch, ffn_part))
            ffn_grads = ring_gather(ffn_part, "dp", ring_size)
            tie = (d_branch,)
    gains = unprep["gains"]
    gains = gains + sum(swap(gains, bit) for bit in (1, 2, 3))
    cuts = [4 * width, width, 2 * cols, 16 * width // cols, 16, pers.shape[1] * 2]
    cuts.append(2 * width // cols)
    payload = stacked_rows(
        [outer(nl, unprep["dproj"][i]) for i in range(4)]
        + [outer(mixed_full, d_branch)],
        unprep["small"],
    )
    payload = lax.dynamic_update_slice(
        payload, gains.reshape(-1, cols).astype(BF16), (sum(cuts[:-1]), 0)
    )
    tie = (payload,)
    payload, ffn_grads = lax.optimization_barrier((payload, ffn_grads))
    ffn_in_grad = ffn_grads[width:].astype(F32).reshape(2, width, -1)
    ffn_out_grad = ffn_grads[:width].astype(F32)
    payload = ring_scatter(payload, "dp", ring_size)
    half = (
        unprep["keep"].astype(F32) + swap(after(unprep["send"], *tie), 1).astype(F32)
    ).astype(BF16)
    inner = unprep["inner"] + swap(unprep["inner"], 1)
    far = swap(half[1], 2)
    input_grad = finish_call(
        peers, layer_input, d_res, half, far, inner, swap(inner, 2), norm_gains
    )
    part_keep, part_send = down_call(peers, after(hidden, half), ffn_out, cols)
    payload, input_grad, ffn_in_grad, ffn_out_grad, part_keep, part_send = (
        lax.optimization_barrier(
            (payload, input_grad, ffn_in_grad, ffn_out_grad, part_keep, part_send)
        )
    )
    payload = ring_gather(payload, "dp", ring_size)
    part = (part_keep.astype(F32) + swap(part_send, 1).astype(F32)).astype(BF16)
    layer_output = res_cols + part[0].astype(F32) + swap(part[1], 2).astype(F32)
    layer_output = layer_output.astype(BF16)
    proj_grad, out_grads, a_grad, b_grad, gate_grad, conv_grad, pers_grad, gains = unpack_call(
        payload, shift, width, mem_hid, taps, persist_kv.shape[2]
    )
    return (
        layer_output,
        input_grad,
        proj_grad,
        conv_grad,
        pers_grad,
        a_grad,
        jnp.transpose(b_grad, (0, 2, 1)),
        jnp.transpose(gate_grad, (2, 0, 1)),
        out_grads,
        ffn_in_grad,
        ffn_out_grad,
        gains,
    )


def solution(mesh):
    in_specs = (
        P("dp", None),
        P(None, None, "head"),
        P(None, None, "head"),
        P(None, "head", None, None),
        P("head", None, None),
        P("head", None, None),
        P(None, None, "head"),
        P(None, "head"),
        P(None, None, "head"),
        P("head", None),
        P(),
        P("dp"),
        P("dp", "head"),
    )
    out_specs = (
        P("dp", "head"),
        P("dp", "head"),
        P(None, None, "head"),
        P(None, None, "head"),
        P(None, "head", None, None),
        P("head", None, None),
        P("head", None, None),
        P(None, None, "head"),
        P(None, "head"),
        P(None, None, "head"),
        P("head", None),
        P(),
    )
    body = functools.partial(per_device, mesh.shape["dp"])
    return jax.shard_map(
        body, mesh=mesh, in_specs=in_specs, out_specs=out_specs, check_vma=False
    )
```

```python
import functools

import jax
import jax.numpy as jnp
from jax import lax
from jax.experimental import pallas as pl
from jax.experimental.pallas import tpu as pltpu
from jax.sharding import PartitionSpec as P

F32 = jnp.float32
BF16 = jnp.bfloat16
HIGH = lax.Precision.HIGHEST
NORM_EPS = 1e-05
UNIT_EPS = 1e-06
SCORE_SCALE = 8.0
SPAN = 512
HALO = 8
COST_UNIT = 1.5e8
SMALL_ROWS = 640


def dot_nn(left, right):
    return jnp.dot(left, right, preferred_element_type=F32)


def dot_nt(left, right, precision=None):
    return lax.dot_general(
        left, right, (((1,), (1,)), ((), ())), preferred_element_type=F32, precision=precision
    )


def iota(shape, axis):
    return lax.broadcasted_iota(jnp.int32, shape, axis)


def cost(microseconds):
    return pl.CostEstimate(
        flops=int(microseconds * COST_UNIT), transcendentals=0, bytes_accessed=1 << 20
    )


def head_blocks(cols, shift):
    same = (iota((cols, cols), 0) >> shift) == (iota((cols, cols), 1) >> shift)
    return jnp.where(same, 1.0, 0.0).astype(BF16)


def head_sum(value, blocks):
    return dot_nn(value.astype(BF16), blocks)


def valid_column(seq_ref, start, rows):
    inside = (start + iota((rows, 1), 0)) < seq_ref[0]
    valid = jnp.where(inside, 1.0, 0.0)
    return valid, jnp.maximum(jnp.sum(valid, 0, keepdims=True), 1.0)


def head_mask(cols, shift, head):
    return jnp.where((iota((1, cols), 1) >> shift) == head, 1.0, 0.0)


def gate_rows(logits, group, heads, head_size, width):
    parts = [
        jnp.broadcast_to(
            logits[0:1, group * heads + head : group * heads + head + 1], (head_size, width)
        )
        for head in range(heads)
    ]
    return jnp.concatenate(parts, 0)


def prep_kernel(
    shift,
    low_block,
    seq_ref,
    x_ref,
    w_ref,
    conv_ref,
    gain_ref,
    gate_ref,
    pers_ref,
    edge_ref,
    q_ref,
    k_ref,
    v_ref,
    kt_ref,
    pre_ref,
    gp_ref,
    nl_ref,
    mean_ref,
    lg_ref,
    pers_out_ref,
    flat_ref,
    ext_ref,
):
    step = pl.program_id(0)
    rows, cols = q_ref.shape
    blocks = head_blocks(cols, shift)

    @pl.when(step == 0)
    def _():
        ext_ref[:, 0:HALO, :] = (
            jnp.zeros((3, HALO, cols), F32) if edge_ref is None else edge_ref[...]
        )
        keys = pers_ref[0]
        keys = keys * lax.rsqrt(head_sum(keys * keys, blocks) + UNIT_EPS)
        pers_out_ref[0] = keys.astype(BF16)
        pers_out_ref[1] = pers_ref[1].astype(BF16)
        heads = gate_ref.shape[1]
        for g in range(3):
            flat_ref[g * heads : (g + 1) * heads, :] = gate_ref[g]

    x = x_ref[...].astype(F32)
    scale = lax.rsqrt(jnp.mean(x * x, -1, keepdims=True) + NORM_EPS)
    normed = x * scale * gain_ref[0:1, :]
    low = normed.astype(BF16)
    nl_ref[...] = low
    inside = ((low_block + step) * rows + iota((8, rows), 1)) < seq_ref[0]
    valid = jnp.where(inside, 1.0, 0.0)
    count = jnp.maximum(jnp.sum(valid, 1, keepdims=True), 1.0)
    mean = dot_nn(valid.astype(BF16), low) / count
    mean_ref[...] = mean
    lg_ref[...] = dot_nt(mean, flat_ref[...], HIGH)
    gp_ref[...] = dot_nn(low, w_ref[3]).astype(BF16)
    for i in range(3):
        pre = dot_nn(low, w_ref[i])
        pre_ref[i] = pre.astype(BF16)
        ext_ref[i, HALO : HALO + rows, :] = pre
        conv = conv_ref[i, 0:1, :] * pre
        for j in range(1, conv_ref.shape[1]):
            conv = conv + conv_ref[i, j : j + 1, :] * ext_ref[i, HALO - j : HALO - j + rows, :]
        ext_ref[i, 0:HALO, :] = pre[rows - HALO :, :]
        act = conv * jax.nn.sigmoid(conv)
        if i < 2:
            act = act * lax.rsqrt(head_sum(act * act, blocks) + UNIT_EPS)
        act_low = act.astype(BF16)
        (q_ref, k_ref, v_ref)[i][...] = act_low
        if i == 1:
            kt_ref[...] = jnp.transpose(act_low.astype(F32)).astype(BF16)


def mix_kernel(block, blocks_all, shift, first, last, *refs):
    it = iter(refs)
    seq_ref, lg_ref, q_ref, k_ref, v_ref, kt_ref, pers_ref, gp_ref, a_ref, bt_ref = (
        next(it) for _ in range(10)
    )
    sa_ref, sbt_ref = (None, None) if first or last else (next(it), next(it))
    mixed_ref, tot_out_ref, att_out_ref, lt_ref = (next(it) for _ in range(4))
    if not last:
        a2_ref, bt2_ref, sa2_ref, sbt2_ref, ga_ref, gbt_ref = (next(it) for _ in range(6))
    tot_ref, att_ref, linv_ref = (next(it) for _ in range(3))
    if not last:
        z_ref, r_ref = next(it), next(it)
    rows, cols = q_ref.shape
    head_size = 1 << shift
    heads = cols // head_size
    a_low = a_ref[...].astype(BF16)
    bt_low = bt_ref[...].astype(BF16)
    valid, count = valid_column(seq_ref, block * rows, rows)
    weight = valid / count
    att_ref[...] = jnp.zeros((rows, cols), F32)
    linv_ref[...] = jnp.zeros((rows, cols), F32)
    tot_ref[...] = jnp.zeros((rows, cols), F32)
    if not last:
        r_ref[...] = jnp.zeros((rows, cols), F32)

    def one_head(head, carry):
        mask = head_mask(cols, shift, head)
        mask_low = mask.astype(BF16)
        ones_low = (1.0 - mask).astype(BF16)
        query = q_ref[...] * mask_low
        scaled = query * SCORE_SCALE
        raised = jnp.exp(dot_nt(scaled, pers_ref[0])).astype(BF16)
        total = dot_nn(raised, pers_ref[1] * mask_low + ones_low)
        for j in range(block + 1):
            span = slice(j * rows, (j + 1) * rows)
            raised = jnp.exp(dot_nt(scaled, k_ref[span, :]))
            if j == block:
                raised = jnp.where(
                    iota((rows, rows), 0) >= iota((rows, rows), 1), raised, 0.0
                )
            total = total + dot_nn(raised.astype(BF16), v_ref[span, :] * mask_low + ones_low)
        inverse = 1.0 / pltpu.roll(total, head_size, 1)
        inside = jnp.broadcast_to(mask, (rows, cols)) > 0.5
        linv_ref[...] = jnp.where(inside, inverse, linv_ref[...])
        attended = jnp.where(inside, total * inverse, 0.0)
        att_ref[...] = att_ref[...] + attended
        hid = dot_nn(query, a_low)
        hid = hid * jax.nn.sigmoid(hid)
        recalled = dot_nt(hid.astype(BF16), bt_low) * mask
        tot_ref[...] = tot_ref[...] + attended + recalled
        if not last:
            hid = dot_nn(k_ref[block * rows : (block + 1) * rows, :] * mask_low, a_low)
            sig = jax.nn.sigmoid(hid)
            act = (hid * sig).astype(BF16)
            z_ref[head] = act
            target = v_ref[block * rows : (block + 1) * rows, :].astype(F32)
            resid = (dot_nt(act, bt_low) - target) * mask * weight
            r_ref[...] = r_ref[...] + resid
            d_hid = dot_nn(resid.astype(BF16), bt_low) * (sig * (1.0 + hid * (1.0 - sig)))
            at = pl.ds(pl.multiple_of(head * head_size, head_size), head_size)
            ga_ref[at, :] = dot_nn(kt_ref[at, :], d_hid.astype(BF16))
        return carry

    lax.fori_loop(0, heads, one_head, 0)
    gate = jax.nn.sigmoid(gp_ref[...].astype(F32))
    mixed_ref[...] = (tot_ref[...] * gate).astype(BF16)
    tot_out_ref[...] = tot_ref[...].astype(BF16)
    att_out_ref[...] = att_ref[...].astype(BF16)
    start = iota((8, cols), 1) == (iota((8, cols), 0) << shift)
    lt_ref[...] = dot_nt(jnp.where(start, 1.0, 0.0), linv_ref[...], HIGH)
    if not last:
        resid_t = jnp.transpose(r_ref[...]).astype(BF16)
        for head in range(heads):
            at = slice(head * head_size, (head + 1) * head_size)
            gbt_ref[at, :] = dot_nn(resid_t[at, :], z_ref[head])
        width = a_ref.shape[1]
        logits = lg_ref[...]
        step = 0.2 * jax.nn.sigmoid(gate_rows(logits, 0, heads, head_size, width))
        keep = jax.nn.sigmoid(gate_rows(logits, 1, heads, head_size, width))
        stay = 1.0 - 0.5 * jax.nn.sigmoid(gate_rows(logits, 2, heads, head_size, width))
        moment_a = -step * ga_ref[...]
        moment_b = -step * gbt_ref[...]
        if not first:
            moment_a = moment_a + keep * sa_ref[...]
            moment_b = moment_b + keep * sbt_ref[...]
        sa2_ref[...] = moment_a
        sbt2_ref[...] = moment_b
        a2_ref[...] = stay * a_ref[...] + moment_a
        bt2_ref[...] = stay * bt_ref[...] + moment_b


def lead_kernel(low, count, nb, shift, *refs):
    it = iter(refs)
    take = lambda n: [next(it) for _ in range(n)]
    final = low + count == nb
    prep_in = take(7)
    k_in_ref, v_in_ref, edge_in_ref = take(3) if low else [None] * 3
    state = take(4 if 0 < low < nb - 1 else 2)
    if low:
        take(12)
    prep_out, kept, (mixed_ref, pers_ref, flat_ref) = take(9), take(3), take(3)
    blocks = range(low, low + count)
    squares = [take(6) if block < nb - 1 else [] for block in blocks]
    k_out_ref, v_out_ref, edge_out_ref = [None] * 3 if final else take(3)
    ext_ref, k_all_ref, v_all_ref = take(3)
    room, more = take(3), take(0 if low == nb - 1 else 2)
    step = pl.program_id(0)
    q_ref, k_ref, v_ref, kt_ref, _, gp_ref, _, _, lg_ref = prep_out
    rows = q_ref.shape[0]
    prep_kernel(shift, low, *prep_in, edge_in_ref, *prep_out, pers_ref, flat_ref, ext_ref)
    for i, block in enumerate(blocks):

        @pl.when(step == i)
        def _(i=i, block=block):
            if low and i == 0:
                k_all_ref[0 : low * rows, :] = k_in_ref[...]
                v_all_ref[0 : low * rows, :] = v_in_ref[...]
            own = slice(block * rows, (block + 1) * rows)
            k_all_ref[own, :] = k_ref[...]
            v_all_ref[own, :] = v_ref[...]
            first, last = block == 0, block == nb - 1
            now = squares[i - 1][:4] if i else state
            now = now[:2] if first or last else now
            mix_kernel(
                block, nb, shift, first, last, prep_in[0], lg_ref, q_ref, k_all_ref, v_all_ref,
                kt_ref, pers_ref, gp_ref, *now, mixed_ref, *kept, *squares[i], *room,
                *([] if last else more),
            )
            if i == count - 1 and not final:
                done = (low + count) * rows
                k_out_ref[...] = k_all_ref[0:done, :]
                v_out_ref[...] = v_all_ref[0:done, :]
                edge_out_ref[...] = ext_ref[:, 0:HALO, :]


def lead_call(blocks, nb, shift, seq, x, w, conv, gains, gate, pers, state, carried, shared):
    rows, width = x.shape
    cols = w.shape[2]
    low, count = blocks[0], len(blocks)
    final = low + count == nb
    gates = 3 * gate.shape[1]
    mem_hid = state[0].shape[1]
    square = (cols, mem_hid)
    once = pl.Buffered(1)
    fixed = lambda a: pl.BlockSpec(a.shape, lambda c, n=len(a.shape): (0,) * n, pipeline_mode=once)
    whole = lambda a: pl.BlockSpec(a.shape, lambda c, n=len(a.shape): (0,) * n)
    at_rows = lambda n: pl.BlockSpec((SPAN, n), lambda c: (low + c, 0))
    eight = lambda n: pl.BlockSpec((8, n), lambda c: (low + c, 0))
    struct = jax.ShapeDtypeStruct
    ins = [seq, x, w, conv, gains, gate, pers, *carried, *state]
    in_specs = [pl.BlockSpec(memory_space=pltpu.SMEM), at_rows(width)]
    in_specs += [fixed(a) for a in ins[2:]]
    aliases = {}
    if shared:
        aliases = {len(ins) + n: n for n in range(len(shared))}
        ins += shared
        in_specs += [pl.BlockSpec(memory_space=pl.ANY)] * len(shared)
    outs = [struct((rows, cols), BF16)] * 3 + [
        struct((cols, rows), BF16),
        struct((3, rows, cols), BF16),
        struct((rows, cols), BF16),
        struct((rows, width), BF16),
        struct((nb * 8, width), F32),
        struct((nb * 8, gates), F32),
        struct((rows, cols), BF16),
        struct((rows, cols), BF16),
        struct((8, rows), F32),
        struct((count * SPAN, cols), BF16),
        struct(pers.shape, BF16),
        struct((gates, width), F32),
    ]
    out_specs = [at_rows(cols)] * 3 + [
        pl.BlockSpec((cols, SPAN), lambda c: (0, low + c)),
        pl.BlockSpec((3, SPAN, cols), lambda c: (0, low + c, 0)),
        at_rows(cols),
        at_rows(width),
        eight(width),
        eight(gates),
        at_rows(cols),
        at_rows(cols),
        pl.BlockSpec((8, SPAN), lambda c: (0, low + c)),
        pl.BlockSpec((SPAN, cols), lambda c: (c, 0)),
        whole(pers),
        pl.BlockSpec((gates, width), lambda c: (0, 0)),
    ]
    updates = [block for block in blocks if block < nb - 1]
    more = [struct(square, F32)] * (6 * len(updates))
    if not final:
        done = ((low + count) * SPAN, cols)
        more += [struct(done, BF16), struct(done, BF16), struct((3, HALO, cols), F32)]
    scratch = [
        pltpu.VMEM((3, HALO + SPAN, cols), F32),
        pltpu.VMEM((rows, cols), BF16),
        pltpu.VMEM((rows, cols), BF16),
    ] + [pltpu.VMEM((SPAN, cols), F32)] * 3
    if updates:
        heads = cols >> shift
        scratch += [pltpu.VMEM((heads, SPAN, mem_hid), BF16), pltpu.VMEM((SPAN, cols), F32)]
    got = pl.pallas_call(
        functools.partial(lead_kernel, low, count, nb, shift),
        grid=(count,),
        in_specs=in_specs,
        out_specs=out_specs + [whole(a) for a in more],
        out_shape=outs + more,
        input_output_aliases=aliases,
        scratch_shapes=scratch,
        cost_estimate=cost(11 * count),
        name=f"lead_{low}",
    )(*ins)
    at = 15 + 6 * len(updates)
    squares = [got[n : n + 6] for n in range(15, at, 6)]
    return got[:12], got[12:15], squares, got[at:]


def cot_kernel(peer_ref, c0_ref, c1_ref, c2_ref, c3_ref, fout_ref, full_ref, dh_ref):
    cols = c0_ref.shape[1]
    for j, piece_ref in enumerate((c0_ref, c1_ref, c2_ref, c3_ref)):
        at = pl.ds(pl.multiple_of(peer_ref[j] * cols, cols), cols)
        full_ref[:, at] = piece_ref[...]
    dh_ref[...] = dot_nt(full_ref[...], fout_ref[...]).astype(BF16)


def cot_call(peers, cot, fout):
    rows, cols = cot[0].shape
    hidden, width = fout.shape
    row = lambda n: pl.BlockSpec((SPAN, n), lambda i: (i, 0))
    return pl.pallas_call(
        cot_kernel,
        grid=(rows // SPAN,),
        in_specs=[pl.BlockSpec(memory_space=pltpu.SMEM)]
        + [row(cols)] * 4
        + [pl.BlockSpec(fout.shape, lambda i: (0, 0), pipeline_mode=pl.Buffered(1))],
        out_specs=[row(width), row(hidden)],
        out_shape=[
            jax.ShapeDtypeStruct((rows, width), BF16),
            jax.ShapeDtypeStruct((rows, hidden), BF16),
        ],
        cost_estimate=cost(6),
        name="cot",
    )(peers, *cot, fout)


def ffn_kernel(groups, *refs):
    it = iter(refs)
    take = lambda n: [next(it) for _ in range(n)]
    peer_ref, x_ref = take(2)
    piece_refs = [take(4) for _ in groups]
    gain_ref, dh_ref = take(2)
    weights = take(5)
    nt_out, hid_ref, dgu_ref, mfull_out, res_out, _ = take(6)
    held = take(5)
    nt_ref, mfull_ref, res_ref = take(3)
    weight_sems, out_sems = take(2)
    step = pl.program_id(0)
    rows, cols = piece_refs[0][0].shape
    loads = [
        pltpu.make_async_copy(source, target, weight_sems.at[n])
        for n, (source, target) in enumerate(zip(weights, held))
    ]
    fin_ref, ow_refs = held[4], held[:4]
    mine = pl.ds(pl.multiple_of(step * rows, rows), rows)
    stores = [
        pltpu.make_async_copy(source, target.at[mine, :], out_sems.at[n])
        for n, (source, target) in enumerate(
            ((mfull_ref, mfull_out), (res_ref, res_out), (nt_ref, nt_out))
        )
    ]

    @pl.when(step == 0)
    def _():
        for load in loads:
            load.start()

    def ready(some):
        @pl.when(step == 0)
        def _():
            for load in some:
                load.wait()

    @pl.when(step > 0)
    def _():
        for store in stores:
            store.wait()

    spots = [pl.ds(pl.multiple_of(peer_ref[j] * cols, cols), cols) for j in range(4)]
    for n, blocks in enumerate(groups):

        @pl.when((step >= blocks[0]) & (step <= blocks[-1]))
        def _(n=n):
            for j in range(4):
                mfull_ref[:, spots[j]] = piece_refs[n][j][...]

    stores[0].start()
    ready(loads[:4])
    mixed = mfull_ref[...]
    for j in range(4):
        branch = dot_nn(mixed, ow_refs[j][...])
        res_ref[:, spots[j]] = x_ref[:, spots[j]].astype(F32) + branch
    stores[1].start()
    residual = res_ref[...]
    scale = lax.rsqrt(jnp.mean(residual * residual, -1, keepdims=True) + NORM_EPS)
    low_rows = (residual * scale * gain_ref[1:2, :]).astype(BF16)
    nt_ref[...] = low_rows
    stores[2].start()
    ready(loads[4:])
    gate_pre = dot_nn(low_rows, fin_ref[0])
    up_pre = dot_nn(low_rows, fin_ref[1])
    sig = jax.nn.sigmoid(gate_pre)
    silu = gate_pre * sig
    hid_ref[...] = (silu * up_pre).astype(BF16)
    slope = sig * (1.0 + gate_pre * (1.0 - sig))
    d_hidden = dh_ref[...].astype(F32)
    dgu_ref[0] = (d_hidden * up_pre * slope).astype(BF16)
    dgu_ref[1] = (d_hidden * silu).astype(BF16)

    @pl.when(step == pl.num_programs(0) - 1)
    def _():
        for store in stores:
            store.wait()


def ffn_call(groups, peers, x, pieces, ow, gains, fin, dh):
    rows, width = x.shape
    cols = pieces[0][0].shape[1]
    hidden = dh.shape[1]
    at_rows = lambda n: pl.BlockSpec((SPAN, n), lambda i: (i, 0))
    anywhere = pl.BlockSpec(memory_space=pl.ANY)
    struct = jax.ShapeDtypeStruct
    ins = [peers, x, *[piece for group in pieces for piece in group], gains, dh, *ow, fin]
    in_specs = [pl.BlockSpec(memory_space=pltpu.SMEM), at_rows(width)]
    for blocks in groups:
        spot = lambda i, low=blocks[0], n=len(blocks): (jnp.clip(i - low, 0, n - 1), 0)
        in_specs += [pl.BlockSpec((SPAN, cols), spot)] * 4
    in_specs += [pl.BlockSpec(gains.shape, lambda i: (0, 0)), at_rows(hidden)] + [anywhere] * 5
    return pl.pallas_call(
        functools.partial(ffn_kernel, groups),
        grid=(rows // SPAN,),
        in_specs=in_specs,
        out_specs=[
            anywhere,
            at_rows(hidden),
            pl.BlockSpec((2, SPAN, hidden), lambda i: (0, i, 0)),
            anywhere,
            anywhere,
            anywhere,
        ],
        out_shape=[
            struct((rows, width), BF16),
            struct((rows, hidden), BF16),
            struct((2, rows, hidden), BF16),
            struct((rows, width), BF16),
            struct((rows, width), F32),
            struct((3 * width, width), BF16),
        ],
        scratch_shapes=[pltpu.VMEM(piece.shape, BF16) for piece in (*ow, fin)]
        + [pltpu.VMEM((SPAN, width), BF16)] * 2
        + [pltpu.VMEM((SPAN, width), F32)]
        + [pltpu.SemaphoreType.DMA((5,)), pltpu.SemaphoreType.DMA((3,))],
        cost_estimate=cost(22),
        name="ffn",
    )(*ins)


def ffn_back_kernel(first_call, *refs):
    it = iter(refs)
    take = lambda n: [next(it) for _ in range(n)]
    peer_ref, dgu_ref, fin_ref, res_ref = take(4)
    gg_in_ref = None if first_call else take(1)[0]
    gg_ref, keep_ref, send_ref, part_ref = take(4)
    width = res_ref.shape[1]
    residual = res_ref[...]
    scale = lax.rsqrt(jnp.mean(residual * residual, -1, keepdims=True) + NORM_EPS)
    d_normed = dot_nt(dgu_ref[0], fin_ref[0]) + dot_nt(dgu_ref[1], fin_ref[1])
    gains = jnp.sum(d_normed * residual * scale, 0, keepdims=True)

    @pl.when(pl.program_id(0) == 0)
    def _():
        gg_ref[...] = jnp.zeros(gg_ref.shape, F32) if first_call else gg_in_ref[...]

    gg_ref[...] = gg_ref[...] + jnp.broadcast_to(gains, gg_ref.shape)
    half = width // 2
    part_ref[...] = d_normed.astype(BF16)
    core = peer_ref[0] & 1
    keep_ref[...] = part_ref[:, pl.ds(pl.multiple_of(core * half, half), half)]
    send_ref[...] = part_ref[:, pl.ds(pl.multiple_of((1 - core) * half, half), half)]


def ffn_back_call(blocks, peers, dgu, fin, res, gains):
    width = res.shape[1]
    tile = SPAN // 2
    steps = SPAN // tile
    low = blocks[0] * steps
    lines = len(blocks) * SPAN
    gain_spec = pl.BlockSpec((8, width), lambda i: (0, 0))
    row = pl.BlockSpec((tile, width // 2), lambda i: (i, 0))
    struct = jax.ShapeDtypeStruct
    return pl.pallas_call(
        functools.partial(ffn_back_kernel, gains is None),
        grid=(len(blocks) * steps,),
        in_specs=[
            pl.BlockSpec(memory_space=pltpu.SMEM),
            pl.BlockSpec((2, tile, dgu.shape[2]), lambda i: (0, low + i, 0)),
            pl.BlockSpec(fin.shape, lambda i: (0, 0, 0), pipeline_mode=pl.Buffered(1)),
            pl.BlockSpec((tile, width), lambda i: (low + i, 0)),
        ]
        + ([] if gains is None else [gain_spec]),
        out_specs=[gain_spec, row, row],
        out_shape=[
            struct((8, width), F32),
            struct((lines, width // 2), BF16),
            struct((lines, width // 2), BF16),
        ],
        scratch_shapes=[pltpu.VMEM((tile, width), BF16)],
        cost_estimate=cost(4 * len(blocks)),
        name=f"ffn_back_{blocks[0]}",
    )(peers, dgu, fin, res, *([] if gains is None else [gains]))


def down_kernel(peer_ref, hid_ref, fout_ref, keep_ref, send_ref, part_ref):
    cols = keep_ref.shape[2]
    part_ref[...] = dot_nn(hid_ref[...], fout_ref[...]).astype(BF16)
    for slot, out_ref in ((0, keep_ref), (1, send_ref)):
        for n in range(2):
            start = pl.multiple_of(peer_ref[slot + 2 * n] * cols, cols)
            out_ref[n] = part_ref[:, pl.ds(start, cols)]


def down_call(peers, hid, fout, cols):
    rows, hidden = hid.shape
    width = fout.shape[1]
    stacked = pl.BlockSpec((2, SPAN, cols), lambda i: (0, i, 0))
    return pl.pallas_call(
        down_kernel,
        grid=(rows // SPAN,),
        in_specs=[
            pl.BlockSpec(memory_space=pltpu.SMEM),
            pl.BlockSpec((SPAN, hidden), lambda i: (i, 0)),
            pl.BlockSpec(fout.shape, lambda i: (0, 0), pipeline_mode=pl.Buffered(1)),
        ],
        out_specs=[stacked, stacked],
        out_shape=[jax.ShapeDtypeStruct((2, rows, cols), BF16)] * 2,
        scratch_shapes=[pltpu.VMEM((SPAN, width), BF16)],
        cost_estimate=cost(6),
        name="down",
    )(peers, hid, fout)


def turn_kernel(first_call, *refs):
    it = iter(refs)
    take = lambda n: [next(it) for _ in range(n)]
    peer_ref, s1_ref, r2_ref, ps1_ref, pr2_ref, res_ref, cot_ref = take(7)
    gain_ref, gp_ref = take(2)
    ow_refs = take(4)
    (tot_ref,) = take(1)
    if not first_call:
        take(4)
    dres_ref, rescol_ref, dbr_ref, dgall_ref, dga_ref, dgp_ref, full_ref = take(7)
    rows, width = res_ref.shape
    cols = gp_ref.shape[1]
    half = width // 2
    core = peer_ref[0] & 1
    at_own = pl.ds(pl.multiple_of(core * half, half), half)
    at_other = pl.ds(pl.multiple_of((1 - core) * half, half), half)
    full_ref[:, at_own] = s1_ref[...].astype(F32) + r2_ref[...].astype(F32)
    full_ref[:, at_other] = ps1_ref[...].astype(F32) + pr2_ref[...].astype(F32)
    residual = res_ref[...]
    scale = lax.rsqrt(jnp.mean(residual * residual, -1, keepdims=True) + NORM_EPS)
    gained = full_ref[...] * gain_ref[1:2, :]
    inner = jnp.sum(gained * residual, -1, keepdims=True) / width
    d_residual = cot_ref[...].astype(F32) + scale * gained - residual * (scale * scale * scale * inner)
    own = pl.ds(pl.multiple_of(peer_ref[0] * cols, cols), cols)
    full_ref[...] = d_residual
    d_mixed = None
    for j in range(4):
        at = pl.ds(pl.multiple_of(peer_ref[j] * cols, cols), cols)
        term = dot_nt(full_ref[:, at].astype(BF16), ow_refs[j][own, :])
        d_mixed = term if d_mixed is None else d_mixed + term
    mine = full_ref[:, own]
    dres_ref[...] = mine
    dbr_ref[...] = mine.astype(BF16)
    rescol_ref[...] = res_ref[:, own]
    gate = jax.nn.sigmoid(gp_ref[...].astype(F32))
    d_gated = d_mixed * gate
    dga_ref[...] = d_gated.astype(BF16)
    d_gate = (d_gated * tot_ref[...].astype(F32) * (1.0 - gate)).astype(BF16)
    dgp_ref[...] = d_gate
    dgall_ref[...] = d_gate


def turn_call(block, spot, peers, pieces, res, cot, ow, gains, gp, tot, shared):
    rows, cols = gp.shape
    width = res.shape[1]
    tile = SPAN // 2
    steps = SPAN // tile
    low = block * steps
    whole = lambda a: pl.BlockSpec(a.shape, lambda i, n=a.ndim: (0,) * n)
    row = lambda n: pl.BlockSpec((tile, n), lambda i: (i, 0))
    piece = pl.BlockSpec((tile, width // 2), lambda i: (spot * steps + i, 0))
    at_rows = lambda n: pl.BlockSpec((tile, n), lambda i: (low + i, 0))
    struct = jax.ShapeDtypeStruct
    ins = [peers, *pieces, res, cot, gains, gp, *ow, tot]
    in_specs = [
        pl.BlockSpec(memory_space=pltpu.SMEM),
        piece,
        piece,
        piece,
        piece,
        at_rows(width),
        at_rows(width),
        whole(gains),
        at_rows(cols),
    ] + [whole(weight) for weight in ow]
    in_specs.append(at_rows(cols))
    aliases = {}
    if shared is not None:
        aliases = {len(ins) + n: n for n in range(len(shared))}
        ins += shared
        in_specs += [pl.BlockSpec(memory_space=pl.ANY)] * len(shared)
    got = pl.pallas_call(
        functools.partial(turn_kernel, shared is None),
        grid=(steps,),
        in_specs=in_specs,
        out_specs=[at_rows(cols)] * 4 + [row(cols)] * 2,
        out_shape=[
            struct((rows, cols), F32),
            struct((rows, cols), F32),
            struct((rows, cols), BF16),
            struct((rows, cols), BF16),
            struct((SPAN, cols), BF16),
            struct((SPAN, cols), BF16),
        ],
        input_output_aliases=aliases,
        scratch_shapes=[pltpu.VMEM((tile, width), F32)],
        cost_estimate=cost(5),
        name=f"turn_{block}",
    )(*ins)
    return list(got[:4]), got[4:]


def back_kernel(block, nb, shift, *refs):
    it = iter(refs)
    take = lambda n: [next(it) for _ in range(n)]
    first, last = block == 0, block == nb - 1
    seq_ref, q_ref, k_ref, v_ref, kt_ref, pers_ref, dga_ref, att_ref, lt_ref = take(9)
    a_ref, bt_ref = take(2)
    if not last:
        dk_in_ref, dv_in_ref, dp_in_ref, lg_ref, ga_ref, gbt_ref, ab_in_ref, btb_in_ref = take(8)
        sab_in_ref, sbtb_in_ref = take(2) if block < nb - 2 else (None, None)
        sa_ref, sbt_ref = (None, None) if first else take(2)
    dq_ref, dk_ref, dv_ref, dp_ref, ab_ref, btb_ref = take(6)
    if not last:
        (dlg_ref,) = take(1)
        sab_ref, sbtb_ref = (None, None) if first else take(2)
    dt_ref, dqt_ref, qt_ref, dot_ref = take(4)
    if not last:
        z_ref, zd_ref, r_ref, y_ref, h_ref = take(5)
    rows, cols = q_ref.shape
    head_size = 1 << shift
    heads = cols // head_size
    own = slice(block * rows, (block + 1) * rows)
    a_low = a_ref[...].astype(BF16)
    bt_low = bt_ref[...].astype(BF16)
    if last:
        dk_ref[...] = jnp.zeros(dk_ref.shape, F32)
        dv_ref[...] = jnp.zeros(dv_ref.shape, F32)
        dp_ref[...] = jnp.zeros(dp_ref.shape, F32)
        ab_ref[...] = jnp.zeros(ab_ref.shape, F32)
        btb_ref[...] = jnp.zeros(btb_ref.shape, F32)
    else:
        dk_ref[...] = dk_in_ref[...]
        dv_ref[...] = dv_in_ref[...]
        dp_ref[...] = dp_in_ref[...]
    pick = (iota((8, cols), 1) >> shift) == iota((8, cols), 0)
    d_gated = dga_ref[...].astype(F32)
    dt_ref[...] = dot_nt(jnp.where(pick, 1.0, 0.0), d_gated * att_ref[...].astype(F32), HIGH)
    dq_ref[...] = jnp.zeros((rows, cols), F32)
    qt_ref[...] = jnp.transpose(q_ref[...].astype(F32)).astype(BF16)
    dot_ref[...] = jnp.transpose(d_gated).astype(BF16)
    if not last:
        valid, count = valid_column(seq_ref, block * rows, rows)
        weight = valid / count
        width = a_ref.shape[1]
        logits = lg_ref[...]
        sig_step = jax.nn.sigmoid(gate_rows(logits, 0, heads, head_size, width))
        keep = jax.nn.sigmoid(gate_rows(logits, 1, heads, head_size, width))
        sig_forget = jax.nn.sigmoid(gate_rows(logits, 2, heads, head_size, width))
        tot_a, tot_b = ab_in_ref[...], btb_in_ref[...]
        if sab_in_ref is not None:
            tot_a, tot_b = tot_a + sab_in_ref[...], tot_b + sbtb_in_ref[...]
        h_ref[0] = (-0.2 * sig_step * tot_a).astype(BF16)
        h_ref[1] = (-0.2 * sig_step * tot_b).astype(BF16)
        d_step = -(ga_ref[...] * tot_a + gbt_ref[...] * tot_b)
        groups = [d_step * (0.2 * sig_step * (1.0 - sig_step)), None, None]
        if not first:
            groups[1] = (sa_ref[...] * tot_a + sbt_ref[...] * tot_b) * (keep * (1.0 - keep))
        d_forget = -(a_ref[...] * ab_in_ref[...] + bt_ref[...] * btb_in_ref[...])
        groups[2] = d_forget * (0.5 * sig_forget * (1.0 - sig_forget))
        d_logits = jnp.zeros(dlg_ref.shape, F32)
        for g, value in enumerate(groups):
            if value is None:
                continue
            for head in range(heads):
                part = value[head * head_size : (head + 1) * head_size, :]
                figure = jnp.sum(jnp.sum(part, 1, keepdims=True), 0, keepdims=True)
                here = iota(dlg_ref.shape, 1) == g * heads + head
                d_logits = d_logits + jnp.where(here, 1.0, 0.0) * figure
        dlg_ref[...] = d_logits
        stay = 1.0 - 0.5 * sig_forget
        ab_ref[...] = stay * ab_in_ref[...]
        btb_ref[...] = stay * btb_in_ref[...]
        if not first:
            sab_ref[...] = keep * tot_a
            sbtb_ref[...] = keep * tot_b
        r_ref[...] = jnp.zeros((rows, cols), F32)
        y_ref[...] = jnp.zeros((rows, cols), F32)

    def one_head(head, carry):
        mask = head_mask(cols, shift, head)
        mask_low = mask.astype(BF16)
        query = q_ref[...] * mask_low
        scaled = query * SCORE_SCALE
        d_out = dga_ref[...] * mask_low
        at = pl.ds(pl.multiple_of(head * head_size, head_size), head_size)
        inverse = lt_ref[pl.ds(head, 1), :]
        delta = dt_ref[pl.ds(head, 1), :]
        probs = jnp.exp(dot_nt(pers_ref[0], scaled)) * inverse
        d_scores = (probs * (dot_nt(pers_ref[1], d_out) - delta)).astype(BF16)
        dp_ref[0] = dp_ref[0] + dot_nn(d_scores, scaled)
        dp_ref[1] = dp_ref[1] + dot_nn(probs.astype(BF16), d_out)
        d_query = lax.dot_general(
            d_scores, pers_ref[0], (((0,), (0,)), ((), ())), preferred_element_type=F32
        )
        d_query = d_query * SCORE_SCALE
        d_query_t = jnp.zeros((head_size, rows), F32)
        for j in range(block + 1):
            span = slice(j * rows, (j + 1) * rows)
            probs = jnp.exp(dot_nt(k_ref[span, :], scaled)) * inverse
            if j == block:
                probs = jnp.where(iota((rows, rows), 0) <= iota((rows, rows), 1), probs, 0.0)
            d_scores = (probs * (dot_nt(v_ref[span, :], d_out) - delta)).astype(BF16)
            dv_ref[span, :] = dv_ref[span, :] + dot_nn(probs.astype(BF16), d_out)
            dk_ref[span, :] = dk_ref[span, :] + dot_nn(d_scores, scaled)
            d_query_t = d_query_t + dot_nn(kt_ref[at, span], d_scores)
        dqt_ref[at, :] = d_query_t * SCORE_SCALE
        hid = dot_nn(query, a_low)
        sig = jax.nn.sigmoid(hid)
        d_hid = dot_nn(d_out, bt_low) * (sig * (1.0 + hid * (1.0 - sig)))
        d_hid = d_hid.astype(BF16)
        dq_ref[...] = dq_ref[...] + (d_query + dot_nt(d_hid, a_low)) * mask
        grad_a = dot_nn(qt_ref[at, :], d_hid)
        grad_b = dot_nn(dot_ref[at, :], (hid * sig).astype(BF16))
        if not last:
            key = k_ref[own, :] * mask_low
            hid = dot_nn(key, a_low)
            probe = dot_nn(key, h_ref[0])
            sig = jax.nn.sigmoid(hid)
            act = (hid * sig).astype(BF16)
            z_ref[head] = act
            slope = sig * (1.0 + hid * (1.0 - sig))
            curve = sig * (1.0 - sig) * (2.0 + hid * (1.0 - 2.0 * sig))
            target = v_ref[own, :].astype(F32)
            resid = (dot_nt(act, bt_low) - target) * mask * weight
            r_ref[...] = r_ref[...] + resid
            resid = resid.astype(BF16)
            d_act = dot_nn(resid, bt_low)
            d_slope = (probe * slope).astype(BF16)
            zd_ref[head] = d_slope
            d_net = (dot_nt(act, h_ref[1]) + dot_nt(d_slope, bt_low)) * mask * weight
            y_ref[...] = y_ref[...] + d_net
            back = dot_nn(resid, h_ref[1]) + dot_nn(d_net.astype(BF16), bt_low)
            d_hid = (probe * d_act * curve + back * slope).astype(BF16)
            direct = (d_act * slope).astype(BF16)
            d_key = (dot_nt(direct, h_ref[0]) + dot_nt(d_hid, a_low)) * mask
            dk_ref[own, :] = dk_ref[own, :] + d_key
            grad_a = grad_a + dot_nn(kt_ref[at, own], d_hid)
        ab_ref[at, :] = ab_ref[at, :] + grad_a
        btb_ref[at, :] = btb_ref[at, :] + grad_b
        return carry

    lax.fori_loop(0, heads, one_head, 0)
    dq_ref[...] = dq_ref[...] + jnp.transpose(dqt_ref[...])
    if not last:
        dv_ref[own, :] = dv_ref[own, :] - y_ref[...]
        resid_t = jnp.transpose(r_ref[...]).astype(BF16)
        net_t = jnp.transpose(y_ref[...]).astype(BF16)
        for head in range(heads):
            at = slice(head * head_size, (head + 1) * head_size)
            grad_b = dot_nn(resid_t[at, :], zd_ref[head]) + dot_nn(net_t[at, :], z_ref[head])
            btb_ref[at, :] = btb_ref[at, :] + grad_b


def back_parts(block, nb, shift, seq, q, k, v, kt, pers, dga, att, linv, state, grads, adjoint):
    cols = q.shape[1]
    heads = cols >> shift
    first, last = block == 0, block == nb - 1
    done = (block + 1) * SPAN
    whole = lambda s: pl.BlockSpec(s, lambda i, n=len(s): (0,) * n)
    at_block = pl.BlockSpec((SPAN, cols), lambda i: (block, 0))
    upto = pl.BlockSpec((done, cols), lambda i: (0, 0))
    square = state["a"].shape
    ins = [seq, q, k, v, kt, pers, dga, att, linv, state["a"], state["bt"]]
    in_specs = [
        pl.BlockSpec(memory_space=pltpu.SMEM),
        at_block,
        upto,
        upto,
        pl.BlockSpec((cols, done), lambda i: (0, 0)),
        whole(pers.shape),
        pl.BlockSpec((SPAN, cols), lambda i: (0, 0)),
        at_block,
        pl.BlockSpec((8, SPAN), lambda i: (0, block)),
        whole(square),
        whole(square),
    ]
    if not last:
        ins += [grads["dk"], grads["dv"], grads["dp"], state["lg"], state["ga"], state["gbt"]]
        ins += [adjoint["ab"], adjoint["btb"]]
        in_specs += [upto, upto, whole(pers.shape)]
        in_specs += [pl.BlockSpec((8, state["lg"].shape[1]), lambda i: (block, 0))]
        in_specs += [whole(square)] * 4
        if block < nb - 2:
            ins += [adjoint["sab"], adjoint["sbtb"]]
            in_specs += [whole(square)] * 2
        if not first:
            ins += [state["sa"], state["sbt"]]
            in_specs += [whole(square)] * 2
    names = ["dq", "dk", "dv", "dp", "ab", "btb"]
    shapes = [(SPAN, cols), (done, cols), (done, cols), pers.shape, square, square]
    if not last:
        names.append("dlg")
        shapes.append((8, state["lg"].shape[1]))
        if not first:
            names += ["sab", "sbtb"]
            shapes += [square, square]
    scratch = [
        pltpu.VMEM((8, SPAN), F32),
        pltpu.VMEM((cols, SPAN), F32),
        pltpu.VMEM((cols, SPAN), BF16),
        pltpu.VMEM((cols, SPAN), BF16),
    ]
    if not last:
        scratch += [
            pltpu.VMEM((heads, SPAN, square[1]), BF16),
            pltpu.VMEM((heads, SPAN, square[1]), BF16),
            pltpu.VMEM((SPAN, cols), F32),
            pltpu.VMEM((SPAN, cols), F32),
            pltpu.VMEM((2,) + square, BF16),
        ]
    return ins, in_specs, names, shapes, scratch


def back_call(block, nb, shift, *args):
    ins, in_specs, names, shapes, scratch = back_parts(block, nb, shift, *args)
    outs = pl.pallas_call(
        functools.partial(back_kernel, block, nb, shift),
        grid=(1,),
        in_specs=in_specs,
        out_specs=[pl.BlockSpec(s, lambda i, n=len(s): (0,) * n) for s in shapes],
        out_shape=[jax.ShapeDtypeStruct(s, F32) for s in shapes],
        scratch_shapes=scratch,
        cost_estimate=cost(17),
        name=f"back_{block}",
    )(*ins)
    return dict(zip(names, outs))


def unprep_kernel(block, nb, shift, *refs):
    it = iter(refs)
    take = lambda n: [next(it) for _ in range(n)]
    first, last = block == 0, block == nb - 1
    seq_ref, peer_ref, dq_ref, dk_ref, dv_ref, dgp_ref, pre_ref, w_ref, conv_ref = take(9)
    x_ref, gain_ref = take(2)
    halo_ref = None if first else take(1)[0]
    dp_ref, pers_ref, ab_ref, btb_ref, gain_two_ref = take(5) if first else [None] * 5
    if not last:
        edge_in_ref, dlg_ref, gate_ref, mean_ref = take(4)
        cg_in_ref, gg_in_ref, gate_in_ref = take(7)[:3]
    cg_ref, gg_ref, gate_out_ref = take(3)
    dproj_ref, keep_ref, send_ref, inner_ref, edge_ref = take(5)
    small_ref, gains_ref = take(2) if first else (None, None)
    ext_ref, dext_ref, low_ref = take(3)
    rows, cols = dq_ref.shape
    width = x_ref.shape[1]
    blocks = head_blocks(cols, shift)
    taps = conv_ref.shape[1]
    d_normed = dot_nt(dgp_ref[...], w_ref[3])
    dproj_ref[3] = dgp_ref[...]
    if last:
        cg_ref[...] = jnp.zeros(cg_ref.shape, F32)
        gg_ref[...] = jnp.zeros(gg_ref.shape, F32)
        gate_out_ref[...] = jnp.zeros(gate_out_ref.shape, F32)
    else:
        cg_ref[...] = cg_in_ref[...]
        gg_ref[...] = gg_in_ref[...]
    for i in range(3):
        pre = pre_ref[i].astype(F32)
        ext_ref[0:HALO, :] = jnp.zeros((HALO, cols), F32) if first else halo_ref[i, HALO:, :].astype(F32)
        ext_ref[HALO : HALO + rows, :] = pre
        shifted = [pre] + [ext_ref[HALO - j : HALO - j + rows, :] for j in range(1, taps)]
        conv = conv_ref[i, 0:1, :] * pre
        for j in range(1, taps):
            conv = conv + conv_ref[i, j : j + 1, :] * shifted[j]
        sig = jax.nn.sigmoid(conv)
        d_act = (dq_ref, dk_ref, dv_ref)[i][...]
        if i < 2:
            act = conv * sig
            scale = lax.rsqrt(head_sum(act * act, blocks) + UNIT_EPS)
            d_act = scale * (d_act - act * (scale * scale * head_sum(d_act * act, blocks)))
        d_conv = d_act * (sig * (1.0 + conv * (1.0 - sig)))
        edge_ref[i] = d_conv[0:HALO, :]
        dext_ref[0:rows, :] = d_conv
        dext_ref[rows : rows + HALO, :] = (
            jnp.zeros((HALO, cols), F32) if last else edge_in_ref[i]
        )
        d_pre = conv_ref[i, 0:1, :] * d_conv
        for j in range(taps):
            if j:
                d_pre = d_pre + conv_ref[i, j : j + 1, :] * dext_ref[j : j + rows, :]
            at = slice(i * taps + j, i * taps + j + 1)
            cg_ref[at, :] = cg_ref[at, :] + jnp.sum(d_conv * shifted[j], 0, keepdims=True)
        d_low = d_pre.astype(BF16)
        dproj_ref[i] = d_low
        d_normed = d_normed + dot_nt(d_low, w_ref[i])
    if not last:
        valid, count = valid_column(seq_ref, block * rows, rows)
        d_mean = jnp.dot(
            dlg_ref[...], gate_ref[...], preferred_element_type=F32, precision=HIGH
        )
        d_normed = d_normed + (valid / count) * d_mean[0:1, :]
        outer = lax.dot_general(
            dlg_ref[...] * 0.125,
            mean_ref[...],
            (((0,), (0,)), ((), ())),
            preferred_element_type=F32,
            precision=HIGH,
        )
        gate_out_ref[...] = gate_in_ref[...]
        at = slice(0, outer.shape[0])
        gate_out_ref[at, :] = gate_in_ref[at, :] + outer
    x = x_ref[...].astype(F32)
    scale = lax.rsqrt(jnp.mean(x * x, -1, keepdims=True) + NORM_EPS)
    weighted = d_normed * x
    gains = jnp.sum(weighted * scale, 0, keepdims=True)
    gg_ref[...] = gg_ref[...] + jnp.broadcast_to(gains, gg_ref.shape)
    gained = jnp.broadcast_to(gain_ref[0:1, :], (8, width))
    inner_ref[...] = dot_nt(gained.astype(BF16), weighted.astype(BF16))
    low_ref[...] = d_normed.astype(BF16)
    for slot, out_ref in ((0, keep_ref), (1, send_ref)):
        for n in range(2):
            start = pl.multiple_of(peer_ref[slot + 2 * n] * cols, cols)
            out_ref[n] = low_ref[:, pl.ds(start, cols)]
    if first:
        keys = pers_ref[0]
        d_keys = dp_ref[0]
        scale = lax.rsqrt(head_sum(keys * keys, blocks) + UNIT_EPS)
        along = head_sum(d_keys * keys, blocks)
        d_keys = scale * (d_keys - keys * (scale * scale * along))
        across = lambda a: [a[:, n : n + cols] for n in range(0, width, cols)]
        parts = [ab_ref[...], btb_ref[...], *across(gate_out_ref[...]), cg_ref[...]]
        parts += [d_keys, dp_ref[1]]
        at = 0
        for part in parts:
            small_ref[at : at + part.shape[0], :] = part.astype(BF16)
            at += part.shape[0]
        gains_ref[0:1, :] = gg_ref[0:1, :]
        gains_ref[1:2, :] = gain_two_ref[0:1, :]
        small_ref[at:, :] = jnp.zeros((small_ref.shape[0] - at, cols), BF16)


def unprep_call(
    block, nb, shift, seq, peers, back, dgp, pre, w, conv, x, gains, gate, mean, pers, gain_two,
    shared,
):
    rows, width = x.shape
    cols = dgp.shape[1]
    first, last = block == 0, block == nb - 1
    whole = lambda a: pl.BlockSpec(a.shape, lambda i, n=len(a.shape): (0,) * n)
    smem = pl.BlockSpec(memory_space=pltpu.SMEM)
    at_block = pl.BlockSpec((SPAN, cols), lambda i: (block, 0))
    stacked = lambda n: pl.BlockSpec((n, SPAN, cols), lambda i: (0, block, 0))
    struct = jax.ShapeDtypeStruct
    gate_rows_out = 16
    names = ["cg", "gg", "gate", "dproj", "keep", "send", "inner", "edge"]
    outs = [
        struct((16, cols), F32),
        struct((8, width), F32),
        struct((gate_rows_out, width), F32),
        struct((4, rows, cols), BF16),
        struct((2, rows, cols), BF16),
        struct((2, rows, cols), BF16),
        struct((8, rows), F32),
        struct((3, HALO, cols), F32),
    ]
    out_specs = [whole(a) for a in outs[:3]]
    out_specs += [
        stacked(4),
        stacked(2),
        stacked(2),
        pl.BlockSpec((8, SPAN), lambda i: (0, block)),
        whole(outs[7]),
    ]
    ins = [seq, peers, back["dq"], back["dk"], back["dv"], dgp, pre, w, conv, x, gains]
    in_specs = [
        smem,
        smem,
        whole(back["dq"]),
        at_block,
        at_block,
        pl.BlockSpec((SPAN, cols), lambda i: (0, 0)),
        stacked(3),
        whole(w),
        whole(conv),
        pl.BlockSpec((SPAN, width), lambda i: (block, 0)),
        whole(gains),
    ]
    aliases = {}
    if not first:
        ins.append(pre)
        in_specs.append(
            pl.BlockSpec((3, 2 * HALO, cols), lambda i: (0, block * (SPAN // HALO // 2) - 1, 0))
        )
    else:
        others = [back["dp"], pers, back["ab"], back["btb"], gain_two]
        ins += others
        in_specs += [whole(a) for a in others]
        names += ["small", "gains"]
        ahead = 5 * width // SMALL_ROWS
        outs.append(struct(((ahead + 1) * SMALL_ROWS, cols), BF16))
        out_specs.append(pl.BlockSpec((SMALL_ROWS, cols), lambda i: (ahead, 0)))
        outs.append(struct((2, width), F32))
        out_specs.append(whole(outs[-1]))
    if not last:
        ins += [shared["edge"], back["dlg"], gate, mean]
        in_specs += [whole(shared["edge"]), whole(back["dlg"]), whole(gate)]
        in_specs.append(pl.BlockSpec((8, width), lambda i: (block, 0)))
        aliases = {len(ins) + n: n for n in range(7)}
        ins += [shared[name] for name in names[:7]]
        in_specs += [whole(a) for a in outs[:3]] + [pl.BlockSpec(memory_space=pl.ANY)] * 4
    got = pl.pallas_call(
        functools.partial(unprep_kernel, block, nb, shift),
        grid=(1,),
        in_specs=in_specs,
        out_specs=out_specs,
        out_shape=outs,
        input_output_aliases=aliases,
        scratch_shapes=[
            pltpu.VMEM((HALO + SPAN, cols), F32),
            pltpu.VMEM((SPAN + HALO, cols), F32),
            pltpu.VMEM((SPAN, width), BF16),
        ],
        cost_estimate=cost(10),
        name=f"unprep_{block}",
    )(*ins)
    return dict(zip(names, got))


def rear_kernel(block, nb, shift, counts, *refs):
    it = iter(refs)
    take = lambda n: [next(it) for _ in range(n)]
    first = block == 0
    back_in = take(counts[0])
    peer_ref, dgp_ref, pre_any, w_any, conv_ref, x_any, gain_ref = take(7)
    halo = take(0 if first else 1)
    pers_ref, gain_two_ref = take(2) if first else (None, None)
    edge_in_ref, gate_ref, mean_ref = take(3)
    before = take(7)
    dk_out_ref, dv_out_ref = (None, None) if first else take(2)
    sums = [] if first else take(5)
    results = take(10 if first else 8)
    dq_ref, dk_ref, dv_ref, dlg_ref = take(4)
    if first:
        sums = take(3)
    back_room, unprep_room = take(counts[1]), take(3)
    pre_ref, w_ref, x_ref, sems = take(4)
    rows = dq_ref.shape[0]
    own = pl.ds(block * rows, rows)
    loads = [
        pltpu.make_async_copy(source, target, sems.at[n])
        for n, (source, target) in enumerate(
            ((pre_any.at[:, own, :], pre_ref), (w_any, w_ref), (x_any.at[own, :], x_ref))
        )
    ]
    for load in loads:
        load.start()
    dp_ref, ab_ref, btb_ref = sums[:3]
    back_kernel(
        block, nb, shift, *back_in, dq_ref, dk_ref, dv_ref, dp_ref, ab_ref, btb_ref, dlg_ref,
        *sums[3:], *back_room,
    )
    for load in loads:
        load.wait()
    unprep_kernel(
        block, nb, shift, back_in[0], peer_ref, dq_ref, dk_ref.at[own, :], dv_ref.at[own, :],
        dgp_ref, pre_ref, w_ref, conv_ref, x_ref, gain_ref, *halo,
        *([dp_ref, pers_ref, ab_ref, btb_ref, gain_two_ref] if first else []),
        edge_in_ref, dlg_ref, gate_ref, mean_ref, *before, *results, *unprep_room,
    )
    if not first:
        dk_out_ref[...] = dk_ref[0 : block * rows, :]
        dv_out_ref[...] = dv_ref[0 : block * rows, :]


def rear_call(
    block, nb, shift, back_args, peers, dgp, pre, w, conv, x, gains, gate, mean, pers, gain_two,
    shared,
):
    rows, width = x.shape
    cols = dgp.shape[1]
    first = block == 0
    ins, in_specs, names, shapes, back_room = back_parts(block, nb, shift, *back_args)
    counts = (len(ins), len(back_room))
    shape_of = dict(zip(names, shapes))
    whole = lambda a: pl.BlockSpec(a.shape, lambda i, n=len(a.shape): (0,) * n)
    anywhere = pl.BlockSpec(memory_space=pl.ANY)
    stacked = lambda n: pl.BlockSpec((n, SPAN, cols), lambda i: (0, block, 0))
    struct = jax.ShapeDtypeStruct
    ins = ins + [peers, dgp, pre, w, conv, x, gains]
    in_specs = in_specs + [
        pl.BlockSpec(memory_space=pltpu.SMEM),
        pl.BlockSpec((SPAN, cols), lambda i: (0, 0)),
        anywhere,
        anywhere,
        whole(conv),
        anywhere,
        whole(gains),
    ]
    kept, outs = [], []
    if first:
        ins += [pers, gain_two]
        in_specs += [whole(pers), whole(gain_two)]
    else:
        ins.append(pre)
        in_specs.append(
            pl.BlockSpec((3, 2 * HALO, cols), lambda i: (0, block * (SPAN // HALO // 2) - 1, 0))
        )
        kept = ["dk", "dv", "dp", "ab", "btb", "sab", "sbtb"]
        outs = [struct((block * SPAN, cols), F32)] * 2
        outs += [struct(shape_of[name], F32) for name in kept[2:]]
    out_specs = [whole(a) for a in outs]
    fresh = ["cg", "gg", "gate", "dproj", "keep", "send", "inner", "edge"]
    ins += [shared["edge"], gate, mean]
    in_specs += [whole(shared["edge"]), whole(gate)]
    in_specs.append(pl.BlockSpec((8, width), lambda i: (block, 0)))
    aliases = {len(ins) + n: len(outs) + n for n in range(7)}
    ins += [shared[name] for name in fresh[:7]]
    in_specs += [whole(shared[name]) for name in fresh[:3]] + [anywhere] * 4
    outs += [struct(shared[name].shape, shared[name].dtype) for name in fresh]
    out_specs += [whole(shared[name]) for name in fresh[:3]]
    out_specs += [
        stacked(4),
        stacked(2),
        stacked(2),
        pl.BlockSpec((8, SPAN), lambda i: (0, block)),
        whole(shared["edge"]),
    ]
    if first:
        fresh += ["small", "gains"]
        ahead = 5 * width // SMALL_ROWS
        outs.append(struct(((ahead + 1) * SMALL_ROWS, cols), BF16))
        out_specs.append(pl.BlockSpec((SMALL_ROWS, cols), lambda i: (ahead, 0)))
        outs.append(struct((2, width), F32))
        out_specs.append(whole(outs[-1]))
    inside = ["dq", "dk", "dv", "dlg"] + (["dp", "ab", "btb"] if first else [])
    got = pl.pallas_call(
        functools.partial(rear_kernel, block, nb, shift, counts),
        grid=(1,),
        in_specs=in_specs,
        out_specs=out_specs,
        out_shape=outs,
        input_output_aliases=aliases,
        scratch_shapes=[pltpu.VMEM(shape_of[name], F32) for name in inside]
        + back_room
        + [
            pltpu.VMEM((HALO + SPAN, cols), F32),
            pltpu.VMEM((SPAN + HALO, cols), F32),
            pltpu.VMEM((SPAN, width), BF16),
            pltpu.VMEM((3, SPAN, cols), BF16),
            pltpu.VMEM(w.shape, BF16),
            pltpu.VMEM((SPAN, width), BF16),
            pltpu.SemaphoreType.DMA((3,)),
        ],
        cost_estimate=cost(25),
        name=f"rear_{block}",
    )(*ins)
    got = dict(zip(kept + fresh, got))
    return {name: got[name] for name in kept}, {name: got[name] for name in fresh}


def finish_kernel(peer_ref, x_ref, dres_ref, half_ref, far_ref, i0_ref, i1_ref, gain_ref, out_ref):
    rows, width = x_ref.shape
    cols = out_ref.shape[1]
    own = pl.ds(pl.multiple_of(peer_ref[0] * cols, cols), cols)
    x = x_ref[...].astype(F32)
    scale = lax.rsqrt(jnp.mean(x * x, -1, keepdims=True) + NORM_EPS)
    inner = jnp.transpose(i0_ref[...] + i1_ref[...])[:, 0:1] / width
    d_normed = half_ref[0].astype(F32) + far_ref[...].astype(F32)
    d_normed = d_normed * gain_ref[0:1, own]
    x_own = x_ref[:, own].astype(F32)
    out_ref[...] = dres_ref[...] + scale * d_normed - x_own * (scale * scale * scale * inner)


def finish_call(peers, x, dres, half, far, inner, inner_far, gains):
    rows, width = x.shape
    cols = dres.shape[1]
    row = lambda n: pl.BlockSpec((SPAN, n), lambda i: (i, 0))
    across = pl.BlockSpec((8, SPAN), lambda i: (0, i))
    return pl.pallas_call(
        finish_kernel,
        grid=(rows // SPAN,),
        in_specs=[
            pl.BlockSpec(memory_space=pltpu.SMEM),
            row(width),
            row(cols),
            pl.BlockSpec((1, SPAN, cols), lambda i: (0, i, 0)),
            row(cols),
            across,
            across,
            pl.BlockSpec(gains.shape, lambda i: (0, 0)),
        ],
        out_specs=row(cols),
        out_shape=jax.ShapeDtypeStruct((rows, cols), F32),
        cost_estimate=cost(4),
        name="finish",
    )(peers, x, dres, half, far, inner, inner_far, gains)


def unpack_kernel(shift, main_ref, small_ref, proj_ref, out_ref, a_ref, b_ref, gate_ref, conv_ref,
                  pers_ref, gain_ref):
    step = pl.program_id(0)
    cols = main_ref.shape[1]
    head_size = 1 << shift
    heads = cols // head_size
    last = pl.num_programs(0) - 1

    @pl.when(step < last)
    def _():
        proj_ref[0] = main_ref[...].astype(F32)

    @pl.when(step == last)
    def _():
        out_ref[...] = main_ref[...].astype(F32)

    @pl.when(step == 0)
    def _():
        small = small_ref[...].astype(F32)
        at = 2 * cols
        for h in range(heads):
            rows = slice(h * head_size, (h + 1) * head_size)
            a_ref[h] = small[rows, :]
            b_ref[h] = small[cols : 2 * cols][rows, :]
        lanes = gain_ref.shape[1] // cols
        for n in range(lanes):
            for g in range(3):
                row = at + 16 * n + g * heads
                gate_ref[g, :, n * cols : (n + 1) * cols] = small[row : row + heads, :]
        at += 16 * lanes
        taps = conv_ref.shape[1]
        for i in range(3):
            conv_ref[i] = small[at + i * taps : at + (i + 1) * taps, :]
        at += 16
        count = pers_ref.shape[2]
        for i in range(2):
            for h in range(heads):
                spot = slice(h * head_size, (h + 1) * head_size)
                pers_ref[i, h] = small[at + i * count : at + (i + 1) * count, spot]
        at += 2 * count
        for i in range(2):
            for n in range(lanes):
                row = at + i * lanes + n
                gain_ref[i : i + 1, n * cols : (n + 1) * cols] = small[row : row + 1, :]


def unpack_call(payload, shift, width, mem_hid, taps, persist_rows):
    cols = payload.shape[1]
    heads = cols >> shift
    head_size = 1 << shift
    ahead = 5 * width // SMALL_ROWS
    struct = jax.ShapeDtypeStruct
    outs = [
        struct((4, width, cols), F32),
        struct((width, cols), F32),
        struct((heads, head_size, mem_hid), F32),
        struct((heads, head_size, mem_hid), F32),
        struct((3, heads, width), F32),
        struct((3, taps, cols), F32),
        struct((2, heads, persist_rows, head_size), F32),
        struct((2, width), F32),
    ]
    whole = lambda a: pl.BlockSpec(a.shape, lambda i, n=len(a.shape): (0,) * n)
    return pl.pallas_call(
        functools.partial(unpack_kernel, shift),
        grid=(5,),
        in_specs=[
            pl.BlockSpec((width, cols), lambda i: (i, 0)),
            pl.BlockSpec((SMALL_ROWS, cols), lambda i: (ahead, 0)),
        ],
        out_specs=[pl.BlockSpec((1, width, cols), lambda i: (jnp.minimum(i, 3), 0, 0))]
        + [whole(a) for a in outs[1:]],
        out_shape=outs,
        cost_estimate=cost(4),
        name="unpack",
    )(payload, payload)


def ring_of(size):
    return [list(range(0, size, 2)) + list(range(size - 1 - size % 2, 0, -2))]


def ring_scatter(payload, axis, size):
    return lax.psum_scatter(
        payload, axis, scatter_dimension=0, axis_index_groups=ring_of(size), tiled=True
    )


def ring_gather(part, axis, size):
    return lax.all_gather(part, axis, axis=0, axis_index_groups=ring_of(size), tiled=True)


def stacked_rows(pieces, full):
    at = 0
    for piece in pieces:
        full = lax.dynamic_update_slice(full, piece, (at, 0))
        at += piece.shape[0]
    return full


def after(value, *others):
    return lax.optimization_barrier((value, *others))[0]


def per_device(
    ring_size,
    layer_input,
    proj_weight,
    conv_weight,
    persist_kv,
    memory_in,
    memory_out,
    memory_gate,
    out_weight,
    ffn_in,
    ffn_out,
    norm_gains,
    seq_len,
    out_grad,
):
    rows, width = layer_input.shape
    cols = proj_weight.shape[2]
    heads = persist_kv.shape[1]
    head_size = persist_kv.shape[3]
    shift = head_size.bit_length() - 1
    mem_hid = memory_in.shape[2]
    nb = rows // SPAN
    taps = conv_weight.shape[1]
    me = lax.axis_index("head")
    count = width // cols
    peers = jnp.stack([me, me ^ 1, me ^ 2, me ^ 3]).astype(jnp.int32)
    swap = lambda a, bit: lax.ppermute(a, "head", [(i, i ^ bit) for i in range(count)])
    far_weight, far_cot = swap(out_weight, 2), swap(out_grad, 2)
    near_weight, near_cot = swap(out_weight, 1), swap(out_grad, 1)
    pers = jnp.transpose(persist_kv, (0, 2, 1, 3)).reshape(2, -1, cols)
    gate = jnp.transpose(memory_gate, (1, 2, 0))
    groups = [list(range(nb - 1)), [nb - 1]] if nb > 1 else [[0]]
    state = [memory_in.reshape(cols, mem_hid)]
    state.append(jnp.transpose(memory_out, (0, 2, 1)).reshape(cols, mem_hid))
    states = [dict(a=state[0], bt=state[1], sa=None, sbt=None)]
    earlier = gathered = [near_weight, near_cot, far_weight]
    shared, carried, pieces = None, [], []
    for n, blocks in enumerate(groups):
        if n:
            state = [after(state[0], *earlier), *state[1:]]
        shared, (mixed, pers_low, flat), squares, carried = lead_call(
            blocks, nb, shift, seq_len, layer_input, proj_weight, conv_weight, norm_gains, gate,
            pers, state, carried, shared,
        )
        for a, bt, sa, sbt, ga, gbt in squares:
            states[-1].update(ga=ga, gbt=gbt)
            states.append(dict(a=a, bt=bt, sa=sa, sbt=sbt))
            state = [a, bt] if blocks[-1] + 1 == nb - 1 else [a, bt, sa, sbt]
        sent = after(mixed, *gathered)
        pieces.append([mixed, swap(sent, 1), swap(sent, 2)])
        gathered = pieces[n][1:]
        if n == 0:
            last_weight = swap(after(far_weight, sent), 1)
            last_cot = swap(after(far_cot, sent), 1)
            gathered = gathered + [last_weight, last_cot]
    q, k, v, kt, pre, gp, nl, mean, lg, tot, att, lt = shared
    for state in states:
        state["lg"] = lg
    gate = flat
    ow = (out_weight, near_weight, far_weight, last_weight)
    if nb > 1:
        pieces[0].append(swap(after(pieces[0][2], pieces[1][0]), 1))
    fout = after(ffn_out, pieces[-1][0])
    cot_full, d_hidden = cot_call(peers, (out_grad, near_cot, far_cot, last_cot), fout)
    pieces[-1].append(swap(after(pieces[-1][2], cot_full), 1))
    normed_two, hidden, dgu, mixed_full, residual, grads_room = ffn_call(
        groups, peers, after(layer_input, cot_full), pieces, ow, norm_gains, ffn_in, d_hidden
    )
    along_rows = (((0,), (0,)), ((), ()))
    outer = lambda left, right: lax.dot_general(
        left, right, along_rows, preferred_element_type=F32
    ).astype(BF16)
    out_part = outer(hidden, cot_full)
    ffn_grads = stacked_rows(
        [out_part, outer(after(normed_two, out_part), dgu[0]), outer(normed_two, dgu[1])],
        grads_room,
    )
    ffn_part = ring_scatter(ffn_grads, "dp", ring_size)
    s1, r2, gain_two = [], [], None
    tie = (ffn_grads,)
    for n, blocks in enumerate(reversed(groups)):
        gain_two, keep, send = ffn_back_call(
            blocks, peers, after(dgu, *tie), ffn_in, residual, gain_two
        )
        send = after(send, *r2) if r2 else send
        s1.append((keep.astype(F32) + swap(send, 1).astype(F32)).astype(BF16))
        r2.append(swap(s1[n], 2))
        tie = (s1[0],)
    tie = (gain_two,)
    back = unprep = None
    gated = [None] * nb

    def relayed(n, *ties):
        return s1[n], r2[n], swap(after(s1[n], *ties), 1), swap(after(r2[n], *ties), 1)

    def turn(c, spot, parts, turned, *ties):
        turned, gated[c] = turn_call(
            c, spot, peers, parts, after(residual, *ties), cot_full, ow, norm_gains, gp, tot, turned
        )
        return turned

    turned = turn(nb - 1, 0, relayed(0, r2[0]), None, *tie)
    tie = tuple(s1[1:])
    for c in reversed(range(nb)):
        back_args = (
            seq_len, after(q, *tie), k, v, kt, pers_low, gated[c][0], att, lt, states[c], back, back
        )
        rest = (
            gated[c][1], pre, proj_weight, conv_weight, layer_input, norm_gains, gate, mean, pers,
            gain_two, unprep,
        )
        if c == nb - 1:
            back = back_call(c, nb, shift, *back_args)
            parts = relayed(1, back["dq"]) if c else None
            unprep = unprep_call(c, nb, shift, seq_len, peers, back, *rest)
        else:
            back, unprep = rear_call(c, nb, shift, back_args, peers, *rest)
        tie = ()
        if c:
            turned = turn(c - 1, c - 1, parts, turned, unprep["edge"])
        if c == nb - 1:
            edge, ffn_part = lax.optimization_barrier((turned[2], ffn_part))
            turned[2] = edge
            ffn_grads = ring_gather(ffn_part, "dp", ring_size)
            tie = (edge,)
    d_res, res_cols, d_branch, d_gate_all = turned
    gains = unprep["gains"]
    gains = gains + sum(swap(gains, bit) for bit in (1, 2, 3))
    cuts = [4 * width, width, 2 * cols, 16 * width // cols, 16, pers.shape[1] * 2]
    cuts.append(2 * width // cols)
    payload = stacked_rows(
        [outer(nl, unprep["dproj"][i]) for i in range(4)]
        + [outer(mixed_full, d_branch)],
        unprep["small"],
    )
    payload = lax.dynamic_update_slice(
        payload, gains.reshape(-1, cols).astype(BF16), (sum(cuts[:-1]), 0)
    )
    tie = (payload,)
    payload, ffn_grads = lax.optimization_barrier((payload, ffn_grads))
    ffn_in_grad = ffn_grads[width:].astype(F32).reshape(2, width, -1)
    ffn_out_grad = ffn_grads[:width].astype(F32)
    payload = ring_scatter(payload, "dp", ring_size)
    half = (
        unprep["keep"].astype(F32) + swap(after(unprep["send"], *tie), 1).astype(F32)
    ).astype(BF16)
    inner = unprep["inner"] + swap(unprep["inner"], 1)
    far = swap(half[1], 2)
    input_grad = finish_call(
        peers, layer_input, d_res, half, far, inner, swap(inner, 2), norm_gains
    )
    part_keep, part_send = down_call(peers, after(hidden, half), ffn_out, cols)
    payload, input_grad, ffn_in_grad, ffn_out_grad, part_keep, part_send = (
        lax.optimization_barrier(
            (payload, input_grad, ffn_in_grad, ffn_out_grad, part_keep, part_send)
        )
    )
    payload = ring_gather(payload, "dp", ring_size)
    part = (part_keep.astype(F32) + swap(part_send, 1).astype(F32)).astype(BF16)
    layer_output = res_cols + part[0].astype(F32) + swap(part[1], 2).astype(F32)
    layer_output = layer_output.astype(BF16)
    proj_grad, out_grads, a_grad, b_grad, gate_grad, conv_grad, pers_grad, gains = unpack_call(
        payload, shift, width, mem_hid, taps, persist_kv.shape[2]
    )
    return (
        layer_output,
        input_grad,
        proj_grad,
        conv_grad,
        pers_grad,
        a_grad,
        jnp.transpose(b_grad, (0, 2, 1)),
        jnp.transpose(gate_grad, (2, 0, 1)),
        out_grads,
        ffn_in_grad,
        ffn_out_grad,
        gains,
    )


def solution(mesh):
    in_specs = (
        P("dp", None),
        P(None, None, "head"),
        P(None, None, "head"),
        P(None, "head", None, None),
        P("head", None, None),
        P("head", None, None),
        P(None, None, "head"),
        P(None, "head"),
        P(None, None, "head"),
        P("head", None),
        P(),
        P("dp"),
        P("dp", "head"),
    )
    out_specs = (
        P("dp", "head"),
        P("dp", "head"),
        P(None, None, "head"),
        P(None, None, "head"),
        P(None, "head", None, None),
        P("head", None, None),
        P("head", None, None),
        P(None, None, "head"),
        P(None, "head"),
        P(None, None, "head"),
        P("head", None),
        P(),
    )
    body = functools.partial(per_device, mesh.shape["dp"])
    return jax.shard_map(
        body, mesh=mesh, in_specs=in_specs, out_specs=out_specs, check_vma=False
    )
```

```python
import functools

import jax
import jax.numpy as jnp
from jax import lax
from jax.experimental import pallas as pl
from jax.experimental.pallas import tpu as pltpu
from jax.sharding import PartitionSpec as P

F32 = jnp.float32
BF16 = jnp.bfloat16
HIGH = lax.Precision.HIGHEST
NORM_EPS = 1e-05
UNIT_EPS = 1e-06
SCORE_SCALE = 8.0
SPAN = 512
HALO = 8
COST_UNIT = 1.5e8
SMALL_ROWS = 640


def dot_nn(left, right):
    return jnp.dot(left, right, preferred_element_type=F32)


def dot_nt(left, right, precision=None):
    return lax.dot_general(
        left, right, (((1,), (1,)), ((), ())), preferred_element_type=F32, precision=precision
    )


def iota(shape, axis):
    return lax.broadcasted_iota(jnp.int32, shape, axis)


def cost(microseconds):
    return pl.CostEstimate(
        flops=int(microseconds * COST_UNIT), transcendentals=0, bytes_accessed=1 << 20
    )


def head_blocks(cols, shift):
    same = (iota((cols, cols), 0) >> shift) == (iota((cols, cols), 1) >> shift)
    return jnp.where(same, 1.0, 0.0).astype(BF16)


def head_sum(value, blocks):
    return dot_nn(value.astype(BF16), blocks)


def valid_column(seq_ref, start, rows):
    inside = (start + iota((rows, 1), 0)) < seq_ref[0]
    valid = jnp.where(inside, 1.0, 0.0)
    return valid, jnp.maximum(jnp.sum(valid, 0, keepdims=True), 1.0)


def head_mask(cols, shift, head):
    return jnp.where((iota((1, cols), 1) >> shift) == head, 1.0, 0.0)


def gate_rows(logits, group, heads, head_size, width):
    parts = [
        jnp.broadcast_to(
            logits[0:1, group * heads + head : group * heads + head + 1], (head_size, width)
        )
        for head in range(heads)
    ]
    return jnp.concatenate(parts, 0)


def prep_kernel(
    shift,
    low_block,
    seq_ref,
    x_ref,
    w_ref,
    conv_ref,
    gain_ref,
    gate_ref,
    pers_ref,
    edge_ref,
    q_ref,
    k_ref,
    v_ref,
    kt_ref,
    pre_ref,
    gp_ref,
    nl_ref,
    mean_ref,
    lg_ref,
    pers_out_ref,
    flat_ref,
    pers_flat_ref,
    ext_ref,
):
    step = pl.program_id(0)
    rows, cols = q_ref.shape
    blocks = head_blocks(cols, shift)

    @pl.when(step == 0)
    def _():
        ext_ref[:, 0:HALO, :] = (
            jnp.zeros((3, HALO, cols), F32) if edge_ref is None else edge_ref[...]
        )
        heads = gate_ref.shape[1]
        for h in range(heads):
            spot = slice(h << shift, (h + 1) << shift)
            for i in range(2):
                pers_flat_ref[i, :, spot] = pers_ref[i, h]
        keys = pers_flat_ref[0]
        keys = keys * lax.rsqrt(head_sum(keys * keys, blocks) + UNIT_EPS)
        pers_out_ref[0] = keys.astype(BF16)
        pers_out_ref[1] = pers_flat_ref[1].astype(BF16)
        for g in range(3):
            flat_ref[g * heads : (g + 1) * heads, :] = gate_ref[g]

    x = x_ref[...].astype(F32)
    scale = lax.rsqrt(jnp.mean(x * x, -1, keepdims=True) + NORM_EPS)
    normed = x * scale * gain_ref[0:1, :]
    low = normed.astype(BF16)
    nl_ref[...] = low
    inside = ((low_block + step) * rows + iota((8, rows), 1)) < seq_ref[0]
    valid = jnp.where(inside, 1.0, 0.0)
    count = jnp.maximum(jnp.sum(valid, 1, keepdims=True), 1.0)
    mean = dot_nn(valid.astype(BF16), low) / count
    mean_ref[...] = mean
    lg_ref[...] = dot_nt(mean, flat_ref[...], HIGH)
    gp_ref[...] = dot_nn(low, w_ref[3]).astype(BF16)
    for i in range(3):
        pre = dot_nn(low, w_ref[i])
        pre_ref[i] = pre.astype(BF16)
        ext_ref[i, HALO : HALO + rows, :] = pre
        conv = conv_ref[i, 0:1, :] * pre
        for j in range(1, conv_ref.shape[1]):
            conv = conv + conv_ref[i, j : j + 1, :] * ext_ref[i, HALO - j : HALO - j + rows, :]
        ext_ref[i, 0:HALO, :] = pre[rows - HALO :, :]
        act = conv * jax.nn.sigmoid(conv)
        if i < 2:
            act = act * lax.rsqrt(head_sum(act * act, blocks) + UNIT_EPS)
        act_low = act.astype(BF16)
        (q_ref, k_ref, v_ref)[i][...] = act_low
        if i == 1:
            kt_ref[...] = jnp.transpose(act_low.astype(F32)).astype(BF16)


def mix_kernel(block, blocks_all, shift, first, last, *refs):
    it = iter(refs)
    seq_ref, lg_ref, q_ref, k_ref, v_ref, kt_ref, pers_ref, gp_ref, a_ref, bt_ref = (
        next(it) for _ in range(10)
    )
    sa_ref, sbt_ref = (None, None) if first or last else (next(it), next(it))
    mixed_ref, tot_out_ref, att_out_ref, lt_ref = (next(it) for _ in range(4))
    if not last:
        a2_ref, bt2_ref, sa2_ref, sbt2_ref, ga_ref, gbt_ref = (next(it) for _ in range(6))
    tot_ref, att_ref, linv_ref = (next(it) for _ in range(3))
    if not last:
        z_ref, r_ref = next(it), next(it)
    rows, cols = q_ref.shape
    head_size = 1 << shift
    heads = cols // head_size
    a_low = a_ref[...].astype(BF16)
    bt_low = bt_ref[...].astype(BF16)
    valid, count = valid_column(seq_ref, block * rows, rows)
    weight = valid / count
    att_ref[...] = jnp.zeros((rows, cols), F32)
    linv_ref[...] = jnp.zeros((rows, cols), F32)
    tot_ref[...] = jnp.zeros((rows, cols), F32)
    if not last:
        r_ref[...] = jnp.zeros((rows, cols), F32)

    def one_head(head, carry):
        mask = head_mask(cols, shift, head)
        mask_low = mask.astype(BF16)
        ones_low = (1.0 - mask).astype(BF16)
        query = q_ref[...] * mask_low
        scaled = query * SCORE_SCALE
        raised = jnp.exp(dot_nt(scaled, pers_ref[0])).astype(BF16)
        total = dot_nn(raised, pers_ref[1] * mask_low + ones_low)
        for j in range(block + 1):
            span = slice(j * rows, (j + 1) * rows)
            raised = jnp.exp(dot_nt(scaled, k_ref[span, :]))
            if j == block:
                raised = jnp.where(
                    iota((rows, rows), 0) >= iota((rows, rows), 1), raised, 0.0
                )
            total = total + dot_nn(raised.astype(BF16), v_ref[span, :] * mask_low + ones_low)
        inverse = 1.0 / pltpu.roll(total, head_size, 1)
        inside = jnp.broadcast_to(mask, (rows, cols)) > 0.5
        linv_ref[...] = jnp.where(inside, inverse, linv_ref[...])
        attended = jnp.where(inside, total * inverse, 0.0)
        att_ref[...] = att_ref[...] + attended
        hid = dot_nn(query, a_low)
        hid = hid * jax.nn.sigmoid(hid)
        recalled = dot_nt(hid.astype(BF16), bt_low) * mask
        tot_ref[...] = tot_ref[...] + attended + recalled
        if not last:
            hid = dot_nn(k_ref[block * rows : (block + 1) * rows, :] * mask_low, a_low)
            sig = jax.nn.sigmoid(hid)
            act = (hid * sig).astype(BF16)
            z_ref[head] = act
            target = v_ref[block * rows : (block + 1) * rows, :].astype(F32)
            resid = (dot_nt(act, bt_low) - target) * mask * weight
            r_ref[...] = r_ref[...] + resid
            d_hid = dot_nn(resid.astype(BF16), bt_low) * (sig * (1.0 + hid * (1.0 - sig)))
            at = pl.ds(pl.multiple_of(head * head_size, head_size), head_size)
            ga_ref[at, :] = dot_nn(kt_ref[at, :], d_hid.astype(BF16))
        return carry

    lax.fori_loop(0, heads, one_head, 0)
    gate = jax.nn.sigmoid(gp_ref[...].astype(F32))
    mixed_ref[...] = (tot_ref[...] * gate).astype(BF16)
    tot_out_ref[...] = tot_ref[...].astype(BF16)
    att_out_ref[...] = att_ref[...].astype(BF16)
    start = iota((8, cols), 1) == (iota((8, cols), 0) << shift)
    lt_ref[...] = dot_nt(jnp.where(start, 1.0, 0.0), linv_ref[...], HIGH)
    if not last:
        resid_t = jnp.transpose(r_ref[...]).astype(BF16)
        for head in range(heads):
            at = slice(head * head_size, (head + 1) * head_size)
            gbt_ref[at, :] = dot_nn(resid_t[at, :], z_ref[head])
        width = a_ref.shape[1]
        logits = lg_ref[...]
        step = 0.2 * jax.nn.sigmoid(gate_rows(logits, 0, heads, head_size, width))
        keep = jax.nn.sigmoid(gate_rows(logits, 1, heads, head_size, width))
        stay = 1.0 - 0.5 * jax.nn.sigmoid(gate_rows(logits, 2, heads, head_size, width))
        moment_a = -step * ga_ref[...]
        moment_b = -step * gbt_ref[...]
        if not first:
            moment_a = moment_a + keep * sa_ref[...]
            moment_b = moment_b + keep * sbt_ref[...]
        sa2_ref[...] = moment_a
        sbt2_ref[...] = moment_b
        a2_ref[...] = stay * a_ref[...] + moment_a
        bt2_ref[...] = stay * bt_ref[...] + moment_b


def lead_kernel(low, count, nb, shift, *refs):
    it = iter(refs)
    take = lambda n: [next(it) for _ in range(n)]
    final = low + count == nb
    prep_in = take(7)
    k_in_ref, v_in_ref, edge_in_ref = take(3) if low else [None] * 3
    state = take(4 if 0 < low < nb - 1 else 2)
    if low:
        take(12)
    prep_out, kept, (mixed_ref, pers_ref, flat_ref, pers_flat_ref) = take(9), take(3), take(4)
    blocks = range(low, low + count)
    squares = [take(6) if block < nb - 1 else [] for block in blocks]
    k_out_ref, v_out_ref, edge_out_ref = [None] * 3 if final else take(3)
    ext_ref, k_all_ref, v_all_ref = take(3)
    room, more = take(3), take(0 if low == nb - 1 else 2)
    step = pl.program_id(0)
    q_ref, k_ref, v_ref, kt_ref, _, gp_ref, _, _, lg_ref = prep_out
    rows = q_ref.shape[0]
    prep_kernel(
        shift, low, *prep_in, edge_in_ref, *prep_out, pers_ref, flat_ref, pers_flat_ref, ext_ref
    )
    for i, block in enumerate(blocks):

        @pl.when(step == i)
        def _(i=i, block=block):
            if low and i == 0:
                k_all_ref[0 : low * rows, :] = k_in_ref[...]
                v_all_ref[0 : low * rows, :] = v_in_ref[...]
            own = slice(block * rows, (block + 1) * rows)
            k_all_ref[own, :] = k_ref[...]
            v_all_ref[own, :] = v_ref[...]
            first, last = block == 0, block == nb - 1
            now = squares[i - 1][:4] if i else state
            now = now[:2] if first or last else now
            mix_kernel(
                block, nb, shift, first, last, prep_in[0], lg_ref, q_ref, k_all_ref, v_all_ref,
                kt_ref, pers_ref, gp_ref, *now, mixed_ref, *kept, *squares[i], *room,
                *([] if last else more),
            )
            if i == count - 1 and not final:
                done = (low + count) * rows
                k_out_ref[...] = k_all_ref[0:done, :]
                v_out_ref[...] = v_all_ref[0:done, :]
                edge_out_ref[...] = ext_ref[:, 0:HALO, :]


def lead_call(blocks, nb, shift, seq, x, w, conv, gains, gate, pers, state, carried, shared):
    rows, width = x.shape
    cols = w.shape[2]
    low, count = blocks[0], len(blocks)
    final = low + count == nb
    gates = 3 * gate.shape[1]
    mem_hid = state[0].shape[1]
    square = (cols, mem_hid)
    once = pl.Buffered(1)
    fixed = lambda a: pl.BlockSpec(a.shape, lambda c, n=len(a.shape): (0,) * n, pipeline_mode=once)
    whole = lambda a: pl.BlockSpec(a.shape, lambda c, n=len(a.shape): (0,) * n)
    at_rows = lambda n: pl.BlockSpec((SPAN, n), lambda c: (low + c, 0))
    eight = lambda n: pl.BlockSpec((8, n), lambda c: (low + c, 0))
    struct = jax.ShapeDtypeStruct
    ins = [seq, x, w, conv, gains, gate, pers, *carried, *state]
    in_specs = [pl.BlockSpec(memory_space=pltpu.SMEM), at_rows(width)]
    in_specs += [fixed(a) for a in ins[2:]]
    aliases = {}
    if shared:
        aliases = {len(ins) + n: n for n in range(len(shared))}
        ins += shared
        in_specs += [pl.BlockSpec(memory_space=pl.ANY)] * len(shared)
    outs = [struct((rows, cols), BF16)] * 3 + [
        struct((cols, rows), BF16),
        struct((3, rows, cols), BF16),
        struct((rows, cols), BF16),
        struct((rows, width), BF16),
        struct((nb * 8, width), F32),
        struct((nb * 8, gates), F32),
        struct((rows, cols), BF16),
        struct((rows, cols), BF16),
        struct((8, rows), F32),
        struct((count * SPAN, cols), BF16),
        struct((2, pers.shape[2], cols), BF16),
        struct((gates, width), F32),
        struct((2, pers.shape[2], cols), F32),
    ]
    out_specs = [at_rows(cols)] * 3 + [
        pl.BlockSpec((cols, SPAN), lambda c: (0, low + c)),
        pl.BlockSpec((3, SPAN, cols), lambda c: (0, low + c, 0)),
        at_rows(cols),
        at_rows(width),
        eight(width),
        eight(gates),
        at_rows(cols),
        at_rows(cols),
        pl.BlockSpec((8, SPAN), lambda c: (0, low + c)),
        pl.BlockSpec((SPAN, cols), lambda c: (c, 0)),
    ] + [whole(a) for a in outs[13:]]
    updates = [block for block in blocks if block < nb - 1]
    more = [struct(square, F32)] * (6 * len(updates))
    if not final:
        done = ((low + count) * SPAN, cols)
        more += [struct(done, BF16), struct(done, BF16), struct((3, HALO, cols), F32)]
    scratch = [
        pltpu.VMEM((3, HALO + SPAN, cols), F32),
        pltpu.VMEM((rows, cols), BF16),
        pltpu.VMEM((rows, cols), BF16),
    ] + [pltpu.VMEM((SPAN, cols), F32)] * 3
    if updates:
        heads = cols >> shift
        scratch += [pltpu.VMEM((heads, SPAN, mem_hid), BF16), pltpu.VMEM((SPAN, cols), F32)]
    got = pl.pallas_call(
        functools.partial(lead_kernel, low, count, nb, shift),
        grid=(count,),
        in_specs=in_specs,
        out_specs=out_specs + [whole(a) for a in more],
        out_shape=outs + more,
        input_output_aliases=aliases,
        scratch_shapes=scratch,
        cost_estimate=cost(11 * count),
        name=f"lead_{low}",
    )(*ins)
    at = 16 + 6 * len(updates)
    squares = [got[n : n + 6] for n in range(16, at, 6)]
    return got[:12], got[12:16], squares, got[at:]


def cot_kernel(peer_ref, c0_ref, c1_ref, c2_ref, c3_ref, fout_ref, full_ref, dh_ref):
    cols = c0_ref.shape[1]
    for j, piece_ref in enumerate((c0_ref, c1_ref, c2_ref, c3_ref)):
        at = pl.ds(pl.multiple_of(peer_ref[j] * cols, cols), cols)
        full_ref[:, at] = piece_ref[...]
    dh_ref[...] = dot_nt(full_ref[...], fout_ref[...]).astype(BF16)


def cot_call(peers, cot, fout):
    rows, cols = cot[0].shape
    hidden, width = fout.shape
    row = lambda n: pl.BlockSpec((SPAN, n), lambda i: (i, 0))
    return pl.pallas_call(
        cot_kernel,
        grid=(rows // SPAN,),
        in_specs=[pl.BlockSpec(memory_space=pltpu.SMEM)]
        + [row(cols)] * 4
        + [pl.BlockSpec(fout.shape, lambda i: (0, 0), pipeline_mode=pl.Buffered(1))],
        out_specs=[row(width), row(hidden)],
        out_shape=[
            jax.ShapeDtypeStruct((rows, width), BF16),
            jax.ShapeDtypeStruct((rows, hidden), BF16),
        ],
        cost_estimate=cost(6),
        name="cot",
    )(peers, *cot, fout)


def ffn_kernel(groups, *refs):
    it = iter(refs)
    take = lambda n: [next(it) for _ in range(n)]
    peer_ref, x_ref = take(2)
    piece_refs = [take(4) for _ in groups]
    gain_ref, dh_ref = take(2)
    weights = take(5)
    nt_out, hid_ref, dgu_ref, mfull_out, res_out, _ = take(6)
    held = take(5)
    nt_ref, mfull_ref, res_ref = take(3)
    weight_sems, out_sems = take(2)
    step = pl.program_id(0)
    rows, cols = piece_refs[0][0].shape
    loads = [
        pltpu.make_async_copy(source, target, weight_sems.at[n])
        for n, (source, target) in enumerate(zip(weights, held))
    ]
    fin_ref, ow_refs = held[4], held[:4]
    mine = pl.ds(pl.multiple_of(step * rows, rows), rows)
    stores = [
        pltpu.make_async_copy(source, target.at[mine, :], out_sems.at[n])
        for n, (source, target) in enumerate(
            ((mfull_ref, mfull_out), (res_ref, res_out), (nt_ref, nt_out))
        )
    ]

    @pl.when(step == 0)
    def _():
        for load in loads:
            load.start()

    def ready(some):
        @pl.when(step == 0)
        def _():
            for load in some:
                load.wait()

    @pl.when(step > 0)
    def _():
        for store in stores:
            store.wait()

    spots = [pl.ds(pl.multiple_of(peer_ref[j] * cols, cols), cols) for j in range(4)]
    for n, blocks in enumerate(groups):

        @pl.when((step >= blocks[0]) & (step <= blocks[-1]))
        def _(n=n):
            for j in range(4):
                mfull_ref[:, spots[j]] = piece_refs[n][j][...]

    stores[0].start()
    ready(loads[:4])
    mixed = mfull_ref[...]
    for j in range(4):
        branch = dot_nn(mixed, ow_refs[j][...])
        res_ref[:, spots[j]] = x_ref[:, spots[j]].astype(F32) + branch
    stores[1].start()
    residual = res_ref[...]
    scale = lax.rsqrt(jnp.mean(residual * residual, -1, keepdims=True) + NORM_EPS)
    low_rows = (residual * scale * gain_ref[1:2, :]).astype(BF16)
    nt_ref[...] = low_rows
    stores[2].start()
    ready(loads[4:])
    gate_pre = dot_nn(low_rows, fin_ref[0])
    up_pre = dot_nn(low_rows, fin_ref[1])
    sig = jax.nn.sigmoid(gate_pre)
    silu = gate_pre * sig
    hid_ref[...] = (silu * up_pre).astype(BF16)
    slope = sig * (1.0 + gate_pre * (1.0 - sig))
    d_hidden = dh_ref[...].astype(F32)
    dgu_ref[0] = (d_hidden * up_pre * slope).astype(BF16)
    dgu_ref[1] = (d_hidden * silu).astype(BF16)

    @pl.when(step == pl.num_programs(0) - 1)
    def _():
        for store in stores:
            store.wait()


def ffn_call(groups, peers, x, pieces, ow, gains, fin, dh):
    rows, width = x.shape
    cols = pieces[0][0].shape[1]
    hidden = dh.shape[1]
    at_rows = lambda n: pl.BlockSpec((SPAN, n), lambda i: (i, 0))
    anywhere = pl.BlockSpec(memory_space=pl.ANY)
    struct = jax.ShapeDtypeStruct
    ins = [peers, x, *[piece for group in pieces for piece in group], gains, dh, *ow, fin]
    in_specs = [pl.BlockSpec(memory_space=pltpu.SMEM), at_rows(width)]
    for blocks in groups:
        spot = lambda i, low=blocks[0], n=len(blocks): (jnp.clip(i - low, 0, n - 1), 0)
        in_specs += [pl.BlockSpec((SPAN, cols), spot)] * 4
    in_specs += [pl.BlockSpec(gains.shape, lambda i: (0, 0)), at_rows(hidden)] + [anywhere] * 5
    return pl.pallas_call(
        functools.partial(ffn_kernel, groups),
        grid=(rows // SPAN,),
        in_specs=in_specs,
        out_specs=[
            anywhere,
            at_rows(hidden),
            pl.BlockSpec((2, SPAN, hidden), lambda i: (0, i, 0)),
            anywhere,
            anywhere,
            anywhere,
        ],
        out_shape=[
            struct((rows, width), BF16),
            struct((rows, hidden), BF16),
            struct((2, rows, hidden), BF16),
            struct((rows, width), BF16),
            struct((rows, width), F32),
            struct((3 * width, width), BF16),
        ],
        scratch_shapes=[pltpu.VMEM(piece.shape, BF16) for piece in (*ow, fin)]
        + [pltpu.VMEM((SPAN, width), BF16)] * 2
        + [pltpu.VMEM((SPAN, width), F32)]
        + [pltpu.SemaphoreType.DMA((5,)), pltpu.SemaphoreType.DMA((3,))],
        compiler_params=pltpu.CompilerParams(vmem_limit_bytes=42 << 20),
        cost_estimate=cost(22),
        name="ffn",
    )(*ins)


def ffn_back_kernel(first_call, *refs):
    it = iter(refs)
    take = lambda n: [next(it) for _ in range(n)]
    peer_ref, dgu_ref, fin_ref, res_ref = take(4)
    gg_in_ref = None if first_call else take(1)[0]
    gg_ref, keep_ref, send_ref, part_ref = take(4)
    width = res_ref.shape[1]
    residual = res_ref[...]
    scale = lax.rsqrt(jnp.mean(residual * residual, -1, keepdims=True) + NORM_EPS)
    d_normed = dot_nt(dgu_ref[0], fin_ref[0]) + dot_nt(dgu_ref[1], fin_ref[1])
    gains = jnp.sum(d_normed * residual * scale, 0, keepdims=True)

    @pl.when(pl.program_id(0) == 0)
    def _():
        gg_ref[...] = jnp.zeros(gg_ref.shape, F32) if first_call else gg_in_ref[...]

    gg_ref[...] = gg_ref[...] + jnp.broadcast_to(gains, gg_ref.shape)
    half = width // 2
    part_ref[...] = d_normed.astype(BF16)
    core = peer_ref[0] & 1
    keep_ref[...] = part_ref[:, pl.ds(pl.multiple_of(core * half, half), half)]
    send_ref[...] = part_ref[:, pl.ds(pl.multiple_of((1 - core) * half, half), half)]


def ffn_back_call(blocks, peers, dgu, fin, res, gains):
    width = res.shape[1]
    tile = SPAN // 2
    steps = SPAN // tile
    low = blocks[0] * steps
    lines = len(blocks) * SPAN
    gain_spec = pl.BlockSpec((8, width), lambda i: (0, 0))
    row = pl.BlockSpec((tile, width // 2), lambda i: (i, 0))
    struct = jax.ShapeDtypeStruct
    return pl.pallas_call(
        functools.partial(ffn_back_kernel, gains is None),
        grid=(len(blocks) * steps,),
        in_specs=[
            pl.BlockSpec(memory_space=pltpu.SMEM),
            pl.BlockSpec((2, tile, dgu.shape[2]), lambda i: (0, low + i, 0)),
            pl.BlockSpec(fin.shape, lambda i: (0, 0, 0), pipeline_mode=pl.Buffered(1)),
            pl.BlockSpec((tile, width), lambda i: (low + i, 0)),
        ]
        + ([] if gains is None else [gain_spec]),
        out_specs=[gain_spec, row, row],
        out_shape=[
            struct((8, width), F32),
            struct((lines, width // 2), BF16),
            struct((lines, width // 2), BF16),
        ],
        scratch_shapes=[pltpu.VMEM((tile, width), BF16)],
        cost_estimate=cost(4 * len(blocks)),
        name=f"ffn_back_{blocks[0]}",
    )(peers, dgu, fin, res, *([] if gains is None else [gains]))


def down_kernel(peer_ref, hid_ref, fout_ref, keep_ref, send_ref, part_ref):
    cols = keep_ref.shape[2]
    part_ref[...] = dot_nn(hid_ref[...], fout_ref[...]).astype(BF16)
    for slot, out_ref in ((0, keep_ref), (1, send_ref)):
        for n in range(2):
            start = pl.multiple_of(peer_ref[slot + 2 * n] * cols, cols)
            out_ref[n] = part_ref[:, pl.ds(start, cols)]


def down_call(peers, hid, fout, cols):
    rows, hidden = hid.shape
    width = fout.shape[1]
    stacked = pl.BlockSpec((2, SPAN, cols), lambda i: (0, i, 0))
    return pl.pallas_call(
        down_kernel,
        grid=(rows // SPAN,),
        in_specs=[
            pl.BlockSpec(memory_space=pltpu.SMEM),
            pl.BlockSpec((SPAN, hidden), lambda i: (i, 0)),
            pl.BlockSpec(fout.shape, lambda i: (0, 0), pipeline_mode=pl.Buffered(1)),
        ],
        out_specs=[stacked, stacked],
        out_shape=[jax.ShapeDtypeStruct((2, rows, cols), BF16)] * 2,
        scratch_shapes=[pltpu.VMEM((SPAN, width), BF16)],
        cost_estimate=cost(6),
        name="down",
    )(peers, hid, fout)


def turn_kernel(first_call, *refs):
    it = iter(refs)
    take = lambda n: [next(it) for _ in range(n)]
    peer_ref, s1_ref, r2_ref, ps1_ref, pr2_ref, res_ref, cot_ref = take(7)
    gain_ref, gp_ref = take(2)
    ow_refs = take(4)
    (tot_ref,) = take(1)
    if not first_call:
        take(4)
    dres_ref, rescol_ref, dbr_ref, dgall_ref, dga_ref, dgp_ref, full_ref = take(7)
    rows, width = res_ref.shape
    cols = gp_ref.shape[1]
    half = width // 2
    core = peer_ref[0] & 1
    at_own = pl.ds(pl.multiple_of(core * half, half), half)
    at_other = pl.ds(pl.multiple_of((1 - core) * half, half), half)
    full_ref[:, at_own] = s1_ref[...].astype(F32) + r2_ref[...].astype(F32)
    full_ref[:, at_other] = ps1_ref[...].astype(F32) + pr2_ref[...].astype(F32)
    residual = res_ref[...]
    scale = lax.rsqrt(jnp.mean(residual * residual, -1, keepdims=True) + NORM_EPS)
    gained = full_ref[...] * gain_ref[1:2, :]
    inner = jnp.sum(gained * residual, -1, keepdims=True) / width
    d_residual = cot_ref[...].astype(F32) + scale * gained - residual * (scale * scale * scale * inner)
    own = pl.ds(pl.multiple_of(peer_ref[0] * cols, cols), cols)
    full_ref[...] = d_residual
    d_mixed = None
    for j in range(4):
        at = pl.ds(pl.multiple_of(peer_ref[j] * cols, cols), cols)
        term = dot_nt(full_ref[:, at].astype(BF16), ow_refs[j][own, :])
        d_mixed = term if d_mixed is None else d_mixed + term
    mine = full_ref[:, own]
    dres_ref[...] = mine
    dbr_ref[...] = mine.astype(BF16)
    rescol_ref[...] = res_ref[:, own]
    gate = jax.nn.sigmoid(gp_ref[...].astype(F32))
    d_gated = d_mixed * gate
    dga_ref[...] = d_gated.astype(BF16)
    d_gate = (d_gated * tot_ref[...].astype(F32) * (1.0 - gate)).astype(BF16)
    dgp_ref[...] = d_gate
    dgall_ref[...] = d_gate


def turn_call(block, spot, peers, pieces, res, cot, ow, gains, gp, tot, shared):
    rows, cols = gp.shape
    width = res.shape[1]
    tile = SPAN // 2
    steps = SPAN // tile
    low = block * steps
    whole = lambda a: pl.BlockSpec(a.shape, lambda i, n=a.ndim: (0,) * n)
    row = lambda n: pl.BlockSpec((tile, n), lambda i: (i, 0))
    piece = pl.BlockSpec((tile, width // 2), lambda i: (spot * steps + i, 0))
    at_rows = lambda n: pl.BlockSpec((tile, n), lambda i: (low + i, 0))
    struct = jax.ShapeDtypeStruct
    ins = [peers, *pieces, res, cot, gains, gp, *ow, tot]
    in_specs = [
        pl.BlockSpec(memory_space=pltpu.SMEM),
        piece,
        piece,
        piece,
        piece,
        at_rows(width),
        at_rows(width),
        whole(gains),
        at_rows(cols),
    ] + [whole(weight) for weight in ow]
    in_specs.append(at_rows(cols))
    aliases = {}
    if shared is not None:
        aliases = {len(ins) + n: n for n in range(len(shared))}
        ins += shared
        in_specs += [pl.BlockSpec(memory_space=pl.ANY)] * len(shared)
    got = pl.pallas_call(
        functools.partial(turn_kernel, shared is None),
        grid=(steps,),
        in_specs=in_specs,
        out_specs=[at_rows(cols)] * 4 + [row(cols)] * 2,
        out_shape=[
            struct((rows, cols), F32),
            struct((rows, cols), F32),
            struct((rows, cols), BF16),
            struct((rows, cols), BF16),
            struct((SPAN, cols), BF16),
            struct((SPAN, cols), BF16),
        ],
        input_output_aliases=aliases,
        scratch_shapes=[pltpu.VMEM((tile, width), F32)],
        cost_estimate=cost(5),
        name=f"turn_{block}",
    )(*ins)
    return list(got[:4]), got[4:]


def back_kernel(block, nb, shift, *refs):
    it = iter(refs)
    take = lambda n: [next(it) for _ in range(n)]
    first, last = block == 0, block == nb - 1
    seq_ref, q_ref, k_ref, v_ref, kt_ref, pers_ref, dga_ref, att_ref, lt_ref = take(9)
    a_ref, bt_ref = take(2)
    if not last:
        dk_in_ref, dv_in_ref, dp_in_ref, lg_ref, ga_ref, gbt_ref, ab_in_ref, btb_in_ref = take(8)
        sab_in_ref, sbtb_in_ref = take(2) if block < nb - 2 else (None, None)
        sa_ref, sbt_ref = (None, None) if first else take(2)
    dq_ref, dk_ref, dv_ref, dp_ref, ab_ref, btb_ref = take(6)
    if not last:
        (dlg_ref,) = take(1)
        sab_ref, sbtb_ref = (None, None) if first else take(2)
    dt_ref, dqt_ref, qt_ref, dot_ref = take(4)
    if not last:
        z_ref, zd_ref, r_ref, y_ref, h_ref = take(5)
    rows, cols = q_ref.shape
    head_size = 1 << shift
    heads = cols // head_size
    own = slice(block * rows, (block + 1) * rows)
    a_low = a_ref[...].astype(BF16)
    bt_low = bt_ref[...].astype(BF16)
    if last:
        dk_ref[...] = jnp.zeros(dk_ref.shape, F32)
        dv_ref[...] = jnp.zeros(dv_ref.shape, F32)
        dp_ref[...] = jnp.zeros(dp_ref.shape, F32)
        ab_ref[...] = jnp.zeros(ab_ref.shape, F32)
        btb_ref[...] = jnp.zeros(btb_ref.shape, F32)
    else:
        dk_ref[...] = dk_in_ref[...]
        dv_ref[...] = dv_in_ref[...]
        dp_ref[...] = dp_in_ref[...]
    pick = (iota((8, cols), 1) >> shift) == iota((8, cols), 0)
    d_gated = dga_ref[...].astype(F32)
    dt_ref[...] = dot_nt(jnp.where(pick, 1.0, 0.0), d_gated * att_ref[...].astype(F32), HIGH)
    dq_ref[...] = jnp.zeros((rows, cols), F32)
    qt_ref[...] = jnp.transpose(q_ref[...].astype(F32)).astype(BF16)
    dot_ref[...] = jnp.transpose(d_gated).astype(BF16)
    if not last:
        valid, count = valid_column(seq_ref, block * rows, rows)
        weight = valid / count
        width = a_ref.shape[1]
        logits = lg_ref[...]
        sig_step = jax.nn.sigmoid(gate_rows(logits, 0, heads, head_size, width))
        keep = jax.nn.sigmoid(gate_rows(logits, 1, heads, head_size, width))
        sig_forget = jax.nn.sigmoid(gate_rows(logits, 2, heads, head_size, width))
        tot_a, tot_b = ab_in_ref[...], btb_in_ref[...]
        if sab_in_ref is not None:
            tot_a, tot_b = tot_a + sab_in_ref[...], tot_b + sbtb_in_ref[...]
        h_ref[0] = (-0.2 * sig_step * tot_a).astype(BF16)
        h_ref[1] = (-0.2 * sig_step * tot_b).astype(BF16)
        d_step = -(ga_ref[...] * tot_a + gbt_ref[...] * tot_b)
        groups = [d_step * (0.2 * sig_step * (1.0 - sig_step)), None, None]
        if not first:
            groups[1] = (sa_ref[...] * tot_a + sbt_ref[...] * tot_b) * (keep * (1.0 - keep))
        d_forget = -(a_ref[...] * ab_in_ref[...] + bt_ref[...] * btb_in_ref[...])
        groups[2] = d_forget * (0.5 * sig_forget * (1.0 - sig_forget))
        d_logits = jnp.zeros(dlg_ref.shape, F32)
        for g, value in enumerate(groups):
            if value is None:
                continue
            for head in range(heads):
                part = value[head * head_size : (head + 1) * head_size, :]
                figure = jnp.sum(jnp.sum(part, 1, keepdims=True), 0, keepdims=True)
                here = iota(dlg_ref.shape, 1) == g * heads + head
                d_logits = d_logits + jnp.where(here, 1.0, 0.0) * figure
        dlg_ref[...] = d_logits
        stay = 1.0 - 0.5 * sig_forget
        ab_ref[...] = stay * ab_in_ref[...]
        btb_ref[...] = stay * btb_in_ref[...]
        if not first:
            sab_ref[...] = keep * tot_a
            sbtb_ref[...] = keep * tot_b
        r_ref[...] = jnp.zeros((rows, cols), F32)
        y_ref[...] = jnp.zeros((rows, cols), F32)

    def one_head(head, carry):
        mask = head_mask(cols, shift, head)
        mask_low = mask.astype(BF16)
        query = q_ref[...] * mask_low
        scaled = query * SCORE_SCALE
        d_out = dga_ref[...] * mask_low
        at = pl.ds(pl.multiple_of(head * head_size, head_size), head_size)
        inverse = lt_ref[pl.ds(head, 1), :]
        delta = dt_ref[pl.ds(head, 1), :]
        probs = jnp.exp(dot_nt(pers_ref[0], scaled)) * inverse
        d_scores = (probs * (dot_nt(pers_ref[1], d_out) - delta)).astype(BF16)
        dp_ref[0] = dp_ref[0] + dot_nn(d_scores, scaled)
        dp_ref[1] = dp_ref[1] + dot_nn(probs.astype(BF16), d_out)
        d_query = lax.dot_general(
            d_scores, pers_ref[0], (((0,), (0,)), ((), ())), preferred_element_type=F32
        )
        d_query = d_query * SCORE_SCALE
        d_query_t = jnp.zeros((head_size, rows), F32)
        for j in range(block + 1):
            span = slice(j * rows, (j + 1) * rows)
            probs = jnp.exp(dot_nt(k_ref[span, :], scaled)) * inverse
            if j == block:
                probs = jnp.where(iota((rows, rows), 0) <= iota((rows, rows), 1), probs, 0.0)
            d_scores = (probs * (dot_nt(v_ref[span, :], d_out) - delta)).astype(BF16)
            dv_ref[span, :] = dv_ref[span, :] + dot_nn(probs.astype(BF16), d_out)
            dk_ref[span, :] = dk_ref[span, :] + dot_nn(d_scores, scaled)
            d_query_t = d_query_t + dot_nn(kt_ref[at, span], d_scores)
        dqt_ref[at, :] = d_query_t * SCORE_SCALE
        hid = dot_nn(query, a_low)
        sig = jax.nn.sigmoid(hid)
        d_hid = dot_nn(d_out, bt_low) * (sig * (1.0 + hid * (1.0 - sig)))
        d_hid = d_hid.astype(BF16)
        dq_ref[...] = dq_ref[...] + (d_query + dot_nt(d_hid, a_low)) * mask
        grad_a = dot_nn(qt_ref[at, :], d_hid)
        grad_b = dot_nn(dot_ref[at, :], (hid * sig).astype(BF16))
        if not last:
            key = k_ref[own, :] * mask_low
            hid = dot_nn(key, a_low)
            probe = dot_nn(key, h_ref[0])
            sig = jax.nn.sigmoid(hid)
            act = (hid * sig).astype(BF16)
            z_ref[head] = act
            slope = sig * (1.0 + hid * (1.0 - sig))
            curve = sig * (1.0 - sig) * (2.0 + hid * (1.0 - 2.0 * sig))
            target = v_ref[own, :].astype(F32)
            resid = (dot_nt(act, bt_low) - target) * mask * weight
            r_ref[...] = r_ref[...] + resid
            resid = resid.astype(BF16)
            d_act = dot_nn(resid, bt_low)
            d_slope = (probe * slope).astype(BF16)
            zd_ref[head] = d_slope
            d_net = (dot_nt(act, h_ref[1]) + dot_nt(d_slope, bt_low)) * mask * weight
            y_ref[...] = y_ref[...] + d_net
            back = dot_nn(resid, h_ref[1]) + dot_nn(d_net.astype(BF16), bt_low)
            d_hid = (probe * d_act * curve + back * slope).astype(BF16)
            direct = (d_act * slope).astype(BF16)
            d_key = (dot_nt(direct, h_ref[0]) + dot_nt(d_hid, a_low)) * mask
            dk_ref[own, :] = dk_ref[own, :] + d_key
            grad_a = grad_a + dot_nn(kt_ref[at, own], d_hid)
        ab_ref[at, :] = ab_ref[at, :] + grad_a
        btb_ref[at, :] = btb_ref[at, :] + grad_b
        return carry

    lax.fori_loop(0, heads, one_head, 0)
    dq_ref[...] = dq_ref[...] + jnp.transpose(dqt_ref[...])
    if not last:
        dv_ref[own, :] = dv_ref[own, :] - y_ref[...]
        resid_t = jnp.transpose(r_ref[...]).astype(BF16)
        net_t = jnp.transpose(y_ref[...]).astype(BF16)
        for head in range(heads):
            at = slice(head * head_size, (head + 1) * head_size)
            grad_b = dot_nn(resid_t[at, :], zd_ref[head]) + dot_nn(net_t[at, :], z_ref[head])
            btb_ref[at, :] = btb_ref[at, :] + grad_b


def back_parts(block, nb, shift, seq, q, k, v, kt, pers, dga, att, linv, state, grads, adjoint):
    cols = q.shape[1]
    heads = cols >> shift
    first, last = block == 0, block == nb - 1
    done = (block + 1) * SPAN
    whole = lambda s: pl.BlockSpec(s, lambda i, n=len(s): (0,) * n)
    at_block = pl.BlockSpec((SPAN, cols), lambda i: (block, 0))
    upto = pl.BlockSpec((done, cols), lambda i: (0, 0))
    square = state["a"].shape
    ins = [seq, q, k, v, kt, pers, dga, att, linv, state["a"], state["bt"]]
    in_specs = [
        pl.BlockSpec(memory_space=pltpu.SMEM),
        at_block,
        upto,
        upto,
        pl.BlockSpec((cols, done), lambda i: (0, 0)),
        whole(pers.shape),
        pl.BlockSpec((SPAN, cols), lambda i: (0, 0)),
        at_block,
        pl.BlockSpec((8, SPAN), lambda i: (0, block)),
        whole(square),
        whole(square),
    ]
    if not last:
        ins += [grads["dk"], grads["dv"], grads["dp"], state["lg"], state["ga"], state["gbt"]]
        ins += [adjoint["ab"], adjoint["btb"]]
        in_specs += [upto, upto, whole(pers.shape)]
        in_specs += [pl.BlockSpec((8, state["lg"].shape[1]), lambda i: (block, 0))]
        in_specs += [whole(square)] * 4
        if block < nb - 2:
            ins += [adjoint["sab"], adjoint["sbtb"]]
            in_specs += [whole(square)] * 2
        if not first:
            ins += [state["sa"], state["sbt"]]
            in_specs += [whole(square)] * 2
    names = ["dq", "dk", "dv", "dp", "ab", "btb"]
    shapes = [(SPAN, cols), (done, cols), (done, cols), pers.shape, square, square]
    if not last:
        names.append("dlg")
        shapes.append((8, state["lg"].shape[1]))
        if not first:
            names += ["sab", "sbtb"]
            shapes += [square, square]
    scratch = [
        pltpu.VMEM((8, SPAN), F32),
        pltpu.VMEM((cols, SPAN), F32),
        pltpu.VMEM((cols, SPAN), BF16),
        pltpu.VMEM((cols, SPAN), BF16),
    ]
    if not last:
        scratch += [
            pltpu.VMEM((heads, SPAN, square[1]), BF16),
            pltpu.VMEM((heads, SPAN, square[1]), BF16),
            pltpu.VMEM((SPAN, cols), F32),
            pltpu.VMEM((SPAN, cols), F32),
            pltpu.VMEM((2,) + square, BF16),
        ]
    return ins, in_specs, names, shapes, scratch


def back_call(block, nb, shift, *args):
    ins, in_specs, names, shapes, scratch = back_parts(block, nb, shift, *args)
    outs = pl.pallas_call(
        functools.partial(back_kernel, block, nb, shift),
        grid=(1,),
        in_specs=in_specs,
        out_specs=[pl.BlockSpec(s, lambda i, n=len(s): (0,) * n) for s in shapes],
        out_shape=[jax.ShapeDtypeStruct(s, F32) for s in shapes],
        scratch_shapes=scratch,
        cost_estimate=cost(17),
        name=f"back_{block}",
    )(*ins)
    return dict(zip(names, outs))


def unprep_kernel(block, nb, shift, *refs):
    it = iter(refs)
    take = lambda n: [next(it) for _ in range(n)]
    first, last = block == 0, block == nb - 1
    seq_ref, peer_ref, dq_ref, dk_ref, dv_ref, dgp_ref, pre_ref, w_ref, conv_ref = take(9)
    x_ref, gain_ref = take(2)
    halo_ref = None if first else take(1)[0]
    dp_ref, pers_ref, ab_ref, btb_ref, gain_two_ref = take(5) if first else [None] * 5
    if not last:
        edge_in_ref, dlg_ref, gate_ref, mean_ref = take(4)
        cg_in_ref, gg_in_ref, gate_in_ref = take(7)[:3]
    cg_ref, gg_ref, gate_out_ref = take(3)
    dproj_ref, keep_ref, send_ref, inner_ref, edge_ref = take(5)
    small_ref, gains_ref = take(2) if first else (None, None)
    ext_ref, dext_ref, low_ref = take(3)
    rows, cols = dq_ref.shape
    width = x_ref.shape[1]
    blocks = head_blocks(cols, shift)
    taps = conv_ref.shape[1]
    d_normed = dot_nt(dgp_ref[...], w_ref[3])
    dproj_ref[3] = dgp_ref[...]
    if last:
        cg_ref[...] = jnp.zeros(cg_ref.shape, F32)
        gg_ref[...] = jnp.zeros(gg_ref.shape, F32)
        gate_out_ref[...] = jnp.zeros(gate_out_ref.shape, F32)
    else:
        cg_ref[...] = cg_in_ref[...]
        gg_ref[...] = gg_in_ref[...]
    for i in range(3):
        pre = pre_ref[i].astype(F32)
        ext_ref[0:HALO, :] = jnp.zeros((HALO, cols), F32) if first else halo_ref[i, HALO:, :].astype(F32)
        ext_ref[HALO : HALO + rows, :] = pre
        shifted = [pre] + [ext_ref[HALO - j : HALO - j + rows, :] for j in range(1, taps)]
        conv = conv_ref[i, 0:1, :] * pre
        for j in range(1, taps):
            conv = conv + conv_ref[i, j : j + 1, :] * shifted[j]
        sig = jax.nn.sigmoid(conv)
        d_act = (dq_ref, dk_ref, dv_ref)[i][...]
        if i < 2:
            act = conv * sig
            scale = lax.rsqrt(head_sum(act * act, blocks) + UNIT_EPS)
            d_act = scale * (d_act - act * (scale * scale * head_sum(d_act * act, blocks)))
        d_conv = d_act * (sig * (1.0 + conv * (1.0 - sig)))
        edge_ref[i] = d_conv[0:HALO, :]
        dext_ref[0:rows, :] = d_conv
        dext_ref[rows : rows + HALO, :] = (
            jnp.zeros((HALO, cols), F32) if last else edge_in_ref[i]
        )
        d_pre = conv_ref[i, 0:1, :] * d_conv
        for j in range(taps):
            if j:
                d_pre = d_pre + conv_ref[i, j : j + 1, :] * dext_ref[j : j + rows, :]
            at = slice(i * taps + j, i * taps + j + 1)
            cg_ref[at, :] = cg_ref[at, :] + jnp.sum(d_conv * shifted[j], 0, keepdims=True)
        d_low = d_pre.astype(BF16)
        dproj_ref[i] = d_low
        d_normed = d_normed + dot_nt(d_low, w_ref[i])
    if not last:
        valid, count = valid_column(seq_ref, block * rows, rows)
        d_mean = jnp.dot(
            dlg_ref[...], gate_ref[...], preferred_element_type=F32, precision=HIGH
        )
        d_normed = d_normed + (valid / count) * d_mean[0:1, :]
        outer = lax.dot_general(
            dlg_ref[...] * 0.125,
            mean_ref[...],
            (((0,), (0,)), ((), ())),
            preferred_element_type=F32,
            precision=HIGH,
        )
        gate_out_ref[...] = gate_in_ref[...]
        at = slice(0, outer.shape[0])
        gate_out_ref[at, :] = gate_in_ref[at, :] + outer
    x = x_ref[...].astype(F32)
    scale = lax.rsqrt(jnp.mean(x * x, -1, keepdims=True) + NORM_EPS)
    weighted = d_normed * x
    gains = jnp.sum(weighted * scale, 0, keepdims=True)
    gg_ref[...] = gg_ref[...] + jnp.broadcast_to(gains, gg_ref.shape)
    gained = jnp.broadcast_to(gain_ref[0:1, :], (8, width))
    inner_ref[...] = dot_nt(gained.astype(BF16), weighted.astype(BF16))
    low_ref[...] = d_normed.astype(BF16)
    for slot, out_ref in ((0, keep_ref), (1, send_ref)):
        for n in range(2):
            start = pl.multiple_of(peer_ref[slot + 2 * n] * cols, cols)
            out_ref[n] = low_ref[:, pl.ds(start, cols)]
    if first:
        keys = pers_ref[0]
        d_keys = dp_ref[0]
        scale = lax.rsqrt(head_sum(keys * keys, blocks) + UNIT_EPS)
        along = head_sum(d_keys * keys, blocks)
        d_keys = scale * (d_keys - keys * (scale * scale * along))
        across = lambda a: [a[:, n : n + cols] for n in range(0, width, cols)]
        parts = [ab_ref[...], btb_ref[...], *across(gate_out_ref[...]), cg_ref[...]]
        parts += [d_keys, dp_ref[1]]
        at = 0
        for part in parts:
            small_ref[at : at + part.shape[0], :] = part.astype(BF16)
            at += part.shape[0]
        gains_ref[0:1, :] = gg_ref[0:1, :]
        gains_ref[1:2, :] = gain_two_ref[0:1, :]
        small_ref[at:, :] = jnp.zeros((small_ref.shape[0] - at, cols), BF16)


def unprep_call(
    block, nb, shift, seq, peers, back, dgp, pre, w, conv, x, gains, gate, mean, pers, gain_two,
    shared,
):
    rows, width = x.shape
    cols = dgp.shape[1]
    first, last = block == 0, block == nb - 1
    whole = lambda a: pl.BlockSpec(a.shape, lambda i, n=len(a.shape): (0,) * n)
    smem = pl.BlockSpec(memory_space=pltpu.SMEM)
    at_block = pl.BlockSpec((SPAN, cols), lambda i: (block, 0))
    stacked = lambda n: pl.BlockSpec((n, SPAN, cols), lambda i: (0, block, 0))
    struct = jax.ShapeDtypeStruct
    gate_rows_out = 16
    names = ["cg", "gg", "gate", "dproj", "keep", "send", "inner", "edge"]
    outs = [
        struct((16, cols), F32),
        struct((8, width), F32),
        struct((gate_rows_out, width), F32),
        struct((4, rows, cols), BF16),
        struct((2, rows, cols), BF16),
        struct((2, rows, cols), BF16),
        struct((8, rows), F32),
        struct((3, HALO, cols), F32),
    ]
    out_specs = [whole(a) for a in outs[:3]]
    out_specs += [
        stacked(4),
        stacked(2),
        stacked(2),
        pl.BlockSpec((8, SPAN), lambda i: (0, block)),
        whole(outs[7]),
    ]
    ins = [seq, peers, back["dq"], back["dk"], back["dv"], dgp, pre, w, conv, x, gains]
    in_specs = [
        smem,
        smem,
        whole(back["dq"]),
        at_block,
        at_block,
        pl.BlockSpec((SPAN, cols), lambda i: (0, 0)),
        stacked(3),
        whole(w),
        whole(conv),
        pl.BlockSpec((SPAN, width), lambda i: (block, 0)),
        whole(gains),
    ]
    aliases = {}
    if not first:
        ins.append(pre)
        in_specs.append(
            pl.BlockSpec((3, 2 * HALO, cols), lambda i: (0, block * (SPAN // HALO // 2) - 1, 0))
        )
    else:
        others = [back["dp"], pers, back["ab"], back["btb"], gain_two]
        ins += others
        in_specs += [whole(a) for a in others]
        names += ["small", "gains"]
        ahead = 5 * width // SMALL_ROWS
        outs.append(struct(((ahead + 1) * SMALL_ROWS, cols), BF16))
        out_specs.append(pl.BlockSpec((SMALL_ROWS, cols), lambda i: (ahead, 0)))
        outs.append(struct((2, width), F32))
        out_specs.append(whole(outs[-1]))
    if not last:
        ins += [shared["edge"], back["dlg"], gate, mean]
        in_specs += [whole(shared["edge"]), whole(back["dlg"]), whole(gate)]
        in_specs.append(pl.BlockSpec((8, width), lambda i: (block, 0)))
        aliases = {len(ins) + n: n for n in range(7)}
        ins += [shared[name] for name in names[:7]]
        in_specs += [whole(a) for a in outs[:3]] + [pl.BlockSpec(memory_space=pl.ANY)] * 4
    got = pl.pallas_call(
        functools.partial(unprep_kernel, block, nb, shift),
        grid=(1,),
        in_specs=in_specs,
        out_specs=out_specs,
        out_shape=outs,
        input_output_aliases=aliases,
        scratch_shapes=[
            pltpu.VMEM((HALO + SPAN, cols), F32),
            pltpu.VMEM((SPAN + HALO, cols), F32),
            pltpu.VMEM((SPAN, width), BF16),
        ],
        cost_estimate=cost(10),
        name=f"unprep_{block}",
    )(*ins)
    return dict(zip(names, got))


def rear_kernel(block, nb, shift, counts, *refs):
    it = iter(refs)
    take = lambda n: [next(it) for _ in range(n)]
    first = block == 0
    back_in = take(counts[0])
    peer_ref, dgp_ref, pre_any, w_any, conv_ref, x_any, gain_ref = take(7)
    halo = take(0 if first else 1)
    pers_ref, gain_two_ref = take(2) if first else (None, None)
    edge_in_ref, gate_ref, mean_ref = take(3)
    before = take(7)
    dk_out_ref, dv_out_ref = (None, None) if first else take(2)
    sums = [] if first else take(5)
    results = take(10 if first else 8)
    dq_ref, dk_ref, dv_ref, dlg_ref = take(4)
    if first:
        sums = take(3)
    back_room, unprep_room = take(counts[1]), take(3)
    pre_ref, w_ref, x_ref, sems = take(4)
    rows = dq_ref.shape[0]
    own = pl.ds(block * rows, rows)
    loads = [
        pltpu.make_async_copy(source, target, sems.at[n])
        for n, (source, target) in enumerate(
            ((pre_any.at[:, own, :], pre_ref), (w_any, w_ref), (x_any.at[own, :], x_ref))
        )
    ]
    for load in loads:
        load.start()
    dp_ref, ab_ref, btb_ref = sums[:3]
    back_kernel(
        block, nb, shift, *back_in, dq_ref, dk_ref, dv_ref, dp_ref, ab_ref, btb_ref, dlg_ref,
        *sums[3:], *back_room,
    )
    for load in loads:
        load.wait()
    unprep_kernel(
        block, nb, shift, back_in[0], peer_ref, dq_ref, dk_ref.at[own, :], dv_ref.at[own, :],
        dgp_ref, pre_ref, w_ref, conv_ref, x_ref, gain_ref, *halo,
        *([dp_ref, pers_ref, ab_ref, btb_ref, gain_two_ref] if first else []),
        edge_in_ref, dlg_ref, gate_ref, mean_ref, *before, *results, *unprep_room,
    )
    if not first:
        dk_out_ref[...] = dk_ref[0 : block * rows, :]
        dv_out_ref[...] = dv_ref[0 : block * rows, :]


def rear_call(
    block, nb, shift, back_args, peers, dgp, pre, w, conv, x, gains, gate, mean, pers, gain_two,
    shared,
):
    rows, width = x.shape
    cols = dgp.shape[1]
    first = block == 0
    ins, in_specs, names, shapes, back_room = back_parts(block, nb, shift, *back_args)
    counts = (len(ins), len(back_room))
    shape_of = dict(zip(names, shapes))
    whole = lambda a: pl.BlockSpec(a.shape, lambda i, n=len(a.shape): (0,) * n)
    anywhere = pl.BlockSpec(memory_space=pl.ANY)
    stacked = lambda n: pl.BlockSpec((n, SPAN, cols), lambda i: (0, block, 0))
    struct = jax.ShapeDtypeStruct
    ins = ins + [peers, dgp, pre, w, conv, x, gains]
    in_specs = in_specs + [
        pl.BlockSpec(memory_space=pltpu.SMEM),
        pl.BlockSpec((SPAN, cols), lambda i: (0, 0)),
        anywhere,
        anywhere,
        whole(conv),
        anywhere,
        whole(gains),
    ]
    kept, outs = [], []
    if first:
        ins += [pers, gain_two]
        in_specs += [whole(pers), whole(gain_two)]
    else:
        ins.append(pre)
        in_specs.append(
            pl.BlockSpec((3, 2 * HALO, cols), lambda i: (0, block * (SPAN // HALO // 2) - 1, 0))
        )
        kept = ["dk", "dv", "dp", "ab", "btb", "sab", "sbtb"]
        outs = [struct((block * SPAN, cols), F32)] * 2
        outs += [struct(shape_of[name], F32) for name in kept[2:]]
    out_specs = [whole(a) for a in outs]
    fresh = ["cg", "gg", "gate", "dproj", "keep", "send", "inner", "edge"]
    ins += [shared["edge"], gate, mean]
    in_specs += [whole(shared["edge"]), whole(gate)]
    in_specs.append(pl.BlockSpec((8, width), lambda i: (block, 0)))
    aliases = {len(ins) + n: len(outs) + n for n in range(7)}
    ins += [shared[name] for name in fresh[:7]]
    in_specs += [whole(shared[name]) for name in fresh[:3]] + [anywhere] * 4
    outs += [struct(shared[name].shape, shared[name].dtype) for name in fresh]
    out_specs += [whole(shared[name]) for name in fresh[:3]]
    out_specs += [
        stacked(4),
        stacked(2),
        stacked(2),
        pl.BlockSpec((8, SPAN), lambda i: (0, block)),
        whole(shared["edge"]),
    ]
    if first:
        fresh += ["small", "gains"]
        ahead = 5 * width // SMALL_ROWS
        outs.append(struct(((ahead + 1) * SMALL_ROWS, cols), BF16))
        out_specs.append(pl.BlockSpec((SMALL_ROWS, cols), lambda i: (ahead, 0)))
        outs.append(struct((2, width), F32))
        out_specs.append(whole(outs[-1]))
    inside = ["dq", "dk", "dv", "dlg"] + (["dp", "ab", "btb"] if first else [])
    got = pl.pallas_call(
        functools.partial(rear_kernel, block, nb, shift, counts),
        grid=(1,),
        in_specs=in_specs,
        out_specs=out_specs,
        out_shape=outs,
        input_output_aliases=aliases,
        scratch_shapes=[pltpu.VMEM(shape_of[name], F32) for name in inside]
        + back_room
        + [
            pltpu.VMEM((HALO + SPAN, cols), F32),
            pltpu.VMEM((SPAN + HALO, cols), F32),
            pltpu.VMEM((SPAN, width), BF16),
            pltpu.VMEM((3, SPAN, cols), BF16),
            pltpu.VMEM(w.shape, BF16),
            pltpu.VMEM((SPAN, width), BF16),
            pltpu.SemaphoreType.DMA((3,)),
        ],
        cost_estimate=cost(25),
        name=f"rear_{block}",
    )(*ins)
    got = dict(zip(kept + fresh, got))
    return {name: got[name] for name in kept}, {name: got[name] for name in fresh}


def finish_kernel(peer_ref, x_ref, dres_ref, half_ref, far_ref, i0_ref, i1_ref, gain_ref, out_ref):
    rows, width = x_ref.shape
    cols = out_ref.shape[1]
    own = pl.ds(pl.multiple_of(peer_ref[0] * cols, cols), cols)
    x = x_ref[...].astype(F32)
    scale = lax.rsqrt(jnp.mean(x * x, -1, keepdims=True) + NORM_EPS)
    inner = jnp.transpose(i0_ref[...] + i1_ref[...])[:, 0:1] / width
    d_normed = half_ref[0].astype(F32) + far_ref[...].astype(F32)
    d_normed = d_normed * gain_ref[0:1, own]
    x_own = x_ref[:, own].astype(F32)
    out_ref[...] = dres_ref[...] + scale * d_normed - x_own * (scale * scale * scale * inner)


def finish_call(peers, x, dres, half, far, inner, inner_far, gains):
    rows, width = x.shape
    cols = dres.shape[1]
    row = lambda n: pl.BlockSpec((SPAN, n), lambda i: (i, 0))
    across = pl.BlockSpec((8, SPAN), lambda i: (0, i))
    return pl.pallas_call(
        finish_kernel,
        grid=(rows // SPAN,),
        in_specs=[
            pl.BlockSpec(memory_space=pltpu.SMEM),
            row(width),
            row(cols),
            pl.BlockSpec((1, SPAN, cols), lambda i: (0, i, 0)),
            row(cols),
            across,
            across,
            pl.BlockSpec(gains.shape, lambda i: (0, 0)),
        ],
        out_specs=row(cols),
        out_shape=jax.ShapeDtypeStruct((rows, cols), F32),
        cost_estimate=cost(4),
        name="finish",
    )(peers, x, dres, half, far, inner, inner_far, gains)


def unpack_kernel(shift, main_ref, small_ref, proj_ref, out_ref, a_ref, b_ref, gate_ref, conv_ref,
                  pers_ref, gain_ref):
    step = pl.program_id(0)
    cols = main_ref.shape[1]
    head_size = 1 << shift
    heads = cols // head_size
    last = pl.num_programs(0) - 1

    @pl.when(step < last)
    def _():
        proj_ref[0] = main_ref[...].astype(F32)

    @pl.when(step == last)
    def _():
        out_ref[...] = main_ref[...].astype(F32)

    @pl.when(step == 0)
    def _():
        small = small_ref[...].astype(F32)
        at = 2 * cols
        for h in range(heads):
            rows = slice(h * head_size, (h + 1) * head_size)
            a_ref[h] = small[rows, :]
            b_ref[h] = small[cols : 2 * cols][rows, :]
        lanes = gain_ref.shape[1] // cols
        for n in range(lanes):
            for g in range(3):
                row = at + 16 * n + g * heads
                gate_ref[g, :, n * cols : (n + 1) * cols] = small[row : row + heads, :]
        at += 16 * lanes
        taps = conv_ref.shape[1]
        for i in range(3):
            conv_ref[i] = small[at + i * taps : at + (i + 1) * taps, :]
        at += 16
        count = pers_ref.shape[2]
        for i in range(2):
            for h in range(heads):
                spot = slice(h * head_size, (h + 1) * head_size)
                pers_ref[i, h] = small[at + i * count : at + (i + 1) * count, spot]
        at += 2 * count
        for i in range(2):
            for n in range(lanes):
                row = at + i * lanes + n
                gain_ref[i : i + 1, n * cols : (n + 1) * cols] = small[row : row + 1, :]


def unpack_call(payload, shift, width, mem_hid, taps, persist_rows):
    cols = payload.shape[1]
    heads = cols >> shift
    head_size = 1 << shift
    ahead = 5 * width // SMALL_ROWS
    struct = jax.ShapeDtypeStruct
    outs = [
        struct((4, width, cols), F32),
        struct((width, cols), F32),
        struct((heads, head_size, mem_hid), F32),
        struct((heads, head_size, mem_hid), F32),
        struct((3, heads, width), F32),
        struct((3, taps, cols), F32),
        struct((2, heads, persist_rows, head_size), F32),
        struct((2, width), F32),
    ]
    whole = lambda a: pl.BlockSpec(a.shape, lambda i, n=len(a.shape): (0,) * n)
    return pl.pallas_call(
        functools.partial(unpack_kernel, shift),
        grid=(5,),
        in_specs=[
            pl.BlockSpec((width, cols), lambda i: (i, 0)),
            pl.BlockSpec((SMALL_ROWS, cols), lambda i: (ahead, 0)),
        ],
        out_specs=[pl.BlockSpec((1, width, cols), lambda i: (jnp.minimum(i, 3), 0, 0))]
        + [whole(a) for a in outs[1:]],
        out_shape=outs,
        cost_estimate=cost(4),
        name="unpack",
    )(payload, payload)


def ring_of(size):
    return [list(range(0, size, 2)) + list(range(size - 1 - size % 2, 0, -2))]


def ring_scatter(payload, axis, size):
    return lax.psum_scatter(
        payload, axis, scatter_dimension=0, axis_index_groups=ring_of(size), tiled=True
    )


def ring_gather(part, axis, size):
    return lax.all_gather(part, axis, axis=0, axis_index_groups=ring_of(size), tiled=True)


def stacked_rows(pieces, full):
    at = 0
    for piece in pieces:
        full = lax.dynamic_update_slice(full, piece, (at, 0))
        at += piece.shape[0]
    return full


def after(value, *others):
    return lax.optimization_barrier((value, *others))[0]


def per_device(
    ring_size,
    layer_input,
    proj_weight,
    conv_weight,
    persist_kv,
    memory_in,
    memory_out,
    memory_gate,
    out_weight,
    ffn_in,
    ffn_out,
    norm_gains,
    seq_len,
    out_grad,
):
    rows, width = layer_input.shape
    cols = proj_weight.shape[2]
    heads = persist_kv.shape[1]
    head_size = persist_kv.shape[3]
    shift = head_size.bit_length() - 1
    mem_hid = memory_in.shape[2]
    nb = rows // SPAN
    taps = conv_weight.shape[1]
    me = lax.axis_index("head")
    count = width // cols
    peers = jnp.stack([me, me ^ 1, me ^ 2, me ^ 3]).astype(jnp.int32)
    swap = lambda a, bit: lax.ppermute(a, "head", [(i, i ^ bit) for i in range(count)])
    far_weight, far_cot = swap(out_weight, 2), swap(out_grad, 2)
    near_weight, near_cot = swap(out_weight, 1), swap(out_grad, 1)
    gate = jnp.transpose(memory_gate, (1, 2, 0))
    groups = [list(range(nb - 1)), [nb - 1]] if nb > 1 else [[0]]
    state = [memory_in.reshape(cols, mem_hid)]
    state.append(jnp.transpose(memory_out, (0, 2, 1)).reshape(cols, mem_hid))
    states = [dict(a=state[0], bt=state[1], sa=None, sbt=None)]
    earlier = gathered = [near_weight, near_cot, far_weight]
    shared, carried, pieces = None, [], []
    for n, blocks in enumerate(groups):
        if n:
            state = [after(state[0], peers, *earlier), *state[1:]]
        shared, (mixed, pers_low, flat, pers), squares, carried = lead_call(
            blocks, nb, shift, seq_len, layer_input, proj_weight, conv_weight, norm_gains, gate,
            persist_kv, state, carried, shared,
        )
        for a, bt, sa, sbt, ga, gbt in squares:
            states[-1].update(ga=ga, gbt=gbt)
            states.append(dict(a=a, bt=bt, sa=sa, sbt=sbt))
            state = [a, bt] if blocks[-1] + 1 == nb - 1 else [a, bt, sa, sbt]
        sent = after(mixed, *gathered)
        pieces.append([mixed, swap(sent, 1), swap(sent, 2)])
        gathered = pieces[n][1:]
        if n == 0:
            last_weight = swap(after(far_weight, sent), 1)
            last_cot = swap(after(far_cot, sent), 1)
            gathered = gathered + [last_weight, last_cot]
    q, k, v, kt, pre, gp, nl, mean, lg, tot, att, lt = shared
    for state in states:
        state["lg"] = lg
    gate = flat
    ow = (out_weight, near_weight, far_weight, last_weight)
    if nb > 1:
        pieces[0].append(swap(after(pieces[0][2], pieces[1][0]), 1))
    fout = after(ffn_out, pieces[-1][0])
    cot_full, d_hidden = cot_call(peers, (out_grad, near_cot, far_cot, last_cot), fout)
    pieces[-1].append(swap(after(pieces[-1][2], cot_full), 1))
    normed_two, hidden, dgu, mixed_full, residual, grads_room = ffn_call(
        groups, peers, after(layer_input, cot_full), pieces, ow, norm_gains, ffn_in, d_hidden
    )
    along_rows = (((0,), (0,)), ((), ()))
    outer = lambda left, right: lax.dot_general(
        left, right, along_rows, preferred_element_type=F32
    ).astype(BF16)
    out_part = outer(hidden, cot_full)
    ffn_grads = stacked_rows(
        [out_part, outer(after(normed_two, out_part), dgu[0]), outer(normed_two, dgu[1])],
        grads_room,
    )
    ffn_part = ring_scatter(ffn_grads, "dp", ring_size)
    s1, r2, gain_two = [], [], None
    tie = (ffn_grads,)
    for n, blocks in enumerate(reversed(groups)):
        gain_two, keep, send = ffn_back_call(
            blocks, peers, after(dgu, *tie), ffn_in, residual, gain_two
        )
        send = after(send, *r2) if r2 else send
        s1.append((keep.astype(F32) + swap(send, 1).astype(F32)).astype(BF16))
        r2.append(swap(s1[n], 2))
        tie = (s1[0],)
    tie = (gain_two,)
    back = unprep = None
    gated = [None] * nb

    def relayed(n, *ties):
        return s1[n], r2[n], swap(after(s1[n], *ties), 1), swap(after(r2[n], *ties), 1)

    def turn(c, spot, parts, turned, *ties):
        turned, gated[c] = turn_call(
            c, spot, peers, parts, after(residual, *ties), cot_full, ow, norm_gains, gp, tot, turned
        )
        return turned

    turned = turn(nb - 1, 0, relayed(0, r2[0]), None, *tie)
    tie = tuple(s1[1:])
    for c in reversed(range(nb)):
        back_args = (
            seq_len, after(q, *tie), k, v, kt, pers_low, gated[c][0], att, lt, states[c], back, back
        )
        rest = (
            gated[c][1], pre, proj_weight, conv_weight, layer_input, norm_gains, gate, mean, pers,
            gain_two, unprep,
        )
        if c == nb - 1:
            back = back_call(c, nb, shift, *back_args)
            parts = relayed(1, back["dq"]) if c else None
            unprep = unprep_call(c, nb, shift, seq_len, peers, back, *rest)
        else:
            back, unprep = rear_call(c, nb, shift, back_args, peers, *rest)
        tie = ()
        if c:
            turned = turn(c - 1, c - 1, parts, turned, unprep["edge"])
        if c == nb - 1:
            edge, ffn_part = lax.optimization_barrier((turned[2], ffn_part))
            turned[2] = edge
            ffn_grads = ring_gather(ffn_part, "dp", ring_size)
            tie = (edge,)
    d_res, res_cols, d_branch, d_gate_all = turned
    gains = unprep["gains"]
    gains = gains + sum(swap(gains, bit) for bit in (1, 2, 3))
    cuts = [4 * width, width, 2 * cols, 16 * width // cols, 16, pers.shape[1] * 2]
    cuts.append(2 * width // cols)
    payload = stacked_rows(
        [outer(nl, unprep["dproj"][i]) for i in range(4)]
        + [outer(mixed_full, d_branch)],
        unprep["small"],
    )
    payload = lax.dynamic_update_slice(
        payload, gains.reshape(-1, cols).astype(BF16), (sum(cuts[:-1]), 0)
    )
    tie = (payload,)
    payload, ffn_grads = lax.optimization_barrier((payload, ffn_grads))
    ffn_in_grad = ffn_grads[width:].astype(F32).reshape(2, width, -1)
    ffn_out_grad = ffn_grads[:width].astype(F32)
    payload = ring_scatter(payload, "dp", ring_size)
    half = (
        unprep["keep"].astype(F32) + swap(after(unprep["send"], *tie), 1).astype(F32)
    ).astype(BF16)
    inner = unprep["inner"] + swap(unprep["inner"], 1)
    far = swap(half[1], 2)
    input_grad = finish_call(
        peers, layer_input, d_res, half, far, inner, swap(inner, 2), norm_gains
    )
    part_keep, part_send = down_call(peers, after(hidden, half), ffn_out, cols)
    payload, input_grad, ffn_in_grad, ffn_out_grad, part_keep, part_send = (
        lax.optimization_barrier(
            (payload, input_grad, ffn_in_grad, ffn_out_grad, part_keep, part_send)
        )
    )
    payload = ring_gather(payload, "dp", ring_size)
    part = (part_keep.astype(F32) + swap(part_send, 1).astype(F32)).astype(BF16)
    layer_output = res_cols + part[0].astype(F32) + swap(part[1], 2).astype(F32)
    layer_output = layer_output.astype(BF16)
    proj_grad, out_grads, a_grad, b_grad, gate_grad, conv_grad, pers_grad, gains = unpack_call(
        payload, shift, width, mem_hid, taps, persist_kv.shape[2]
    )
    return (
        layer_output,
        input_grad,
        proj_grad,
        conv_grad,
        pers_grad,
        a_grad,
        jnp.transpose(b_grad, (0, 2, 1)),
        jnp.transpose(gate_grad, (2, 0, 1)),
        out_grads,
        ffn_in_grad,
        ffn_out_grad,
        gains,
    )


def solution(mesh):
    in_specs = (
        P("dp", None),
        P(None, None, "head"),
        P(None, None, "head"),
        P(None, "head", None, None),
        P("head", None, None),
        P("head", None, None),
        P(None, None, "head"),
        P(None, "head"),
        P(None, None, "head"),
        P("head", None),
        P(),
        P("dp"),
        P("dp", "head"),
    )
    out_specs = (
        P("dp", "head"),
        P("dp", "head"),
        P(None, None, "head"),
        P(None, None, "head"),
        P(None, "head", None, None),
        P("head", None, None),
        P("head", None, None),
        P(None, None, "head"),
        P(None, "head"),
        P(None, None, "head"),
        P("head", None),
        P(),
    )
    body = functools.partial(per_device, mesh.shape["dp"])
    return jax.shard_map(
        body, mesh=mesh, in_specs=in_specs, out_specs=out_specs, check_vma=False
    )
```

```python
import functools

import jax
import jax.numpy as jnp
from jax import lax
from jax.experimental import pallas as pl
from jax.experimental.pallas import tpu as pltpu
from jax.sharding import PartitionSpec as P

F32 = jnp.float32
BF16 = jnp.bfloat16
HIGH = lax.Precision.HIGHEST
NORM_EPS = 1e-05
UNIT_EPS = 1e-06
SCORE_SCALE = 8.0
SPAN = 512
HALO = 8
COST_UNIT = 1.5e8
SMALL_ROWS = 640


def dot_nn(left, right):
    return jnp.dot(left, right, preferred_element_type=F32)


def dot_nt(left, right, precision=None):
    return lax.dot_general(
        left, right, (((1,), (1,)), ((), ())), preferred_element_type=F32, precision=precision
    )


def iota(shape, axis):
    return lax.broadcasted_iota(jnp.int32, shape, axis)


def cost(microseconds):
    return pl.CostEstimate(
        flops=int(microseconds * COST_UNIT), transcendentals=0, bytes_accessed=1 << 20
    )


def head_blocks(cols, shift):
    same = (iota((cols, cols), 0) >> shift) == (iota((cols, cols), 1) >> shift)
    return jnp.where(same, 1.0, 0.0).astype(BF16)


def head_sum(value, blocks):
    return dot_nn(value.astype(BF16), blocks)


def valid_column(seq_ref, start, rows):
    inside = (start + iota((rows, 1), 0)) < seq_ref[0]
    valid = jnp.where(inside, 1.0, 0.0)
    return valid, jnp.maximum(jnp.sum(valid, 0, keepdims=True), 1.0)


def head_mask(cols, shift, head):
    return jnp.where((iota((1, cols), 1) >> shift) == head, 1.0, 0.0)


def gate_rows(logits, group, heads, head_size, width):
    parts = [
        jnp.broadcast_to(
            logits[0:1, group * heads + head : group * heads + head + 1], (head_size, width)
        )
        for head in range(heads)
    ]
    return jnp.concatenate(parts, 0)


def prep_kernel(
    shift,
    low_block,
    seq_ref,
    x_ref,
    w_ref,
    conv_ref,
    gain_ref,
    gate_ref,
    pers_ref,
    edge_ref,
    q_ref,
    k_ref,
    v_ref,
    kt_ref,
    pre_ref,
    gp_ref,
    nl_ref,
    mean_ref,
    lg_ref,
    pers_out_ref,
    flat_ref,
    pers_flat_ref,
    ext_ref,
):
    step = pl.program_id(0)
    rows, cols = q_ref.shape
    blocks = head_blocks(cols, shift)

    @pl.when(step == 0)
    def _():
        ext_ref[:, 0:HALO, :] = (
            jnp.zeros((3, HALO, cols), F32) if edge_ref is None else edge_ref[...]
        )
        heads = gate_ref.shape[1]
        for h in range(heads):
            spot = slice(h << shift, (h + 1) << shift)
            for i in range(2):
                pers_flat_ref[i, :, spot] = pers_ref[i, h]
        keys = pers_flat_ref[0]
        keys = keys * lax.rsqrt(head_sum(keys * keys, blocks) + UNIT_EPS)
        pers_out_ref[0] = keys.astype(BF16)
        pers_out_ref[1] = pers_flat_ref[1].astype(BF16)
        for g in range(3):
            flat_ref[g * heads : (g + 1) * heads, :] = gate_ref[g]

    x = x_ref[...].astype(F32)
    scale = lax.rsqrt(jnp.mean(x * x, -1, keepdims=True) + NORM_EPS)
    normed = x * scale * gain_ref[0:1, :]
    low = normed.astype(BF16)
    nl_ref[...] = low
    inside = ((low_block + step) * rows + iota((8, rows), 1)) < seq_ref[0]
    valid = jnp.where(inside, 1.0, 0.0)
    count = jnp.maximum(jnp.sum(valid, 1, keepdims=True), 1.0)
    mean = dot_nn(valid.astype(BF16), low) / count
    mean_ref[...] = mean
    lg_ref[...] = dot_nt(mean, flat_ref[...], HIGH)
    gp_ref[...] = dot_nn(low, w_ref[3]).astype(BF16)
    for i in range(3):
        pre = dot_nn(low, w_ref[i])
        pre_ref[i] = pre.astype(BF16)
        ext_ref[i, HALO : HALO + rows, :] = pre
        conv = conv_ref[i, 0:1, :] * pre
        for j in range(1, conv_ref.shape[1]):
            conv = conv + conv_ref[i, j : j + 1, :] * ext_ref[i, HALO - j : HALO - j + rows, :]
        ext_ref[i, 0:HALO, :] = pre[rows - HALO :, :]
        act = conv * jax.nn.sigmoid(conv)
        if i < 2:
            act = act * lax.rsqrt(head_sum(act * act, blocks) + UNIT_EPS)
        act_low = act.astype(BF16)
        (q_ref, k_ref, v_ref)[i][...] = act_low
        if i == 1:
            kt_ref[...] = jnp.transpose(act_low.astype(F32)).astype(BF16)


def mix_kernel(block, blocks_all, shift, first, last, *refs):
    it = iter(refs)
    seq_ref, lg_ref, q_ref, k_ref, v_ref, kt_ref, pers_ref, gp_ref, a_ref, bt_ref = (
        next(it) for _ in range(10)
    )
    sa_ref, sbt_ref = (None, None) if first or last else (next(it), next(it))
    mixed_ref, tot_out_ref, att_out_ref, lt_ref = (next(it) for _ in range(4))
    if not last:
        a2_ref, bt2_ref, sa2_ref, sbt2_ref, ga_ref, gbt_ref = (next(it) for _ in range(6))
    tot_ref, att_ref, linv_ref = (next(it) for _ in range(3))
    if not last:
        z_ref, r_ref = next(it), next(it)
    rows, cols = q_ref.shape
    head_size = 1 << shift
    heads = cols // head_size
    a_low = a_ref[...].astype(BF16)
    bt_low = bt_ref[...].astype(BF16)
    valid, count = valid_column(seq_ref, block * rows, rows)
    weight = valid / count
    att_ref[...] = jnp.zeros((rows, cols), F32)
    linv_ref[...] = jnp.zeros((rows, cols), F32)
    tot_ref[...] = jnp.zeros((rows, cols), F32)
    if not last:
        r_ref[...] = jnp.zeros((rows, cols), F32)

    def one_head(head, carry):
        mask = head_mask(cols, shift, head)
        mask_low = mask.astype(BF16)
        ones_low = (1.0 - mask).astype(BF16)
        query = q_ref[...] * mask_low
        scaled = query * SCORE_SCALE
        raised = jnp.exp(dot_nt(scaled, pers_ref[0])).astype(BF16)
        total = dot_nn(raised, pers_ref[1] * mask_low + ones_low)
        for j in range(block + 1):
            span = slice(j * rows, (j + 1) * rows)
            raised = jnp.exp(dot_nt(scaled, k_ref[span, :]))
            if j == block:
                raised = jnp.where(
                    iota((rows, rows), 0) >= iota((rows, rows), 1), raised, 0.0
                )
            total = total + dot_nn(raised.astype(BF16), v_ref[span, :] * mask_low + ones_low)
        inverse = 1.0 / pltpu.roll(total, head_size, 1)
        inside = jnp.broadcast_to(mask, (rows, cols)) > 0.5
        linv_ref[...] = jnp.where(inside, inverse, linv_ref[...])
        attended = jnp.where(inside, total * inverse, 0.0)
        att_ref[...] = att_ref[...] + attended
        hid = dot_nn(query, a_low)
        hid = hid * jax.nn.sigmoid(hid)
        recalled = dot_nt(hid.astype(BF16), bt_low) * mask
        tot_ref[...] = tot_ref[...] + attended + recalled
        if not last:
            hid = dot_nn(k_ref[block * rows : (block + 1) * rows, :] * mask_low, a_low)
            sig = jax.nn.sigmoid(hid)
            act = (hid * sig).astype(BF16)
            z_ref[head] = act
            target = v_ref[block * rows : (block + 1) * rows, :].astype(F32)
            resid = (dot_nt(act, bt_low) - target) * mask * weight
            r_ref[...] = r_ref[...] + resid
            d_hid = dot_nn(resid.astype(BF16), bt_low) * (sig * (1.0 + hid * (1.0 - sig)))
            at = pl.ds(pl.multiple_of(head * head_size, head_size), head_size)
            ga_ref[at, :] = dot_nn(kt_ref[at, :], d_hid.astype(BF16))
        return carry

    lax.fori_loop(0, heads, one_head, 0)
    gate = jax.nn.sigmoid(gp_ref[...].astype(F32))
    mixed_ref[...] = (tot_ref[...] * gate).astype(BF16)
    tot_out_ref[...] = tot_ref[...].astype(BF16)
    att_out_ref[...] = att_ref[...].astype(BF16)
    start = iota((8, cols), 1) == (iota((8, cols), 0) << shift)
    lt_ref[...] = dot_nt(jnp.where(start, 1.0, 0.0), linv_ref[...], HIGH)
    if not last:
        resid_t = jnp.transpose(r_ref[...]).astype(BF16)
        for head in range(heads):
            at = slice(head * head_size, (head + 1) * head_size)
            gbt_ref[at, :] = dot_nn(resid_t[at, :], z_ref[head])
        width = a_ref.shape[1]
        logits = lg_ref[...]
        step = 0.2 * jax.nn.sigmoid(gate_rows(logits, 0, heads, head_size, width))
        keep = jax.nn.sigmoid(gate_rows(logits, 1, heads, head_size, width))
        stay = 1.0 - 0.5 * jax.nn.sigmoid(gate_rows(logits, 2, heads, head_size, width))
        moment_a = -step * ga_ref[...]
        moment_b = -step * gbt_ref[...]
        if not first:
            moment_a = moment_a + keep * sa_ref[...]
            moment_b = moment_b + keep * sbt_ref[...]
        sa2_ref[...] = moment_a
        sbt2_ref[...] = moment_b
        a2_ref[...] = stay * a_ref[...] + moment_a
        bt2_ref[...] = stay * bt_ref[...] + moment_b


def lead_kernel(low, count, nb, shift, *refs):
    it = iter(refs)
    take = lambda n: [next(it) for _ in range(n)]
    final = low + count == nb
    prep_in = take(7)
    k_in_ref, v_in_ref, edge_in_ref = take(3) if low else [None] * 3
    state = take(4 if 0 < low < nb - 1 else 2)
    if low:
        take(12)
    prep_out, kept, (mixed_ref, pers_ref, flat_ref, pers_flat_ref) = take(9), take(3), take(4)
    blocks = range(low, low + count)
    squares = [take(6) if block < nb - 1 else [] for block in blocks]
    k_out_ref, v_out_ref, edge_out_ref = [None] * 3 if final else take(3)
    ext_ref, k_all_ref, v_all_ref = take(3)
    room, more = take(3), take(0 if low == nb - 1 else 2)
    step = pl.program_id(0)
    q_ref, k_ref, v_ref, kt_ref, _, gp_ref, _, _, lg_ref = prep_out
    rows = q_ref.shape[0]
    prep_kernel(
        shift, low, *prep_in, edge_in_ref, *prep_out, pers_ref, flat_ref, pers_flat_ref, ext_ref
    )
    for i, block in enumerate(blocks):

        @pl.when(step == i)
        def _(i=i, block=block):
            if low and i == 0:
                k_all_ref[0 : low * rows, :] = k_in_ref[...]
                v_all_ref[0 : low * rows, :] = v_in_ref[...]
            own = slice(block * rows, (block + 1) * rows)
            k_all_ref[own, :] = k_ref[...]
            v_all_ref[own, :] = v_ref[...]
            first, last = block == 0, block == nb - 1
            now = squares[i - 1][:4] if i else state
            now = now[:2] if first or last else now
            mix_kernel(
                block, nb, shift, first, last, prep_in[0], lg_ref, q_ref, k_all_ref, v_all_ref,
                kt_ref, pers_ref, gp_ref, *now, mixed_ref, *kept, *squares[i], *room,
                *([] if last else more),
            )
            if i == count - 1 and not final:
                done = (low + count) * rows
                k_out_ref[...] = k_all_ref[0:done, :]
                v_out_ref[...] = v_all_ref[0:done, :]
                edge_out_ref[...] = ext_ref[:, 0:HALO, :]


def lead_call(blocks, nb, shift, seq, x, w, conv, gains, gate, pers, state, carried, shared):
    rows, width = x.shape
    cols = w.shape[2]
    low, count = blocks[0], len(blocks)
    final = low + count == nb
    gates = 3 * gate.shape[1]
    mem_hid = state[0].shape[1]
    square = (cols, mem_hid)
    once = pl.Buffered(1)
    fixed = lambda a: pl.BlockSpec(a.shape, lambda c, n=len(a.shape): (0,) * n, pipeline_mode=once)
    whole = lambda a: pl.BlockSpec(a.shape, lambda c, n=len(a.shape): (0,) * n)
    at_rows = lambda n: pl.BlockSpec((SPAN, n), lambda c: (low + c, 0))
    eight = lambda n: pl.BlockSpec((8, n), lambda c: (low + c, 0))
    struct = jax.ShapeDtypeStruct
    ins = [seq, x, w, conv, gains, gate, pers, *carried, *state]
    in_specs = [pl.BlockSpec(memory_space=pltpu.SMEM), at_rows(width)]
    in_specs += [fixed(a) for a in ins[2:]]
    aliases = {}
    if shared:
        aliases = {len(ins) + n: n for n in range(len(shared))}
        ins += shared
        in_specs += [pl.BlockSpec(memory_space=pl.ANY)] * len(shared)
    outs = [struct((rows, cols), BF16)] * 3 + [
        struct((cols, rows), BF16),
        struct((3, rows, cols), BF16),
        struct((rows, cols), BF16),
        struct((rows, width), BF16),
        struct((nb * 8, width), F32),
        struct((nb * 8, gates), F32),
        struct((rows, cols), BF16),
        struct((rows, cols), BF16),
        struct((8, rows), F32),
        struct((count * SPAN, cols), BF16),
        struct((2, pers.shape[2], cols), BF16),
        struct((gates, width), F32),
        struct((2, pers.shape[2], cols), F32),
    ]
    out_specs = [at_rows(cols)] * 3 + [
        pl.BlockSpec((cols, SPAN), lambda c: (0, low + c)),
        pl.BlockSpec((3, SPAN, cols), lambda c: (0, low + c, 0)),
        at_rows(cols),
        at_rows(width),
        eight(width),
        eight(gates),
        at_rows(cols),
        at_rows(cols),
        pl.BlockSpec((8, SPAN), lambda c: (0, low + c)),
        pl.BlockSpec((SPAN, cols), lambda c: (c, 0)),
    ] + [whole(a) for a in outs[13:]]
    updates = [block for block in blocks if block < nb - 1]
    more = [struct(square, F32)] * (6 * len(updates))
    if not final:
        done = ((low + count) * SPAN, cols)
        more += [struct(done, BF16), struct(done, BF16), struct((3, HALO, cols), F32)]
    scratch = [
        pltpu.VMEM((3, HALO + SPAN, cols), F32),
        pltpu.VMEM((rows, cols), BF16),
        pltpu.VMEM((rows, cols), BF16),
    ] + [pltpu.VMEM((SPAN, cols), F32)] * 3
    if updates:
        heads = cols >> shift
        scratch += [pltpu.VMEM((heads, SPAN, mem_hid), BF16), pltpu.VMEM((SPAN, cols), F32)]
    got = pl.pallas_call(
        functools.partial(lead_kernel, low, count, nb, shift),
        grid=(count,),
        in_specs=in_specs,
        out_specs=out_specs + [whole(a) for a in more],
        out_shape=outs + more,
        input_output_aliases=aliases,
        scratch_shapes=scratch,
        cost_estimate=cost(11 * count),
        name=f"lead_{low}",
    )(*ins)
    at = 16 + 6 * len(updates)
    squares = [got[n : n + 6] for n in range(16, at, 6)]
    return got[:12], got[12:16], squares, got[at:]


def cot_kernel(peer_ref, c0_ref, c1_ref, c2_ref, c3_ref, fout_ref, full_ref, dh_ref):
    cols = c0_ref.shape[1]
    for j, piece_ref in enumerate((c0_ref, c1_ref, c2_ref, c3_ref)):
        at = pl.ds(pl.multiple_of(peer_ref[j] * cols, cols), cols)
        full_ref[:, at] = piece_ref[...]
    dh_ref[...] = dot_nt(full_ref[...], fout_ref[...]).astype(BF16)


def cot_call(peers, cot, fout):
    rows, cols = cot[0].shape
    hidden, width = fout.shape
    row = lambda n: pl.BlockSpec((SPAN, n), lambda i: (i, 0))
    return pl.pallas_call(
        cot_kernel,
        grid=(rows // SPAN,),
        in_specs=[pl.BlockSpec(memory_space=pltpu.SMEM)]
        + [row(cols)] * 4
        + [pl.BlockSpec(fout.shape, lambda i: (0, 0), pipeline_mode=pl.Buffered(1))],
        out_specs=[row(width), row(hidden)],
        out_shape=[
            jax.ShapeDtypeStruct((rows, width), BF16),
            jax.ShapeDtypeStruct((rows, hidden), BF16),
        ],
        cost_estimate=cost(6),
        name="cot",
    )(peers, *cot, fout)


def ffn_kernel(groups, *refs):
    it = iter(refs)
    take = lambda n: [next(it) for _ in range(n)]
    peer_ref, x_ref = take(2)
    piece_refs = [take(4) for _ in groups]
    gain_ref, dh_ref = take(2)
    weights = take(5)
    nt_out, hid_ref, dgu_ref, mfull_out, res_out, _ = take(6)
    held = take(5)
    nt_ref, mfull_ref, res_ref = take(3)
    weight_sems, out_sems = take(2)
    step = pl.program_id(0)
    rows, cols = piece_refs[0][0].shape
    loads = [
        pltpu.make_async_copy(source, target, weight_sems.at[n])
        for n, (source, target) in enumerate(zip(weights, held))
    ]
    fin_ref, ow_refs = held[4], held[:4]
    mine = pl.ds(pl.multiple_of(step * rows, rows), rows)
    stores = [
        pltpu.make_async_copy(source, target.at[mine, :], out_sems.at[n])
        for n, (source, target) in enumerate(
            ((mfull_ref, mfull_out), (res_ref, res_out), (nt_ref, nt_out))
        )
    ]

    @pl.when(step == 0)
    def _():
        for load in loads:
            load.start()

    def ready(some):
        @pl.when(step == 0)
        def _():
            for load in some:
                load.wait()

    @pl.when(step > 0)
    def _():
        for store in stores:
            store.wait()

    spots = [pl.ds(pl.multiple_of(peer_ref[j] * cols, cols), cols) for j in range(4)]
    for n, blocks in enumerate(groups):

        @pl.when((step >= blocks[0]) & (step <= blocks[-1]))
        def _(n=n):
            for j in range(4):
                mfull_ref[:, spots[j]] = piece_refs[n][j][...]

    stores[0].start()
    ready(loads[:4])
    mixed = mfull_ref[...]
    for j in range(4):
        branch = dot_nn(mixed, ow_refs[j][...])
        res_ref[:, spots[j]] = x_ref[:, spots[j]].astype(F32) + branch
    stores[1].start()
    residual = res_ref[...]
    scale = lax.rsqrt(jnp.mean(residual * residual, -1, keepdims=True) + NORM_EPS)
    low_rows = (residual * scale * gain_ref[1:2, :]).astype(BF16)
    nt_ref[...] = low_rows
    stores[2].start()
    ready(loads[4:])
    gate_pre = dot_nn(low_rows, fin_ref[0])
    up_pre = dot_nn(low_rows, fin_ref[1])
    sig = jax.nn.sigmoid(gate_pre)
    silu = gate_pre * sig
    hid_ref[...] = (silu * up_pre).astype(BF16)
    slope = sig * (1.0 + gate_pre * (1.0 - sig))
    d_hidden = dh_ref[...].astype(F32)
    dgu_ref[0] = (d_hidden * up_pre * slope).astype(BF16)
    dgu_ref[1] = (d_hidden * silu).astype(BF16)

    @pl.when(step == pl.num_programs(0) - 1)
    def _():
        for store in stores:
            store.wait()


def ffn_call(groups, peers, x, pieces, ow, gains, fin, dh):
    rows, width = x.shape
    cols = pieces[0][0].shape[1]
    hidden = dh.shape[1]
    at_rows = lambda n: pl.BlockSpec((SPAN, n), lambda i: (i, 0))
    anywhere = pl.BlockSpec(memory_space=pl.ANY)
    struct = jax.ShapeDtypeStruct
    ins = [peers, x, *[piece for group in pieces for piece in group], gains, dh, *ow, fin]
    in_specs = [pl.BlockSpec(memory_space=pltpu.SMEM), at_rows(width)]
    for blocks in groups:
        spot = lambda i, low=blocks[0], n=len(blocks): (jnp.clip(i - low, 0, n - 1), 0)
        in_specs += [pl.BlockSpec((SPAN, cols), spot)] * 4
    in_specs += [pl.BlockSpec(gains.shape, lambda i: (0, 0)), at_rows(hidden)] + [anywhere] * 5
    return pl.pallas_call(
        functools.partial(ffn_kernel, groups),
        grid=(rows // SPAN,),
        in_specs=in_specs,
        out_specs=[
            anywhere,
            at_rows(hidden),
            pl.BlockSpec((2, SPAN, hidden), lambda i: (0, i, 0)),
            anywhere,
            anywhere,
            anywhere,
        ],
        out_shape=[
            struct((rows, width), BF16),
            struct((rows, hidden), BF16),
            struct((2, rows, hidden), BF16),
            struct((rows, width), BF16),
            struct((rows, width), F32),
            struct((3 * width, width), BF16),
        ],
        scratch_shapes=[pltpu.VMEM(piece.shape, BF16) for piece in (*ow, fin)]
        + [pltpu.VMEM((SPAN, width), BF16)] * 2
        + [pltpu.VMEM((SPAN, width), F32)]
        + [pltpu.SemaphoreType.DMA((5,)), pltpu.SemaphoreType.DMA((3,))],
        compiler_params=pltpu.CompilerParams(vmem_limit_bytes=42 << 20),
        cost_estimate=cost(22),
        name="ffn",
    )(*ins)


def ffn_back_kernel(first_call, *refs):
    it = iter(refs)
    take = lambda n: [next(it) for _ in range(n)]
    peer_ref, dgu_ref, fin_ref, res_ref = take(4)
    gg_in_ref = None if first_call else take(1)[0]
    gg_ref, keep_ref, send_ref, part_ref = take(4)
    width = res_ref.shape[1]
    residual = res_ref[...]
    scale = lax.rsqrt(jnp.mean(residual * residual, -1, keepdims=True) + NORM_EPS)
    d_normed = dot_nt(dgu_ref[0], fin_ref[0]) + dot_nt(dgu_ref[1], fin_ref[1])
    gains = jnp.sum(d_normed * residual * scale, 0, keepdims=True)

    @pl.when(pl.program_id(0) == 0)
    def _():
        gg_ref[...] = jnp.zeros(gg_ref.shape, F32) if first_call else gg_in_ref[...]

    gg_ref[...] = gg_ref[...] + jnp.broadcast_to(gains, gg_ref.shape)
    half = width // 2
    part_ref[...] = d_normed.astype(BF16)
    core = peer_ref[0] & 1
    keep_ref[...] = part_ref[:, pl.ds(pl.multiple_of(core * half, half), half)]
    send_ref[...] = part_ref[:, pl.ds(pl.multiple_of((1 - core) * half, half), half)]


def ffn_back_call(blocks, peers, dgu, fin, res, gains):
    width = res.shape[1]
    tile = SPAN // 2
    steps = SPAN // tile
    low = blocks[0] * steps
    lines = len(blocks) * SPAN
    gain_spec = pl.BlockSpec((8, width), lambda i: (0, 0))
    row = pl.BlockSpec((tile, width // 2), lambda i: (i, 0))
    struct = jax.ShapeDtypeStruct
    return pl.pallas_call(
        functools.partial(ffn_back_kernel, gains is None),
        grid=(len(blocks) * steps,),
        in_specs=[
            pl.BlockSpec(memory_space=pltpu.SMEM),
            pl.BlockSpec((2, tile, dgu.shape[2]), lambda i: (0, low + i, 0)),
            pl.BlockSpec(fin.shape, lambda i: (0, 0, 0), pipeline_mode=pl.Buffered(1)),
            pl.BlockSpec((tile, width), lambda i: (low + i, 0)),
        ]
        + ([] if gains is None else [gain_spec]),
        out_specs=[gain_spec, row, row],
        out_shape=[
            struct((8, width), F32),
            struct((lines, width // 2), BF16),
            struct((lines, width // 2), BF16),
        ],
        scratch_shapes=[pltpu.VMEM((tile, width), BF16)],
        cost_estimate=cost(4 * len(blocks)),
        name=f"ffn_back_{blocks[0]}",
    )(peers, dgu, fin, res, *([] if gains is None else [gains]))


def down_kernel(peer_ref, hid_ref, fout_ref, keep_ref, send_ref, part_ref):
    cols = keep_ref.shape[2]
    part_ref[...] = dot_nn(hid_ref[...], fout_ref[...]).astype(BF16)
    for slot, out_ref in ((0, keep_ref), (1, send_ref)):
        for n in range(2):
            start = pl.multiple_of(peer_ref[slot + 2 * n] * cols, cols)
            out_ref[n] = part_ref[:, pl.ds(start, cols)]


def down_call(peers, hid, fout, cols):
    rows, hidden = hid.shape
    width = fout.shape[1]
    stacked = pl.BlockSpec((2, SPAN, cols), lambda i: (0, i, 0))
    return pl.pallas_call(
        down_kernel,
        grid=(rows // SPAN,),
        in_specs=[
            pl.BlockSpec(memory_space=pltpu.SMEM),
            pl.BlockSpec((SPAN, hidden), lambda i: (i, 0)),
            pl.BlockSpec(fout.shape, lambda i: (0, 0), pipeline_mode=pl.Buffered(1)),
        ],
        out_specs=[stacked, stacked],
        out_shape=[jax.ShapeDtypeStruct((2, rows, cols), BF16)] * 2,
        scratch_shapes=[pltpu.VMEM((SPAN, width), BF16)],
        cost_estimate=cost(6),
        name="down",
    )(peers, hid, fout)


def turn_kernel(first_call, *refs):
    it = iter(refs)
    take = lambda n: [next(it) for _ in range(n)]
    peer_ref, s1_ref, r2_ref, ps1_ref, pr2_ref, res_ref, cot_ref = take(7)
    gain_ref, gp_ref = take(2)
    ow_refs = take(4)
    (tot_ref,) = take(1)
    if not first_call:
        take(4)
    dres_ref, rescol_ref, dbr_ref, dgall_ref, dga_ref, dgp_ref, full_ref = take(7)
    rows, width = res_ref.shape
    cols = gp_ref.shape[1]
    half = width // 2
    core = peer_ref[0] & 1
    at_own = pl.ds(pl.multiple_of(core * half, half), half)
    at_other = pl.ds(pl.multiple_of((1 - core) * half, half), half)
    full_ref[:, at_own] = s1_ref[...].astype(F32) + r2_ref[...].astype(F32)
    full_ref[:, at_other] = ps1_ref[...].astype(F32) + pr2_ref[...].astype(F32)
    residual = res_ref[...]
    scale = lax.rsqrt(jnp.mean(residual * residual, -1, keepdims=True) + NORM_EPS)
    gained = full_ref[...] * gain_ref[1:2, :]
    inner = jnp.sum(gained * residual, -1, keepdims=True) / width
    d_residual = cot_ref[...].astype(F32) + scale * gained - residual * (scale * scale * scale * inner)
    own = pl.ds(pl.multiple_of(peer_ref[0] * cols, cols), cols)
    full_ref[...] = d_residual
    d_mixed = None
    for j in range(4):
        at = pl.ds(pl.multiple_of(peer_ref[j] * cols, cols), cols)
        term = dot_nt(full_ref[:, at].astype(BF16), ow_refs[j][own, :])
        d_mixed = term if d_mixed is None else d_mixed + term
    mine = full_ref[:, own]
    dres_ref[...] = mine
    dbr_ref[...] = mine.astype(BF16)
    rescol_ref[...] = res_ref[:, own]
    gate = jax.nn.sigmoid(gp_ref[...].astype(F32))
    d_gated = d_mixed * gate
    dga_ref[...] = d_gated.astype(BF16)
    d_gate = (d_gated * tot_ref[...].astype(F32) * (1.0 - gate)).astype(BF16)
    dgp_ref[...] = d_gate
    dgall_ref[...] = d_gate


def turn_call(block, spot, peers, pieces, res, cot, ow, gains, gp, tot, shared):
    rows, cols = gp.shape
    width = res.shape[1]
    tile = SPAN // 2
    steps = SPAN // tile
    low = block * steps
    whole = lambda a: pl.BlockSpec(a.shape, lambda i, n=a.ndim: (0,) * n)
    row = lambda n: pl.BlockSpec((tile, n), lambda i: (i, 0))
    piece = pl.BlockSpec((tile, width // 2), lambda i: (spot * steps + i, 0))
    at_rows = lambda n: pl.BlockSpec((tile, n), lambda i: (low + i, 0))
    struct = jax.ShapeDtypeStruct
    ins = [peers, *pieces, res, cot, gains, gp, *ow, tot]
    in_specs = [
        pl.BlockSpec(memory_space=pltpu.SMEM),
        piece,
        piece,
        piece,
        piece,
        at_rows(width),
        at_rows(width),
        whole(gains),
        at_rows(cols),
    ] + [whole(weight) for weight in ow]
    in_specs.append(at_rows(cols))
    aliases = {}
    if shared is not None:
        aliases = {len(ins) + n: n for n in range(len(shared))}
        ins += shared
        in_specs += [pl.BlockSpec(memory_space=pl.ANY)] * len(shared)
    got = pl.pallas_call(
        functools.partial(turn_kernel, shared is None),
        grid=(steps,),
        in_specs=in_specs,
        out_specs=[at_rows(cols)] * 4 + [row(cols)] * 2,
        out_shape=[
            struct((rows, cols), F32),
            struct((rows, cols), F32),
            struct((rows, cols), BF16),
            struct((rows, cols), BF16),
            struct((SPAN, cols), BF16),
            struct((SPAN, cols), BF16),
        ],
        input_output_aliases=aliases,
        scratch_shapes=[pltpu.VMEM((tile, width), F32)],
        cost_estimate=cost(5),
        name=f"turn_{block}",
    )(*ins)
    return list(got[:4]), got[4:]


def back_kernel(block, nb, shift, *refs):
    it = iter(refs)
    take = lambda n: [next(it) for _ in range(n)]
    first, last = block == 0, block == nb - 1
    seq_ref, q_ref, k_ref, v_ref, kt_ref, pers_ref, dga_ref, att_ref, lt_ref = take(9)
    a_ref, bt_ref = take(2)
    if not last:
        dk_in_ref, dv_in_ref, dp_in_ref, lg_ref, ga_ref, gbt_ref, ab_in_ref, btb_in_ref = take(8)
        sab_in_ref, sbtb_in_ref = take(2) if block < nb - 2 else (None, None)
        sa_ref, sbt_ref = (None, None) if first else take(2)
    dq_ref, dk_ref, dv_ref, dp_ref, ab_ref, btb_ref = take(6)
    if not last:
        (dlg_ref,) = take(1)
        sab_ref, sbtb_ref = (None, None) if first else take(2)
    dt_ref, dqt_ref, qt_ref, dot_ref = take(4)
    if not last:
        z_ref, zd_ref, r_ref, y_ref, h_ref = take(5)
    rows, cols = q_ref.shape
    head_size = 1 << shift
    heads = cols // head_size
    own = slice(block * rows, (block + 1) * rows)
    a_low = a_ref[...].astype(BF16)
    bt_low = bt_ref[...].astype(BF16)
    if last:
        dk_ref[...] = jnp.zeros(dk_ref.shape, F32)
        dv_ref[...] = jnp.zeros(dv_ref.shape, F32)
        dp_ref[...] = jnp.zeros(dp_ref.shape, F32)
        ab_ref[...] = jnp.zeros(ab_ref.shape, F32)
        btb_ref[...] = jnp.zeros(btb_ref.shape, F32)
    else:
        dk_ref[...] = dk_in_ref[...]
        dv_ref[...] = dv_in_ref[...]
        dp_ref[...] = dp_in_ref[...]
    pick = (iota((8, cols), 1) >> shift) == iota((8, cols), 0)
    d_gated = dga_ref[...].astype(F32)
    dt_ref[...] = dot_nt(jnp.where(pick, 1.0, 0.0), d_gated * att_ref[...].astype(F32), HIGH)
    dq_ref[...] = jnp.zeros((rows, cols), F32)
    qt_ref[...] = jnp.transpose(q_ref[...].astype(F32)).astype(BF16)
    dot_ref[...] = jnp.transpose(d_gated).astype(BF16)
    if not last:
        valid, count = valid_column(seq_ref, block * rows, rows)
        weight = valid / count
        width = a_ref.shape[1]
        logits = lg_ref[...]
        sig_step = jax.nn.sigmoid(gate_rows(logits, 0, heads, head_size, width))
        keep = jax.nn.sigmoid(gate_rows(logits, 1, heads, head_size, width))
        sig_forget = jax.nn.sigmoid(gate_rows(logits, 2, heads, head_size, width))
        tot_a, tot_b = ab_in_ref[...], btb_in_ref[...]
        if sab_in_ref is not None:
            tot_a, tot_b = tot_a + sab_in_ref[...], tot_b + sbtb_in_ref[...]
        h_ref[0] = (-0.2 * sig_step * tot_a).astype(BF16)
        h_ref[1] = (-0.2 * sig_step * tot_b).astype(BF16)
        d_step = -(ga_ref[...] * tot_a + gbt_ref[...] * tot_b)
        groups = [d_step * (0.2 * sig_step * (1.0 - sig_step)), None, None]
        if not first:
            groups[1] = (sa_ref[...] * tot_a + sbt_ref[...] * tot_b) * (keep * (1.0 - keep))
        d_forget = -(a_ref[...] * ab_in_ref[...] + bt_ref[...] * btb_in_ref[...])
        groups[2] = d_forget * (0.5 * sig_forget * (1.0 - sig_forget))
        d_logits = jnp.zeros(dlg_ref.shape, F32)
        for g, value in enumerate(groups):
            if value is None:
                continue
            for head in range(heads):
                part = value[head * head_size : (head + 1) * head_size, :]
                figure = jnp.sum(jnp.sum(part, 1, keepdims=True), 0, keepdims=True)
                here = iota(dlg_ref.shape, 1) == g * heads + head
                d_logits = d_logits + jnp.where(here, 1.0, 0.0) * figure
        dlg_ref[...] = d_logits
        stay = 1.0 - 0.5 * sig_forget
        ab_ref[...] = stay * ab_in_ref[...]
        btb_ref[...] = stay * btb_in_ref[...]
        if not first:
            sab_ref[...] = keep * tot_a
            sbtb_ref[...] = keep * tot_b
        r_ref[...] = jnp.zeros((rows, cols), F32)
        y_ref[...] = jnp.zeros((rows, cols), F32)

    def one_head(head, carry):
        mask = head_mask(cols, shift, head)
        mask_low = mask.astype(BF16)
        query = q_ref[...] * mask_low
        scaled = query * SCORE_SCALE
        d_out = dga_ref[...] * mask_low
        at = pl.ds(pl.multiple_of(head * head_size, head_size), head_size)
        inverse = lt_ref[pl.ds(head, 1), :]
        delta = dt_ref[pl.ds(head, 1), :]
        probs = jnp.exp(dot_nt(pers_ref[0], scaled)) * inverse
        d_scores = (probs * (dot_nt(pers_ref[1], d_out) - delta)).astype(BF16)
        dp_ref[0] = dp_ref[0] + dot_nn(d_scores, scaled)
        dp_ref[1] = dp_ref[1] + dot_nn(probs.astype(BF16), d_out)
        d_query = lax.dot_general(
            d_scores, pers_ref[0], (((0,), (0,)), ((), ())), preferred_element_type=F32
        )
        d_query = d_query * SCORE_SCALE
        d_query_t = jnp.zeros((head_size, rows), F32)
        for j in range(block + 1):
            span = slice(j * rows, (j + 1) * rows)
            probs = jnp.exp(dot_nt(k_ref[span, :], scaled)) * inverse
            if j == block:
                probs = jnp.where(iota((rows, rows), 0) <= iota((rows, rows), 1), probs, 0.0)
            d_scores = (probs * (dot_nt(v_ref[span, :], d_out) - delta)).astype(BF16)
            dv_ref[span, :] = dv_ref[span, :] + dot_nn(probs.astype(BF16), d_out)
            dk_ref[span, :] = dk_ref[span, :] + dot_nn(d_scores, scaled)
            d_query_t = d_query_t + dot_nn(kt_ref[at, span], d_scores)
        dqt_ref[at, :] = d_query_t * SCORE_SCALE
        hid = dot_nn(query, a_low)
        sig = jax.nn.sigmoid(hid)
        d_hid = dot_nn(d_out, bt_low) * (sig * (1.0 + hid * (1.0 - sig)))
        d_hid = d_hid.astype(BF16)
        dq_ref[...] = dq_ref[...] + (d_query + dot_nt(d_hid, a_low)) * mask
        grad_a = dot_nn(qt_ref[at, :], d_hid)
        grad_b = dot_nn(dot_ref[at, :], (hid * sig).astype(BF16))
        if not last:
            key = k_ref[own, :] * mask_low
            hid = dot_nn(key, a_low)
            probe = dot_nn(key, h_ref[0])
            sig = jax.nn.sigmoid(hid)
            act = (hid * sig).astype(BF16)
            z_ref[head] = act
            slope = sig * (1.0 + hid * (1.0 - sig))
            curve = sig * (1.0 - sig) * (2.0 + hid * (1.0 - 2.0 * sig))
            target = v_ref[own, :].astype(F32)
            resid = (dot_nt(act, bt_low) - target) * mask * weight
            r_ref[...] = r_ref[...] + resid
            resid = resid.astype(BF16)
            d_act = dot_nn(resid, bt_low)
            d_slope = (probe * slope).astype(BF16)
            zd_ref[head] = d_slope
            d_net = (dot_nt(act, h_ref[1]) + dot_nt(d_slope, bt_low)) * mask * weight
            y_ref[...] = y_ref[...] + d_net
            back = dot_nn(resid, h_ref[1]) + dot_nn(d_net.astype(BF16), bt_low)
            d_hid = (probe * d_act * curve + back * slope).astype(BF16)
            direct = (d_act * slope).astype(BF16)
            d_key = (dot_nt(direct, h_ref[0]) + dot_nt(d_hid, a_low)) * mask
            dk_ref[own, :] = dk_ref[own, :] + d_key
            grad_a = grad_a + dot_nn(kt_ref[at, own], d_hid)
        ab_ref[at, :] = ab_ref[at, :] + grad_a
        btb_ref[at, :] = btb_ref[at, :] + grad_b
        return carry

    lax.fori_loop(0, heads, one_head, 0)
    dq_ref[...] = dq_ref[...] + jnp.transpose(dqt_ref[...])
    if not last:
        dv_ref[own, :] = dv_ref[own, :] - y_ref[...]
        resid_t = jnp.transpose(r_ref[...]).astype(BF16)
        net_t = jnp.transpose(y_ref[...]).astype(BF16)
        for head in range(heads):
            at = slice(head * head_size, (head + 1) * head_size)
            grad_b = dot_nn(resid_t[at, :], zd_ref[head]) + dot_nn(net_t[at, :], z_ref[head])
            btb_ref[at, :] = btb_ref[at, :] + grad_b


def back_parts(block, nb, shift, seq, q, k, v, kt, pers, dga, att, linv, state, grads, adjoint):
    cols = q.shape[1]
    heads = cols >> shift
    first, last = block == 0, block == nb - 1
    done = (block + 1) * SPAN
    whole = lambda s: pl.BlockSpec(s, lambda i, n=len(s): (0,) * n)
    at_block = pl.BlockSpec((SPAN, cols), lambda i: (block, 0))
    upto = pl.BlockSpec((done, cols), lambda i: (0, 0))
    square = state["a"].shape
    ins = [seq, q, k, v, kt, pers, dga, att, linv, state["a"], state["bt"]]
    in_specs = [
        pl.BlockSpec(memory_space=pltpu.SMEM),
        at_block,
        upto,
        upto,
        pl.BlockSpec((cols, done), lambda i: (0, 0)),
        whole(pers.shape),
        pl.BlockSpec((SPAN, cols), lambda i: (0, 0)),
        at_block,
        pl.BlockSpec((8, SPAN), lambda i: (0, block)),
        whole(square),
        whole(square),
    ]
    if not last:
        ins += [grads["dk"], grads["dv"], grads["dp"], state["lg"], state["ga"], state["gbt"]]
        ins += [adjoint["ab"], adjoint["btb"]]
        in_specs += [upto, upto, whole(pers.shape)]
        in_specs += [pl.BlockSpec((8, state["lg"].shape[1]), lambda i: (block, 0))]
        in_specs += [whole(square)] * 4
        if block < nb - 2:
            ins += [adjoint["sab"], adjoint["sbtb"]]
            in_specs += [whole(square)] * 2
        if not first:
            ins += [state["sa"], state["sbt"]]
            in_specs += [whole(square)] * 2
    names = ["dq", "dk", "dv", "dp", "ab", "btb"]
    shapes = [(SPAN, cols), (done, cols), (done, cols), pers.shape, square, square]
    if not last:
        names.append("dlg")
        shapes.append((8, state["lg"].shape[1]))
        if not first:
            names += ["sab", "sbtb"]
            shapes += [square, square]
    scratch = [
        pltpu.VMEM((8, SPAN), F32),
        pltpu.VMEM((cols, SPAN), F32),
        pltpu.VMEM((cols, SPAN), BF16),
        pltpu.VMEM((cols, SPAN), BF16),
    ]
    if not last:
        scratch += [
            pltpu.VMEM((heads, SPAN, square[1]), BF16),
            pltpu.VMEM((heads, SPAN, square[1]), BF16),
            pltpu.VMEM((SPAN, cols), F32),
            pltpu.VMEM((SPAN, cols), F32),
            pltpu.VMEM((2,) + square, BF16),
        ]
    return ins, in_specs, names, shapes, scratch


def back_call(block, nb, shift, *args):
    ins, in_specs, names, shapes, scratch = back_parts(block, nb, shift, *args)
    outs = pl.pallas_call(
        functools.partial(back_kernel, block, nb, shift),
        grid=(1,),
        in_specs=in_specs,
        out_specs=[pl.BlockSpec(s, lambda i, n=len(s): (0,) * n) for s in shapes],
        out_shape=[jax.ShapeDtypeStruct(s, F32) for s in shapes],
        scratch_shapes=scratch,
        cost_estimate=cost(17),
        name=f"back_{block}",
    )(*ins)
    return dict(zip(names, outs))


def unprep_kernel(block, nb, shift, *refs):
    it = iter(refs)
    take = lambda n: [next(it) for _ in range(n)]
    first, last = block == 0, block == nb - 1
    seq_ref, peer_ref, dq_ref, dk_ref, dv_ref, dgp_ref, pre_ref, w_ref, conv_ref = take(9)
    x_ref, gain_ref = take(2)
    halo_ref = None if first else take(1)[0]
    dp_ref, pers_ref, ab_ref, btb_ref, gain_two_ref = take(5) if first else [None] * 5
    if not last:
        edge_in_ref, dlg_ref, gate_ref, mean_ref = take(4)
        cg_in_ref, gg_in_ref, gate_in_ref = take(7)[:3]
    cg_ref, gg_ref, gate_out_ref = take(3)
    dproj_ref, keep_ref, send_ref, inner_ref, edge_ref = take(5)
    small_ref, gains_ref = take(2) if first else (None, None)
    ext_ref, dext_ref, low_ref = take(3)
    rows, cols = dq_ref.shape
    width = x_ref.shape[1]
    blocks = head_blocks(cols, shift)
    taps = conv_ref.shape[1]
    d_normed = dot_nt(dgp_ref[...], w_ref[3])
    dproj_ref[3] = dgp_ref[...]
    if last:
        cg_ref[...] = jnp.zeros(cg_ref.shape, F32)
        gg_ref[...] = jnp.zeros(gg_ref.shape, F32)
        gate_out_ref[...] = jnp.zeros(gate_out_ref.shape, F32)
    else:
        cg_ref[...] = cg_in_ref[...]
        gg_ref[...] = gg_in_ref[...]
    for i in range(3):
        pre = pre_ref[i].astype(F32)
        ext_ref[0:HALO, :] = jnp.zeros((HALO, cols), F32) if first else halo_ref[i, HALO:, :].astype(F32)
        ext_ref[HALO : HALO + rows, :] = pre
        shifted = [pre] + [ext_ref[HALO - j : HALO - j + rows, :] for j in range(1, taps)]
        conv = conv_ref[i, 0:1, :] * pre
        for j in range(1, taps):
            conv = conv + conv_ref[i, j : j + 1, :] * shifted[j]
        sig = jax.nn.sigmoid(conv)
        d_act = (dq_ref, dk_ref, dv_ref)[i][...]
        if i < 2:
            act = conv * sig
            scale = lax.rsqrt(head_sum(act * act, blocks) + UNIT_EPS)
            d_act = scale * (d_act - act * (scale * scale * head_sum(d_act * act, blocks)))
        d_conv = d_act * (sig * (1.0 + conv * (1.0 - sig)))
        edge_ref[i] = d_conv[0:HALO, :]
        dext_ref[0:rows, :] = d_conv
        dext_ref[rows : rows + HALO, :] = (
            jnp.zeros((HALO, cols), F32) if last else edge_in_ref[i]
        )
        d_pre = conv_ref[i, 0:1, :] * d_conv
        for j in range(taps):
            if j:
                d_pre = d_pre + conv_ref[i, j : j + 1, :] * dext_ref[j : j + rows, :]
            at = slice(i * taps + j, i * taps + j + 1)
            cg_ref[at, :] = cg_ref[at, :] + jnp.sum(d_conv * shifted[j], 0, keepdims=True)
        d_low = d_pre.astype(BF16)
        dproj_ref[i] = d_low
        d_normed = d_normed + dot_nt(d_low, w_ref[i])
    if not last:
        valid, count = valid_column(seq_ref, block * rows, rows)
        d_mean = jnp.dot(
            dlg_ref[...], gate_ref[...], preferred_element_type=F32, precision=HIGH
        )
        d_normed = d_normed + (valid / count) * d_mean[0:1, :]
        outer = lax.dot_general(
            dlg_ref[...] * 0.125,
            mean_ref[...],
            (((0,), (0,)), ((), ())),
            preferred_element_type=F32,
            precision=HIGH,
        )
        gate_out_ref[...] = gate_in_ref[...]
        at = slice(0, outer.shape[0])
        gate_out_ref[at, :] = gate_in_ref[at, :] + outer
    x = x_ref[...].astype(F32)
    scale = lax.rsqrt(jnp.mean(x * x, -1, keepdims=True) + NORM_EPS)
    weighted = d_normed * x
    gains = jnp.sum(weighted * scale, 0, keepdims=True)
    gg_ref[...] = gg_ref[...] + jnp.broadcast_to(gains, gg_ref.shape)
    gained = jnp.broadcast_to(gain_ref[0:1, :], (8, width))
    inner_ref[...] = dot_nt(gained.astype(BF16), weighted.astype(BF16))
    low_ref[...] = d_normed.astype(BF16)
    for slot, out_ref in ((0, keep_ref), (1, send_ref)):
        for n in range(2):
            start = pl.multiple_of(peer_ref[slot + 2 * n] * cols, cols)
            out_ref[n] = low_ref[:, pl.ds(start, cols)]
    if first:
        keys = pers_ref[0]
        d_keys = dp_ref[0]
        scale = lax.rsqrt(head_sum(keys * keys, blocks) + UNIT_EPS)
        along = head_sum(d_keys * keys, blocks)
        d_keys = scale * (d_keys - keys * (scale * scale * along))
        across = lambda a: [a[:, n : n + cols] for n in range(0, width, cols)]
        parts = [ab_ref[...], btb_ref[...], *across(gate_out_ref[...]), cg_ref[...]]
        parts += [d_keys, dp_ref[1]]
        at = 0
        for part in parts:
            small_ref[at : at + part.shape[0], :] = part.astype(BF16)
            at += part.shape[0]
        gains_ref[0:1, :] = gg_ref[0:1, :]
        gains_ref[1:2, :] = gain_two_ref[0:1, :]
        small_ref[at:, :] = jnp.zeros((small_ref.shape[0] - at, cols), BF16)


def unprep_call(
    block, nb, shift, seq, peers, back, dgp, pre, w, conv, x, gains, gate, mean, pers, gain_two,
    shared,
):
    rows, width = x.shape
    cols = dgp.shape[1]
    first, last = block == 0, block == nb - 1
    whole = lambda a: pl.BlockSpec(a.shape, lambda i, n=len(a.shape): (0,) * n)
    smem = pl.BlockSpec(memory_space=pltpu.SMEM)
    at_block = pl.BlockSpec((SPAN, cols), lambda i: (block, 0))
    stacked = lambda n: pl.BlockSpec((n, SPAN, cols), lambda i: (0, block, 0))
    struct = jax.ShapeDtypeStruct
    gate_rows_out = 16
    names = ["cg", "gg", "gate", "dproj", "keep", "send", "inner", "edge"]
    outs = [
        struct((16, cols), F32),
        struct((8, width), F32),
        struct((gate_rows_out, width), F32),
        struct((4, rows, cols), BF16),
        struct((2, rows, cols), BF16),
        struct((2, rows, cols), BF16),
        struct((8, rows), F32),
        struct((3, HALO, cols), F32),
    ]
    out_specs = [whole(a) for a in outs[:3]]
    out_specs += [
        stacked(4),
        stacked(2),
        stacked(2),
        pl.BlockSpec((8, SPAN), lambda i: (0, block)),
        whole(outs[7]),
    ]
    ins = [seq, peers, back["dq"], back["dk"], back["dv"], dgp, pre, w, conv, x, gains]
    in_specs = [
        smem,
        smem,
        whole(back["dq"]),
        at_block,
        at_block,
        pl.BlockSpec((SPAN, cols), lambda i: (0, 0)),
        stacked(3),
        whole(w),
        whole(conv),
        pl.BlockSpec((SPAN, width), lambda i: (block, 0)),
        whole(gains),
    ]
    aliases = {}
    if not first:
        ins.append(pre)
        in_specs.append(
            pl.BlockSpec((3, 2 * HALO, cols), lambda i: (0, block * (SPAN // HALO // 2) - 1, 0))
        )
    else:
        others = [back["dp"], pers, back["ab"], back["btb"], gain_two]
        ins += others
        in_specs += [whole(a) for a in others]
        names += ["small", "gains"]
        ahead = 5 * width // SMALL_ROWS
        outs.append(struct(((ahead + 1) * SMALL_ROWS, cols), BF16))
        out_specs.append(pl.BlockSpec((SMALL_ROWS, cols), lambda i: (ahead, 0)))
        outs.append(struct((2, width), F32))
        out_specs.append(whole(outs[-1]))
    if not last:
        ins += [shared["edge"], back["dlg"], gate, mean]
        in_specs += [whole(shared["edge"]), whole(back["dlg"]), whole(gate)]
        in_specs.append(pl.BlockSpec((8, width), lambda i: (block, 0)))
        aliases = {len(ins) + n: n for n in range(7)}
        ins += [shared[name] for name in names[:7]]
        in_specs += [whole(a) for a in outs[:3]] + [pl.BlockSpec(memory_space=pl.ANY)] * 4
    got = pl.pallas_call(
        functools.partial(unprep_kernel, block, nb, shift),
        grid=(1,),
        in_specs=in_specs,
        out_specs=out_specs,
        out_shape=outs,
        input_output_aliases=aliases,
        scratch_shapes=[
            pltpu.VMEM((HALO + SPAN, cols), F32),
            pltpu.VMEM((SPAN + HALO, cols), F32),
            pltpu.VMEM((SPAN, width), BF16),
        ],
        cost_estimate=cost(10),
        name=f"unprep_{block}",
    )(*ins)
    return dict(zip(names, got))


def rear_kernel(block, nb, shift, counts, *refs):
    it = iter(refs)
    take = lambda n: [next(it) for _ in range(n)]
    first = block == 0
    back_in = take(counts[0])
    peer_ref, dgp_ref, pre_any, w_any, conv_ref, x_any, gain_ref = take(7)
    halo = take(0 if first else 1)
    pers_ref, gain_two_ref = take(2) if first else (None, None)
    edge_in_ref, gate_ref, mean_ref = take(3)
    before = take(7)
    dk_out_ref, dv_out_ref = (None, None) if first else take(2)
    sums = [] if first else take(5)
    results = take(10 if first else 8)
    dq_ref, dk_ref, dv_ref, dlg_ref = take(4)
    if first:
        sums = take(3)
    back_room, unprep_room = take(counts[1]), take(3)
    pre_ref, w_ref, x_ref, sems = take(4)
    rows = dq_ref.shape[0]
    own = pl.ds(block * rows, rows)
    loads = [
        pltpu.make_async_copy(source, target, sems.at[n])
        for n, (source, target) in enumerate(
            ((pre_any.at[:, own, :], pre_ref), (w_any, w_ref), (x_any.at[own, :], x_ref))
        )
    ]
    for load in loads:
        load.start()
    dp_ref, ab_ref, btb_ref = sums[:3]
    back_kernel(
        block, nb, shift, *back_in, dq_ref, dk_ref, dv_ref, dp_ref, ab_ref, btb_ref, dlg_ref,
        *sums[3:], *back_room,
    )
    for load in loads:
        load.wait()
    unprep_kernel(
        block, nb, shift, back_in[0], peer_ref, dq_ref, dk_ref.at[own, :], dv_ref.at[own, :],
        dgp_ref, pre_ref, w_ref, conv_ref, x_ref, gain_ref, *halo,
        *([dp_ref, pers_ref, ab_ref, btb_ref, gain_two_ref] if first else []),
        edge_in_ref, dlg_ref, gate_ref, mean_ref, *before, *results, *unprep_room,
    )
    if not first:
        dk_out_ref[...] = dk_ref[0 : block * rows, :]
        dv_out_ref[...] = dv_ref[0 : block * rows, :]


def rear_call(
    block, nb, shift, back_args, peers, dgp, pre, w, conv, x, gains, gate, mean, pers, gain_two,
    shared,
):
    rows, width = x.shape
    cols = dgp.shape[1]
    first = block == 0
    ins, in_specs, names, shapes, back_room = back_parts(block, nb, shift, *back_args)
    counts = (len(ins), len(back_room))
    shape_of = dict(zip(names, shapes))
    whole = lambda a: pl.BlockSpec(a.shape, lambda i, n=len(a.shape): (0,) * n)
    anywhere = pl.BlockSpec(memory_space=pl.ANY)
    stacked = lambda n: pl.BlockSpec((n, SPAN, cols), lambda i: (0, block, 0))
    struct = jax.ShapeDtypeStruct
    ins = ins + [peers, dgp, pre, w, conv, x, gains]
    in_specs = in_specs + [
        pl.BlockSpec(memory_space=pltpu.SMEM),
        pl.BlockSpec((SPAN, cols), lambda i: (0, 0)),
        anywhere,
        anywhere,
        whole(conv),
        anywhere,
        whole(gains),
    ]
    kept, outs = [], []
    if first:
        ins += [pers, gain_two]
        in_specs += [whole(pers), whole(gain_two)]
    else:
        ins.append(pre)
        in_specs.append(
            pl.BlockSpec((3, 2 * HALO, cols), lambda i: (0, block * (SPAN // HALO // 2) - 1, 0))
        )
        kept = ["dk", "dv", "dp", "ab", "btb", "sab", "sbtb"]
        outs = [struct((block * SPAN, cols), F32)] * 2
        outs += [struct(shape_of[name], F32) for name in kept[2:]]
    out_specs = [whole(a) for a in outs]
    fresh = ["cg", "gg", "gate", "dproj", "keep", "send", "inner", "edge"]
    ins += [shared["edge"], gate, mean]
    in_specs += [whole(shared["edge"]), whole(gate)]
    in_specs.append(pl.BlockSpec((8, width), lambda i: (block, 0)))
    aliases = {len(ins) + n: len(outs) + n for n in range(7)}
    ins += [shared[name] for name in fresh[:7]]
    in_specs += [whole(shared[name]) for name in fresh[:3]] + [anywhere] * 4
    outs += [struct(shared[name].shape, shared[name].dtype) for name in fresh]
    out_specs += [whole(shared[name]) for name in fresh[:3]]
    out_specs += [
        stacked(4),
        stacked(2),
        stacked(2),
        pl.BlockSpec((8, SPAN), lambda i: (0, block)),
        whole(shared["edge"]),
    ]
    if first:
        fresh += ["small", "gains"]
        ahead = 5 * width // SMALL_ROWS
        outs.append(struct(((ahead + 1) * SMALL_ROWS, cols), BF16))
        out_specs.append(pl.BlockSpec((SMALL_ROWS, cols), lambda i: (ahead, 0)))
        outs.append(struct((2, width), F32))
        out_specs.append(whole(outs[-1]))
    inside = ["dq", "dk", "dv", "dlg"] + (["dp", "ab", "btb"] if first else [])
    got = pl.pallas_call(
        functools.partial(rear_kernel, block, nb, shift, counts),
        grid=(1,),
        in_specs=in_specs,
        out_specs=out_specs,
        out_shape=outs,
        input_output_aliases=aliases,
        scratch_shapes=[pltpu.VMEM(shape_of[name], F32) for name in inside]
        + back_room
        + [
            pltpu.VMEM((HALO + SPAN, cols), F32),
            pltpu.VMEM((SPAN + HALO, cols), F32),
            pltpu.VMEM((SPAN, width), BF16),
            pltpu.VMEM((3, SPAN, cols), BF16),
            pltpu.VMEM(w.shape, BF16),
            pltpu.VMEM((SPAN, width), BF16),
            pltpu.SemaphoreType.DMA((3,)),
        ],
        cost_estimate=cost(25),
        name=f"rear_{block}",
    )(*ins)
    got = dict(zip(kept + fresh, got))
    return {name: got[name] for name in kept}, {name: got[name] for name in fresh}


def finish_kernel(peer_ref, x_ref, dres_ref, half_ref, far_ref, i0_ref, i1_ref, gain_ref, out_ref):
    rows, width = x_ref.shape
    cols = out_ref.shape[1]
    own = pl.ds(pl.multiple_of(peer_ref[0] * cols, cols), cols)
    x = x_ref[...].astype(F32)
    scale = lax.rsqrt(jnp.mean(x * x, -1, keepdims=True) + NORM_EPS)
    inner = jnp.transpose(i0_ref[...] + i1_ref[...])[:, 0:1] / width
    d_normed = half_ref[0].astype(F32) + far_ref[...].astype(F32)
    d_normed = d_normed * gain_ref[0:1, own]
    x_own = x_ref[:, own].astype(F32)
    out_ref[...] = dres_ref[...] + scale * d_normed - x_own * (scale * scale * scale * inner)


def finish_call(peers, x, dres, half, far, inner, inner_far, gains):
    rows, width = x.shape
    cols = dres.shape[1]
    row = lambda n: pl.BlockSpec((SPAN, n), lambda i: (i, 0))
    across = pl.BlockSpec((8, SPAN), lambda i: (0, i))
    return pl.pallas_call(
        finish_kernel,
        grid=(rows // SPAN,),
        in_specs=[
            pl.BlockSpec(memory_space=pltpu.SMEM),
            row(width),
            row(cols),
            pl.BlockSpec((1, SPAN, cols), lambda i: (0, i, 0)),
            row(cols),
            across,
            across,
            pl.BlockSpec(gains.shape, lambda i: (0, 0)),
        ],
        out_specs=row(cols),
        out_shape=jax.ShapeDtypeStruct((rows, cols), F32),
        cost_estimate=cost(4),
        name="finish",
    )(peers, x, dres, half, far, inner, inner_far, gains)


def unpack_kernel(shift, main_ref, small_ref, proj_ref, out_ref, a_ref, b_ref, gate_ref, conv_ref,
                  pers_ref, gain_ref):
    step = pl.program_id(0)
    cols = main_ref.shape[1]
    head_size = 1 << shift
    heads = cols // head_size
    last = pl.num_programs(0) - 1

    @pl.when(step < last)
    def _():
        proj_ref[0] = main_ref[...].astype(F32)

    @pl.when(step == last)
    def _():
        out_ref[...] = main_ref[...].astype(F32)

    @pl.when(step == 1)
    def _():
        small = small_ref[...].astype(F32)
        at = 2 * cols
        for h in range(heads):
            rows = slice(h * head_size, (h + 1) * head_size)
            a_ref[h] = small[rows, :]
            b_ref[h] = small[cols : 2 * cols][rows, :]
        lanes = gain_ref.shape[1] // cols
        for n in range(lanes):
            for g in range(3):
                row = at + 16 * n + g * heads
                gate_ref[g, :, n * cols : (n + 1) * cols] = small[row : row + heads, :]
        at += 16 * lanes
        taps = conv_ref.shape[1]
        for i in range(3):
            conv_ref[i] = small[at + i * taps : at + (i + 1) * taps, :]
        at += 16
        count = pers_ref.shape[2]
        for i in range(2):
            for h in range(heads):
                spot = slice(h * head_size, (h + 1) * head_size)
                pers_ref[i, h] = small[at + i * count : at + (i + 1) * count, spot]
        at += 2 * count
        for i in range(2):
            for n in range(lanes):
                row = at + i * lanes + n
                gain_ref[i : i + 1, n * cols : (n + 1) * cols] = small[row : row + 1, :]


def unpack_call(payload, shift, width, mem_hid, taps, persist_rows):
    cols = payload.shape[1]
    heads = cols >> shift
    head_size = 1 << shift
    ahead = 5 * width // SMALL_ROWS
    struct = jax.ShapeDtypeStruct
    outs = [
        struct((4, width, cols), F32),
        struct((width, cols), F32),
        struct((heads, head_size, mem_hid), F32),
        struct((heads, head_size, mem_hid), F32),
        struct((3, heads, width), F32),
        struct((3, taps, cols), F32),
        struct((2, heads, persist_rows, head_size), F32),
        struct((2, width), F32),
    ]
    whole = lambda a: pl.BlockSpec(a.shape, lambda i, n=len(a.shape): (0,) * n)
    return pl.pallas_call(
        functools.partial(unpack_kernel, shift),
        grid=(5,),
        in_specs=[
            pl.BlockSpec((width, cols), lambda i: (i, 0)),
            pl.BlockSpec((SMALL_ROWS, cols), lambda i: (ahead, 0)),
        ],
        out_specs=[pl.BlockSpec((1, width, cols), lambda i: (jnp.minimum(i, 3), 0, 0))]
        + [whole(a) for a in outs[1:]],
        out_shape=outs,
        cost_estimate=cost(4),
        name="unpack",
    )(payload, payload)


def ring_of(size):
    return [list(range(0, size, 2)) + list(range(size - 1 - size % 2, 0, -2))]


def ring_scatter(payload, axis, size):
    return lax.psum_scatter(
        payload, axis, scatter_dimension=0, axis_index_groups=ring_of(size), tiled=True
    )


def ring_gather(part, axis, size):
    return lax.all_gather(part, axis, axis=0, axis_index_groups=ring_of(size), tiled=True)


def stacked_rows(pieces, full):
    at = 0
    for piece in pieces:
        full = lax.dynamic_update_slice(full, piece, (at, 0))
        at += piece.shape[0]
    return full


def after(value, *others):
    return lax.optimization_barrier((value, *others))[0]


def per_device(
    ring_size,
    layer_input,
    proj_weight,
    conv_weight,
    persist_kv,
    memory_in,
    memory_out,
    memory_gate,
    out_weight,
    ffn_in,
    ffn_out,
    norm_gains,
    seq_len,
    out_grad,
):
    rows, width = layer_input.shape
    cols = proj_weight.shape[2]
    heads = persist_kv.shape[1]
    head_size = persist_kv.shape[3]
    shift = head_size.bit_length() - 1
    mem_hid = memory_in.shape[2]
    nb = rows // SPAN
    taps = conv_weight.shape[1]
    me = lax.axis_index("head")
    count = width // cols
    peers = jnp.stack([me, me ^ 1, me ^ 2, me ^ 3]).astype(jnp.int32)
    swap = lambda a, bit: lax.ppermute(a, "head", [(i, i ^ bit) for i in range(count)])
    far_weight, far_cot = swap(out_weight, 2), swap(out_grad, 2)
    near_weight, near_cot = swap(out_weight, 1), swap(out_grad, 1)
    gate = jnp.transpose(memory_gate, (1, 2, 0))
    groups = [list(range(nb - 1)), [nb - 1]] if nb > 1 else [[0]]
    state = [memory_in.reshape(cols, mem_hid)]
    state.append(jnp.transpose(memory_out, (0, 2, 1)).reshape(cols, mem_hid))
    states = [dict(a=state[0], bt=state[1], sa=None, sbt=None)]
    earlier = gathered = [near_weight, near_cot, far_weight]
    shared, carried, pieces = None, [], []
    for n, blocks in enumerate(groups):
        if n:
            state = [after(state[0], peers, *earlier), *state[1:]]
        shared, (mixed, pers_low, flat, pers), squares, carried = lead_call(
            blocks, nb, shift, seq_len, layer_input, proj_weight, conv_weight, norm_gains, gate,
            persist_kv, state, carried, shared,
        )
        for a, bt, sa, sbt, ga, gbt in squares:
            states[-1].update(ga=ga, gbt=gbt)
            states.append(dict(a=a, bt=bt, sa=sa, sbt=sbt))
            state = [a, bt] if blocks[-1] + 1 == nb - 1 else [a, bt, sa, sbt]
        sent = after(mixed, *gathered)
        pieces.append([mixed, swap(sent, 1), swap(sent, 2)])
        gathered = pieces[n][1:]
        if n == 0:
            last_weight = swap(after(far_weight, sent), 1)
            last_cot = swap(after(far_cot, sent), 1)
            gathered = gathered + [last_weight, last_cot]
    q, k, v, kt, pre, gp, nl, mean, lg, tot, att, lt = shared
    for state in states:
        state["lg"] = lg
    gate = flat
    ow = (out_weight, near_weight, far_weight, last_weight)
    if nb > 1:
        pieces[0].append(swap(after(pieces[0][2], pieces[1][0]), 1))
    fout = after(ffn_out, pieces[-1][0])
    cot_full, d_hidden = cot_call(peers, (out_grad, near_cot, far_cot, last_cot), fout)
    pieces[-1].append(swap(after(pieces[-1][2], cot_full), 1))
    normed_two, hidden, dgu, mixed_full, residual, grads_room = ffn_call(
        groups, peers, after(layer_input, cot_full), pieces, ow, norm_gains, ffn_in, d_hidden
    )
    along_rows = (((0,), (0,)), ((), ()))
    outer = lambda left, right: lax.dot_general(
        left, right, along_rows, preferred_element_type=F32
    ).astype(BF16)
    out_part = outer(hidden, cot_full)
    ffn_grads = stacked_rows(
        [out_part, outer(after(normed_two, out_part), dgu[0]), outer(normed_two, dgu[1])],
        grads_room,
    )
    ffn_part = ring_scatter(ffn_grads, "dp", ring_size)
    s1, r2, gain_two = [], [], None
    tie = (ffn_grads,)
    for n, blocks in enumerate(reversed(groups)):
        gain_two, keep, send = ffn_back_call(
            blocks, peers, after(dgu, *tie), ffn_in, residual, gain_two
        )
        send = after(send, *r2) if r2 else send
        s1.append((keep.astype(F32) + swap(send, 1).astype(F32)).astype(BF16))
        r2.append(swap(s1[n], 2))
        tie = (s1[0],)
    tie = (gain_two,)
    back = unprep = None
    gated = [None] * nb

    def relayed(n, *ties):
        return s1[n], r2[n], swap(after(s1[n], *ties), 1), swap(after(r2[n], *ties), 1)

    def turn(c, spot, parts, turned, *ties):
        turned, gated[c] = turn_call(
            c, spot, peers, parts, after(residual, *ties), cot_full, ow, norm_gains, gp, tot, turned
        )
        return turned

    turned = turn(nb - 1, 0, relayed(0, r2[0]), None, *tie)
    tie = tuple(s1[1:])
    for c in reversed(range(nb)):
        back_args = (
            seq_len, after(q, *tie), k, v, kt, pers_low, gated[c][0], att, lt, states[c], back, back
        )
        rest = (
            gated[c][1], pre, proj_weight, conv_weight, layer_input, norm_gains, gate, mean, pers,
            gain_two, unprep,
        )
        if c == nb - 1:
            back = back_call(c, nb, shift, *back_args)
            parts = relayed(1, back["dq"]) if c else None
            unprep = unprep_call(c, nb, shift, seq_len, peers, back, *rest)
        else:
            back, unprep = rear_call(c, nb, shift, back_args, peers, *rest)
        tie = ()
        if c:
            turned = turn(c - 1, c - 1, parts, turned, unprep["edge"])
        if c == nb - 1:
            edge, ffn_part = lax.optimization_barrier((turned[2], ffn_part))
            turned[2] = edge
            ffn_grads = ring_gather(ffn_part, "dp", ring_size)
            tie = (edge,)
    d_res, res_cols, d_branch, d_gate_all = turned
    gains = unprep["gains"]
    gains = gains + sum(swap(gains, bit) for bit in (1, 2, 3))
    cuts = [4 * width, width, 2 * cols, 16 * width // cols, 16, pers.shape[1] * 2]
    cuts.append(2 * width // cols)
    payload = stacked_rows(
        [outer(nl, unprep["dproj"][i]) for i in range(4)]
        + [outer(mixed_full, d_branch)],
        unprep["small"],
    )
    payload = lax.dynamic_update_slice(
        payload, gains.reshape(-1, cols).astype(BF16), (sum(cuts[:-1]), 0)
    )
    tie = (payload,)
    payload, ffn_grads = lax.optimization_barrier((payload, ffn_grads))
    ffn_in_grad = ffn_grads[width:].astype(F32).reshape(2, width, -1)
    ffn_out_grad = ffn_grads[:width].astype(F32)
    payload = ring_scatter(payload, "dp", ring_size)
    half = (
        unprep["keep"].astype(F32) + swap(after(unprep["send"], *tie), 1).astype(F32)
    ).astype(BF16)
    inner = unprep["inner"] + swap(unprep["inner"], 1)
    far = swap(half[1], 2)
    input_grad = finish_call(
        peers, layer_input, d_res, half, far, inner, swap(inner, 2), norm_gains
    )
    part_keep, part_send = down_call(peers, after(hidden, half), ffn_out, cols)
    payload, input_grad, ffn_in_grad, ffn_out_grad, part_keep, part_send = (
        lax.optimization_barrier(
            (payload, input_grad, ffn_in_grad, ffn_out_grad, part_keep, part_send)
        )
    )
    payload = ring_gather(payload, "dp", ring_size)
    part = (part_keep.astype(F32) + swap(part_send, 1).astype(F32)).astype(BF16)
    layer_output = res_cols + part[0].astype(F32) + swap(part[1], 2).astype(F32)
    layer_output = layer_output.astype(BF16)
    proj_grad, out_grads, a_grad, b_grad, gate_grad, conv_grad, pers_grad, gains = unpack_call(
        payload, shift, width, mem_hid, taps, persist_kv.shape[2]
    )
    return (
        layer_output,
        input_grad,
        proj_grad,
        conv_grad,
        pers_grad,
        a_grad,
        jnp.transpose(b_grad, (0, 2, 1)),
        jnp.transpose(gate_grad, (2, 0, 1)),
        out_grads,
        ffn_in_grad,
        ffn_out_grad,
        gains,
    )


def solution(mesh):
    in_specs = (
        P("dp", None),
        P(None, None, "head"),
        P(None, None, "head"),
        P(None, "head", None, None),
        P("head", None, None),
        P("head", None, None),
        P(None, None, "head"),
        P(None, "head"),
        P(None, None, "head"),
        P("head", None),
        P(),
        P("dp"),
        P("dp", "head"),
    )
    out_specs = (
        P("dp", "head"),
        P("dp", "head"),
        P(None, None, "head"),
        P(None, None, "head"),
        P(None, "head", None, None),
        P("head", None, None),
        P("head", None, None),
        P(None, None, "head"),
        P(None, "head"),
        P(None, None, "head"),
        P("head", None),
        P(),
    )
    body = functools.partial(per_device, mesh.shape["dp"])
    return jax.shard_map(
        body, mesh=mesh, in_specs=in_specs, out_specs=out_specs, check_vma=False
    )
```
